32 devices in a mesh: dp: 16 (over z, y, x), rep: 2 (over core).
Axes of the slice: x: 2, y: 2, z: 4, core: 2. Of those that a mesh axis runs over, the one named last changes fastest.
Arguments:
- table: float32 [131072, 400], P(('dp', 'rep')), may hold values from -6 to 6
- batch_index: int32 [32768], P(('dp', 'rep')), may hold values from 0 to 4095
- labels: int32 [32768], P(('dp', 'rep')), may hold values from 0 to 46
- w_branch: float32 [4, 100, 512], P(None, None, 'dp'), may hold values from -0.625 to 0.625
- w_merge: float32 [2048, 512], P('dp'), may hold values from -0.125 to 0.125
- w_class: float32 [512, 47], P('dp'), may hold values from -0.5 to 0.5
- small_params: float32 [20, 512], P(None, 'dp'), as said below
- first_branch: float32 [4, 100, 512], P(None, None, 'dp'), may hold values from -0.0014648438 to 0.0014648438
- first_merge: float32 [2048, 512], P('dp'), may hold values from -0.0014648438 to 0.0014648438
- first_class: float32 [512, 47], P('dp'), may hold values from -0.0014648438 to 0.0014648438
- first_small: float32 [20, 512], P(None, 'dp'), may hold values from -0.00390625 to 0.00390625
- second_branch: float32 [4, 100, 512], P(None, None, 'dp'), may hold values from 7.7659046e-10 to 3.1063618e-09
- second_merge: float32 [2048, 512], P('dp'), may hold values from 7.7659046e-10 to 3.1063618e-09
- second_class: float32 [512, 47], P('dp'), may hold values from 7.7659046e-10 to 3.1063618e-09
- second_small: float32 [20, 512], P(None, 'dp'), may hold values from 6.989314e-09 to 2.7957256e-08
Outputs:
- new_branch: float32 [4, 100, 512], P(None, None, 'dp')
- new_merge: float32 [2048, 512], P('dp')
- new_class: float32 [512, 47], P('dp')
- new_small: float32 [20, 512], P(None, 'dp')
- moment_branch: float32 [4, 100, 512], P(None, None, 'dp')
- moment_merge: float32 [2048, 512], P('dp')
- moment_class: float32 [512, 47], P('dp')
- moment_small: float32 [20, 512], P(None, 'dp')
- square_branch: float32 [4, 100, 512], P(None, None, 'dp')
- square_merge: float32 [2048, 512], P('dp')
- square_class: float32 [512, 47], P('dp')
- square_small: float32 [20, 512], P(None, 'dp')
- copy_branch: bfloat16 [4, 100, 512], P(None, None, 'dp')
- copy_merge: bfloat16 [2048, 512], P('dp')
- copy_class: bfloat16 [512, 47], P('dp')
- copy_small: bfloat16 [20, 512], P(None, 'dp')
- grad_norm: float32 [], replicated
- row_grads: float32 [32768, 400], P(('dp', 'rep'))
The draws below stay inside these ranges and needn't reach their ends.
Inputs may be any that keep to these rules, and one draw needn't show every extreme that they name: `batch_index`: each entry indexes a row of the block of 4096 table rows that lies on the same device as the entry. `small_params`: gains lie in 0.3 to 2.0, slopes in 0.05 to 0.45.
All inputs are finite; a program needn't handle non-finite values.
Results may differ from the reference program's by a relative error of at most 0.011.
Values may be sent and summed in bfloat16 or wider, within the bound.
No kernel may reach another device: no remote copies, remote signals or barrier semaphores. Data moves between devices by JAX's collectives and lax.ppermute only.
A program may use at most 128 MiB of HBM per device.

```python
import math
import jax
import jax.numpy as jnp
from jax import lax

HOPS = 4
D_IN = 100
HID = 512
CLS = 47
STEP = 7
B_DEV = 1024
NODE_DEV = 4096
SMALL = 20
PARAMS = 1287680
BATCH = 32768
NODES = 131072


def draw_small_params(key, part):
    keys = jax.random.split(jax.random.fold_in(key, 7), 8)
    place = jnp.arange(HOPS * HID, dtype=jnp.float32) / (HOPS * HID - 1)
    base = 0.45 + place
    jitter = jax.random.uniform(keys[7], (HOPS * HID,), jnp.float32, 0.9, 1.1)
    gain_rows = (base * jitter).reshape(HOPS, HID)
    shift_rows = 0.3 * jax.random.normal(keys[1], (HOPS, HID), jnp.float32)
    slope_rows = jax.random.uniform(keys[2], (2 * HOPS, HID), jnp.float32, 0.05, 0.45)
    gain_two = 1.0 + 0.3 * jax.random.uniform(keys[3], (1, HID), jnp.float32, -1.0, 1.0)
    shift_two = 0.3 * jax.random.normal(keys[4], (1, HID), jnp.float32)
    slope_two = jax.random.uniform(keys[5], (1, HID), jnp.float32, 0.05, 0.45)
    bias_row = 0.5 * jax.random.normal(keys[6], (1, HID), jnp.float32)
    return jnp.concatenate([gain_rows, shift_rows, slope_rows, gain_two, shift_two, slope_two, bias_row], axis=0)


def with_ends(result, key, least, top_value):
    longest = result.shape.index(max(result.shape))
    spots = []
    for shift in (0, 1):
        where = [jax.random.randint(jax.random.fold_in(key, axis), (), 0, length) for axis, length in enumerate(result.shape)]
        where[longest] = (where[longest] + shift) % result.shape[longest]
        spots.append(tuple(where))
    return result.at[spots[0]].set(least).at[spots[1]].set(top_value)


def levels(stream_key, extent, cuts, smallest, largest):
    def one(dim, parts):
        draws = jax.random.uniform(jax.random.fold_in(jax.random.fold_in(stream_key, 6), dim), (parts,), jnp.float32, smallest / len(cuts), largest / len(cuts))
        return jnp.repeat(jnp.exp(draws), extent[dim] // parts).reshape((-1,) + (1,) * (len(extent) - dim - 1))

    level = one(*cuts[0])
    for cut in cuts[1:]:
        level = level * one(*cut)
    return level


def centred(own_key, shape, spread, reach, cuts=(), held_as=jnp.bfloat16):
    values = spread * jax.random.normal(own_key, shape, jnp.float32)
    if cuts:
        values = values * levels(own_key, shape, cuts, -0.22, 0.18)
    return jnp.clip(values, -reach, reach).astype(held_as)


def setup_inputs(seed: int = 0) -> dict:
    key_list = jax.random.split(jax.random.key(seed), 16)
    table = centred(key_list[0], (NODES, HOPS * D_IN), 1.0, 6.0, ((0, 32),), jnp.float32)
    batch_index = with_ends(jax.random.randint(key_list[1], (BATCH,), 0, NODE_DEV), jax.random.fold_in(key_list[1], 1), 0, NODE_DEV - 1).astype(jnp.int32)
    labels = with_ends(jax.random.randint(key_list[2], (BATCH,), 0, CLS), jax.random.fold_in(key_list[2], 1), 0, CLS - 1).astype(jnp.int32)
    w_branch = centred(key_list[3], (HOPS, D_IN, HID), D_IN ** -0.5, 0.625, ((2, 16),), jnp.float32)
    w_merge = centred(key_list[4], (HOPS * HID, HID), (HOPS * HID) ** -0.5, 0.125, ((0, 16),), jnp.float32)
    w_class = centred(key_list[5], (HID, CLS), (HID // 4) ** -0.5, 0.5, ((0, 16),), jnp.float32)
    small_params = draw_small_params(jax.random.fold_in(key_list[15], 71), 0)
    first_branch = centred(key_list[7], (HOPS, D_IN, HID), (0.11 / PARAMS ** 0.5), 0.0014648438, ((2, 16),), jnp.float32)
    first_merge = centred(key_list[8], (HOPS * HID, HID), (0.11 / PARAMS ** 0.5), 0.0014648438, ((0, 16),), jnp.float32)
    first_class = centred(key_list[9], (HID, CLS), (0.11 / PARAMS ** 0.5), 0.0014648438, ((0, 16),), jnp.float32)
    first_small = centred(key_list[10], (SMALL, HID), (0.33 / PARAMS ** 0.5), 0.00390625, ((1, 16),), jnp.float32)
    second_branch = jnp.clip(jnp.exp(math.log(3.1063618344262522e-09) - 1.3862944 * jax.random.uniform(key_list[11], (HOPS, D_IN, HID), jnp.float32) ** levels(key_list[11], (HOPS, D_IN, HID), ((2, 16),), -0.2, 0.2)), 7.765904586065631e-10, 3.1063618344262522e-09)
    second_merge = jnp.clip(jnp.exp(math.log(3.1063618344262522e-09) - 1.3862944 * jax.random.uniform(key_list[12], (HOPS * HID, HID), jnp.float32) ** levels(key_list[12], (HOPS * HID, HID), ((0, 16),), -0.2, 0.2)), 7.765904586065631e-10, 3.1063618344262522e-09)
    second_class = jnp.clip(jnp.exp(math.log(3.1063618344262522e-09) - 1.3862944 * jax.random.uniform(key_list[13], (HID, CLS), jnp.float32) ** levels(key_list[13], (HID, CLS), ((0, 16),), -0.2, 0.2)), 7.765904586065631e-10, 3.1063618344262522e-09)
    second_small = jnp.clip(jnp.exp(math.log(2.795725606574706e-08) - 1.3862944 * jax.random.uniform(key_list[14], (SMALL, HID), jnp.float32) ** levels(key_list[14], (SMALL, HID), ((1, 16),), -0.2, 0.2)), 6.989314016436765e-09, 2.795725606574706e-08)
    return dict(table=table, batch_index=batch_index, labels=labels, w_branch=w_branch, w_merge=w_merge, w_class=w_class, small_params=small_params, first_branch=first_branch, first_merge=first_merge, first_class=first_class, first_small=first_small, second_branch=second_branch, second_merge=second_merge, second_class=second_class, second_small=second_small)


@jax.custom_vjp
def low(v):
    return lax.optimization_barrier(v.astype(jnp.bfloat16)).astype(jnp.float32)

@jax.custom_vjp
def low_back(v):
    return v

def low_keep(v):
    return (low(v), None)

def low_pass(kept, grad):
    return (grad,)

def back_keep(v):
    return (v, None)

def back_low(kept, grad):
    return (low(grad),)
low.defvjp(low_keep, low_pass)
low_back.defvjp(back_keep, back_low)
EPS_NORM = 1e-05
HIGHEST_ACCURACY = lax.Precision.HIGHEST

def leaky(value, slope):
    return slope * value + (1.0 - slope) * value * jax.nn.sigmoid(value)

def batch_norm(pre):
    mean = lax.optimization_barrier(jnp.mean(pre, axis=0))
    var = lax.optimization_barrier(jnp.mean(pre * pre, axis=0)) - mean * mean
    return (pre - mean) * lax.rsqrt(var + EPS_NORM)

def forward(rows, w_branch, w_merge, w_class, small_params, labels):
    entry_count = rows.shape[0]
    input_features = low(rows).reshape(entry_count, HOPS, D_IN)
    branch_weight = low(w_branch)
    merge_weight = low(w_merge)
    class_weight = low(w_class)
    params = low(small_params)
    hidden_width = HOPS * HID
    gain1 = params[0:HOPS].reshape(hidden_width)
    shift1 = params[HOPS:2 * HOPS].reshape(hidden_width)
    slope1 = params[2 * HOPS:3 * HOPS].reshape(hidden_width)
    slope_join = params[3 * HOPS:4 * HOPS].reshape(hidden_width)
    gain2 = params[4 * HOPS]
    shift2 = params[4 * HOPS + 1]
    slope2 = params[4 * HOPS + 2]
    bias3 = params[4 * HOPS + 3, :CLS]
    first_pre = low_back(jnp.einsum('fsq,sqv->fsv', input_features, branch_weight, precision=HIGHEST_ACCURACY)).reshape(entry_count, hidden_width)
    act1 = leaky(gain1 * batch_norm(first_pre) + shift1, slope1)
    joined = leaky(act1, slope_join)
    pre2 = low_back(jnp.dot(low(joined), merge_weight, precision=HIGHEST_ACCURACY))
    act2 = leaky(gain2 * batch_norm(pre2) + shift2, slope2)
    logits = low_back(jnp.dot(low(act2), class_weight, precision=HIGHEST_ACCURACY) + bias3)
    total = jax.nn.logsumexp(logits, axis=1)
    picked = jnp.take_along_axis(logits, labels[:, None], axis=1)[:, 0]
    return jnp.sum(total - picked)

def adamw(weight, grad, moment, square, scale, rate):
    clipped = grad * scale
    moment_new = 0.9 * moment + 0.1 * clipped
    square_new = 0.999 * square + 0.001 * clipped * clipped
    fix_one = 1.0 - 0.9 ** STEP
    fix_two = 1.0 - 0.999 ** STEP
    update = moment_new / fix_one / (jnp.sqrt(square_new / fix_two) + 1e-08) + 0.01 * weight
    weight_new = weight - rate * update
    return (weight_new, moment_new, square_new)

def reference(table, batch_index, labels, w_branch, w_merge, w_class, small_params, first_branch, first_merge, first_class, first_small, second_branch, second_merge, second_class, second_small):
    owner = jnp.arange(BATCH, dtype=jnp.int32) // B_DEV
    rows = table[(owner * NODE_DEV + batch_index).astype(jnp.int32)]

    def loss_of(rows_in, branch_weight, merge_weight, class_weight, small_in):
        return forward(rows_in, branch_weight, merge_weight, class_weight, small_in, labels)
    loss, pullback = jax.vjp(loss_of, rows, w_branch, w_merge, w_class, small_params)
    grad_rows, branch_gradient, grad_merge, grad_class, grad_small = pullback(jnp.ones((), rows.dtype))
    grads = (branch_gradient, grad_merge, grad_class, grad_small)
    total = jnp.zeros((), rows.dtype)
    for grad in grads:
        total = total + jnp.sum(grad * grad)
    grad_norm = jnp.sqrt(total)
    scale = 1.0 / jnp.maximum(grad_norm, 1.0)
    weights = (w_branch, w_merge, w_class, small_params)
    firsts = (first_branch, first_merge, first_class, first_small)
    seconds = (second_branch, second_merge, second_class, second_small)
    rates = (0.05, 0.05, 0.05, 0.3)
    results = [adamw(w, g, m, v, scale, r) for w, g, m, v, r in zip(weights, grads, firsts, seconds, rates)]
    news = tuple((r[0] for r in results))
    moments = tuple((r[1] for r in results))
    squares = tuple((r[2] for r in results))
    copies = tuple((r.astype(jnp.bfloat16) for r in news))
    return (news[0], news[1], news[2], news[3], moments[0], moments[1], moments[2], moments[3], squares[0], squares[1], squares[2], squares[3], copies[0], copies[1], copies[2], copies[3], grad_norm, grad_rows)
```

```python
import functools

import jax
import jax.numpy as jnp
from jax import lax
from jax.experimental import pallas as pl
from jax.experimental.pallas import tpu as pltpu
from jax.sharding import PartitionSpec as P

HOPS = 4
STEP = 7
EPS_NORM = 1e-05
LANES = 128
PCOL = 64
BOTH = ("dp", "rep")
F32 = jnp.float32
BF16 = jnp.bfloat16
HIGHEST = lax.Precision.HIGHEST


def dot(left, right, left_dim, right_dim, precision=None):
    return lax.dot_general(
        left,
        right,
        (((left_dim,), (right_dim,)), ((), ())),
        precision=precision,
        preferred_element_type=F32,
    )


def call(body, outs, *args, smem=(), grid=None, in_specs=None, out_specs=None, scratch=(), mib=40, flops=0, moved=0):
    if in_specs is None:
        in_specs = [
            pl.BlockSpec(memory_space=pltpu.SMEM if i in smem else pltpu.VMEM) for i in range(len(args))
        ]
    if out_specs is None:
        out_specs = tuple(pl.BlockSpec(memory_space=pltpu.VMEM) for _ in outs)
    if not moved:
        moved = sum(a.size * a.dtype.itemsize for a in args)
        moved += sum(o.size * o.dtype.itemsize for o in outs)
    kwargs = {} if grid is None else {"grid": grid}
    return pl.pallas_call(
        body,
        out_shape=tuple(outs),
        in_specs=in_specs,
        out_specs=out_specs,
        scratch_shapes=list(scratch),
        compiler_params=pltpu.CompilerParams(vmem_limit_bytes=mib << 20),
        cost_estimate=pl.CostEstimate(flops=flops, bytes_accessed=moved, transcendentals=0),
        **kwargs,
    )(*args)


def sds(shape, dtype=F32):
    return jax.ShapeDtypeStruct(shape, dtype)


def lane_of(shape):
    return lax.broadcasted_iota(jnp.int32, shape, len(shape) - 1)


def to_cols(rows, first):
    parts = []
    for i in range(4):
        row = rows[first + i : first + i + 1, :]
        parts.append(jnp.transpose(jnp.broadcast_to(row, (LANES, LANES))))
    return jnp.concatenate(parts, axis=0)


def lane_sums(part):
    total = jnp.sum(jnp.transpose(part), axis=0, keepdims=True)
    return jnp.concatenate([total[:, i * LANES : (i + 1) * LANES] for i in range(4)], axis=0)


def fold_lanes(value):
    out = value[:, :LANES]
    for i in range(1, value.shape[1] // LANES):
        out = out + value[:, i * LANES : (i + 1) * LANES]
    return out


def prep_kernel(pos_ref, wb_ref, wc_ref, sp_ref, wm_ref, pack_ref, wmh_ref):
    cb = wc_ref.shape[0]
    d_in = wb_ref.shape[2]
    half = wmh_ref.shape[1]
    pack_ref[...] = jnp.zeros_like(pack_ref)
    pack_ref[0:HOPS, :, 0:d_in] = wb_ref[...].astype(BF16)
    pack_ref[HOPS, :, 0 : wc_ref.shape[1]] = wc_ref[...].astype(BF16)
    pack_ref[HOPS, :, PCOL : PCOL + sp_ref.shape[0]] = jnp.transpose(sp_ref[...]).astype(BF16)
    first = pos_ref[1] == 0
    wmh_ref[...] = jnp.where(first, wm_ref[:, :half], wm_ref[:, half:]).astype(BF16)


def gather_kernel(idx_ref, tab_ref, x_ref, gram_ref, acc, pad):
    i = pl.program_id(0)
    width = tab_ref.shape[1]
    d_in = tab_ref.shape[0] // HOPS
    batch = idx_ref.shape[1]
    rows = lax.broadcasted_iota(jnp.int32, (width, batch), 0) + i * width
    hot = jnp.where(rows == idx_ref[...], 1.0, 0.0).astype(BF16)
    part = dot(tab_ref[...].astype(BF16), hot, 1, 0)

    @pl.when(i == 0)
    def _():
        acc[...] = part

    @pl.when(i > 0)
    def _():
        acc[...] += part

    @pl.when(i == pl.num_programs(0) - 1)
    def _():
        row = lax.broadcasted_iota(jnp.int32, pad.shape, 0)
        pad[...] = jnp.where(row == d_in, 1.0, 0.0)
        for k in range(HOPS):
            pad[0:d_in, :] = acc[k * d_in : (k + 1) * d_in, :]
            x = pad[...].astype(BF16)
            x_ref[k] = x
            gram_ref[k] = dot(x, x, 1, 1)


def sum_spread_kernel(in_ref, out_ref):
    out_ref[...] = jnp.broadcast_to(jnp.sum(in_ref[...], axis=0, keepdims=True), out_ref.shape)


def stats_kernel(count, pos_ref, gram_ref, pack_ref, wb_ref, wc_ref, coef_ref, par_ref, tail):
    dp, _, cb, _ = pack_ref.shape
    lane = lane_of((cb * dp, LANES))
    for s in range(dp):
        if dp == 16:
            other = s ^ pos_ref[0]
            j = (other % 4) * 4 + other // 4
        else:
            j = s
        block = pack_ref[j]
        for k in range(HOPS):
            wb_ref[k, s * cb : (s + 1) * cb, :] = block[k]
        tail[s * cb : (s + 1) * cb, :] = block[HOPS].astype(F32)
    small = tail[...]
    wc_ref[...] = jnp.where(lane < PCOL, small, 0.0).astype(BF16)

    def col(i):
        return small[:, PCOL + i : PCOL + i + 1]

    par = jnp.where(lane == 0, col(4 * HOPS), 0.0)
    for i in range(1, 4):
        par = jnp.where(lane == i, col(4 * HOPS + i), par)
    par_ref[...] = par
    for k in range(HOPS):
        w = wb_ref[k].astype(F32)
        wg = dot(w, gram_ref[k], 1, 0, HIGHEST)
        mean = wg[:, ONE : ONE + 1] / count
        second = jnp.sum(wg * w, axis=1, keepdims=True) / count
        inv = lax.rsqrt(second - mean * mean + EPS_NORM)
        gain, shift, slope, join = col(k), col(HOPS + k), col(2 * HOPS + k), col(3 * HOPS + k)
        v = gain * inv
        values = (
            0.5 * v,
            0.5 * (shift - v * mean),
            1.0 + slope,
            1.0 - slope,
            1.0 + join,
            1.0 - join,
            v,
            mean,
            inv,
        )
        coef = jnp.where(lane == 0, values[0], 0.0)
        for i in range(1, len(values)):
            coef = jnp.where(lane == i, values[i], coef)
        coef_ref[k] = coef


ONE = 100


def shard_at(pos_ref, s, dp):
    if dp != 16:
        return s
    other = s ^ pos_ref[0]
    return (other % 4) * 4 + other // 4


ROWS = 16
WIDE = 256


def forward_kernel(pos_ref, x_ref, wb_ref, coef_ref, mine_ref, other_ref, joined_ref, pre2_ref, pay_ref, pre):
    k = pl.program_id(0)
    hid = wb_ref.shape[1]
    batch = x_ref.shape[2]
    half = mine_ref.shape[2]
    pre[...] = dot(wb_ref[0], x_ref[0], 1, 0)

    def group(g, carry):
        at = pl.ds(pl.multiple_of(g * ROWS, ROWS), ROWS)
        cf = coef_ref[0, at, :]
        c = [jnp.broadcast_to(cf[:, i : i + 1], (ROWS, WIDE)) for i in range(6)]
        for b in range(batch // WIDE):
            lanes = slice(b * WIDE, (b + 1) * WIDE)
            u = pre[at, lanes] * c[0] + c[1]
            u = u * (c[2] + c[3] * jnp.tanh(u)) * 0.5
            joined_ref[0, at, lanes] = (u * (c[4] + c[5] * jnp.tanh(u))).astype(BF16)
        return carry

    lax.fori_loop(0, hid // ROWS, group, 0, unroll=2)
    joined = joined_ref[0]
    for ref, which in ((mine_ref, pos_ref[1]), (other_ref, 1 - pos_ref[1])):
        at = pl.ds(pl.multiple_of(which * half, half), half)
        part = dot(merge_at(ref, pos_ref, k), joined, 0, 0)

        @pl.when(k == 0)
        def _():
            pre2_ref[at, :] = part

        @pl.when(k > 0)
        def _():
            pre2_ref[at, :] += part

    @pl.when(k == HOPS - 1)
    def _():
        value = pre2_ref[...]
        sums = jnp.concatenate([lane_sums(fold_lanes(value)), lane_sums(fold_lanes(value * value))], axis=0)
        pay_ref[...] = jnp.broadcast_to(sums[None], pay_ref.shape)


def merge_at(ref, pos_ref, k):
    dp = ref.shape[0]
    per = dp // HOPS
    blocks = []
    for i in range(per):
        s = k * per + i
        blocks.append(ref[shard_at(pos_ref, s, dp)])
    return jnp.concatenate(blocks, axis=0)


def columns2(count, rows, par):
    mean = to_cols(rows, 0) / count
    inv = lax.rsqrt(to_cols(rows, 4) / count - mean * mean + EPS_NORM)
    shape = mean.shape
    gain = jnp.broadcast_to(par[:, 0:1], shape)
    shift = jnp.broadcast_to(par[:, 1:2], shape)
    slope = jnp.broadcast_to(par[:, 2:3], shape)
    return mean, inv, gain, shift, slope


def head_kernel(
    count, classes, got_ref, pre2_ref, par_ref, wc_ref, lab_ref, dy2_ref, pay_ref, class_ref, stat_ref, act, dact, cols, sums
):
    hid, batch = pre2_ref.shape
    par = par_ref[...]
    mean, inv, gain, shift, slope = columns2(count, jnp.sum(got_ref[...], axis=0), par)
    stat_ref[0] = mean
    stat_ref[1] = inv
    cols[0] = 0.5 * gain * inv
    cols[1] = 0.5 * (shift - gain * inv * mean)
    cols[2] = 1.0 + slope
    cols[3] = 1.0 - slope
    reps = WIDE // LANES

    def tiled(c, at):
        return jnp.concatenate([cols[c, at, :]] * reps, axis=1)

    def first(g, carry):
        at = pl.ds(pl.multiple_of(g * ROWS, ROWS), ROWS)
        c = [tiled(i, at) for i in range(4)]
        for b in range(batch // WIDE):
            lanes = slice(b * WIDE, (b + 1) * WIDE)
            u = pre2_ref[at, lanes] * c[0] + c[1]
            act[at, lanes] = (u * (c[2] + c[3] * jnp.tanh(u))).astype(BF16)
        return carry

    lax.fori_loop(0, hid // ROWS, first, 0, unroll=2)
    logits = dot(wc_ref[...], act[...], 0, 0)
    row = lax.broadcasted_iota(jnp.int32, (LANES, batch), 0)
    logits = jnp.where(row < classes, logits + par[0:LANES, 3:4], -jnp.inf)
    top = jnp.max(logits, axis=0, keepdims=True)
    e = jnp.exp(logits - top)
    probs = e / jnp.sum(e, axis=0, keepdims=True)
    dlog = (probs - jnp.where(row == lab_ref[...], 1.0, 0.0)).astype(BF16)
    grad_class = dot(act[...], dlog, 1, 1)
    bias = jnp.sum(dlog.astype(F32), axis=1, keepdims=True)
    dact[...] = dot(wc_ref[...], dlog, 1, 0)

    def second(g, carry):
        at = pl.ds(pl.multiple_of(g * ROWS, ROWS), ROWS)
        c = [tiled(i, at) for i in range(4)]
        m = jnp.concatenate([stat_ref[0, at, :]] * reps, axis=1)
        v = jnp.concatenate([stat_ref[1, at, :]] * reps, axis=1)
        acc = [jnp.zeros((ROWS, WIDE), F32) for _ in range(3)]
        for b in range(batch // WIDE):
            lanes = slice(b * WIDE, (b + 1) * WIDE)
            p = pre2_ref[at, lanes]
            d = dact[at, lanes]
            u = p * c[0] + c[1]
            t = jnp.tanh(u)
            w = u * (1.0 - t)
            dy = d * (0.5 * (c[2] + c[3] * (t + w * (1.0 + t))))
            dy2_ref[at, lanes] = dy
            acc[0] = acc[0] + dy
            acc[1] = acc[1] + dy * ((p - m) * v)
            acc[2] = acc[2] + d * w
        for i in range(3):
            sums[i, at, :] = fold_lanes(acc[i])
        return carry

    lax.fori_loop(0, hid // ROWS, second, 0, unroll=2)
    pay = jnp.concatenate([lane_sums(sums[0]), lane_sums(sums[1])], axis=0)
    pay_ref[...] = jnp.broadcast_to(pay[None], pay_ref.shape)
    lane = lane_of((hid, LANES))
    slope_sum = jnp.sum(sums[2], axis=1, keepdims=True)
    bias = jnp.concatenate([bias, jnp.zeros((hid - LANES, 1), F32)], axis=0)
    block = jnp.where(lane < classes, grad_class, 0.0)
    block = jnp.where(lane == PCOL, slope_sum, block)
    class_ref[...] = jnp.where(lane == PCOL + 1, bias, block)


def turn_kernel(count, pos_ref, got_ref, stat_ref, par_ref, pre2_ref, dy2_ref, joined_ref, class_ref, dpre_ref, keep_ref, send_ref, sum2_ref, cols):
    hid, batch = pre2_ref.shape
    half = keep_ref.shape[2]
    dp, rows, _ = keep_ref.shape
    mr = joined_ref.shape[0] // dp
    cb = hid // dp
    rows8 = jnp.sum(got_ref[...], axis=0)
    sum2_ref[...] = rows8
    shift_sum = to_cols(rows8, 0)
    gain_sum = to_cols(rows8, 4)
    mean, inv = stat_ref[0], stat_ref[1]
    v = jnp.broadcast_to(par_ref[:, 0:1], mean.shape) * inv
    cols[0] = v
    cols[1] = v * shift_sum / count
    cols[2] = v * inv * gain_sum / count
    reps = WIDE // LANES

    def group(g, carry):
        at = pl.ds(pl.multiple_of(g * ROWS, ROWS), ROWS)
        c = [jnp.concatenate([cols[i, at, :]] * reps, axis=1) for i in range(3)]
        m = jnp.concatenate([stat_ref[0, at, :]] * reps, axis=1)
        for b in range(batch // WIDE):
            lanes = slice(b * WIDE, (b + 1) * WIDE)
            value = c[0] * dy2_ref[at, lanes] - c[1] - (pre2_ref[at, lanes] - m) * c[2]
            dpre_ref[at, lanes] = value.astype(BF16)
        return carry

    lax.fori_loop(0, hid // ROWS, group, 0, unroll=2)
    mine = pl.multiple_of(pos_ref[1] * half, half)
    theirs = pl.multiple_of((1 - pos_ref[1]) * half, half)
    for s in range(dp):
        block = joined_ref[s * mr : (s + 1) * mr, :]
        keep_ref[s, 0:mr, :] = dot(block, dpre_ref[pl.ds(mine, half), :], 1, 1)
        send_ref[s, 0:mr, :] = dot(block, dpre_ref[pl.ds(theirs, half), :], 1, 1).astype(BF16)
    first = pos_ref[1] == 0
    for s in range(dp):
        block = class_ref[s * cb : (s + 1) * cb, :]
        wide = jnp.concatenate([block[: cb // 2], block[cb // 2 :]], axis=1)
        keep_ref[s, mr:rows, :] = jnp.where(first, wide, 0.0)
        send_ref[s, mr:rows, :] = jnp.where(first, 0.0, wide).astype(BF16)


def back_kernel(
    pos_ref, dpre_ref, x_ref, wb_ref, coef_ref, mine_ref, other_ref, b_ref, a_ref, pre, dj, dyv, sums, *, hop
):
    hid = wb_ref.shape[1]
    batch = x_ref.shape[2]
    half = mine_ref.shape[2]
    pre[...] = dot(wb_ref[hop], x_ref[hop], 1, 0)
    at0 = pl.ds(pl.multiple_of(pos_ref[1] * half, half), half)
    at1 = pl.ds(pl.multiple_of((1 - pos_ref[1]) * half, half), half)
    dj[...] = dot(merge_at(mine_ref, pos_ref, hop), dpre_ref[at0, :], 1, 0)
    dj[...] += dot(merge_at(other_ref, pos_ref, hop), dpre_ref[at1, :], 1, 0)

    def group(g, carry):
        at = pl.ds(pl.multiple_of(g * ROWS, ROWS), ROWS)
        cf = coef_ref[hop, at, :]
        c = [jnp.broadcast_to(cf[:, i : i + 1], (ROWS, WIDE)) for i in range(7)]
        scale = 0.25 * c[6]
        acc = [jnp.zeros((ROWS, WIDE), F32) for _ in range(2)]
        for b in range(batch // WIDE):
            lanes = slice(b * WIDE, (b + 1) * WIDE)
            u = pre[at, lanes] * c[0] + c[1]
            t = jnp.tanh(u)
            u2 = u * (c[2] + c[3] * t) * 0.5
            t2 = jnp.tanh(u2)
            d = dj[at, lanes]
            w2 = u2 * (1.0 - t2)
            acc[1] = acc[1] + d * w2
            d = d * (c[4] + c[5] * (t2 + w2 * (1.0 + t2)))
            w = u * (1.0 - t)
            acc[0] = acc[0] + d * w
            d = d * (c[2] + c[3] * (t + w * (1.0 + t)))
            dyv[at, lanes] = (d * scale).astype(BF16)
        for i in range(2):
            sums[i, at, :] = fold_lanes(acc[i])
        return carry

    lax.fori_loop(0, hid // ROWS, group, 0, unroll=2)
    lane = lane_of((hid, LANES))
    block = dot(dyv[...], x_ref[hop], 1, 1)
    block = jnp.where(lane == ONE + 1, 0.5 * jnp.sum(sums[0], axis=1, keepdims=True), block)
    block = jnp.where(lane == ONE + 2, jnp.sum(sums[1], axis=1, keepdims=True), block)
    dp = b_ref.shape[0]
    cb = hid // dp
    for s in range(dp):
        b_ref[s] = block[s * cb : (s + 1) * cb, :]
    a_ref[...] = dot(wb_ref[hop], dyv[...], 0, 0)


def split_low_kernel(pos_ref, keep_ref, got_ref, o0_ref, o1_ref, o2_ref, o3_ref):
    low = pos_ref[0] % 4
    for m, ref in enumerate((o0_ref, o1_ref, o2_ref, o3_ref)):
        for z in range(4):
            j = z * 4 + (low ^ m)
            ref[z] = (keep_ref[j] + got_ref[j].astype(F32)).astype(ref.dtype)


def split_high_kernel(pos_ref, own_ref, g1_ref, g2_ref, g3_ref, o0_ref, o1_ref, o2_ref, o3_ref):
    high = pos_ref[0] // 4
    for k, ref in enumerate((o0_ref, o1_ref, o2_ref, o3_ref)):
        j = high ^ k
        value = own_ref[j] + g1_ref[j].astype(F32) + g2_ref[j].astype(F32) + g3_ref[j].astype(F32)
        ref[...] = value.astype(ref.dtype)


def pick_kernel(pos_ref, a_ref, b_ref, c_ref, d_ref, keep_ref, send_ref):
    first = pos_ref[1] == 0
    refs = (a_ref, b_ref, c_ref, d_ref)
    for i in range(2):
        low, high = refs[i][...], refs[2 + i][...]
        keep_ref[:, i] = jnp.where(first, low, high)
        send_ref[:, i] = jnp.where(first, high, low)


def owner_kernel(
    count, classes, pos_ref, got_ref, w0_ref, w1_ref, w2_ref, w3_ref, pack_ref, coef_ref, gram_ref, sum2_ref,
    grad_ref, pay_ref,
):
    _, _, cb, _ = got_ref.shape
    total = jnp.sum(got_ref[...], axis=0)
    rep = pos_ref[1]
    start = pl.multiple_of(pos_ref[0] * cb, cb)
    lane = lane_of((cb, LANES))
    tail = pack_ref[HOPS].astype(F32)
    squares = jnp.zeros((1, 1), F32)
    spread = jnp.zeros((cb, LANES), F32)

    def all_sum(v):
        return jnp.sum(jnp.sum(v, axis=1, keepdims=True), axis=0, keepdims=True)

    for i in range(2):
        hop = rep * 2 + i
        b = total[i]
        coef = coef_ref[hop, pl.ds(start, cb), :]
        v, mean, inv = coef[:, 6:7], coef[:, 7:8], coef[:, 8:9]
        w = pack_ref[hop].astype(F32)
        gram = gram_ref[hop]
        s = b[:, ONE : ONE + 1]
        g = inv * (jnp.sum(jnp.where(lane < ONE, b * w, 0.0), axis=1, keepdims=True) - mean * s)
        beta = inv * g / count
        alpha = s / count - beta * mean
        wg = dot(w, gram, 1, 0, HIGHEST)
        fixed = jnp.where(lane < ONE, b - alpha * gram[ONE : ONE + 1, :] - beta * wg, 0.0)
        fixed = jnp.where(lane == ONE, g / v, fixed)
        fixed = jnp.where(lane == ONE + 1, s / v, fixed)
        fixed = jnp.where(lane == ONE + 2, b[:, ONE + 1 : ONE + 2], fixed)
        fixed = jnp.where(lane == ONE + 3, b[:, ONE + 2 : ONE + 3], fixed)
        grad_ref[i * cb : (i + 1) * cb, :] = fixed
        squares = squares + all_sum(fixed * fixed)
        spread = jnp.where(lane == 2 * i, alpha, spread)
        spread = jnp.where(lane == 2 * i + 1, beta, spread)
    wide = w0_ref[...].astype(F32) + w1_ref[...].astype(F32) + w2_ref[...].astype(F32) + w3_ref[...].astype(F32)
    mr = wide.shape[0] - cb // 2
    merge = wide[:mr]
    squares = squares + all_sum(merge * merge)
    at = 2 * cb
    for i in range(2):
        grad_ref[at + i * mr : at + (i + 1) * mr, :] = merge[:, i * LANES : (i + 1) * LANES]
    at = at + 2 * mr
    block = jnp.concatenate([wide[mr:, :LANES], wide[mr:, LANES:]], axis=0)
    shift_own = own_column(sum2_ref, 0, pos_ref[0], cb)
    gain_own = own_column(sum2_ref, 4, pos_ref[0], cb)
    block = jnp.where(lane == PCOL + 2, gain_own, block)
    block = jnp.where(lane == PCOL + 3, shift_own, block)
    grad_ref[at : at + cb, :] = block
    squares = squares + jnp.where(rep == 0, all_sum(block * block), 0.0)
    spread = jnp.where(lane == 4, jnp.broadcast_to(squares, spread.shape), spread)
    rows = jnp.transpose(jnp.concatenate([spread, jnp.zeros((LANES - cb, LANES), F32)], axis=0))[0:8]
    offset = (pos_ref[0] * cb) % LANES
    rows = pltpu.roll(rows, offset, 1)
    row8 = lax.broadcasted_iota(jnp.int32, rows.shape, 0)
    rows = jnp.where((row8 == 4) & (lane_of(rows.shape) != offset), 0.0, rows)
    pay_ref[...] = jnp.broadcast_to(rows[None], pay_ref.shape)


def own_column(ref, first, me, cb):
    block = (me * cb) // LANES
    row = ref[pl.ds(first + block, 1), :]
    lane = lane_of((cb, LANES))
    sub = lax.broadcasted_iota(jnp.int32, (cb, LANES), 0)
    hit = lane == sub + (me * cb) % LANES
    return jnp.sum(jnp.where(hit, jnp.broadcast_to(row, (cb, LANES)), 0.0), axis=1, keepdims=True)


def adam_into(weight_ref, moment_ref, square_ref, grad, scale, rate, outs, at=Ellipsis):
    new_ref, new_m_ref, new_s_ref, copy_ref = outs
    weight = weight_ref[at]
    clipped = grad * scale
    moment = 0.9 * moment_ref[at] + 0.1 * clipped
    square = 0.999 * square_ref[at] + 0.001 * clipped * clipped
    fix_one = 1.0 - 0.9**STEP
    fix_two = 1.0 - 0.999**STEP
    update = moment / fix_one / (jnp.sqrt(square / fix_two) + 1e-08) + 0.01 * weight
    new = weight - rate * update
    new_ref[at] = new
    new_m_ref[at] = moment
    new_s_ref[at] = square
    copy_ref[at] = new.astype(BF16)


def final_kernel(pos_ref, got_ref, mine_ref, other_ref, x_ref, wb_ref, a0_ref, a1_ref, a2_ref, a3_ref, *refs):
    weights, firsts, seconds = refs[0:4], refs[4:8], refs[8:12]
    outs = refs[12:28]
    norm_ref, rows_ref = refs[28:30]
    dp = got_ref.shape[0] // 2
    blocks = 4
    per = dp // blocks
    parts = []
    for b in range(blocks):
        for r in range(2):
            total = got_ref[(b * per) * 2 + r]
            for i in range(1, per):
                total = total + got_ref[(b * per + i) * 2 + r]
            parts.append(total)
    squares = parts[0][4:5, :]
    for part in parts[1:]:
        squares = squares + part[4:5, :]
    norm = jnp.sqrt(jnp.sum(squares, axis=1, keepdims=True))
    norm_ref[...] = norm
    scale = 1.0 / jnp.maximum(norm, 1.0)

    cb = weights[0].shape[1]
    d_in = weights[0].shape[2]
    mr = weights[1].shape[0]
    classes = weights[2].shape[1]
    first = pos_ref[1] == 0
    mine, other = mine_ref[...], other_ref[...]
    low = jnp.where(first, mine, other)
    high = jnp.where(first, other, mine)

    def group(i):
        return [o for o in outs[i::4]]

    hops = [low[0:cb], low[cb : 2 * cb], high[0:cb], high[cb : 2 * cb]]
    for k in range(HOPS):
        adam_into(weights[0], firsts[0], seconds[0], hops[k][:, :d_in], scale, 0.05, group(0), k)
    at = 2 * cb
    for half, part in enumerate((low, high)):
        for i in range(2):
            lanes = (slice(None), slice((2 * half + i) * LANES, (2 * half + i + 1) * LANES))
            grad = part[at + i * mr : at + (i + 1) * mr]
            adam_into(weights[1], firsts[1], seconds[1], grad, scale, 0.05, group(1), lanes)
    at = at + 2 * mr
    block = low[at : at + cb]
    adam_into(weights[2], firsts[2], seconds[2], block[:, :classes], scale, 0.05, group(2))
    lane = lane_of((cb, LANES))
    small = jnp.zeros((cb, LANES), F32)
    for kind in range(4):
        for k in range(HOPS):
            small = jnp.where(lane == kind * HOPS + k, hops[k][:, ONE + kind : ONE + kind + 1], small)
    for i, source in enumerate((2, 3, 0, 1)):
        small = jnp.where(lane == 4 * HOPS + i, block[:, PCOL + source : PCOL + source + 1], small)
    small = jnp.transpose(jnp.concatenate([small, jnp.zeros((LANES - cb, LANES), F32)], axis=0))
    adam_into(weights[3], firsts[3], seconds[3], small[: weights[3].shape[0], :cb], scale, 0.3, group(3))

    sub = lax.broadcasted_iota(jnp.int32, (LANES, LANES), 0)
    for k in range(HOPS):
        a_ref = (a0_ref, a1_ref, a2_ref, a3_ref)[k]
        r, i = k // 2, k % 2
        alpha = jnp.concatenate([parts[b * 2 + r][2 * i : 2 * i + 1] for b in range(blocks)], axis=1)
        beta = jnp.concatenate([parts[b * 2 + r][2 * i + 1 : 2 * i + 2] for b in range(blocks)], axis=1)
        w = jnp.transpose(wb_ref[k].astype(F32))
        right = jnp.where(lax.broadcasted_iota(jnp.int32, w.shape, 0) == ONE, alpha, w * beta)
        fix = dot(w, right, 1, 1, HIGHEST)
        hi = fix.astype(BF16)
        lo = (fix - hi.astype(F32)).astype(BF16)
        value = a_ref[...] - dot(hi, x_ref[k], 1, 0) - dot(lo, x_ref[k], 1, 0)
        rows_ref[k * d_in : (k + 1) * d_in, :] = value[:d_in]


def flip(value, mask, dp):
    return lax.ppermute(value, "dp", [(i, i ^ mask) for i in range(dp)])


def swap(value):
    return lax.ppermute(value, "rep", [(0, 1), (1, 0)])


def spread_blocks(block, dp):
    if dp != 16:
        return lax.all_gather(block, "dp")
    high = jnp.stack([block] + [flip(block, 4 * k, dp) for k in range(1, 4)])
    return jnp.concatenate([high] + [flip(high, m, dp) for m in range(1, 4)])


def exchange(value):
    return lax.all_to_all(value, BOTH, 0, 0, tiled=True)


def on_device(table, batch_index, labels, *state):
    weights, firsts, seconds = state[0:4], state[4:8], state[8:12]
    dp, rep = lax.axis_size("dp"), lax.axis_size("rep")
    n = dp * rep
    me, core = lax.axis_index("dp"), lax.axis_index("rep")
    pos = jnp.stack([me, core]).astype(jnp.int32)
    batch = batch_index.shape[0]
    count = float(batch * n)
    nodes, width = table.shape
    d_in = weights[0].shape[1]
    cb = weights[0].shape[2]
    mr, hid = weights[1].shape
    classes = weights[2].shape[1]
    half = hid // 2
    lhs = [v.transpose(0, 2, 1) for v in (weights[0], firsts[0], seconds[0])]
    idx = batch_index.reshape(1, batch)
    lab = labels.reshape(1, batch)

    with jax.named_scope("prep"):
        pack, wmh = call(
            prep_kernel,
            [sds((HOPS + 1, cb, LANES), BF16), sds((mr, half), BF16)],
            pos, lhs[0], weights[2], weights[3], weights[1],
            smem=(0,),
        )
    packs = spread_blocks(pack, dp)
    wm_mine = spread_blocks(wmh, dp)
    wm_other = swap(wm_mine)

    with jax.named_scope("gather"):
        step = 512
        x, gram = call(
            gather_kernel,
            [sds((HOPS, LANES, batch), BF16), sds((HOPS, LANES, LANES))],
            idx, table.T,
            grid=(nodes // step,),
            in_specs=[
                pl.BlockSpec((1, batch), lambda i: (0, 0)),
                pl.BlockSpec((width, step), lambda i: (0, i)),
            ],
            out_specs=(
                pl.BlockSpec((HOPS, LANES, batch), lambda i: (0, 0, 0)),
                pl.BlockSpec((HOPS, LANES, LANES), lambda i: (0, 0, 0)),
            ),
            scratch=[pltpu.VMEM((width, batch), F32), pltpu.VMEM((LANES, batch), F32)],
            flops=2 * nodes * width * batch,
        )
    with jax.named_scope("gram_sum"):
        parts = exchange(gram.reshape(n, HOPS * LANES // n, LANES))
        (parts,) = call(sum_spread_kernel, [sds(parts.shape)], parts)
        gram = exchange(parts).reshape(HOPS, LANES, LANES)
    with jax.named_scope("stats"):
        wb, wc, coef, par = call(
            functools.partial(stats_kernel, count),
            [sds((HOPS, hid, LANES), BF16), sds((hid, LANES), BF16), sds((HOPS, hid, LANES)), sds((hid, LANES))],
            pos, gram, packs,
            smem=(0,),
            scratch=[pltpu.VMEM((hid, LANES), F32)],
            flops=2 * HOPS * hid * LANES * LANES * 6,
        )
    smem = pl.BlockSpec(memory_space=pltpu.SMEM)
    with jax.named_scope("forward"):
        joined, pre2, pay = call(
            forward_kernel,
            [sds((HOPS, hid, batch), BF16), sds((hid, batch)), sds((n, 8, LANES))],
            pos, x, wb, coef, wm_mine, wm_other,
            grid=(HOPS,),
            in_specs=[
                smem,
                pl.BlockSpec((1, LANES, batch), lambda k: (k, 0, 0)),
                pl.BlockSpec((1, hid, LANES), lambda k: (k, 0, 0)),
                pl.BlockSpec((1, hid, LANES), lambda k: (k, 0, 0)),
                pl.BlockSpec((dp, mr, half), lambda k: (0, 0, 0)),
                pl.BlockSpec((dp, mr, half), lambda k: (0, 0, 0)),
            ],
            out_specs=(
                pl.BlockSpec((1, hid, batch), lambda k: (k, 0, 0)),
                pl.BlockSpec((hid, batch), lambda k: (0, 0)),
                pl.BlockSpec((n, 8, LANES), lambda k: (0, 0, 0)),
            ),
            scratch=[pltpu.VMEM((hid, batch), F32)],
            flops=2 * batch * HOPS * hid * (LANES + hid),
        )
    got = exchange(pay)
    with jax.named_scope("head"):
        dy2, pay, block, stat = call(
            functools.partial(head_kernel, count, classes),
            [sds((hid, batch)), sds((n, 8, LANES)), sds((hid, LANES)), sds((2, hid, LANES))],
            got, pre2, par, wc, lab,
            scratch=[
                pltpu.VMEM((hid, batch), BF16),
                pltpu.VMEM((hid, batch), F32),
                pltpu.VMEM((4, hid, LANES), F32),
                pltpu.VMEM((3, hid, LANES), F32),
            ],
            flops=6 * batch * hid * LANES,
        )
    got = exchange(pay)
    with jax.named_scope("turn"):
        rows = mr + cb // 2
        dpre, keep, send, sum2 = call(
            functools.partial(turn_kernel, count),
            [sds((hid, batch), BF16), sds((dp, rows, half)), sds((dp, rows, half), BF16), sds((8, LANES))],
            pos, got, stat, par, pre2, dy2, joined.reshape(HOPS * hid, batch), block,
            smem=(0,),
            scratch=[pltpu.VMEM((3, hid, LANES), F32)],
            flops=2 * batch * HOPS * hid * hid,
        )
    recv = swap(send)
    bs, rs = [], []
    for hop in range(HOPS):
        with jax.named_scope("back"):
            b, a = call(
                functools.partial(back_kernel, hop=hop),
                [sds((dp, cb, LANES)), sds((LANES, batch))],
                pos, dpre, x, wb, coef, wm_mine, wm_other,
                smem=(0,),
                scratch=[
                    pltpu.VMEM((hid, batch), F32),
                    pltpu.VMEM((hid, batch), F32),
                    pltpu.VMEM((hid, batch), BF16),
                    pltpu.VMEM((2, hid, LANES), F32),
                ],
                flops=2 * batch * hid * (hid + 3 * LANES) * 3,
            )
        bs.append(b)
        rs.append(a)
    with jax.named_scope("merge_sum"):
        if dp == 16:
            shape = (4, rows, half)
            low = call(
                split_low_kernel, [sds(shape)] + [sds(shape, BF16)] * 3, pos, keep, recv, smem=(0,)
            )
            moved = [flip(low[m], m, dp) for m in range(1, 4)]
            high = call(
                split_high_kernel,
                [sds(shape[1:])] + [sds(shape[1:], BF16)] * 3,
                pos, low[0], *moved,
                smem=(0,),
            )
            wide = [high[0]] + [flip(high[k], 4 * k, dp) for k in range(1, 4)]
        else:
            total = lax.psum_scatter(keep + recv.astype(F32), "dp", scatter_dimension=0)
            wide = [total] + [jnp.zeros_like(total)] * 3
    with jax.named_scope("branch_sum"):
        keep_b, send_b = call(
            pick_kernel, [sds((dp, 2, cb, LANES))] * 2, pos, *bs, smem=(0,)
        )
        pair = keep_b + swap(send_b)
        got_b = lax.all_to_all(pair, "dp", 0, 0, tiled=True)
    with jax.named_scope("owner"):
        shares, pay = call(
            functools.partial(owner_kernel, count, classes),
            [sds((3 * cb + 2 * mr, LANES)), sds((n, 8, LANES))],
            pos, got_b, *wide, pack, coef, gram, sum2,
            smem=(0,),
        )
    theirs = swap(shares)
    got = exchange(pay)
    with jax.named_scope("final"):
        tr = [(lhs[i],) + tuple(s[1:]) for i, s in enumerate((weights, firsts, seconds))]
        shapes = [t.shape for t in tr[0]]
        outs = []
        for dtype in (F32, F32, F32, BF16):
            outs += [sds(s, dtype) for s in shapes]
        outs += [sds((1, 1)), sds((width, batch))]
        res = call(
            final_kernel, outs, pos, got, shares, theirs, x, wb, *rs, *tr[0], *tr[1], *tr[2],
            smem=(0,),
            flops=2 * batch * LANES * LANES * 3 * HOPS,
        )
    result = list(res[:16])
    for i in range(0, 16, 4):
        result[i] = result[i].transpose(0, 2, 1)
    return (*result, res[16].reshape(()), res[17].T)


def solution(mesh):
    tables = (P(BOTH, None), P(BOTH), P(BOTH))
    params = (P(None, None, "dp"), P("dp", None), P("dp", None), P(None, "dp"))
    return jax.shard_map(
        on_device,
        mesh=mesh,
        in_specs=tables + params * 3,
        out_specs=params * 4 + (P(), P(BOTH, None)),
        check_vma=False,
    )
```

```python
import functools
import math

import jax
import jax.numpy as jnp
from jax import lax
from jax.experimental import pallas as pl
from jax.experimental.pallas import tpu as pltpu
from jax.sharding import PartitionSpec as P

HOPS = 4
STEP = 7
EPS_NORM = 1e-05
LANES = 128
PCOL = 64
ONE = 100
ROWS, WIDE, CHUNK = 32, 256, 256
BOTH = ("dp", "rep")
F32 = jnp.float32
BF16 = jnp.bfloat16


def dot(left, right, left_dim, right_dim):
    return lax.dot_general(
        left,
        right,
        (((left_dim,), (right_dim,)), ((), ())),
        preferred_element_type=F32,
    )


def call(body, outs, *args, smem=(), hbm=(), chip=(), after=(), grid=None, in_specs=None, out_specs=None, scratch=(), mib=12, flops=0):
    skip = len(args)
    if in_specs is None:
        spaces = {**{i: pltpu.SMEM for i in smem}, **{i: pltpu.HBM for i in hbm}}
        in_specs = [pl.BlockSpec(memory_space=spaces.get(i, pltpu.VMEM)) for i in range(skip)]
    if out_specs is None:
        out_specs = tuple(pl.BlockSpec(memory_space=pltpu.VMEM) for _ in outs)
    in_specs = list(in_specs) + [pl.BlockSpec(memory_space=pl.ANY) for _ in after]
    places = {**{i: pltpu.HBM for i in hbm}, **{i: pltpu.VMEM for i in chip}}
    args = [pltpu.with_memory_space_constraint(a, places[i]) if i in places else a for i, a in enumerate(args)]
    moved = sum(math.prod(a.shape) * jnp.dtype(a.dtype).itemsize for a in (*args, *outs))

    def kernel(*refs):
        body(*refs[:skip], *refs[skip + len(after) :])

    kwargs = {} if grid is None else {"grid": grid}
    return pl.pallas_call(
        kernel,
        out_shape=tuple(outs),
        in_specs=in_specs,
        out_specs=out_specs,
        scratch_shapes=list(scratch),
        compiler_params=pltpu.CompilerParams(vmem_limit_bytes=mib << 20),
        cost_estimate=pl.CostEstimate(flops=flops, bytes_accessed=moved, transcendentals=0),
        **kwargs,
    )(*args, *after)


def fetch(sources, buffers, sems):
    copies = [pltpu.make_async_copy(s, b, sems.at[i]) for i, (s, b) in enumerate(zip(sources, buffers))]
    for copy in copies:
        copy.start()

    def wait():
        for copy in copies:
            copy.wait()

    return wait


def sds(shape, dtype=F32):
    return jax.ShapeDtypeStruct(shape, dtype)


def vmem(shape, dtype=F32):
    return pltpu.VMEM(shape, dtype)


def hbm_out(shape, dtype=F32):
    return pltpu.HBM(shape, dtype)


def lane_of(shape):
    return lax.broadcasted_iota(jnp.int32, shape, len(shape) - 1)


def to_cols(rows, first):
    parts = []
    for i in range(4):
        row = rows[first + i : first + i + 1, :]
        parts.append(jnp.transpose(jnp.broadcast_to(row, (LANES, LANES))))
    return jnp.concatenate(parts, axis=0)


def lane_sums(part):
    total = jnp.sum(jnp.transpose(part), axis=0, keepdims=True)
    return jnp.concatenate([total[:, i * LANES : (i + 1) * LANES] for i in range(4)], axis=0)


def fold_lanes(value):
    out = value[:, :LANES]
    for i in range(1, value.shape[1] // LANES):
        out = out + value[:, i * LANES : (i + 1) * LANES]
    return out


def prep_kernel(pos_ref, wb_hbm, wc_hbm, sp_hbm, wm_hbm, own_ref, block_ref, wb_ref, wc_ref, sp_ref, wm_ref, sems):
    wait = fetch((wb_hbm, wc_hbm, sp_hbm, wm_hbm), (wb_ref, wc_ref, sp_ref, wm_ref), sems)
    cb = wc_ref.shape[0]
    mr, hid = wm_ref.shape
    own_ref[...] = jnp.zeros_like(own_ref)
    wait()
    own_ref[0:HOPS, :, 0 : wb_ref.shape[2]] = wb_ref[...].astype(BF16)
    own_ref[HOPS, :, 0 : wc_ref.shape[1]] = wc_ref[...].astype(BF16)
    own_ref[HOPS, :, PCOL : PCOL + sp_ref.shape[0]] = jnp.transpose(sp_ref[...]).astype(BF16)
    first = pos_ref[1] == 0
    part = cb // 2
    for k in range(HOPS + 1):
        block_ref[k * part : (k + 1) * part, :] = jnp.where(first, own_ref[k, :part], own_ref[k, part:])
    at = (HOPS + 1) * part
    for i in range(2):
        left = wm_ref[:, i * LANES : (i + 1) * LANES]
        right = wm_ref[:, hid // 2 + i * LANES : hid // 2 + (i + 1) * LANES]
        block_ref[at + i * mr : at + (i + 1) * mr, :] = jnp.where(first, left, right).astype(BF16)


def stack_kernel(a_ref, b_ref, c_ref, d_ref, out_ref):
    for i, ref in enumerate((a_ref, b_ref, c_ref, d_ref)):
        out_ref[i] = ref[...]


def assemble_kernel(pos_ref, *refs):
    wb_ref, wm_ref = refs[8:]
    cb = wb_ref.shape[1] // 16
    mr = wm_ref.shape[1] // 16
    part = cb // 2
    first = (HOPS + 1) * part
    for which in range(2):
        half = pos_ref[1] if which == 0 else 1 - pos_ref[1]
        for m in range(4):
            for k in range(4):
                s = pos_ref[0] ^ (4 * k + m)
                block = refs[which * 4 + m][k]
                rows = pl.ds(pl.multiple_of(s * cb + half * part, part), part)
                for j in range(HOPS + 1):
                    wb_ref[j, rows, :] = block[j * part : (j + 1) * part]
                rows = pl.ds(pl.multiple_of(s * mr, mr), mr)
                for i in range(2):
                    wm_ref[half * 2 + i, rows, :] = block[first + i * mr : first + (i + 1) * mr]


def gather_kernel(idx_ref, tab_ref, x_ref, gram_ref, acc, pad):
    i = pl.program_id(0)
    width = tab_ref.shape[1]
    d_in = tab_ref.shape[0] // HOPS
    batch = idx_ref.shape[1]
    rows = lax.broadcasted_iota(jnp.int16, (width, batch), 0)
    hot = jnp.where(rows == (idx_ref[...] - i * width).astype(jnp.int16), BF16(1.0), BF16(0.0))
    part = dot(tab_ref[...].astype(BF16), hot, 1, 0)

    @pl.when(i == 0)
    def _():
        acc[...] = part

    @pl.when(i > 0)
    def _():
        acc[...] += part

    @pl.when(i == pl.num_programs(0) - 1)
    def _():
        row = lax.broadcasted_iota(jnp.int32, pad.shape, 0)
        pad[...] = jnp.where(row == d_in, 1.0, 0.0)
        for k in range(HOPS):
            pad[0:d_in, :] = acc[k * d_in : (k + 1) * d_in, :]
            x = pad[...].astype(BF16)
            x_ref[k] = x
            gram_ref[k] = dot(x, x, 1, 1)


def sum_spread_kernel(in_ref, out_ref):
    out_ref[...] = jnp.broadcast_to(jnp.sum(in_ref[...], axis=0, keepdims=True), out_ref.shape)


def three_terms(wide):
    terms = []
    for _ in range(3):
        terms.append(wide.astype(BF16))
        wide = wide - terms[-1].astype(F32)
    return terms


def exact_dot(low, wide):
    total = None
    for term in three_terms(wide):
        part = dot(low, term, 1, 0)
        total = part if total is None else total + part
    return total


def stats_kernel(count, gram_ref, wb_ref, coef_ref, par_ref, mu_ref, wt_ref):
    hid = wb_ref.shape[1]
    small = jnp.transpose(wb_ref[HOPS].astype(F32))
    row = lax.broadcasted_iota(jnp.int32, (16, hid), 0)

    def at(i):
        return small[PCOL + i : PCOL + i + 1, :]

    def columns(values):
        block = jnp.zeros((16, hid), F32)
        for i, value in enumerate(values):
            block = jnp.where(row == i, value, block)
        return jnp.transpose(jnp.concatenate([block, jnp.zeros((LANES - 16, hid), F32)], axis=0))

    par_ref[...] = columns([at(4 * HOPS + i) for i in range(4)])
    mu_ref[...] = jnp.zeros_like(mu_ref)
    for k in range(HOPS):
        gram = gram_ref[k]
        mu_ref[k : k + 1, :] = gram[ONE : ONE + 1, :] / count
        wide = jnp.transpose(wb_ref[k].astype(F32))
        w = wide.astype(BF16)
        wt_ref[k] = w
        wg = None
        for term in three_terms(gram):
            part = dot(term, w, 1, 0)
            wg = part if wg is None else wg + part
        mean = wg[ONE : ONE + 1, :] / count
        second = jnp.sum(wg * wide, axis=0, keepdims=True) / count
        inv = lax.rsqrt(second - mean * mean + EPS_NORM)
        gain, shift, slope, join = at(k), at(HOPS + k), at(2 * HOPS + k), at(3 * HOPS + k)
        v = gain * inv
        coef_ref[k] = columns(
            (
                0.5 * v,
                0.5 * (shift - v * mean),
                0.5 * (1.0 + slope),
                0.5 * (1.0 - slope),
                1.0 + join,
                1.0 - join,
                join,
                0.5 * (1.0 - join),
                v * slope,
                0.5 * v * (1.0 - slope),
                mean,
                inv,
                v,
            )
        )


def column_set(ref, hop, at, lanes):
    block = ref[hop, at, :]
    return [jnp.broadcast_to(block[:, i : i + 1], (ROWS, WIDE)) for i in lanes]


def merge_block(wm_ref, rows):
    return jnp.concatenate([wm_ref[i, rows, :] for i in range(wm_ref.shape[0])], axis=1)


def forward_kernel(x_ref, wb_ref, coef_ref, wm_hbm, joined_out, pre2_out, pay_ref, pre, wm_ref, joined_ref, pre2_ref, sems, out_sems):
    wait = fetch((wm_hbm,), (wm_ref,), sems)
    stores = []
    hid = wb_ref.shape[1]
    batch = x_ref.shape[2]
    per = hid // CHUNK
    jobs = [(k, c) for k in range(HOPS) for c in range(per)]

    def project(i):
        k, c = jobs[i]
        pre[i % 2] = dot(wb_ref[k, c * CHUNK : (c + 1) * CHUNK, :], x_ref[k], 1, 0)

    def units(i):
        k, c = jobs[i]
        for g in range(CHUNK // ROWS):
            at = slice(c * CHUNK + g * ROWS, c * CHUNK + (g + 1) * ROWS)
            cs = column_set(coef_ref, k, at, range(6))
            for b in range(batch // WIDE):
                lanes = slice(b * WIDE, (b + 1) * WIDE)
                u = pre[i % 2, g * ROWS : (g + 1) * ROWS, lanes] * cs[0] + cs[1]
                u = u * (cs[2] + cs[3] * jnp.tanh(u))
                joined_ref[k, at, lanes] = (u * (cs[4] + cs[5] * jnp.tanh(u))).astype(BF16)

    project(0)
    for i in range(len(jobs)):
        if i + 1 < len(jobs):
            project(i + 1)
        units(i)
        if i % per == per - 1:
            k = i // per
            stores.append(fetch((joined_ref.at[k],), (joined_out.at[k],), out_sems.at[pl.ds(k, 1)]))
            if k == 0:
                wait()
            part = dot(merge_block(wm_ref, slice(k * hid, (k + 1) * hid)), joined_ref[k], 0, 0)
            if k == 0:
                pre2_ref[...] = part
            else:
                pre2_ref[...] += part
    stores.append(fetch((pre2_ref,), (pre2_out,), out_sems.at[pl.ds(HOPS, 1)]))
    value = pre2_ref[...]
    sums = jnp.concatenate([lane_sums(fold_lanes(value)), lane_sums(fold_lanes(value * value))], axis=0)
    pay_ref[...] = jnp.broadcast_to(sums[None], pay_ref.shape)
    for done in stores:
        done()


def columns2(count, rows, par):
    mean = to_cols(rows, 0) / count
    inv = lax.rsqrt(to_cols(rows, 4) / count - mean * mean + EPS_NORM)
    shape = mean.shape
    gain = jnp.broadcast_to(par[:, 0:1], shape)
    shift = jnp.broadcast_to(par[:, 1:2], shape)
    slope = jnp.broadcast_to(par[:, 2:3], shape)
    return mean, inv, gain, shift, slope


def head_kernel(
    count, classes, got_ref, pre2_hbm, par_ref, wb_ref, lab_hbm, dy2_ref, pay_ref, class_ref, stat_ref, act, dact, cols, sums, lab_ref, pre2_ref, sems
):
    wait = fetch((pre2_hbm, lab_hbm), (pre2_ref, lab_ref), sems)
    hid, batch = dy2_ref.shape
    par = par_ref[...]
    mean, inv, gain, shift, slope = columns2(count, jnp.sum(got_ref[...], axis=0), par)
    stat_ref[0] = mean
    stat_ref[1] = inv
    cols[0] = 0.5 * gain * inv
    cols[1] = 0.5 * (shift - gain * inv * mean)
    cols[2] = 1.0 + slope
    cols[3] = 1.0 - slope
    reps = WIDE // LANES

    def tiled(c, at):
        return jnp.concatenate([cols[c, at, :]] * reps, axis=1)

    def first(g, carry):
        at = pl.ds(pl.multiple_of(g * ROWS, ROWS), ROWS)
        c = [tiled(i, at) for i in range(4)]
        for b in range(batch // WIDE):
            lanes = slice(b * WIDE, (b + 1) * WIDE)
            u = pre2_ref[at, lanes] * c[0] + c[1]
            act[at, lanes] = (u * (c[2] + c[3] * jnp.tanh(u))).astype(BF16)
        return carry

    wait()
    lax.fori_loop(0, hid // ROWS, first, 0, unroll=4)
    tail = wb_ref[HOPS]
    wc = jnp.where(lane_of(tail.shape) < PCOL, tail.astype(F32), 0.0).astype(BF16)
    logits = dot(wc, act[...], 0, 0)
    row = lax.broadcasted_iota(jnp.int32, (LANES, batch), 0)
    logits = jnp.where(row < classes, logits + par[0:LANES, 3:4], -jnp.inf)
    top = jnp.max(logits, axis=0, keepdims=True)
    e = jnp.exp(logits - top)
    probs = e / jnp.sum(e, axis=0, keepdims=True)
    dlog = (probs - jnp.where(row == lab_ref[...], 1.0, 0.0)).astype(BF16)
    grad_class = dot(act[...], dlog, 1, 1)
    bias = jnp.sum(dlog.astype(F32), axis=1, keepdims=True)
    dact[...] = dot(wc, dlog, 1, 0)

    def second(g, carry):
        at = pl.ds(pl.multiple_of(g * ROWS, ROWS), ROWS)
        c = [tiled(i, at) for i in range(4)]
        m = jnp.concatenate([stat_ref[0, at, :]] * reps, axis=1)
        v = jnp.concatenate([stat_ref[1, at, :]] * reps, axis=1)
        acc = [jnp.zeros((ROWS, WIDE), F32) for _ in range(3)]
        for b in range(batch // WIDE):
            lanes = slice(b * WIDE, (b + 1) * WIDE)
            p = pre2_ref[at, lanes]
            d = dact[at, lanes]
            u = p * c[0] + c[1]
            t = jnp.tanh(u)
            w = u * (1.0 - t)
            dy = d * (0.5 * (c[2] + c[3] * (t + w * (1.0 + t))))
            dy2_ref[at, lanes] = dy
            acc[0] = acc[0] + dy
            acc[1] = acc[1] + dy * ((p - m) * v)
            acc[2] = acc[2] + d * w
        for i in range(3):
            sums[i, at, :] = fold_lanes(acc[i])
        return carry

    lax.fori_loop(0, hid // ROWS, second, 0, unroll=4)
    pay = jnp.concatenate([lane_sums(sums[0]), lane_sums(sums[1])], axis=0)
    pay_ref[...] = jnp.broadcast_to(pay[None], pay_ref.shape)
    lane = lane_of((hid, LANES))
    slope_sum = jnp.sum(sums[2], axis=1, keepdims=True)
    bias = jnp.concatenate([bias, jnp.zeros((hid - LANES, 1), F32)], axis=0)
    block = jnp.where(lane < classes, grad_class, 0.0)
    block = jnp.where(lane == PCOL, slope_sum, block)
    class_ref[...] = jnp.where(lane == PCOL + 1, bias, block)


def turn_kernel(
    count, pos_ref, got_ref, stat_ref, par_ref, pre2_hbm, dy2_ref, joined_hbm, class_ref, dpre_ref, keep_ref, send_ref, sum2_ref, cols, joined_ref, pre2_ref, sems
):
    hid, batch = dy2_ref.shape
    wait = fetch((pre2_hbm,), (pre2_ref,), sems.at[pl.ds(HOPS, 1)])
    dp, rows, half = keep_ref.shape
    hops = joined_ref.shape[0]
    waits = [fetch((joined_hbm.at[k],), (joined_ref.at[k],), sems.at[pl.ds(k, 1)]) for k in range(hops)]
    mr = hops * hid // dp
    cb = hid // dp
    rows8 = jnp.sum(got_ref[...], axis=0)
    sum2_ref[...] = rows8
    mean, inv = stat_ref[0], stat_ref[1]
    v = jnp.broadcast_to(par_ref[:, 0:1], mean.shape) * inv
    cols[0] = v
    cols[1] = v * to_cols(rows8, 0) / count
    cols[2] = v * inv * to_cols(rows8, 4) / count
    reps = WIDE // LANES
    wait()
    for g in range(hid // ROWS):
        at = slice(g * ROWS, (g + 1) * ROWS)
        c = [jnp.concatenate([cols[i, at, :]] * reps, axis=1) for i in range(3)]
        m = jnp.concatenate([stat_ref[0, at, :]] * reps, axis=1)
        for b in range(batch // WIDE):
            lanes = slice(b * WIDE, (b + 1) * WIDE)
            value = c[0] * dy2_ref[at, lanes] - c[1] - (pre2_ref[at, lanes] - m) * c[2]
            dpre_ref[at, lanes] = value.astype(BF16)
    mine = pl.ds(pl.multiple_of(pos_ref[1] * half, half), half)
    theirs = pl.ds(pl.multiple_of((1 - pos_ref[1]) * half, half), half)
    per = dp // hops
    for k in range(hops):
        waits[k]()
        block = joined_ref[k]
        own = dot(block, dpre_ref[mine, :], 1, 1)
        other = dot(block, dpre_ref[theirs, :], 1, 1).astype(BF16)
        for j in range(per):
            keep_ref[k * per + j, 0:mr, :] = own[j * mr : (j + 1) * mr]
            send_ref[k * per + j, 0:mr, :] = other[j * mr : (j + 1) * mr]
    first = pos_ref[1] == 0
    for s in range(dp):
        block = class_ref[s * cb : (s + 1) * cb, :]
        wide = jnp.concatenate([block[: cb // 2], block[cb // 2 :]], axis=1)
        keep_ref[s, mr:rows, :] = jnp.where(first, wide, 0.0)
        send_ref[s, mr:rows, :] = jnp.where(first, 0.0, wide).astype(BF16)


def factor_kernel(x_ref, wb_ref, coef_ref, e_ref, f_ref, g_ref, pre):
    hid = wb_ref.shape[1]
    batch = x_ref.shape[2]
    per = hid // CHUNK

    def project(c):
        pre[c % 2] = dot(wb_ref[0, c * CHUNK : (c + 1) * CHUNK, :], x_ref[0], 1, 0)

    project(0)
    for c in range(per):
        if c + 1 < per:
            project(c + 1)
        for g in range(CHUNK // ROWS):
            at = slice(c * CHUNK + g * ROWS, c * CHUNK + (g + 1) * ROWS)
            here = slice(g * ROWS, (g + 1) * ROWS)
            a1, b1, p1, q1, s2, q2, s1, r1 = column_set(coef_ref, 0, at, (0, 1, 2, 3, 6, 7, 8, 9))
            for b in range(batch // WIDE):
                lanes = slice(b * WIDE, (b + 1) * WIDE)
                u = pre[c % 2, here, lanes] * a1 + b1
                t = jnp.tanh(u)
                u2 = u * (p1 + q1 * t)
                t2 = jnp.tanh(u2)
                w = u2 * (1.0 - t2)
                g_ref[0, at, lanes] = w.astype(BF16)
                d = s2 + q2 * ((1.0 + t2) * (1.0 + w))
                w = u * (1.0 - t)
                f_ref[0, at, lanes] = (d * w).astype(BF16)
                e_ref[0, at, lanes] = (d * (s1 + r1 * ((1.0 + t) * (1.0 + w)))).astype(BF16)


SMALLS = 4


def back_kernel(own, pos_ref, dpre_ref, x_ref, wb_ref, mu_ref, wm_hbm, e_hbm, f_hbm, g_hbm, *refs):
    if own:
        recv_ref, refs = refs[0], refs[1:]
    b_ref, a_out, dj, dyv, sums, a_ref, wm_ref, e_ref, f_ref, g_ref, sems, out_sems = refs
    hid = wb_ref.shape[1]
    batch = x_ref.shape[2]
    per = hid // CHUNK
    jobs = [(k, c) for k in range(2) for c in range(per)]
    base = 2 * (pos_ref[1] if own else 1 - pos_ref[1])
    lane = lane_of((hid, LANES))
    dp, _, cb, _ = b_ref.shape
    copies = []
    waits = []
    for k in range(2):
        at = pl.ds(pl.multiple_of((base + k) * hid, hid), hid)
        sources = [wm_hbm.at[:, at, :]] + [ref.at[base + k] for ref in (e_hbm, f_hbm, g_hbm)]
        buffers = [ref.at[k] for ref in (wm_ref, e_ref, f_ref, g_ref)]
        waits.append(fetch(sources, buffers, sems.at[k]))

    def project(i):
        k, c = jobs[i]
        if c == 0:
            waits[k]()
        dj[i % 2] = dot(merge_block(wm_ref.at[k], slice(c * CHUNK, (c + 1) * CHUNK)), dpre_ref[...], 1, 0)

    def units(i):
        k, c = jobs[i]
        for g in range(CHUNK // ROWS):
            at = slice(c * CHUNK + g * ROWS, c * CHUNK + (g + 1) * ROWS)
            here = slice(g * ROWS, (g + 1) * ROWS)
            first = jnp.zeros((ROWS, WIDE), F32)
            second = jnp.zeros((ROWS, WIDE), F32)
            for b in range(batch // WIDE):
                lanes = slice(b * WIDE, (b + 1) * WIDE)
                d = dj[i % 2, here, lanes]
                dyv[k, at, lanes] = (d * e_ref[k, at, lanes].astype(F32)).astype(BF16)
                first = first + d * f_ref[k, at, lanes].astype(F32)
                second = second + d * g_ref[k, at, lanes].astype(F32)
            sums[k, 0, at, :] = fold_lanes(first)
            sums[k, 1, at, :] = fold_lanes(second)

    def close(k):
        w = wb_ref[base + k]
        a_ref[k] = dot(w, dyv[k], 0, 0)
        copies.append(fetch((a_ref.at[k],), (a_out.at[k],), out_sems.at[pl.ds(k, 1)]))
        block = dot(dyv[k], x_ref[base + k], 1, 1)
        total = block[:, ONE : ONE + 1]
        block = jnp.where(lane < ONE, block - total * mu_ref[pl.ds(base + k, 1), :], 0.0)
        smalls = (
            total,
            jnp.sum(block * w.astype(F32), axis=1, keepdims=True),
            jnp.sum(sums[k, 0], axis=1, keepdims=True),
            jnp.sum(sums[k, 1], axis=1, keepdims=True),
        )
        for i, value in enumerate(smalls):
            block = jnp.where(lane == ONE + i, value, block)
        for s in range(dp):
            piece = block[s * cb : (s + 1) * cb, :]
            if own:
                piece = piece + join_smalls(recv_ref[s, k].astype(F32))
            b_ref[s, k] = split_smalls(piece)

    project(0)
    for i in range(len(jobs)):
        if i + 1 < len(jobs):
            project(i + 1)
        units(i)
        if i % per == per - 1:
            close(i // per)
    for done in copies:
        done()


def split_smalls(block):
    lane = lane_of(block.shape)
    rest = block - block.astype(BF16).astype(F32)
    moved = pltpu.roll(rest, SMALLS, 1)
    return jnp.where((lane >= ONE + SMALLS) & (lane < ONE + 2 * SMALLS), moved, block).astype(BF16)


def join_smalls(block):
    lane = lane_of(block.shape)
    moved = pltpu.roll(block, LANES - SMALLS, 1)
    block = jnp.where((lane >= ONE) & (lane < ONE + SMALLS), block + moved, block)
    return jnp.where(lane < ONE + SMALLS, block, 0.0)


def split_low_kernel(pos_ref, keep_ref, got_ref, o0_ref, o1_ref, o2_ref, o3_ref):
    low = pos_ref[0] % 4
    for m, ref in enumerate((o0_ref, o1_ref, o2_ref, o3_ref)):
        for z in range(4):
            j = z * 4 + (low ^ m)
            ref[z] = (keep_ref[j] + got_ref[j].astype(F32)).astype(ref.dtype)


def split_high_kernel(pos_ref, own_ref, g1_ref, g2_ref, g3_ref, o0_ref, o1_ref, o2_ref, o3_ref):
    high = pos_ref[0] // 4
    for k, ref in enumerate((o0_ref, o1_ref, o2_ref, o3_ref)):
        j = high ^ k
        value = own_ref[j] + g1_ref[j].astype(F32) + g2_ref[j].astype(F32) + g3_ref[j].astype(F32)
        ref[...] = value.astype(ref.dtype)


def owner_kernel(
    count, classes, pos_ref, got_ref, sum2_ref, w1_ref, w2_ref, w3_ref, *refs
):
    grad_ref, pay_ref, sems = refs[4], refs[5], refs[10]
    w0_ref, pack_ref, coef_ref, gram_ref = refs[6:10]
    fetch(refs[:4], refs[6:10], sems)()
    _, _, cb, _ = got_ref.shape
    total = jnp.sum(got_ref[...].astype(F32), axis=0)
    rep = pos_ref[1]
    start = pl.multiple_of(pos_ref[0] * cb, cb)
    lane = lane_of((cb, LANES))
    squares = jnp.zeros((1, 1), F32)
    spread = jnp.zeros((cb, LANES), F32)

    def all_sum(v):
        return jnp.sum(jnp.sum(v, axis=1, keepdims=True), axis=0, keepdims=True)

    for i in range(2):
        hop = rep * 2 + i
        b = join_smalls(total[i])
        coef = coef_ref[hop, pl.ds(start, cb), :]
        mean, inv, v = coef[:, 10:11], coef[:, 11:12], coef[:, 12:13]
        gram = gram_ref[hop]
        s = b[:, ONE : ONE + 1]
        g = inv * b[:, ONE + 1 : ONE + 2]
        beta = inv * g / count
        alpha = s / count - beta * mean
        wg = exact_dot(pack_ref[hop], gram) - mean * gram[ONE : ONE + 1, :]
        fixed = jnp.where(lane < ONE, b - beta * wg, 0.0)
        fixed = jnp.where(lane == ONE, g / v, fixed)
        fixed = jnp.where(lane == ONE + 1, s / v, fixed)
        fixed = jnp.where(lane == ONE + 2, b[:, ONE + 2 : ONE + 3], fixed)
        fixed = jnp.where(lane == ONE + 3, b[:, ONE + 3 : ONE + 4], fixed)
        grad_ref[i * cb : (i + 1) * cb, :] = fixed
        squares = squares + all_sum(fixed * fixed)
        spread = jnp.where(lane == 2 * i, alpha, spread)
        spread = jnp.where(lane == 2 * i + 1, beta, spread)
    wide = w0_ref[...].astype(F32) + w1_ref[...].astype(F32) + w2_ref[...].astype(F32) + w3_ref[...].astype(F32)
    mr = wide.shape[0] - cb // 2
    merge = wide[:mr]
    squares = squares + all_sum(merge * merge)
    at = 2 * cb
    for i in range(2):
        grad_ref[at + i * mr : at + (i + 1) * mr, :] = merge[:, i * LANES : (i + 1) * LANES]
    at = at + 2 * mr
    block = jnp.concatenate([wide[mr:, :LANES], wide[mr:, LANES:]], axis=0)
    shift_own = own_column(sum2_ref, 0, pos_ref[0], cb)
    gain_own = own_column(sum2_ref, 4, pos_ref[0], cb)
    block = jnp.where(lane == PCOL + 2, gain_own, block)
    block = jnp.where(lane == PCOL + 3, shift_own, block)
    grad_ref[at : at + cb, :] = block
    squares = squares + jnp.where(rep == 0, all_sum(block * block), 0.0)
    spread = jnp.where(lane == 4, jnp.broadcast_to(squares, spread.shape), spread)
    rows = jnp.transpose(jnp.concatenate([spread, jnp.zeros((LANES - cb, LANES), F32)], axis=0))[0:8]
    offset = (pos_ref[0] * cb) % LANES
    rows = pltpu.roll(rows, offset, 1)
    row8 = lax.broadcasted_iota(jnp.int32, rows.shape, 0)
    rows = jnp.where((row8 == 4) & (lane_of(rows.shape) != offset), 0.0, rows)
    pay_ref[...] = jnp.broadcast_to(rows[None], pay_ref.shape)


def own_column(ref, first, me, cb):
    block = (me * cb) // LANES
    row = ref[pl.ds(first + block, 1), :]
    lane = lane_of((cb, LANES))
    sub = lax.broadcasted_iota(jnp.int32, (cb, LANES), 0)
    hit = lane == sub + (me * cb) % LANES
    return jnp.sum(jnp.where(hit, jnp.broadcast_to(row, (cb, LANES)), 0.0), axis=1, keepdims=True)


def adam_into(weight_ref, moment_ref, square_ref, grad, scale, rate, outs, at=Ellipsis):
    new_ref, new_m_ref, new_s_ref, copy_ref = outs
    weight = weight_ref[at]
    clipped = grad * scale
    moment = 0.9 * moment_ref[at] + 0.1 * clipped
    square = 0.999 * square_ref[at] + 0.001 * clipped * clipped
    fix_one = 1.0 - 0.9**STEP
    fix_two = 1.0 - 0.999**STEP
    update = moment / fix_one / (jnp.sqrt(square / fix_two) + 1e-08) + 0.01 * weight
    new = weight - rate * update
    new_ref[at] = new
    new_m_ref[at] = moment
    new_s_ref[at] = square
    copy_ref[at] = new.astype(BF16)


def final_kernel(pos_ref, got_ref, mine_ref, other_ref, x_ref, wt_ref, own_hbm, sent_hbm, *refs):
    states_hbm, refs = refs[:12], refs[12:]
    outs, norm_ref, rows_ref = refs[:16], refs[16], refs[17]
    own_ref, sent_ref = refs[18:20]
    states, sems, more = refs[20:32], refs[32], refs[33]
    wait_rows = fetch((own_hbm, sent_hbm), (own_ref, sent_ref), more)
    wait = fetch(states_hbm, states, sems)
    weights, firsts, seconds = states[0:4], states[4:8], states[8:12]
    dp = got_ref.shape[0] // 2
    blocks = 4
    per = dp // blocks
    parts = []
    for b in range(blocks):
        for r in range(2):
            total = got_ref[(b * per) * 2 + r]
            for i in range(1, per):
                total = total + got_ref[(b * per + i) * 2 + r]
            parts.append(total)
    squares = parts[0][4:5, :]
    for part in parts[1:]:
        squares = squares + part[4:5, :]
    norm = jnp.sqrt(jnp.sum(squares, axis=1, keepdims=True))
    norm_ref[...] = norm
    scale = 1.0 / jnp.maximum(norm, 1.0)

    cb = weights[0].shape[1]
    d_in = weights[0].shape[2]
    mr = weights[1].shape[0]
    classes = weights[2].shape[1]
    first = pos_ref[1] == 0
    mine, other = mine_ref[...], other_ref[...]
    low = jnp.where(first, mine, other)
    high = jnp.where(first, other, mine)
    wait_rows()

    for k in range(HOPS):
        r, i = k // 2, k % 2
        alpha = jnp.concatenate([parts[b * 2 + r][2 * i : 2 * i + 1] for b in range(blocks)], axis=1)
        beta = jnp.concatenate([parts[b * 2 + r][2 * i + 1 : 2 * i + 2] for b in range(blocks)], axis=1)
        low_w = wt_ref[k]
        right = jnp.where(lax.broadcasted_iota(jnp.int32, low_w.shape, 0) == ONE, alpha, low_w.astype(F32) * beta)
        hi = right.astype(BF16)
        fix = dot(low_w, hi, 1, 1) + dot(low_w, (right - hi.astype(F32)).astype(BF16), 1, 1)
        hi = fix.astype(BF16)
        lo = (fix - hi.astype(F32)).astype(BF16)
        kept = pos_ref[1] == r
        value = jnp.where(kept, own_ref[i], sent_ref[i])
        value = value - (dot(hi, x_ref[k], 1, 0) + dot(lo, x_ref[k], 1, 0))
        rows_ref[k * d_in : (k + 1) * d_in, :] = value[:d_in]

    def group(i):
        return [o for o in outs[i::4]]

    wait()
    hops = [low[0:cb], low[cb : 2 * cb], high[0:cb], high[cb : 2 * cb]]
    for k in range(HOPS):
        adam_into(weights[0], firsts[0], seconds[0], hops[k][:, :d_in], scale, 0.05, group(0), k)
    at = 2 * cb
    for half, part in enumerate((low, high)):
        for i in range(2):
            lanes = (slice(None), slice((2 * half + i) * LANES, (2 * half + i + 1) * LANES))
            grad = part[at + i * mr : at + (i + 1) * mr]
            adam_into(weights[1], firsts[1], seconds[1], grad, scale, 0.05, group(1), lanes)
    at = at + 2 * mr
    block = low[at : at + cb]
    adam_into(weights[2], firsts[2], seconds[2], block[:, :classes], scale, 0.05, group(2))
    lane = lane_of((cb, LANES))
    small = jnp.zeros((cb, LANES), F32)
    for kind in range(4):
        for k in range(HOPS):
            small = jnp.where(lane == kind * HOPS + k, hops[k][:, ONE + kind : ONE + kind + 1], small)
    for i, source in enumerate((2, 3, 0, 1)):
        small = jnp.where(lane == 4 * HOPS + i, block[:, PCOL + source : PCOL + source + 1], small)
    small = jnp.transpose(jnp.concatenate([small, jnp.zeros((LANES - cb, LANES), F32)], axis=0))
    adam_into(weights[3], firsts[3], seconds[3], small[: weights[3].shape[0], :cb], scale, 0.3, group(3))


def flip(value, mask, dp):
    return lax.ppermute(value, "dp", [(i, i ^ mask) for i in range(dp)])


def swap(value):
    return lax.ppermute(value, "rep", [(0, 1), (1, 0)])


def exchange(value):
    return lax.all_to_all(value, BOTH, 0, 0, tiled=True)


def weights_plain(wbt, wc, sp, wm, dp):
    cb, classes = wc.shape
    mr, hid = wm.shape
    own = jnp.zeros((HOPS + 1, cb, LANES), BF16)
    own = own.at[:HOPS, :, : wbt.shape[2]].set(wbt.astype(BF16))
    own = own.at[HOPS, :, :classes].set(wc.astype(BF16))
    own = own.at[HOPS, :, PCOL : PCOL + sp.shape[0]].set(sp.T.astype(BF16))
    wb = lax.all_gather(own, "dp", axis=1, tiled=True)
    whole = lax.all_gather(wm.astype(BF16), "dp", axis=0, tiled=True)
    return own, wb, whole.reshape(HOPS * hid, hid // LANES, LANES).transpose(1, 0, 2)


def on_device(table, batch_index, labels, *state):
    weights, firsts, seconds = state[0:4], state[4:8], state[8:12]
    dp, rep = lax.axis_size("dp"), lax.axis_size("rep")
    n = dp * rep
    staged = dp == 16 and rep == 2
    me, core = lax.axis_index("dp"), lax.axis_index("rep")
    pos = jnp.stack([me, core]).astype(jnp.int32)
    batch = batch_index.shape[0]
    count = float(batch * n)
    nodes, width = table.shape
    cb = weights[0].shape[2]
    mr, hid = weights[1].shape
    classes = weights[2].shape[1]
    half = hid // 2
    lhs = [v.transpose(0, 2, 1) for v in (weights[0], firsts[0], seconds[0])]
    idx = batch_index.reshape(1, batch)
    lab = labels.reshape(1, batch)

    if staged:
        with jax.named_scope("prep"):
            sources = (lhs[0], weights[2], weights[3], weights[1])
            size = (HOPS + 1) * cb // 2 + 2 * mr
            own, block = call(
                prep_kernel,
                [hbm_out((HOPS + 1, cb, LANES), BF16), sds((size, LANES), BF16)],
                pos, *sources,
                smem=(0,), hbm=(1, 2, 3, 4),
                scratch=[pltpu.VMEM(v.shape, F32) for v in sources] + [pltpu.SemaphoreType.DMA((4,))],
            )
        far = [flip(block, 4 * k, dp) for k in range(1, 4)]

    with jax.named_scope("gather"):
        step = 2048
        x, gram = call(
            gather_kernel,
            [vmem((HOPS, LANES, batch), BF16), hbm_out((HOPS, LANES, LANES))],
            pltpu.with_memory_space_constraint(idx, pltpu.HBM),
            pltpu.with_memory_space_constraint(table.T, pltpu.HBM),
            grid=(nodes // step,),
            in_specs=[
                pl.BlockSpec((1, batch), lambda i: (0, 0)),
                pl.BlockSpec((width, step), lambda i: (0, i)),
            ],
            out_specs=(
                pl.BlockSpec((HOPS, LANES, batch), lambda i: (0, 0, 0)),
                pl.BlockSpec((HOPS, LANES, LANES), lambda i: (0, 0, 0)),
            ),
            scratch=[pltpu.VMEM((width, batch), F32), pltpu.VMEM((LANES, batch), F32)],
            flops=2 * nodes * width * batch,
            after=(block,) if staged else (),
            mib=24,
        )
    with jax.named_scope("gram_sum"):
        parts = gram.reshape(n, HOPS * LANES // n, LANES)
        if staged:
            (stacked,) = call(stack_kernel, [sds((4,) + block.shape, BF16)], block, *far, after=(x,))
            parts, stacked = lax.optimization_barrier((parts, stacked))
        parts = exchange(parts)
        (parts,) = call(sum_spread_kernel, [hbm_out(parts.shape)], parts)
        gram = exchange(parts).reshape(HOPS, LANES, LANES)
    with jax.named_scope("weights"):
        if staged:
            mine = [stacked] + [flip(stacked, m, dp) for m in range(1, 4)]
            mine, _ = lax.optimization_barrier((mine, parts))
            other = [swap(v) for v in mine]
            wb, wm = call(
                assemble_kernel,
                [vmem((HOPS + 1, hid, LANES), BF16), hbm_out((hid // LANES, HOPS * hid, LANES), BF16)],
                pos, *mine, *other,
                smem=(0,),
            )
        else:
            own, wb, wm = weights_plain(lhs[0], weights[2], weights[3], weights[1], dp)
    with jax.named_scope("stats"):
        coef, par, mu, wt = call(
            functools.partial(stats_kernel, count),
            [vmem((HOPS, hid, LANES)), vmem((hid, LANES)), vmem((8, LANES)), vmem((HOPS, LANES, hid), BF16)],
            gram, wb,
            flops=2 * HOPS * hid * LANES * LANES * 3,
        )
    with jax.named_scope("forward"):
        joined, pre2, pay = call(
            forward_kernel,
            [hbm_out((HOPS, hid, batch), BF16), hbm_out((hid, batch)), sds((n, 8, LANES))],
            x, wb, coef, wm,
            hbm=(3,),
            out_specs=(pl.BlockSpec(memory_space=pltpu.HBM),) * 2 + (pl.BlockSpec(memory_space=pltpu.VMEM),),
            scratch=[
                pltpu.VMEM((2, CHUNK, batch), F32),
                pltpu.VMEM(wm.shape, BF16),
                pltpu.VMEM((HOPS, hid, batch), BF16),
                pltpu.VMEM((hid, batch), F32),
                pltpu.SemaphoreType.DMA((1,)),
                pltpu.SemaphoreType.DMA((HOPS + 1,)),
            ],
            mib=16,
            flops=2 * batch * HOPS * hid * (LANES + hid),
        )
    got = exchange(pay)
    with jax.named_scope("factors"):
        hop = lambda *shape: pl.BlockSpec((1,) + shape, lambda k: (k, 0, 0))
        factors = call(
            factor_kernel,
            [hbm_out((HOPS, hid, batch), BF16)] * 3,
            x, wb, coef,
            grid=(HOPS,),
            in_specs=[hop(LANES, batch), hop(hid, LANES), hop(hid, LANES)],
            out_specs=(hop(hid, batch),) * 3,
            scratch=[pltpu.VMEM((2, CHUNK, batch), F32)],
            after=(pay,),
            flops=2 * batch * HOPS * hid * LANES * 16,
            mib=12,
        )
    with jax.named_scope("head"):
        dy2, pay, block2, stat = call(
            functools.partial(head_kernel, count, classes),
            [vmem((hid, batch)), sds((n, 8, LANES)), vmem((hid, LANES)), vmem((2, hid, LANES))],
            got, pre2, par, wb, lab,
            hbm=(1, 4),
            after=(pltpu.with_memory_space_constraint(factors[0], pltpu.HBM),),
            scratch=[
                pltpu.VMEM((hid, batch), BF16),
                pltpu.VMEM((hid, batch), F32),
                pltpu.VMEM((4, hid, LANES), F32),
                pltpu.VMEM((3, hid, LANES), F32),
                pltpu.VMEM(lab.shape, lab.dtype),
                pltpu.VMEM((hid, batch), F32),
                pltpu.SemaphoreType.DMA((2,)),
            ],
            flops=6 * batch * hid * LANES,
        )
    got = exchange(pay)
    with jax.named_scope("turn"):
        rows = mr + cb // 2
        turned = vmem if staged else sds
        dpre, keep, send, sum2 = call(
            functools.partial(turn_kernel, count),
            [vmem((hid, batch), BF16), turned((dp, rows, half)), sds((dp, rows, half), BF16), vmem((8, LANES))],
            pos, got, stat, par, pre2, dy2, joined, block2,
            smem=(0,), hbm=(4, 6),
            scratch=[
                pltpu.VMEM((3, hid, LANES), F32),
                pltpu.VMEM((HOPS, hid, batch), BF16),
                pltpu.VMEM((hid, batch), F32),
                pltpu.SemaphoreType.DMA((HOPS + 1,)),
            ],
            flops=2 * batch * HOPS * hid * hid,
        )

    def back(own_hops, *more, after=()):
        outs = [(hbm_out if own_hops else sds)((dp, 2, cb, LANES), BF16), hbm_out((2, LANES, batch))]
        with jax.named_scope("back"):
            return call(
                functools.partial(back_kernel, own_hops),
                outs,
                pos, dpre, x, wb, mu, wm, *factors, *more,
                smem=(0,),
                hbm=(5, 6, 7, 8),
                after=after,
                out_specs=(pl.BlockSpec(memory_space=pltpu.VMEM), pl.BlockSpec(memory_space=pltpu.HBM)),
                scratch=[
                    pltpu.VMEM((2, CHUNK, batch), F32),
                    pltpu.VMEM((2, hid, batch), BF16),
                    pltpu.VMEM((2, 2, hid, LANES), F32),
                    pltpu.VMEM((2, LANES, batch), F32),
                    pltpu.VMEM((2, hid // LANES, hid, LANES), BF16),
                ]
                + [pltpu.VMEM((2, hid, batch), BF16)] * 3
                + [pltpu.SemaphoreType.DMA((2, 4)), pltpu.SemaphoreType.DMA((2,))],
                flops=4 * batch * hid * (hid + 3 * LANES),
                mib=20,
            )

    recv = swap(send)
    sent_b, sent_a = back(False)
    recv_b = swap(sent_b)
    with jax.named_scope("merge_sum"):
        if staged:
            shape = (4, rows, half)
            low = call(
                split_low_kernel, [vmem(shape)] + [sds(shape, BF16)] * 3, pos, keep, recv, smem=(0,), after=(sent_b,)
            )
            moved = [flip(low[m], m, dp) for m in range(1, 4)]
            kept_b, kept_a = back(True, recv_b, after=(low[0],))
            high = call(
                split_high_kernel,
                [sds(shape[1:])] + [sds(shape[1:], BF16)] * 3,
                pos, low[0], *moved,
                smem=(0,),
            )
            kept_b, high = lax.optimization_barrier((kept_b, high))
            wide = [high[0]] + [flip(high[k], 4 * k, dp) for k in range(1, 4)]
        else:
            kept_b, kept_a = back(True, recv_b)
            total = lax.psum_scatter(keep + recv.astype(F32), "dp", scatter_dimension=0)
            wide = [total] + [jnp.zeros_like(total)] * 3
    with jax.named_scope("branch_sum"):
        got_b = lax.all_to_all(kept_b, "dp", 0, 0, tiled=True)
    with jax.named_scope("owner"):
        late = (wide[0], own, coef, gram)
        shares, pay = call(
            functools.partial(owner_kernel, count, classes),
            [sds((3 * cb + 2 * mr, LANES)), hbm_out((n, 8, LANES))],
            pos, got_b, sum2, *wide[1:], *late,
            smem=(0,),
            hbm=tuple(range(6, 10)),
            scratch=[pltpu.VMEM(v.shape, v.dtype) for v in late] + [pltpu.SemaphoreType.DMA((4,))],
        )
    theirs = swap(shares)
    got = exchange(pay)
    with jax.named_scope("final"):
        tr = [(lhs[i],) + tuple(s[1:]) for i, s in enumerate((weights, firsts, seconds))]
        shapes = [t.shape for t in tr[0]]
        outs = []
        for dtype in (F32, F32, F32, BF16):
            outs += [sds(s, dtype) for s in shapes]
        outs += [sds((1, 1)), sds((width, batch))]
        local = (*tr[0], *tr[1], *tr[2])
        res = call(
            final_kernel, outs, pos, got, shares, theirs, x, wt, kept_a, sent_a, *local,
            smem=(0,), hbm=tuple(range(6, 8 + len(local))),
            scratch=[pltpu.VMEM(v.shape, v.dtype) for v in (kept_a, sent_a) + local]
            + [pltpu.SemaphoreType.DMA((len(local),)), pltpu.SemaphoreType.DMA((2,))],
            flops=2 * batch * LANES * LANES * 3 * HOPS,
        )
    result = list(res[:16])
    for i in range(0, 16, 4):
        result[i] = result[i].transpose(0, 2, 1)
    return (*result, res[16].reshape(()), res[17].T)


def solution(mesh):
    tables = (P(BOTH, None), P(BOTH), P(BOTH))
    params = (P(None, None, "dp"), P("dp", None), P("dp", None), P(None, "dp"))
    return jax.shard_map(
        on_device,
        mesh=mesh,
        in_specs=tables + params * 3,
        out_specs=params * 4 + (P(), P(BOTH, None)),
        check_vma=False,
    )
```

```python
import functools
import math

import jax
import jax.numpy as jnp
from jax import lax
from jax.experimental import pallas as pl
from jax.experimental.pallas import tpu as pltpu
from jax.sharding import PartitionSpec as P

HOPS = 4
STEP = 7
EPS_NORM = 1e-05
LANES = 128
PCOL = 64
ONE = 100
ROWS, WIDE, CHUNK = 32, 256, 256
BOTH = ("dp", "rep")
F32 = jnp.float32
BF16 = jnp.bfloat16


def dot(left, right, left_dim, right_dim):
    return lax.dot_general(
        left,
        right,
        (((left_dim,), (right_dim,)), ((), ())),
        preferred_element_type=F32,
    )


def call(body, outs, *args, smem=(), hbm=(), after=(), grid=None, in_specs=None, out_specs=None, scratch=(), mib=12, flops=0):
    skip = len(args)
    if in_specs is None:
        spaces = {**{i: pltpu.SMEM for i in smem}, **{i: pltpu.HBM for i in hbm}}
        in_specs = [pl.BlockSpec(memory_space=spaces.get(i, pltpu.VMEM)) for i in range(skip)]
    if out_specs is None:
        out_specs = tuple(pl.BlockSpec(memory_space=pltpu.VMEM) for _ in outs)
    in_specs = list(in_specs) + [pl.BlockSpec(memory_space=pl.ANY) for _ in after]
    args = [pltpu.with_memory_space_constraint(a, pltpu.HBM) if i in hbm else a for i, a in enumerate(args)]
    moved = sum(math.prod(a.shape) * jnp.dtype(a.dtype).itemsize for a in (*args, *outs))

    def kernel(*refs):
        body(*refs[:skip], *refs[skip + len(after) :])

    kwargs = {} if grid is None else {"grid": grid}
    return pl.pallas_call(
        kernel,
        out_shape=tuple(outs),
        in_specs=in_specs,
        out_specs=out_specs,
        scratch_shapes=list(scratch),
        compiler_params=pltpu.CompilerParams(vmem_limit_bytes=mib << 20),
        cost_estimate=pl.CostEstimate(flops=1024, bytes_accessed=1024, transcendentals=0),
        **kwargs,
    )(*args, *[pltpu.with_memory_space_constraint(a, pltpu.HBM) for a in after])


def fetch(sources, buffers, sems):
    copies = [pltpu.make_async_copy(s, b, sems.at[i]) for i, (s, b) in enumerate(zip(sources, buffers))]
    for copy in copies:
        copy.start()

    def wait():
        for copy in copies:
            copy.wait()

    return wait


def sds(shape, dtype=F32):
    return jax.ShapeDtypeStruct(shape, dtype)


def vmem(shape, dtype=F32):
    return pltpu.VMEM(shape, dtype)


def hbm_out(shape, dtype=F32):
    return pltpu.HBM(shape, dtype)


def lane_of(shape):
    return lax.broadcasted_iota(jnp.int32, shape, len(shape) - 1)


def to_cols(rows, first):
    parts = []
    for i in range(4):
        row = rows[first + i : first + i + 1, :]
        parts.append(jnp.transpose(jnp.broadcast_to(row, (LANES, LANES))))
    return jnp.concatenate(parts, axis=0)


def lane_sums(part):
    total = jnp.sum(jnp.transpose(part), axis=0, keepdims=True)
    return jnp.concatenate([total[:, i * LANES : (i + 1) * LANES] for i in range(4)], axis=0)


def fold_lanes(value):
    out = value[:, :LANES]
    for i in range(1, value.shape[1] // LANES):
        out = out + value[:, i * LANES : (i + 1) * LANES]
    return out


def prep_kernel(pos_ref, wb_hbm, wc_hbm, sp_hbm, wm_hbm, own_ref, block_ref, wb_ref, wc_ref, sp_ref, wm_ref, sems):
    wait = fetch((wb_hbm, wc_hbm, sp_hbm, wm_hbm), (wb_ref, wc_ref, sp_ref, wm_ref), sems)
    mr, hid = wm_ref.shape
    own_ref[...] = jnp.zeros_like(own_ref)
    wait()
    own_ref[0:HOPS, :, 0 : wb_ref.shape[2]] = wb_ref[...].astype(BF16)
    own_ref[HOPS, :, 0 : wc_ref.shape[1]] = wc_ref[...].astype(BF16)
    own_ref[HOPS, :, PCOL : PCOL + sp_ref.shape[0]] = jnp.transpose(sp_ref[...]).astype(BF16)
    first = pos_ref[1] == 0
    part = wc_ref.shape[0] // 2
    for k in range(HOPS + 1):
        block_ref[k * part : (k + 1) * part, :] = jnp.where(first, own_ref[k, :part], own_ref[k, part:])
    at = (HOPS + 1) * part
    for i in range(2):
        left = wm_ref[:, i * LANES : (i + 1) * LANES]
        right = wm_ref[:, hid // 2 + i * LANES : hid // 2 + (i + 1) * LANES]
        block_ref[at + i * mr : at + (i + 1) * mr, :] = jnp.where(first, left, right).astype(BF16)


def stack_kernel(a_ref, b_ref, c_ref, d_ref, out_ref):
    for i, ref in enumerate((a_ref, b_ref, c_ref, d_ref)):
        out_ref[i] = ref[...]


def each_block(pos_ref, arrays):
    for which in range(2):
        half = pos_ref[1] if which == 0 else 1 - pos_ref[1]
        for t in range(4):
            for e in range(4):
                yield arrays[which * 4 + t].at[e], pos_ref[0] ^ (4 * e + t), half


def gather_kernel(idx_ref, tab_ref, x_ref, gram_ref, acc, pad):
    i = pl.program_id(0)
    width = tab_ref.shape[1]
    d_in = tab_ref.shape[0] // HOPS
    batch = idx_ref.shape[1]
    rows = lax.broadcasted_iota(jnp.int16, (width, batch), 0)
    hot = jnp.where(rows == (idx_ref[...] - i * width).astype(jnp.int16), BF16(1.0), BF16(0.0))
    part = dot(tab_ref[...].astype(BF16), hot, 1, 0)

    @pl.when(i == 0)
    def _():
        acc[...] = part

    @pl.when(i > 0)
    def _():
        acc[...] += part

    @pl.when(i == pl.num_programs(0) - 1)
    def _():
        row = lax.broadcasted_iota(jnp.int32, pad.shape, 0)
        pad[...] = jnp.where(row == d_in, 1.0, 0.0)
        for k in range(HOPS):
            pad[0:d_in, :] = acc[k * d_in : (k + 1) * d_in, :]
            x = pad[...].astype(BF16)
            x_ref[k] = x
            gram_ref[k] = dot(x, x, 1, 1)


def sum_spread_kernel(in_ref, out_ref):
    out_ref[...] = jnp.broadcast_to(jnp.sum(in_ref[...], axis=0, keepdims=True), out_ref.shape)


def three_terms(wide):
    terms = []
    for _ in range(3):
        terms.append(wide.astype(BF16))
        wide = wide - terms[-1].astype(F32)
    return terms


def exact_dot(low, wide):
    total = None
    for term in three_terms(wide):
        part = dot(low, term, 1, 0)
        total = part if total is None else total + part
    return total


def assemble_kernel(pos_ref, *refs):
    wb_ref, wm_ref = refs[8:]
    cb = wb_ref.shape[1] // 16
    mr = wm_ref.shape[1] // 16
    part = cb // 2
    first = (HOPS + 1) * part
    for ref, s, half in each_block(pos_ref, refs[:8]):
        block = ref[...]
        rows = pl.ds(pl.multiple_of(s * cb + half * part, part), part)
        for j in range(HOPS + 1):
            wb_ref[j, rows, :] = block[j * part : (j + 1) * part]
        rows = pl.ds(pl.multiple_of(s * mr, mr), mr)
        for i in range(2):
            wm_ref[half * 2 + i, rows, :] = block[first + i * mr : first + (i + 1) * mr]


def own_stats(count, rep, gram_ref, own_ref, fix_ref):
    lane = lane_of(fix_ref.shape[1:])
    tail = own_ref[HOPS].astype(F32)
    for i in range(2):
        gram = gram_ref[rep * 2 + i]
        w = own_ref[rep * 2 + i]
        wg = exact_dot(w, gram)
        mean = wg[:, ONE : ONE + 1] / count
        second = jnp.sum(wg * w.astype(F32), axis=1, keepdims=True) / count
        inv = lax.rsqrt(second - mean * mean + EPS_NORM)
        gain = jnp.where(rep == 0, tail[:, PCOL + i : PCOL + i + 1], tail[:, PCOL + 2 + i : PCOL + 3 + i])
        block = wg - mean * gram[ONE : ONE + 1, :]
        for j, value in enumerate((mean, inv, gain * inv)):
            block = jnp.where(lane == ONE + j, value, block)
        fix_ref[i] = block


def stats_kernel(count, pos_ref, gram_ref, wb_ref, own_ref, coef_ref, mu_ref, wt_ref, fix_ref):
    own_stats(count, pos_ref[1], gram_ref, own_ref, fix_ref)
    hid = wb_ref.shape[1]
    small = jnp.transpose(wb_ref[HOPS].astype(F32))
    row = lax.broadcasted_iota(jnp.int32, (16, hid), 0)

    def at(i):
        return small[PCOL + i : PCOL + i + 1, :]

    def columns(values):
        block = jnp.zeros((16, hid), F32)
        for i, value in enumerate(values):
            block = jnp.where(row == i, value, block)
        return jnp.transpose(jnp.concatenate([block, jnp.zeros((LANES - 16, hid), F32)], axis=0))

    mu_ref[...] = jnp.zeros_like(mu_ref)
    for k in range(HOPS):
        gram = gram_ref[k]
        mu_ref[k : k + 1, :] = gram[ONE : ONE + 1, :] / count
        wide = jnp.transpose(wb_ref[k].astype(F32))
        w = wide.astype(BF16)
        wt_ref[k] = w
        wg = None
        for term in three_terms(gram):
            part = dot(term, w, 1, 0)
            wg = part if wg is None else wg + part
        mean = wg[ONE : ONE + 1, :] / count
        second = jnp.sum(wg * wide, axis=0, keepdims=True) / count
        inv = lax.rsqrt(second - mean * mean + EPS_NORM)
        gain, shift, slope, join = at(k), at(HOPS + k), at(2 * HOPS + k), at(3 * HOPS + k)
        v = gain * inv
        coef_ref[k] = columns(
            (
                0.5 * v,
                0.5 * (shift - v * mean),
                0.5 * (1.0 + slope),
                0.5 * (1.0 - slope),
                1.0 + join,
                1.0 - join,
                join,
                0.5 * (1.0 - join),
                v * slope,
                0.5 * v * (1.0 - slope),
                mean,
                inv,
                v,
            )
        )


def column_set(ref, hop, at, lanes):
    block = ref[hop, at, :]
    return [jnp.broadcast_to(block[:, i : i + 1], (ROWS, WIDE)) for i in lanes]


def merge_block(wm_ref, rows):
    return jnp.concatenate([wm_ref[i, rows, :] for i in range(wm_ref.shape[0])], axis=1)


def forward_kernel(
    x_ref, wb_ref, coef_ref, wm_hbm, joined_ref, pre2_ref, pay_ref, pre, wm_ref, in_sems
):
    wait = fetch((wm_hbm,), (wm_ref,), in_sems)
    hid = wb_ref.shape[1]
    batch = x_ref.shape[2]
    per = hid // CHUNK
    jobs = [(k, c) for k in range(HOPS) for c in range(per)]

    def project(i):
        k, c = jobs[i]
        pre[i % 2] = dot(wb_ref[k, c * CHUNK : (c + 1) * CHUNK, :], x_ref[k], 1, 0)

    def units(i):
        k, c = jobs[i]
        for g in range(CHUNK // ROWS):
            at = slice(c * CHUNK + g * ROWS, c * CHUNK + (g + 1) * ROWS)
            cs = column_set(coef_ref, k, at, range(6))
            for b in range(batch // WIDE):
                lanes = slice(b * WIDE, (b + 1) * WIDE)
                u = pre[i % 2, g * ROWS : (g + 1) * ROWS, lanes] * cs[0] + cs[1]
                u = u * (cs[2] + cs[3] * jnp.tanh(u))
                joined_ref[k, at, lanes] = (u * (cs[4] + cs[5] * jnp.tanh(u))).astype(BF16)

    project(0)
    for i in range(len(jobs)):
        if i + 1 < len(jobs):
            project(i + 1)
        units(i)
        if i % per == per - 1:
            k = i // per
            if k == 0:
                wait()
            part = dot(merge_block(wm_ref, slice(k * hid, (k + 1) * hid)), joined_ref[k], 0, 0)
            if k == 0:
                pre2_ref[...] = part
            else:
                pre2_ref[...] += part
    value = pre2_ref[...]
    sums = jnp.concatenate([lane_sums(fold_lanes(value)), lane_sums(fold_lanes(value * value))], axis=0)
    pay_ref[...] = jnp.broadcast_to(sums[None], pay_ref.shape)


def par_columns(wb_ref):
    return wb_ref[HOPS][:, PCOL:].astype(F32)[:, 4 * HOPS : 5 * HOPS]


def columns2(count, rows, par):
    mean = to_cols(rows, 0) / count
    inv = lax.rsqrt(to_cols(rows, 4) / count - mean * mean + EPS_NORM)
    shape = mean.shape
    gain = jnp.broadcast_to(par[:, 0:1], shape)
    shift = jnp.broadcast_to(par[:, 1:2], shape)
    slope = jnp.broadcast_to(par[:, 2:3], shape)
    return mean, inv, gain, shift, slope


def head_kernel(
    count, classes, got_ref, pre2_ref, wb_ref, lab_hbm, dy2_ref, pay_ref, class_ref, stat_ref, act, dact, cols, sums, lab_ref, sems
):
    wait = fetch((lab_hbm,), (lab_ref,), sems)
    hid, batch = dy2_ref.shape
    par = par_columns(wb_ref)
    mean, inv, gain, shift, slope = columns2(count, jnp.sum(got_ref[...], axis=0), par)
    stat_ref[0] = mean
    stat_ref[1] = inv
    cols[0] = 0.5 * gain * inv
    cols[1] = 0.5 * (shift - gain * inv * mean)
    cols[2] = 1.0 + slope
    cols[3] = 1.0 - slope
    reps = WIDE // LANES

    def tiled(c, at):
        return jnp.concatenate([cols[c, at, :]] * reps, axis=1)

    def first(g, carry):
        at = pl.ds(pl.multiple_of(g * ROWS, ROWS), ROWS)
        c = [tiled(i, at) for i in range(4)]
        for b in range(batch // WIDE):
            lanes = slice(b * WIDE, (b + 1) * WIDE)
            u = pre2_ref[at, lanes] * c[0] + c[1]
            act[at, lanes] = (u * (c[2] + c[3] * jnp.tanh(u))).astype(BF16)
        return carry

    lax.fori_loop(0, hid // ROWS, first, 0, unroll=4)
    tail = wb_ref[HOPS]
    wc = jnp.where(lane_of(tail.shape) < PCOL, tail.astype(F32), 0.0).astype(BF16)
    logits = dot(wc, act[...], 0, 0)
    row = lax.broadcasted_iota(jnp.int32, (LANES, batch), 0)
    logits = jnp.where(row < classes, logits + par[0:LANES, 3:4], -jnp.inf)
    top = jnp.max(logits, axis=0, keepdims=True)
    e = jnp.exp(logits - top)
    probs = e / jnp.sum(e, axis=0, keepdims=True)
    wait()
    dlog = (probs - jnp.where(row == lab_ref[...], 1.0, 0.0)).astype(BF16)
    grad_class = dot(act[...], dlog, 1, 1)
    bias = jnp.sum(dlog.astype(F32), axis=1, keepdims=True)
    dact[...] = dot(wc, dlog, 1, 0)

    def second(g, carry):
        at = pl.ds(pl.multiple_of(g * ROWS, ROWS), ROWS)
        c = [tiled(i, at) for i in range(4)]
        m = jnp.concatenate([stat_ref[0, at, :]] * reps, axis=1)
        v = jnp.concatenate([stat_ref[1, at, :]] * reps, axis=1)
        acc = [jnp.zeros((ROWS, WIDE), F32) for _ in range(3)]
        for b in range(batch // WIDE):
            lanes = slice(b * WIDE, (b + 1) * WIDE)
            p = pre2_ref[at, lanes]
            d = dact[at, lanes]
            u = p * c[0] + c[1]
            t = jnp.tanh(u)
            w = u * (1.0 - t)
            dy = d * (0.5 * (c[2] + c[3] * (t + w * (1.0 + t))))
            dy2_ref[at, lanes] = dy
            acc[0] = acc[0] + dy
            acc[1] = acc[1] + dy * ((p - m) * v)
            acc[2] = acc[2] + d * w
        for i in range(3):
            sums[i, at, :] = fold_lanes(acc[i])
        return carry

    lax.fori_loop(0, hid // ROWS, second, 0, unroll=4)
    pay = jnp.concatenate([lane_sums(sums[0]), lane_sums(sums[1])], axis=0)
    pay_ref[...] = jnp.broadcast_to(pay[None], pay_ref.shape)
    lane = lane_of((hid, LANES))
    slope_sum = jnp.sum(sums[2], axis=1, keepdims=True)
    bias = jnp.concatenate([bias, jnp.zeros((hid - LANES, 1), F32)], axis=0)
    block = jnp.where(lane < classes, grad_class, 0.0)
    block = jnp.where(lane == PCOL, slope_sum, block)
    class_ref[...] = jnp.where(lane == PCOL + 1, bias, block)


def turn_kernel(
    count, pos_ref, got_ref, stat_ref, wb_ref, pre2_ref, dy2_ref, joined_ref, class_ref, dpre_ref, keep_ref, send_ref, sum2_ref, cols
):
    hid, batch = dy2_ref.shape
    half = send_ref.shape[2]
    rows8 = jnp.sum(got_ref[...], axis=0)
    sum2_ref[...] = rows8
    mean, inv = stat_ref[0], stat_ref[1]
    v = jnp.broadcast_to(par_columns(wb_ref)[:, 0:1], mean.shape) * inv
    cols[0] = v
    cols[1] = v * to_cols(rows8, 0) / count
    cols[2] = v * inv * to_cols(rows8, 4) / count
    reps = WIDE // LANES
    for g in range(hid // ROWS):
        at = slice(g * ROWS, (g + 1) * ROWS)
        c = [jnp.concatenate([cols[i, at, :]] * reps, axis=1) for i in range(3)]
        m = jnp.concatenate([stat_ref[0, at, :]] * reps, axis=1)
        for b in range(batch // WIDE):
            lanes = slice(b * WIDE, (b + 1) * WIDE)
            value = c[0] * dy2_ref[at, lanes] - c[1] - (pre2_ref[at, lanes] - m) * c[2]
            dpre_ref[at, lanes] = value.astype(BF16)
    mine = pl.ds(pl.multiple_of(pos_ref[1] * half, half), half)
    theirs = pl.ds(pl.multiple_of((1 - pos_ref[1]) * half, half), half)
    dp, size, _ = send_ref.shape
    per = dp // HOPS
    mr = hid // per
    cb = hid // dp
    for k in range(HOPS):
        other = dot(joined_ref[k], dpre_ref[theirs, :], 1, 1).astype(BF16)
        own = dot(joined_ref[k], dpre_ref[mine, :], 1, 1)
        for j in range(per):
            send_ref[k * per + j, 0:mr, :] = other[j * mr : (j + 1) * mr]
            keep_ref[k * per + j, 0:mr, :] = own[j * mr : (j + 1) * mr]
    first = pos_ref[1] == 0
    for s in range(dp):
        block = class_ref[s * cb : (s + 1) * cb, :]
        wide = jnp.concatenate([block[: cb // 2], block[cb // 2 :]], axis=1)
        send_ref[s, mr:size, :] = jnp.where(first, 0.0, wide).astype(BF16)
        keep_ref[s, mr:size, :] = jnp.where(first, wide, 0.0)


SMALLS = 4


def back_kernel(own, first, count, pos_ref, dpre_ref, x_ref, wb_ref, coef_ref, mu_ref, wt_hbm, wm_hbm, *refs):
    if own:
        recv_refs, refs = refs[:count], refs[count:]
    b_ref, a_out, pre, dj, dyv, sums, a_ref, wm_ref, wt_ref, sems, out_sems = refs
    hid = wt_ref.shape[2]
    batch = x_ref.shape[2]
    per = hid // CHUNK
    jobs = [(k, c) for k in range(count) for c in range(per)]
    base = 2 * (pos_ref[1] if own else 1 - pos_ref[1]) + first
    dp, _, cb, _ = b_ref.shape
    copies = []
    waits = []
    wait_wt = fetch((wt_hbm.at[pl.ds(base, count)],), (wt_ref,), out_sems.at[pl.ds(count, 1)])
    for i, (k, c) in enumerate(jobs):
        at = pl.ds(pl.multiple_of((base + k) * hid + c * CHUNK, CHUNK), CHUNK)
        rows = pl.ds(c * CHUNK, CHUNK)
        waits.append(fetch((wm_hbm.at[:, at, :],), (wm_ref.at[k, :, rows, :],), sems.at[pl.ds(i, 1)]))

    def project(i):
        k, c = jobs[i]
        rows = slice(c * CHUNK, (c + 1) * CHUNK)
        pre[i % 2] = dot(wb_ref[base + k, rows, :], x_ref[base + k], 1, 0)
        waits[i]()
        dj[i % 2] = dot(merge_block(wm_ref.at[k], rows), dpre_ref[...], 1, 0)

    def units(i):
        k, c = jobs[i]
        for g in range(CHUNK // ROWS):
            at = slice(c * CHUNK + g * ROWS, c * CHUNK + (g + 1) * ROWS)
            here = slice(g * ROWS, (g + 1) * ROWS)
            a1, b1, p1, q1, s2, q2, s1, r1 = column_set(coef_ref, base + k, at, (0, 1, 2, 3, 6, 7, 8, 9))
            one = jnp.zeros((ROWS, WIDE), F32)
            two = jnp.zeros((ROWS, WIDE), F32)
            for b in range(batch // WIDE):
                lanes = slice(b * WIDE, (b + 1) * WIDE)
                u = pre[i % 2, here, lanes] * a1 + b1
                t = jnp.tanh(u)
                u2 = u * (p1 + q1 * t)
                t2 = jnp.tanh(u2)
                d = dj[i % 2, here, lanes]
                w = u2 * (1.0 - t2)
                two = two + d * w
                d = d * (s2 + q2 * ((1.0 + t2) * (1.0 + w)))
                w = u * (1.0 - t)
                one = one + d * w
                dyv[k, at, lanes] = (d * (s1 + r1 * ((1.0 + t) * (1.0 + w)))).astype(BF16)
            sums[k, 0, at, :] = fold_lanes(one)
            sums[k, 1, at, :] = fold_lanes(two)

    def close(k):
        if k == 0:
            wait_wt()
        w = wt_ref[k]
        a_ref[k] = dot(w, dyv[k], 1, 0)
        copies.append(fetch((a_ref.at[k],), (a_out.at[k],), out_sems.at[pl.ds(k, 1)]))
        block = dot(x_ref[base + k], dyv[k], 1, 1)
        row = lax.broadcasted_iota(jnp.int32, block.shape, 0)
        total = block[ONE : ONE + 1, :]
        center = jnp.transpose(jnp.broadcast_to(mu_ref[pl.ds(base + k, 1), :], (LANES, LANES)))
        block = jnp.where(row < ONE, block - jnp.concatenate([center] * (hid // LANES), axis=1) * total, 0.0)
        smalls = (
            total,
            jnp.sum(block * w.astype(F32), axis=0, keepdims=True),
            jnp.sum(jnp.transpose(sums[k, 0]), axis=0, keepdims=True),
            jnp.sum(jnp.transpose(sums[k, 1]), axis=0, keepdims=True),
        )
        for i, value in enumerate(smalls):
            block = jnp.where(row == ONE + i, value, block)
            if not own:
                block = jnp.where(row == ONE + SMALLS + i, value - value.astype(BF16).astype(F32), block)
        block = jnp.transpose(block)
        if own:
            received = jnp.concatenate([recv_refs[k][s, 0] for s in range(dp)], axis=0).astype(F32)
            block = split_smalls(block + join_smalls(received))
        for s in range(dp):
            b_ref[s, k] = block[s * cb : (s + 1) * cb, :].astype(BF16)

    project(0)
    for i in range(len(jobs)):
        if i + 1 < len(jobs):
            project(i + 1)
        units(i)
        if i % per == per - 1:
            close(i // per)
    for done in copies:
        done()


def split_smalls(block):
    lane = lane_of(block.shape)
    rest = block - block.astype(BF16).astype(F32)
    moved = pltpu.roll(rest, SMALLS, 1)
    return jnp.where((lane >= ONE + SMALLS) & (lane < ONE + 2 * SMALLS), moved, block)


def join_smalls(block):
    lane = lane_of(block.shape)
    moved = pltpu.roll(block, LANES - SMALLS, 1)
    block = jnp.where((lane >= ONE) & (lane < ONE + SMALLS), block + moved, block)
    return jnp.where(lane < ONE + SMALLS, block, 0.0)


def split_low_kernel(pos_ref, keep_ref, got_ref, o0_ref, o1_ref, o2_ref, o3_ref):
    low, high = pos_ref[0] % 4, pos_ref[0] // 4
    for t, ref in enumerate((o0_ref, o1_ref, o2_ref, o3_ref)):
        for e in range(4):
            j = jnp.where(pos_ref[1] == 0, e * 4 + (low ^ t), (high ^ t) * 4 + e)
            ref[e] = (keep_ref[j] + got_ref[j].astype(F32)).astype(ref.dtype)


def split_high_kernel(pos_ref, own_ref, g1_ref, g2_ref, g3_ref, o0_ref, o1_ref, o2_ref, o3_ref):
    mine = jnp.where(pos_ref[1] == 0, pos_ref[0] // 4, pos_ref[0] % 4)
    for t, ref in enumerate((o0_ref, o1_ref, o2_ref, o3_ref)):
        j = mine ^ t
        value = own_ref[j] + g1_ref[j].astype(F32) + g2_ref[j].astype(F32) + g3_ref[j].astype(F32)
        ref[...] = value.astype(ref.dtype)


def owner_kernel(
    count, classes, pos_ref, got_ref, sum2_ref, w1_ref, w2_ref, w3_ref, *refs
):
    grad_ref, pay_ref, w0_ref, fix_ref, sems = refs[2:]
    wait = fetch(refs[:2], (w0_ref, fix_ref), sems)
    _, _, cb, _ = got_ref.shape
    total = jnp.sum(got_ref[...].astype(F32), axis=0)
    rep = pos_ref[1]
    lane = lane_of((cb, LANES))
    squares = jnp.zeros((1, 1), F32)
    spread = jnp.zeros((cb, LANES), F32)

    def all_sum(v):
        return jnp.sum(jnp.sum(v, axis=1, keepdims=True), axis=0, keepdims=True)

    wait()
    for i in range(2):
        b = join_smalls(total[i])
        wg = fix_ref[i]
        mean, inv, v = [wg[:, ONE + j : ONE + j + 1] for j in range(3)]
        s = b[:, ONE : ONE + 1]
        g = inv * b[:, ONE + 1 : ONE + 2]
        beta = inv * g / count
        alpha = s / count - beta * mean
        fixed = jnp.where(lane < ONE, b - beta * wg, 0.0)
        fixed = jnp.where(lane == ONE, g / v, fixed)
        fixed = jnp.where(lane == ONE + 1, s / v, fixed)
        fixed = jnp.where(lane == ONE + 2, b[:, ONE + 2 : ONE + 3], fixed)
        fixed = jnp.where(lane == ONE + 3, b[:, ONE + 3 : ONE + 4], fixed)
        grad_ref[i * cb : (i + 1) * cb, :] = fixed
        squares = squares + all_sum(fixed * fixed)
        spread = jnp.where(lane == 2 * i, alpha, spread)
        spread = jnp.where(lane == 2 * i + 1, beta, spread)
    wide = w0_ref[...].astype(F32) + w1_ref[...].astype(F32) + w2_ref[...].astype(F32) + w3_ref[...].astype(F32)
    mr = wide.shape[0] - cb // 2
    merge = wide[:mr]
    squares = squares + all_sum(merge * merge)
    at = 2 * cb
    for i in range(2):
        grad_ref[at + i * mr : at + (i + 1) * mr, :] = merge[:, i * LANES : (i + 1) * LANES]
    at = at + 2 * mr
    block = jnp.concatenate([wide[mr:, :LANES], wide[mr:, LANES:]], axis=0)
    shift_own = own_column(sum2_ref, 0, pos_ref[0], cb)
    gain_own = own_column(sum2_ref, 4, pos_ref[0], cb)
    block = jnp.where(lane == PCOL + 2, gain_own, block)
    block = jnp.where(lane == PCOL + 3, shift_own, block)
    grad_ref[at : at + cb, :] = block
    squares = squares + jnp.where(rep == 0, all_sum(block * block), 0.0)
    spread = jnp.where(lane == 4, jnp.broadcast_to(squares, spread.shape), spread)
    rows = jnp.transpose(jnp.concatenate([spread, jnp.zeros((LANES - cb, LANES), F32)], axis=0))[0:8]
    offset = (pos_ref[0] * cb) % LANES
    rows = pltpu.roll(rows, offset, 1)
    row8 = lax.broadcasted_iota(jnp.int32, rows.shape, 0)
    rows = jnp.where((row8 == 4) & (lane_of(rows.shape) != offset), 0.0, rows)
    pay_ref[...] = jnp.broadcast_to(rows[None], pay_ref.shape)


def own_column(ref, first, me, cb):
    block = (me * cb) // LANES
    row = ref[pl.ds(first + block, 1), :]
    lane = lane_of((cb, LANES))
    sub = lax.broadcasted_iota(jnp.int32, (cb, LANES), 0)
    hit = lane == sub + (me * cb) % LANES
    return jnp.sum(jnp.where(hit, jnp.broadcast_to(row, (cb, LANES)), 0.0), axis=1, keepdims=True)


def adam_into(weight_ref, moment_ref, square_ref, grad, scale, rate, outs, at=Ellipsis):
    new_ref, new_m_ref, new_s_ref, copy_ref = outs
    weight = weight_ref[at]
    clipped = grad * scale
    moment = 0.9 * moment_ref[at] + 0.1 * clipped
    square = 0.999 * square_ref[at] + 0.001 * clipped * clipped
    fix_one = 1.0 - 0.9**STEP
    fix_two = 1.0 - 0.999**STEP
    update = moment / fix_one / (jnp.sqrt(square / fix_two) + 1e-08) + 0.01 * weight
    new = weight - rate * update
    new_ref[at] = new
    new_m_ref[at] = moment
    new_s_ref[at] = square
    copy_ref[at] = new.astype(BF16)


def final_kernel(pos_ref, got_ref, mine_ref, other_ref, x_ref, wt_hbm, own_hbm, sent0_hbm, sent1_hbm, *refs):
    states_hbm, refs = refs[:12], refs[12:]
    outs, norm_ref, rows_ref = refs[:16], refs[16], refs[17]
    wt_ref, own_ref, sent_ref = refs[18:21]
    states, sems, more = refs[21:33], refs[33], refs[34]
    wait_rows = fetch(
        (wt_hbm, own_hbm, sent0_hbm, sent1_hbm),
        (wt_ref, own_ref, sent_ref.at[pl.ds(0, 1)], sent_ref.at[pl.ds(1, 1)]),
        more,
    )
    wait = fetch(states_hbm, states, sems)
    weights, firsts, seconds = states[0:4], states[4:8], states[8:12]
    dp = got_ref.shape[0] // 2
    blocks = 4
    per = dp // blocks
    parts = []
    for b in range(blocks):
        for r in range(2):
            total = got_ref[(b * per) * 2 + r]
            for i in range(1, per):
                total = total + got_ref[(b * per + i) * 2 + r]
            parts.append(total)
    squares = parts[0][4:5, :]
    for part in parts[1:]:
        squares = squares + part[4:5, :]
    norm = jnp.sqrt(jnp.sum(squares, axis=1, keepdims=True))
    norm_ref[...] = norm
    scale = 1.0 / jnp.maximum(norm, 1.0)

    cb = weights[0].shape[1]
    d_in = weights[0].shape[2]
    mr = weights[1].shape[0]
    classes = weights[2].shape[1]
    first = pos_ref[1] == 0
    mine, other = mine_ref[...], other_ref[...]
    low = jnp.where(first, mine, other)
    high = jnp.where(first, other, mine)
    wait_rows()

    for k in range(HOPS):
        r, i = k // 2, k % 2
        alpha = jnp.concatenate([parts[b * 2 + r][2 * i : 2 * i + 1] for b in range(blocks)], axis=1)
        beta = jnp.concatenate([parts[b * 2 + r][2 * i + 1 : 2 * i + 2] for b in range(blocks)], axis=1)
        low_w = wt_ref[k]
        right = jnp.where(lax.broadcasted_iota(jnp.int32, low_w.shape, 0) == ONE, alpha, low_w.astype(F32) * beta)
        hi = right.astype(BF16)
        fix = dot(low_w, hi, 1, 1) + dot(low_w, (right - hi.astype(F32)).astype(BF16), 1, 1)
        hi = fix.astype(BF16)
        lo = (fix - hi.astype(F32)).astype(BF16)
        kept = pos_ref[1] == r
        value = jnp.where(kept, own_ref[i], sent_ref[i])
        value = value - (dot(hi, x_ref[k], 1, 0) + dot(lo, x_ref[k], 1, 0))
        rows_ref[k * d_in : (k + 1) * d_in, :] = value[:d_in]

    def group(i):
        return [o for o in outs[i::4]]

    wait()
    hops = [low[0:cb], low[cb : 2 * cb], high[0:cb], high[cb : 2 * cb]]
    for k in range(HOPS):
        adam_into(weights[0], firsts[0], seconds[0], hops[k][:, :d_in], scale, 0.05, group(0), k)
    at = 2 * cb
    for half, part in enumerate((low, high)):
        for i in range(2):
            lanes = (slice(None), slice((2 * half + i) * LANES, (2 * half + i + 1) * LANES))
            grad = part[at + i * mr : at + (i + 1) * mr]
            adam_into(weights[1], firsts[1], seconds[1], grad, scale, 0.05, group(1), lanes)
    at = at + 2 * mr
    block = low[at : at + cb]
    adam_into(weights[2], firsts[2], seconds[2], block[:, :classes], scale, 0.05, group(2))
    lane = lane_of((cb, LANES))
    small = jnp.zeros((cb, LANES), F32)
    for kind in range(4):
        for k in range(HOPS):
            small = jnp.where(lane == kind * HOPS + k, hops[k][:, ONE + kind : ONE + kind + 1], small)
    for i, source in enumerate((2, 3, 0, 1)):
        small = jnp.where(lane == 4 * HOPS + i, block[:, PCOL + source : PCOL + source + 1], small)
    small = jnp.transpose(jnp.concatenate([small, jnp.zeros((LANES - cb, LANES), F32)], axis=0))
    adam_into(weights[3], firsts[3], seconds[3], small[: weights[3].shape[0], :cb], scale, 0.3, group(3))


def flip(value, mask, dp):
    return lax.ppermute(value, "dp", [(i, i ^ mask) for i in range(dp)])


def turn_flip(value, digit, dp, stage):
    pairs = []
    for i in range(dp):
        for core in range(2):
            mask = digit if (core + stage) % 2 else 4 * digit
            pairs.append((i * 2 + core, (i ^ mask) * 2 + core))
    return lax.ppermute(value, BOTH, pairs)


def swap(value):
    return lax.ppermute(value, "rep", [(0, 1), (1, 0)])


def exchange(value):
    return lax.all_to_all(value, BOTH, 0, 0, tiled=True)


def weights_plain(wbt, wc, sp, wm, dp):
    cb, classes = wc.shape
    mr, hid = wm.shape
    own = jnp.zeros((HOPS + 1, cb, LANES), BF16)
    own = own.at[:HOPS, :, : wbt.shape[2]].set(wbt.astype(BF16))
    own = own.at[HOPS, :, :classes].set(wc.astype(BF16))
    own = own.at[HOPS, :, PCOL : PCOL + sp.shape[0]].set(sp.T.astype(BF16))
    wb = lax.all_gather(own, "dp", axis=1, tiled=True)
    whole = lax.all_gather(wm.astype(BF16), "dp", axis=0, tiled=True)
    return own, wb, whole.reshape(HOPS * hid, hid // LANES, LANES).transpose(1, 0, 2)


def on_device(table, batch_index, labels, *state):
    weights, firsts, seconds = state[0:4], state[4:8], state[8:12]
    dp, rep = lax.axis_size("dp"), lax.axis_size("rep")
    n = dp * rep
    staged = dp == 16 and rep == 2
    me, core = lax.axis_index("dp"), lax.axis_index("rep")
    pos = jnp.stack([me, core]).astype(jnp.int32)
    batch = batch_index.shape[0]
    count = float(batch * n)
    nodes, width = table.shape
    cb = weights[0].shape[2]
    mr, hid = weights[1].shape
    classes = weights[2].shape[1]
    half = hid // 2
    lhs = [v.transpose(0, 2, 1) for v in (weights[0], firsts[0], seconds[0])]
    idx = batch_index.reshape(1, batch)
    lab = labels.reshape(1, batch)

    if staged:
        with jax.named_scope("prep"):
            sources = (lhs[0], weights[2], weights[3], weights[1])
            size = (HOPS + 1) * cb // 2 + 2 * mr
            own, block = call(
                prep_kernel,
                [hbm_out((HOPS + 1, cb, LANES), BF16), sds((size, LANES), BF16)],
                pos, *sources,
                smem=(0,), hbm=(1, 2, 3, 4),
                scratch=[pltpu.VMEM(v.shape, F32) for v in sources] + [pltpu.SemaphoreType.DMA((4,))],
            )
        far = [flip(block, 4 * k, dp) for k in range(1, 4)]

    with jax.named_scope("gather"):
        step = 2048
        x, gram = call(
            gather_kernel,
            [vmem((HOPS, LANES, batch), BF16), hbm_out((HOPS, LANES, LANES))],
            pltpu.with_memory_space_constraint(idx, pltpu.HBM),
            pltpu.with_memory_space_constraint(table.T, pltpu.HBM),
            grid=(nodes // step,),
            in_specs=[
                pl.BlockSpec((1, batch), lambda i: (0, 0)),
                pl.BlockSpec((width, step), lambda i: (0, i)),
            ],
            out_specs=(
                pl.BlockSpec((HOPS, LANES, batch), lambda i: (0, 0, 0)),
                pl.BlockSpec((HOPS, LANES, LANES), lambda i: (0, 0, 0)),
            ),
            scratch=[pltpu.VMEM((width, batch), F32), pltpu.VMEM((LANES, batch), F32)],
            flops=2 * nodes * width * batch,
            after=(block,) if staged else (),
            mib=24,
        )
    with jax.named_scope("gram_sum"):
        parts = gram.reshape(n, HOPS * LANES // n, LANES)
        if staged:
            (stacked,) = call(stack_kernel, [sds((4,) + block.shape, BF16)], block, *far, after=(gram,))
            parts, stacked = lax.optimization_barrier((parts, stacked))
        parts = exchange(parts)
        (parts,) = call(sum_spread_kernel, [hbm_out(parts.shape)], parts)
        gram = exchange(parts).reshape(HOPS, LANES, LANES)
    if staged:
        mine = [stacked] + [flip(stacked, t, dp) for t in range(1, 4)]
        mine, _ = lax.optimization_barrier((mine, parts))
        with jax.named_scope("weights"):
            wb, wm = call(
                assemble_kernel,
                [vmem((HOPS + 1, hid, LANES), BF16), hbm_out((hid // LANES, HOPS * hid, LANES), BF16)],
                pos, *mine, *[swap(v) for v in mine],
                smem=(0,),
            )
    else:
        own, wb, wm = weights_plain(lhs[0], weights[2], weights[3], weights[1], dp)
    with jax.named_scope("stats"):
        coef, mu, wt, fix = call(
            functools.partial(stats_kernel, count),
            [
                vmem((HOPS, hid, LANES)),
                vmem((8, LANES)),
                hbm_out((HOPS, LANES, hid), BF16),
                hbm_out((2, cb, LANES)),
            ],
            pos, gram, wb, own,
            smem=(0,),
        )
    with jax.named_scope("forward"):
        joined, pre2, pay = call(
            forward_kernel,
            [vmem((HOPS, hid, batch), BF16), vmem((hid, batch)), sds((n, 8, LANES))],
            x, wb, coef, wm,
            hbm=(3,),
            scratch=[
                pltpu.VMEM((2, CHUNK, batch), F32),
                pltpu.VMEM(wm.shape, BF16),
                pltpu.SemaphoreType.DMA((1,)),
            ],
            mib=16,
        )
    got = exchange(pay)
    with jax.named_scope("head"):
        dy2, pay, block2, stat = call(
            functools.partial(head_kernel, count, classes),
            [vmem((hid, batch)), sds((n, 8, LANES)), vmem((hid, LANES)), vmem((2, hid, LANES))],
            got, pre2, wb, lab,
            hbm=(3,),
            scratch=[
                pltpu.VMEM((hid, batch), BF16),
                pltpu.VMEM((hid, batch), F32),
                pltpu.VMEM((4, hid, LANES), F32),
                pltpu.VMEM((3, hid, LANES), F32),
                pltpu.VMEM(lab.shape, lab.dtype),
                pltpu.SemaphoreType.DMA((1,)),
            ],
            flops=6 * batch * hid * LANES,
        )
    got = exchange(pay)
    with jax.named_scope("turn"):
        rows = mr + cb // 2
        dpre, keep, send, sum2 = call(
            functools.partial(turn_kernel, count),
            [vmem((hid, batch), BF16), sds((dp, rows, half)), sds((dp, rows, half), BF16), vmem((8, LANES))],
            pos, got, stat, wb, pre2, dy2, joined, block2,
            smem=(0,),
            scratch=[pltpu.VMEM((3, hid, LANES), F32)],
            flops=2 * batch * HOPS * hid * hid,
        )

    def back(own_hops, first, num, *more, after=()):
        outs = [(hbm_out if own_hops else sds)((dp, num, cb, LANES), BF16), hbm_out((num, LANES, batch))]
        with jax.named_scope("back"):
            return call(
                functools.partial(back_kernel, own_hops, first, num),
                outs,
                pos, dpre, x, wb, coef, mu, wt, wm, *more,
                smem=(0,),
                hbm=(6, 7),
                after=after,
                out_specs=(pl.BlockSpec(memory_space=pltpu.VMEM), pl.BlockSpec(memory_space=pltpu.HBM)),
                scratch=[
                    pltpu.VMEM((2, CHUNK, batch), F32),
                    pltpu.VMEM((2, CHUNK, batch), F32),
                    pltpu.VMEM((num, hid, batch), BF16),
                    pltpu.VMEM((num, 2, hid, LANES), F32),
                    pltpu.VMEM((num, LANES, batch), F32),
                    pltpu.VMEM((num, hid // LANES, hid, LANES), BF16),
                    pltpu.VMEM((num, LANES, hid), BF16),
                    pltpu.SemaphoreType.DMA((num * hid // CHUNK,)),
                    pltpu.SemaphoreType.DMA((num + 1,)),
                ],
                mib=16,
            )

    recv = swap(send)
    sent = [back(False, 0, 1)]
    with jax.named_scope("merge_sum"):
        if staged:
            shape = (4, rows, half)
            low = call(
                split_low_kernel,
                [vmem(shape)] + [sds(shape, BF16)] * 3,
                pos, keep, recv,
                smem=(0,),
                after=(sent[0][1],),
            )
            sent.append(back(False, 1, 1, after=(low[1],)))
            recv_b = [swap(v[0]) for v in sent]
            moved = [turn_flip(low[t], t, dp, 1) for t in range(1, 4)]
            kept_b, kept_a = back(True, 0, 2, *recv_b)
            kept_b, moved = lax.optimization_barrier((kept_b, moved))
            high = call(
                split_high_kernel,
                [sds(shape[1:])] + [sds(shape[1:], BF16)] * 3,
                pos, low[0], *moved,
                smem=(0,),
            )
            wide = [high[0]] + [turn_flip(high[t], t, dp, 0) for t in range(1, 4)]
        else:
            sent.append(back(False, 1, 1))
            kept_b, kept_a = back(True, 0, 2, *[swap(v[0]) for v in sent])
            total = lax.psum_scatter(keep + recv.astype(F32), "dp", scatter_dimension=0)
            wide = [total] + [jnp.zeros_like(total)] * 3
    with jax.named_scope("branch_sum"):
        got_b = lax.all_to_all(kept_b, "dp", 0, 0, tiled=True)
    with jax.named_scope("owner"):
        late = (wide[0], fix)
        shares, pay = call(
            functools.partial(owner_kernel, count, classes),
            [sds((3 * cb + 2 * mr, LANES)), hbm_out((n, 8, LANES))],
            pos, got_b, sum2, *wide[1:], *late,
            smem=(0,),
            hbm=(6, 7),
            scratch=[pltpu.VMEM(v.shape, v.dtype) for v in late] + [pltpu.SemaphoreType.DMA((2,))],
        )
    theirs = swap(shares)
    got = exchange(pay)
    with jax.named_scope("final"):
        tr = [(lhs[i],) + tuple(s[1:]) for i, s in enumerate((weights, firsts, seconds))]
        shapes = [t.shape for t in tr[0]]
        outs = []
        for dtype in (F32, F32, F32, BF16):
            outs += [sds(s, dtype) for s in shapes]
        outs += [sds((1, 1)), sds((width, batch))]
        local = (*tr[0], *tr[1], *tr[2])
        res = call(
            final_kernel, outs, pos, got, shares, theirs, x, wt, kept_a, sent[0][1], sent[1][1], *local,
            smem=(0,), hbm=tuple(range(5, 9 + len(local))),
            scratch=[pltpu.VMEM(v.shape, v.dtype) for v in (wt, kept_a, kept_a) + local]
            + [pltpu.SemaphoreType.DMA((len(local),)), pltpu.SemaphoreType.DMA((4,))],
            flops=2 * batch * LANES * LANES * 3 * HOPS,
        )
    result = list(res[:16])
    for i in range(0, 16, 4):
        result[i] = result[i].transpose(0, 2, 1)
    return (*result, res[16].reshape(()), res[17].T)


def solution(mesh):
    tables = (P(BOTH, None), P(BOTH), P(BOTH))
    params = (P(None, None, "dp"), P("dp", None), P("dp", None), P(None, "dp"))
    return jax.shard_map(
        on_device,
        mesh=mesh,
        in_specs=tables + params * 3,
        out_specs=params * 4 + (P(), P(BOTH, None)),
        check_vma=False,
    )
```

```python
import functools
import math

import jax
import jax.numpy as jnp
from jax import lax
from jax.experimental import pallas as pl
from jax.experimental.pallas import tpu as pltpu
from jax.sharding import PartitionSpec as P

HOPS = 4
STEP = 7
EPS_NORM = 1e-05
LANES = 128
PCOL = 64
ONE = 100
ROWS, WIDE, CHUNK = 32, 256, 256
BOTH = ("dp", "rep")
F32 = jnp.float32
BF16 = jnp.bfloat16


def dot(left, right, left_dim, right_dim):
    return lax.dot_general(
        left,
        right,
        (((left_dim,), (right_dim,)), ((), ())),
        preferred_element_type=F32,
    )


def call(body, outs, *args, smem=(), hbm=(), after=(), grid=None, in_specs=None, out_specs=None, scratch=(), mib=12, flops=0):
    skip = len(args)
    if in_specs is None:
        spaces = {**{i: pltpu.SMEM for i in smem}, **{i: pltpu.HBM for i in hbm}}
        in_specs = [pl.BlockSpec(memory_space=spaces.get(i, pltpu.VMEM)) for i in range(skip)]
    if out_specs is None:
        out_specs = tuple(pl.BlockSpec(memory_space=pltpu.VMEM) for _ in outs)
    in_specs = list(in_specs) + [pl.BlockSpec(memory_space=pl.ANY) for _ in after]
    args = [pltpu.with_memory_space_constraint(a, pltpu.HBM) if i in hbm else a for i, a in enumerate(args)]
    moved = sum(math.prod(a.shape) * jnp.dtype(a.dtype).itemsize for a in (*args, *outs))

    def kernel(*refs):
        body(*refs[:skip], *refs[skip + len(after) :])

    kwargs = {} if grid is None else {"grid": grid}
    return pl.pallas_call(
        kernel,
        out_shape=tuple(outs),
        in_specs=in_specs,
        out_specs=out_specs,
        scratch_shapes=list(scratch),
        compiler_params=pltpu.CompilerParams(vmem_limit_bytes=mib << 20),
        cost_estimate=pl.CostEstimate(flops=1024, bytes_accessed=1024, transcendentals=0),
        **kwargs,
    )(*args, *[pltpu.with_memory_space_constraint(a, pltpu.HBM) for a in after])


def fetch(sources, buffers, sems):
    copies = [pltpu.make_async_copy(s, b, sems.at[i]) for i, (s, b) in enumerate(zip(sources, buffers))]
    for copy in copies:
        copy.start()

    def wait():
        for copy in copies:
            copy.wait()

    return wait


def sds(shape, dtype=F32):
    return jax.ShapeDtypeStruct(shape, dtype)


def vmem(shape, dtype=F32):
    return pltpu.VMEM(shape, dtype)


def hbm_out(shape, dtype=F32):
    return pltpu.HBM(shape, dtype)


def lane_of(shape):
    return lax.broadcasted_iota(jnp.int32, shape, len(shape) - 1)


def to_cols(rows, first):
    parts = []
    for i in range(4):
        row = rows[first + i : first + i + 1, :]
        parts.append(jnp.transpose(jnp.broadcast_to(row, (LANES, LANES))))
    return jnp.concatenate(parts, axis=0)


def lane_sums(part):
    total = jnp.sum(jnp.transpose(part), axis=0, keepdims=True)
    return jnp.concatenate([total[:, i * LANES : (i + 1) * LANES] for i in range(4)], axis=0)


def fold_lanes(value):
    out = value[:, :LANES]
    for i in range(1, value.shape[1] // LANES):
        out = out + value[:, i * LANES : (i + 1) * LANES]
    return out


def prep_kernel(pos_ref, wb_hbm, wc_hbm, sp_hbm, wm_hbm, own_ref, block_ref, wb_ref, wc_ref, sp_ref, wm_ref, sems):
    wait = fetch((wb_hbm, wc_hbm, sp_hbm, wm_hbm), (wb_ref, wc_ref, sp_ref, wm_ref), sems)
    mr, hid = wm_ref.shape
    own_ref[...] = jnp.zeros_like(own_ref)
    wait()
    own_ref[0:HOPS, :, 0 : wb_ref.shape[2]] = wb_ref[...].astype(BF16)
    own_ref[HOPS, :, 0 : wc_ref.shape[1]] = wc_ref[...].astype(BF16)
    own_ref[HOPS, :, PCOL : PCOL + sp_ref.shape[0]] = jnp.transpose(sp_ref[...]).astype(BF16)
    first = pos_ref[1] == 0
    part = wc_ref.shape[0] // 2
    for k in range(HOPS + 1):
        block_ref[k * part : (k + 1) * part, :] = jnp.where(first, own_ref[k, :part], own_ref[k, part:])
    at = (HOPS + 1) * part
    for i in range(2):
        left = wm_ref[:, i * LANES : (i + 1) * LANES]
        right = wm_ref[:, hid // 2 + i * LANES : hid // 2 + (i + 1) * LANES]
        block_ref[at + i * mr : at + (i + 1) * mr, :] = jnp.where(first, left, right).astype(BF16)


def stack_kernel(a_ref, b_ref, c_ref, d_ref, out_ref):
    for i, ref in enumerate((a_ref, b_ref, c_ref, d_ref)):
        out_ref[i] = ref[...]


def each_block(pos_ref, arrays):
    for which in range(2):
        half = pos_ref[1] if which == 0 else 1 - pos_ref[1]
        for t in range(4):
            for e in range(4):
                yield arrays[which * 4 + t].at[e], pos_ref[0] ^ (4 * e + t), half


def gather_kernel(idx_ref, tab_ref, x_ref, gram_ref, acc, pad):
    i = pl.program_id(0)
    width = tab_ref.shape[1]
    d_in = tab_ref.shape[0] // HOPS
    batch = idx_ref.shape[1]
    rows = lax.broadcasted_iota(jnp.int16, (width, batch), 0)
    hot = jnp.where(rows == (idx_ref[...] - i * width).astype(jnp.int16), BF16(1.0), BF16(0.0))
    part = dot(tab_ref[...].astype(BF16), hot, 1, 0)

    @pl.when(i == 0)
    def _():
        acc[...] = part

    @pl.when(i > 0)
    def _():
        acc[...] += part

    @pl.when(i == pl.num_programs(0) - 1)
    def _():
        row = lax.broadcasted_iota(jnp.int32, pad.shape, 0)
        pad[...] = jnp.where(row == d_in, 1.0, 0.0)
        for k in range(HOPS):
            pad[0:d_in, :] = acc[k * d_in : (k + 1) * d_in, :]
            x = pad[...].astype(BF16)
            x_ref[k] = x
            gram_ref[k] = dot(x, x, 1, 1)


def sum_spread_kernel(in_ref, out_ref):
    out_ref[...] = jnp.broadcast_to(jnp.sum(in_ref[...], axis=0, keepdims=True), out_ref.shape)


def three_terms(wide):
    terms = []
    for _ in range(3):
        terms.append(wide.astype(BF16))
        wide = wide - terms[-1].astype(F32)
    return terms


def exact_dot(low, wide):
    total = None
    for term in three_terms(wide):
        part = dot(low, term, 1, 0)
        total = part if total is None else total + part
    return total


def assemble_kernel(pos_ref, *refs):
    wb_ref, wm_ref = refs[8:]
    cb = wb_ref.shape[1] // 16
    mr = wm_ref.shape[1] // 16
    part = cb // 2
    first = (HOPS + 1) * part
    for ref, s, half in each_block(pos_ref, refs[:8]):
        block = ref[...]
        rows = pl.ds(pl.multiple_of(s * cb + half * part, part), part)
        for j in range(HOPS + 1):
            wb_ref[j, rows, :] = block[j * part : (j + 1) * part]
        rows = pl.ds(pl.multiple_of(s * mr, mr), mr)
        for i in range(2):
            wm_ref[half * 2 + i, rows, :] = block[first + i * mr : first + (i + 1) * mr]


def own_stats(count, rep, gram_ref, own_ref, fix_ref):
    lane = lane_of(fix_ref.shape[1:])
    tail = own_ref[HOPS].astype(F32)
    for i in range(2):
        gram = gram_ref[rep * 2 + i]
        w = own_ref[rep * 2 + i]
        wg = exact_dot(w, gram)
        mean = wg[:, ONE : ONE + 1] / count
        second = jnp.sum(wg * w.astype(F32), axis=1, keepdims=True) / count
        inv = lax.rsqrt(second - mean * mean + EPS_NORM)
        gain = jnp.where(rep == 0, tail[:, PCOL + i : PCOL + i + 1], tail[:, PCOL + 2 + i : PCOL + 3 + i])
        block = wg - mean * gram[ONE : ONE + 1, :]
        for j, value in enumerate((mean, inv, gain * inv)):
            block = jnp.where(lane == ONE + j, value, block)
        fix_ref[i] = block


def stats_kernel(count, pos_ref, gram_ref, wb_ref, own_ref, ws_ref, coef_ref, mu_ref, wt_ref, fix_ref):
    own_stats(count, pos_ref[1], gram_ref, own_ref, fix_ref)
    hid = wb_ref.shape[1]
    small = jnp.transpose(wb_ref[HOPS].astype(F32))
    row = lax.broadcasted_iota(jnp.int32, (16, hid), 0)

    def at(i):
        return small[PCOL + i : PCOL + i + 1, :]

    def columns(values):
        block = jnp.zeros((16, hid), F32)
        for i, value in enumerate(values):
            block = jnp.where(row == i, value, block)
        return jnp.transpose(jnp.concatenate([block, jnp.zeros((LANES - 16, hid), F32)], axis=0))

    mu_ref[...] = jnp.zeros_like(mu_ref)
    for k in range(HOPS):
        gram = gram_ref[k]
        mu_ref[k : k + 1, :] = gram[ONE : ONE + 1, :] / count
        wide = jnp.transpose(wb_ref[k].astype(F32))
        w = wide.astype(BF16)
        wt_ref[k] = w
        wg = None
        for term in three_terms(gram):
            part = dot(term, w, 1, 0)
            wg = part if wg is None else wg + part
        mean = wg[ONE : ONE + 1, :] / count
        second = jnp.sum(wg * wide, axis=0, keepdims=True) / count
        inv = lax.rsqrt(second - mean * mean + EPS_NORM)
        gain, shift, slope, join = at(k), at(HOPS + k), at(2 * HOPS + k), at(3 * HOPS + k)
        v = gain * inv
        half = 0.5 * v
        scaled = jnp.where(
            lax.broadcasted_iota(jnp.int32, wide.shape, 0) == ONE, 0.5 * shift - half * mean, half * wide
        )
        scaled = jnp.transpose(scaled)
        high = scaled.astype(BF16)
        ws_ref[k, :, 0:LANES] = high
        ws_ref[k, :, LANES : 2 * LANES] = (scaled - high.astype(F32)).astype(BF16)
        scale = 0.5 * (1.0 - join)
        coef_ref[k] = columns(
            (
                0.5 * (1.0 + slope),
                0.5 * (1.0 - slope),
                1.0 + join,
                1.0 - join,
                join / scale,
                scale,
                scale * v * slope,
                scale * 0.5 * v * (1.0 - slope),
            )
        )


def project_units(ws_ref, x_ref, k, rows):
    x = x_ref[k]
    return dot(ws_ref[k, rows, :], jnp.concatenate([x, x], axis=0), 1, 0)


def column_set(ref, hop, at, lanes):
    block = ref[hop, at, :]
    return [jnp.broadcast_to(block[:, i : i + 1], (ROWS, WIDE)) for i in lanes]


def merge_block(wm_ref, rows):
    return jnp.concatenate([wm_ref[i, rows, :] for i in range(wm_ref.shape[0])], axis=1)


def forward_kernel(
    x_ref, ws_ref, coef_ref, wt_ref, fix_ref, wm_hbm, joined_ref, pre2_ref, pay_ref, wt_out, fix_out, pre, wm_ref, sems
):
    wait = fetch((wm_hbm,), (wm_ref,), sems.at[pl.ds(2, 1)])
    stored = fetch((wt_ref, fix_ref), (wt_out, fix_out), sems)
    hid = ws_ref.shape[1]
    batch = x_ref.shape[2]
    per = hid // CHUNK
    jobs = [(k, c) for k in range(HOPS) for c in range(per)]

    def project(i):
        k, c = jobs[i]
        pre[i % 2] = project_units(ws_ref, x_ref, k, slice(c * CHUNK, (c + 1) * CHUNK))

    def units(i):
        k, c = jobs[i]
        for g in range(CHUNK // ROWS):
            at = slice(c * CHUNK + g * ROWS, c * CHUNK + (g + 1) * ROWS)
            cs = column_set(coef_ref, k, at, range(4))
            for b in range(batch // WIDE):
                lanes = slice(b * WIDE, (b + 1) * WIDE)
                u = pre[i % 2, g * ROWS : (g + 1) * ROWS, lanes]
                u = u * (cs[0] + cs[1] * jnp.tanh(u))
                joined_ref[k, at, lanes] = (u * (cs[2] + cs[3] * jnp.tanh(u))).astype(BF16)

    project(0)
    for i in range(len(jobs)):
        if i + 1 < len(jobs):
            project(i + 1)
        units(i)
        if i % per == per - 1:
            k = i // per
            if k == 0:
                wait()
            part = dot(merge_block(wm_ref, slice(k * hid, (k + 1) * hid)), joined_ref[k], 0, 0)
            if k == 0:
                pre2_ref[...] = part
            else:
                pre2_ref[...] += part
    value = pre2_ref[...]
    sums = jnp.concatenate([lane_sums(fold_lanes(value)), lane_sums(fold_lanes(value * value))], axis=0)
    pay_ref[...] = jnp.broadcast_to(sums[None], pay_ref.shape)
    stored()


def par_columns(wb_ref):
    return wb_ref[HOPS][:, PCOL:].astype(F32)[:, 4 * HOPS : 5 * HOPS]


def columns2(count, rows, par):
    mean = to_cols(rows, 0) / count
    inv = lax.rsqrt(to_cols(rows, 4) / count - mean * mean + EPS_NORM)
    shape = mean.shape
    gain = jnp.broadcast_to(par[:, 0:1], shape)
    shift = jnp.broadcast_to(par[:, 1:2], shape)
    slope = jnp.broadcast_to(par[:, 2:3], shape)
    return mean, inv, gain, shift, slope


def head_kernel(
    count, classes, got_ref, pre2_ref, wb_ref, lab_hbm, dy2_ref, pay_ref, class_ref, stat_ref, act, dact, cols, sums, lab_ref, sems
):
    wait = fetch((lab_hbm,), (lab_ref,), sems)
    hid, batch = dy2_ref.shape
    par = par_columns(wb_ref)
    mean, inv, gain, shift, slope = columns2(count, jnp.sum(got_ref[...], axis=0), par)
    stat_ref[0] = mean
    stat_ref[1] = inv
    cols[0] = 0.5 * gain * inv
    cols[1] = 0.5 * (shift - gain * inv * mean)
    cols[2] = 1.0 + slope
    cols[3] = 1.0 - slope
    reps = WIDE // LANES

    def tiled(c, at):
        return jnp.concatenate([cols[c, at, :]] * reps, axis=1)

    def first(g, carry):
        at = pl.ds(pl.multiple_of(g * ROWS, ROWS), ROWS)
        c = [tiled(i, at) for i in range(4)]
        for b in range(batch // WIDE):
            lanes = slice(b * WIDE, (b + 1) * WIDE)
            u = pre2_ref[at, lanes] * c[0] + c[1]
            act[at, lanes] = (u * (c[2] + c[3] * jnp.tanh(u))).astype(BF16)
        return carry

    lax.fori_loop(0, hid // ROWS, first, 0, unroll=4)
    tail = wb_ref[HOPS]
    wc = jnp.where(lane_of(tail.shape) < PCOL, tail.astype(F32), 0.0).astype(BF16)
    logits = dot(wc, act[...], 0, 0)
    row = lax.broadcasted_iota(jnp.int32, (LANES, batch), 0)
    logits = jnp.where(row < classes, logits + par[0:LANES, 3:4], -jnp.inf)
    top = jnp.max(logits, axis=0, keepdims=True)
    e = jnp.exp(logits - top)
    probs = e / jnp.sum(e, axis=0, keepdims=True)
    wait()
    dlog = (probs - jnp.where(row == lab_ref[...], 1.0, 0.0)).astype(BF16)
    grad_class = dot(act[...], dlog, 1, 1)
    bias = jnp.sum(dlog.astype(F32), axis=1, keepdims=True)
    dact[...] = dot(wc, dlog, 1, 0)

    def second(g, carry):
        at = pl.ds(pl.multiple_of(g * ROWS, ROWS), ROWS)
        c = [tiled(i, at) for i in range(4)]
        m = jnp.concatenate([stat_ref[0, at, :]] * reps, axis=1)
        v = jnp.concatenate([stat_ref[1, at, :]] * reps, axis=1)
        acc = [jnp.zeros((ROWS, WIDE), F32) for _ in range(3)]
        for b in range(batch // WIDE):
            lanes = slice(b * WIDE, (b + 1) * WIDE)
            p = pre2_ref[at, lanes]
            d = dact[at, lanes]
            u = p * c[0] + c[1]
            t = jnp.tanh(u)
            w = u * (1.0 - t)
            dy = d * (0.5 * (c[2] + c[3] * (t + w * (1.0 + t))))
            dy2_ref[at, lanes] = dy
            acc[0] = acc[0] + dy
            acc[1] = acc[1] + dy * ((p - m) * v)
            acc[2] = acc[2] + d * w
        for i in range(3):
            sums[i, at, :] = fold_lanes(acc[i])
        return carry

    lax.fori_loop(0, hid // ROWS, second, 0, unroll=4)
    pay = jnp.concatenate([lane_sums(sums[0]), lane_sums(sums[1])], axis=0)
    pay_ref[...] = jnp.broadcast_to(pay[None], pay_ref.shape)
    lane = lane_of((hid, LANES))
    slope_sum = jnp.sum(sums[2], axis=1, keepdims=True)
    bias = jnp.concatenate([bias, jnp.zeros((hid - LANES, 1), F32)], axis=0)
    block = jnp.where(lane < classes, grad_class, 0.0)
    block = jnp.where(lane == PCOL, slope_sum, block)
    class_ref[...] = jnp.where(lane == PCOL + 1, bias, block)


def turn_kernel(
    count, pos_ref, got_ref, stat_ref, wb_ref, pre2_ref, dy2_ref, joined_ref, class_ref, wm_hbm, dpre_ref, keep_ref, send_ref, sum2_ref, wm_ref, cols, sems
):
    wait = fetch((wm_hbm,), (wm_ref,), sems)
    hid, batch = dy2_ref.shape
    half = send_ref.shape[2]
    rows8 = jnp.sum(got_ref[...], axis=0)
    sum2_ref[...] = rows8
    mean, inv = stat_ref[0], stat_ref[1]
    v = jnp.broadcast_to(par_columns(wb_ref)[:, 0:1], mean.shape) * inv
    cols[0] = v
    cols[1] = v * to_cols(rows8, 0) / count
    cols[2] = v * inv * to_cols(rows8, 4) / count
    reps = WIDE // LANES
    for g in range(hid // ROWS):
        at = slice(g * ROWS, (g + 1) * ROWS)
        c = [jnp.concatenate([cols[i, at, :]] * reps, axis=1) for i in range(3)]
        m = jnp.concatenate([stat_ref[0, at, :]] * reps, axis=1)
        for b in range(batch // WIDE):
            lanes = slice(b * WIDE, (b + 1) * WIDE)
            value = c[0] * dy2_ref[at, lanes] - c[1] - (pre2_ref[at, lanes] - m) * c[2]
            dpre_ref[at, lanes] = value.astype(BF16)
    mine = pl.ds(pl.multiple_of(pos_ref[1] * half, half), half)
    theirs = pl.ds(pl.multiple_of((1 - pos_ref[1]) * half, half), half)
    dp, size, _ = send_ref.shape
    per = dp // HOPS
    mr = hid // per
    cb = hid // dp
    for k in range(HOPS):
        other = dot(joined_ref[k], dpre_ref[theirs, :], 1, 1).astype(BF16)
        own = dot(joined_ref[k], dpre_ref[mine, :], 1, 1)
        for j in range(per):
            send_ref[k * per + j, 0:mr, :] = other[j * mr : (j + 1) * mr]
            keep_ref[k * per + j, 0:mr, :] = own[j * mr : (j + 1) * mr]
    first = pos_ref[1] == 0
    for s in range(dp):
        block = class_ref[s * cb : (s + 1) * cb, :]
        wide = jnp.concatenate([block[: cb // 2], block[cb // 2 :]], axis=1)
        send_ref[s, mr:size, :] = jnp.where(first, 0.0, wide).astype(BF16)
        keep_ref[s, mr:size, :] = jnp.where(first, wide, 0.0)
    wait()


SMALLS = 4


def back_kernel(own, first, count, pos_ref, dpre_ref, x_ref, ws_ref, coef_ref, mu_ref, wm_ref, wt_hbm, *refs):
    if own:
        recv_refs, refs = refs[:count], refs[count:]
    b_ref, a_out, pre, dj, dyv, sums, a_ref, wt_ref, out_sems = refs
    hid = wt_ref.shape[2]
    batch = x_ref.shape[2]
    per = hid // CHUNK
    jobs = [(k, c) for k in range(count) for c in range(per)]
    base = 2 * (pos_ref[1] if own else 1 - pos_ref[1]) + first
    dp, _, cb, _ = b_ref.shape
    copies = []
    wait_wt = fetch((wt_hbm.at[pl.ds(base, count)],), (wt_ref,), out_sems.at[pl.ds(count, 1)])

    def project(i):
        k, c = jobs[i]
        rows = slice(c * CHUNK, (c + 1) * CHUNK)
        pre[i % 2] = project_units(ws_ref, x_ref, base + k, rows)
        at = pl.ds(pl.multiple_of((base + k) * hid + c * CHUNK, CHUNK), CHUNK)
        dj[i % 2] = dot(merge_block(wm_ref, at), dpre_ref[...], 1, 0)

    def units(i):
        k, c = jobs[i]
        for g in range(CHUNK // ROWS):
            at = slice(c * CHUNK + g * ROWS, c * CHUNK + (g + 1) * ROWS)
            here = slice(g * ROWS, (g + 1) * ROWS)
            p1, q1, s2, s1, r1 = column_set(coef_ref, base + k, at, (0, 1, 4, 6, 7))
            one = jnp.zeros((ROWS, WIDE), F32)
            two = jnp.zeros((ROWS, WIDE), F32)
            for b in range(batch // WIDE):
                lanes = slice(b * WIDE, (b + 1) * WIDE)
                u = pre[i % 2, here, lanes]
                t = jnp.tanh(u)
                u2 = u * (p1 + q1 * t)
                t2 = jnp.tanh(u2)
                d = dj[i % 2, here, lanes]
                w = u2 * (1.0 - t2)
                two = two + d * w
                d = d * (s2 + (1.0 + t2) * (1.0 + w))
                w = u * (1.0 - t)
                one = one + d * w
                dyv[k, at, lanes] = (d * (s1 + r1 * ((1.0 + t) * (1.0 + w)))).astype(BF16)
            sums[k, 0, at, :] = fold_lanes(one)
            sums[k, 1, at, :] = fold_lanes(two)

    def close(k):
        if k == 0:
            wait_wt()
        w = wt_ref[k]
        a_ref[k] = dot(w, dyv[k], 1, 0)
        copies.append(fetch((a_ref.at[k],), (a_out.at[k],), out_sems.at[pl.ds(k, 1)]))
        block = dot(x_ref[base + k], dyv[k], 1, 1)
        row = lax.broadcasted_iota(jnp.int32, block.shape, 0)
        total = block[ONE : ONE + 1, :]
        center = jnp.transpose(jnp.broadcast_to(mu_ref[pl.ds(base + k, 1), :], (LANES, LANES)))
        block = jnp.where(row < ONE, block - jnp.concatenate([center] * (hid // LANES), axis=1) * total, 0.0)
        smalls = (
            total,
            jnp.sum(block * w.astype(F32), axis=0, keepdims=True),
            jnp.sum(jnp.transpose(sums[k, 0] * coef_ref[base + k, :, 5:6]), axis=0, keepdims=True),
            jnp.sum(jnp.transpose(sums[k, 1]), axis=0, keepdims=True),
        )
        for i, value in enumerate(smalls):
            block = jnp.where(row == ONE + i, value, block)
            if not own:
                block = jnp.where(row == ONE + SMALLS + i, value - value.astype(BF16).astype(F32), block)
        block = jnp.transpose(block)
        if own:
            received = jnp.concatenate([recv_refs[k][s, 0] for s in range(dp)], axis=0).astype(F32)
            block = split_smalls(block + join_smalls(received))
        for s in range(dp):
            b_ref[s, k] = block[s * cb : (s + 1) * cb, :].astype(BF16)

    project(0)
    for i in range(len(jobs)):
        if i + 1 < len(jobs):
            project(i + 1)
        units(i)
        if i % per == per - 1:
            close(i // per)
    for done in copies:
        done()


def split_smalls(block):
    lane = lane_of(block.shape)
    rest = block - block.astype(BF16).astype(F32)
    moved = pltpu.roll(rest, SMALLS, 1)
    return jnp.where((lane >= ONE + SMALLS) & (lane < ONE + 2 * SMALLS), moved, block)


def join_smalls(block):
    lane = lane_of(block.shape)
    moved = pltpu.roll(block, LANES - SMALLS, 1)
    block = jnp.where((lane >= ONE) & (lane < ONE + SMALLS), block + moved, block)
    return jnp.where(lane < ONE + SMALLS, block, 0.0)


def split_low_kernel(pos_ref, keep_ref, got_ref, o0_ref, o1_ref, o2_ref, o3_ref):
    low, high = pos_ref[0] % 4, pos_ref[0] // 4
    for t, ref in enumerate((o0_ref, o1_ref, o2_ref, o3_ref)):
        for e in range(4):
            j = jnp.where(pos_ref[1] == 0, e * 4 + (low ^ t), (high ^ t) * 4 + e)
            ref[e] = (keep_ref[j] + got_ref[j].astype(F32)).astype(ref.dtype)


def split_high_kernel(pos_ref, own_ref, g1_ref, g2_ref, g3_ref, o0_ref, o1_ref, o2_ref, o3_ref):
    mine = jnp.where(pos_ref[1] == 0, pos_ref[0] // 4, pos_ref[0] % 4)
    for t, ref in enumerate((o0_ref, o1_ref, o2_ref, o3_ref)):
        j = mine ^ t
        value = own_ref[j] + g1_ref[j].astype(F32) + g2_ref[j].astype(F32) + g3_ref[j].astype(F32)
        ref[...] = value.astype(ref.dtype)


def owner_kernel(
    count, classes, pos_ref, got_ref, sum2_ref, w1_ref, w2_ref, w3_ref, *refs
):
    grad_ref, pay_ref, w0_ref, fix_ref, sems = refs[2:]
    wait = fetch(refs[:2], (w0_ref, fix_ref), sems)
    _, _, cb, _ = got_ref.shape
    total = jnp.sum(got_ref[...].astype(F32), axis=0)
    rep = pos_ref[1]
    lane = lane_of((cb, LANES))
    squares = jnp.zeros((1, 1), F32)
    spread = jnp.zeros((cb, LANES), F32)

    def all_sum(v):
        return jnp.sum(jnp.sum(v, axis=1, keepdims=True), axis=0, keepdims=True)

    others = w1_ref[...].astype(F32) + w2_ref[...].astype(F32) + w3_ref[...].astype(F32)
    wait()
    for i in range(2):
        b = join_smalls(total[i])
        wg = fix_ref[i]
        mean, inv, v = [wg[:, ONE + j : ONE + j + 1] for j in range(3)]
        s = b[:, ONE : ONE + 1]
        g = inv * b[:, ONE + 1 : ONE + 2]
        beta = inv * g / count
        alpha = s / count - beta * mean
        fixed = jnp.where(lane < ONE, b - beta * wg, 0.0)
        fixed = jnp.where(lane == ONE, g / v, fixed)
        fixed = jnp.where(lane == ONE + 1, s / v, fixed)
        fixed = jnp.where(lane == ONE + 2, b[:, ONE + 2 : ONE + 3], fixed)
        fixed = jnp.where(lane == ONE + 3, b[:, ONE + 3 : ONE + 4], fixed)
        grad_ref[i * cb : (i + 1) * cb, :] = fixed
        squares = squares + all_sum(fixed * fixed)
        spread = jnp.where(lane == 2 * i, alpha, spread)
        spread = jnp.where(lane == 2 * i + 1, beta, spread)
    wide = w0_ref[...].astype(F32) + others
    mr = wide.shape[0] - cb // 2
    merge = wide[:mr]
    squares = squares + all_sum(merge * merge)
    at = 2 * cb
    for i in range(2):
        grad_ref[at + i * mr : at + (i + 1) * mr, :] = merge[:, i * LANES : (i + 1) * LANES]
    at = at + 2 * mr
    block = jnp.concatenate([wide[mr:, :LANES], wide[mr:, LANES:]], axis=0)
    shift_own = own_column(sum2_ref, 0, pos_ref[0], cb)
    gain_own = own_column(sum2_ref, 4, pos_ref[0], cb)
    block = jnp.where(lane == PCOL + 2, gain_own, block)
    block = jnp.where(lane == PCOL + 3, shift_own, block)
    grad_ref[at : at + cb, :] = block
    squares = squares + jnp.where(rep == 0, all_sum(block * block), 0.0)
    rows = jnp.transpose(jnp.concatenate([spread, jnp.zeros((LANES - cb, LANES), F32)], axis=0))[0:8]
    packed = jnp.concatenate([rows[i : i + 1, :cb] for i in range(4)], axis=1)
    if 4 * cb < LANES:
        packed = jnp.concatenate([packed, jnp.zeros((1, LANES - 4 * cb), F32)], axis=1)
    pay = jnp.concatenate([packed, jnp.where(lane_of((1, LANES)) == 0, squares, 0.0)], axis=0)
    pay_ref[...] = jnp.broadcast_to(pay[None], pay_ref.shape)


def own_column(ref, first, me, cb):
    block = (me * cb) // LANES
    row = ref[pl.ds(first + block, 1), :]
    lane = lane_of((cb, LANES))
    sub = lax.broadcasted_iota(jnp.int32, (cb, LANES), 0)
    hit = lane == sub + (me * cb) % LANES
    return jnp.sum(jnp.where(hit, jnp.broadcast_to(row, (cb, LANES)), 0.0), axis=1, keepdims=True)


def adam_into(weight_ref, moment_ref, square_ref, grad, scale, rate, outs, at=Ellipsis):
    new_ref, new_m_ref, new_s_ref, copy_ref = outs
    weight = weight_ref[at]
    clipped = grad * scale
    moment = 0.9 * moment_ref[at] + 0.1 * clipped
    square = 0.999 * square_ref[at] + 0.001 * clipped * clipped
    fix_one = 1.0 - 0.9**STEP
    fix_two = 1.0 - 0.999**STEP
    update = moment / fix_one / (jnp.sqrt(square / fix_two) + 1e-08) + 0.01 * weight
    new = weight - rate * update
    new_ref[at] = new
    new_m_ref[at] = moment
    new_s_ref[at] = square
    copy_ref[at] = new.astype(BF16)


def final_kernel(pos_ref, got_ref, mine_ref, other_ref, x_ref, wt_hbm, own_hbm, sent0_hbm, sent1_hbm, *refs):
    states_hbm, outs_hbm, norm_ref, rows_hbm = refs[:12], refs[12:28], refs[28], refs[29]
    wt_ref, own_ref, sent_ref = refs[30:33]
    states, outs, rows_ref, sems, more, out_sems = refs[33:45], refs[45:61], refs[61], refs[62], refs[63], refs[64]
    wait_wt = fetch((wt_hbm,), (wt_ref,), more)
    wait_rows = fetch(
        (own_hbm, sent0_hbm, sent1_hbm),
        (own_ref, sent_ref.at[pl.ds(0, 1)], sent_ref.at[pl.ds(1, 1)]),
        more.at[pl.ds(1, 3)],
    )
    wait = fetch(states_hbm, states, sems)
    weights, firsts, seconds = states[0:4], states[4:8], states[8:12]
    n = got_ref.shape[0]
    cb = weights[0].shape[1]
    blocks = 4
    per = n // 2 // blocks
    lane = lane_of((blocks, LANES))
    parts = [[jnp.zeros((blocks, LANES), F32) for _ in range(4)] for _ in range(2)]
    for r in range(2):
        for j in range(per):
            rows = [got_ref[(b * per + j) * 2 + r, 0:1, :] for b in range(blocks)]
            rows = jnp.concatenate(rows, axis=0)
            here = (lane >= j * cb) & (lane < (j + 1) * cb)
            for i in range(4):
                shift = (j - i) * cb % LANES
                moved = pltpu.roll(rows, shift, 1) if shift else rows
                parts[r][i] = jnp.where(here, moved, parts[r][i])

    def spread_row(r, i):
        return jnp.concatenate([parts[r][i][b : b + 1] for b in range(blocks)], axis=1)

    squares = jnp.sum(got_ref[...], axis=0)[1:2, :]
    norm = jnp.sqrt(jnp.sum(squares, axis=1, keepdims=True))
    norm_ref[...] = norm
    scale = 1.0 / jnp.maximum(norm, 1.0)

    d_in = weights[0].shape[2]
    mr = weights[1].shape[0]
    classes = weights[2].shape[1]
    first = pos_ref[1] == 0
    mine, other = mine_ref[...], other_ref[...]
    low = jnp.where(first, mine, other)
    high = jnp.where(first, other, mine)
    stores = []
    fixes = []
    wait_wt()
    for k in range(HOPS):
        r, i = k // 2, k % 2
        alpha, beta = spread_row(r, 2 * i), spread_row(r, 2 * i + 1)
        low_w = wt_ref[k]
        right = jnp.where(lax.broadcasted_iota(jnp.int32, low_w.shape, 0) == ONE, alpha, low_w.astype(F32) * beta)
        high_part = right.astype(BF16)
        fix = dot(low_w, high_part, 1, 1) + dot(low_w, (right - high_part.astype(F32)).astype(BF16), 1, 1)
        high_part = fix.astype(BF16)
        fixes.append(jnp.concatenate([high_part, (fix - high_part.astype(F32)).astype(BF16)], axis=1))
    wait_rows()
    for k in range(HOPS):
        r, i = k // 2, k % 2
        value = jnp.where(pos_ref[1] == r, own_ref[i], sent_ref[i])
        value = value - dot(fixes[k], jnp.concatenate([x_ref[k], x_ref[k]], axis=0), 1, 0)
        rows_ref[k * d_in : (k + 1) * d_in, :] = value[:d_in]
        if i == 1:
            part = pl.ds(r * 2 * d_in, 2 * d_in)
            stores.append(fetch((rows_ref.at[part, :],), (rows_hbm.at[part, :],), out_sems.at[pl.ds(16 + r, 1)]))

    def group(i):
        return [o for o in outs[i::4]]

    wait()
    hops = [low[0:cb], low[cb : 2 * cb], high[0:cb], high[cb : 2 * cb]]
    for k in range(HOPS):
        adam_into(weights[0], firsts[0], seconds[0], hops[k][:, :d_in], scale, 0.05, group(0), k)
    at = 2 * cb
    for half, part in enumerate((low, high)):
        for i in range(2):
            lanes = (slice(None), slice((2 * half + i) * LANES, (2 * half + i + 1) * LANES))
            grad = part[at + i * mr : at + (i + 1) * mr]
            adam_into(weights[1], firsts[1], seconds[1], grad, scale, 0.05, group(1), lanes)
    at = at + 2 * mr
    block = low[at : at + cb]
    adam_into(weights[2], firsts[2], seconds[2], block[:, :classes], scale, 0.05, group(2))
    lane = lane_of((cb, LANES))
    small = jnp.zeros((cb, LANES), F32)
    for kind in range(4):
        for k in range(HOPS):
            small = jnp.where(lane == kind * HOPS + k, hops[k][:, ONE + kind : ONE + kind + 1], small)
    for i, source in enumerate((2, 3, 0, 1)):
        small = jnp.where(lane == 4 * HOPS + i, block[:, PCOL + source : PCOL + source + 1], small)
    small = jnp.transpose(jnp.concatenate([small, jnp.zeros((LANES - cb, LANES), F32)], axis=0))
    adam_into(weights[3], firsts[3], seconds[3], small[: weights[3].shape[0], :cb], scale, 0.3, group(3))
    stores.append(fetch(outs, outs_hbm, out_sems))
    for done in stores:
        done()


def flip(value, mask, dp):
    return lax.ppermute(value, "dp", [(i, i ^ mask) for i in range(dp)])


def turn_flip(value, digit, dp, stage):
    pairs = []
    for i in range(dp):
        for core in range(2):
            mask = digit if (core + stage) % 2 else 4 * digit
            pairs.append((i * 2 + core, (i ^ mask) * 2 + core))
    return lax.ppermute(value, BOTH, pairs)


def swap(value):
    return lax.ppermute(value, "rep", [(0, 1), (1, 0)])


def exchange(value):
    return lax.all_to_all(value, BOTH, 0, 0, tiled=True)


def weights_plain(wbt, wc, sp, wm, dp):
    cb, classes = wc.shape
    mr, hid = wm.shape
    own = jnp.zeros((HOPS + 1, cb, LANES), BF16)
    own = own.at[:HOPS, :, : wbt.shape[2]].set(wbt.astype(BF16))
    own = own.at[HOPS, :, :classes].set(wc.astype(BF16))
    own = own.at[HOPS, :, PCOL : PCOL + sp.shape[0]].set(sp.T.astype(BF16))
    wb = lax.all_gather(own, "dp", axis=1, tiled=True)
    whole = lax.all_gather(wm.astype(BF16), "dp", axis=0, tiled=True)
    return own, wb, whole.reshape(HOPS * hid, hid // LANES, LANES).transpose(1, 0, 2)


def on_device(table, batch_index, labels, *state):
    weights, firsts, seconds = state[0:4], state[4:8], state[8:12]
    dp, rep = lax.axis_size("dp"), lax.axis_size("rep")
    n = dp * rep
    staged = dp == 16 and rep == 2
    me, core = lax.axis_index("dp"), lax.axis_index("rep")
    pos = jnp.stack([me, core]).astype(jnp.int32)
    batch = batch_index.shape[0]
    count = float(batch * n)
    nodes, width = table.shape
    cb = weights[0].shape[2]
    mr, hid = weights[1].shape
    classes = weights[2].shape[1]
    half = hid // 2
    lhs = [v.transpose(0, 2, 1) for v in (weights[0], firsts[0], seconds[0])]
    idx = batch_index.reshape(1, batch)
    lab = labels.reshape(1, batch)

    if staged:
        with jax.named_scope("prep"):
            sources = (lhs[0], weights[2], weights[3], weights[1])
            size = (HOPS + 1) * cb // 2 + 2 * mr
            own, block = call(
                prep_kernel,
                [hbm_out((HOPS + 1, cb, LANES), BF16), sds((size, LANES), BF16)],
                pos, *sources,
                smem=(0,), hbm=(1, 2, 3, 4),
                scratch=[pltpu.VMEM(v.shape, F32) for v in sources] + [pltpu.SemaphoreType.DMA((4,))],
            )
        far = [flip(block, 4 * k, dp) for k in range(1, 4)]

    with jax.named_scope("gather"):
        step = 2048
        x, gram = call(
            gather_kernel,
            [vmem((HOPS, LANES, batch), BF16), hbm_out((HOPS, LANES, LANES))],
            pltpu.with_memory_space_constraint(idx, pltpu.HBM),
            pltpu.with_memory_space_constraint(table.T, pltpu.HBM),
            grid=(nodes // step,),
            in_specs=[
                pl.BlockSpec((1, batch), lambda i: (0, 0)),
                pl.BlockSpec((width, step), lambda i: (0, i)),
            ],
            out_specs=(
                pl.BlockSpec((HOPS, LANES, batch), lambda i: (0, 0, 0)),
                pl.BlockSpec((HOPS, LANES, LANES), lambda i: (0, 0, 0)),
            ),
            scratch=[pltpu.VMEM((width, batch), F32), pltpu.VMEM((LANES, batch), F32)],
            flops=2 * nodes * width * batch,
            after=(own,) if staged else (),
            mib=24,
        )
    with jax.named_scope("gram_sum"):
        parts = gram.reshape(n, HOPS * LANES // n, LANES)
        if staged:
            (stacked,) = call(stack_kernel, [sds((4,) + block.shape, BF16)], block, *far)
            parts, stacked = lax.optimization_barrier((parts, stacked))
        parts = exchange(parts)
        (parts,) = call(sum_spread_kernel, [hbm_out(parts.shape)], parts)
        gram = exchange(parts).reshape(HOPS, LANES, LANES)
    if staged:
        mine = [stacked] + [flip(stacked, t, dp) for t in range(1, 4)]
        mine, _ = lax.optimization_barrier((mine, parts))
        with jax.named_scope("weights"):
            wb, wm = call(
                assemble_kernel,
                [vmem((HOPS + 1, hid, LANES), BF16), hbm_out((hid // LANES, HOPS * hid, LANES), BF16)],
                pos, *mine, *[swap(v) for v in mine],
                smem=(0,),
            )
    else:
        own, wb, wm = weights_plain(lhs[0], weights[2], weights[3], weights[1], dp)
    with jax.named_scope("stats"):
        ws, coef, mu, wt, fix = call(
            functools.partial(stats_kernel, count),
            [
                vmem((HOPS, hid, 2 * LANES), BF16),
                vmem((HOPS, hid, LANES)),
                vmem((8, LANES)),
                vmem((HOPS, LANES, hid), BF16),
                vmem((2, cb, LANES)),
            ],
            pos, gram, wb, own,
            smem=(0,),
        )
    with jax.named_scope("forward"):
        joined, pre2, pay, wt, fix = call(
            forward_kernel,
            [vmem((HOPS, hid, batch), BF16), vmem((hid, batch)), sds((n, 8, LANES))]
            + [hbm_out(v.shape, v.dtype) for v in (wt, fix)],
            x, ws, coef, wt, fix, wm,
            hbm=(5,),
            out_specs=tuple(pl.BlockSpec(memory_space=m) for m in (pltpu.VMEM,) * 3 + (pltpu.HBM,) * 2),
            scratch=[
                pltpu.VMEM((2, CHUNK, batch), F32),
                pltpu.VMEM(wm.shape, BF16),
                pltpu.SemaphoreType.DMA((3,)),
            ],
        )
    got = exchange(pay)
    with jax.named_scope("head"):
        dy2, pay, block2, stat = call(
            functools.partial(head_kernel, count, classes),
            [vmem((hid, batch)), sds((n, 8, LANES)), vmem((hid, LANES)), vmem((2, hid, LANES))],
            got, pre2, wb, lab,
            hbm=(3,),
            scratch=[
                pltpu.VMEM((hid, batch), BF16),
                pltpu.VMEM((hid, batch), F32),
                pltpu.VMEM((4, hid, LANES), F32),
                pltpu.VMEM((3, hid, LANES), F32),
                pltpu.VMEM(lab.shape, lab.dtype),
                pltpu.SemaphoreType.DMA((1,)),
            ],
            flops=6 * batch * hid * LANES,
        )
    got = exchange(pay)
    with jax.named_scope("turn"):
        rows = mr + cb // 2
        dpre, keep, send, sum2, wm = call(
            functools.partial(turn_kernel, count),
            [
                vmem((hid, batch), BF16),
                sds((dp, rows, half)),
                sds((dp, rows, half), BF16),
                vmem((8, LANES)),
                vmem(wm.shape, BF16),
            ],
            pos, got, stat, wb, pre2, dy2, joined, block2, wm,
            smem=(0,), hbm=(8,),
            scratch=[pltpu.VMEM((3, hid, LANES), F32), pltpu.SemaphoreType.DMA((1,))],
            flops=2 * batch * HOPS * hid * hid,
        )

    def back(own_hops, first, num, *more, after=()):
        outs = [(hbm_out if own_hops else sds)((dp, num, cb, LANES), BF16), hbm_out((num, LANES, batch))]
        with jax.named_scope("back"):
            return call(
                functools.partial(back_kernel, own_hops, first, num),
                outs,
                pos, dpre, x, ws, coef, mu, wm, wt, *more,
                smem=(0,),
                hbm=(7,),
                after=after,
                out_specs=(pl.BlockSpec(memory_space=pltpu.VMEM), pl.BlockSpec(memory_space=pltpu.HBM)),
                scratch=[
                    pltpu.VMEM((2, CHUNK, batch), F32),
                    pltpu.VMEM((2, CHUNK, batch), F32),
                    pltpu.VMEM((num, hid, batch), BF16),
                    pltpu.VMEM((num, 2, hid, LANES), F32),
                    pltpu.VMEM((num, LANES, batch), F32),
                    pltpu.VMEM((num, LANES, hid), BF16),
                    pltpu.SemaphoreType.DMA((num + 1,)),
                ],
                mib=16,
            )

    recv = swap(send)
    sent = [back(False, 0, 1)]
    with jax.named_scope("merge_sum"):
        if staged:
            shape = (4, rows, half)
            low = call(
                split_low_kernel,
                [vmem(shape)] + [sds(shape, BF16)] * 3,
                pos, keep, recv,
                smem=(0,),
                after=(sent[0][1],),
            )
            sent.append(back(False, 1, 1, after=(low[1],)))
            recv_b = [swap(v[0]) for v in sent]
            moved = [turn_flip(low[t], t, dp, 1) for t in range(1, 4)]
            kept_b, kept_a = back(True, 0, 2, *recv_b)
            kept_b, moved = lax.optimization_barrier((kept_b, moved))
            high = call(
                split_high_kernel,
                [sds(shape[1:])] + [sds(shape[1:], BF16)] * 3,
                pos, low[0], *moved,
                smem=(0,),
            )
            wide = [high[0]] + [turn_flip(high[t], t, dp, 0) for t in range(1, 4)]
        else:
            sent.append(back(False, 1, 1))
            kept_b, kept_a = back(True, 0, 2, *[swap(v[0]) for v in sent])
            total = lax.psum_scatter(keep + recv.astype(F32), "dp", scatter_dimension=0)
            wide = [total] + [jnp.zeros_like(total)] * 3
    with jax.named_scope("branch_sum"):
        got_b = lax.all_to_all(kept_b, "dp", 0, 0, tiled=True)
    with jax.named_scope("owner"):
        late = (wide[0], fix)
        shares, pay = call(
            functools.partial(owner_kernel, count, classes),
            [sds((3 * cb + 2 * mr, LANES)), hbm_out((n, 2, LANES))],
            pos, got_b, sum2, *wide[1:], *late,
            smem=(0,),
            hbm=(6, 7),
            scratch=[pltpu.VMEM(v.shape, v.dtype) for v in late] + [pltpu.SemaphoreType.DMA((2,))],
        )
    theirs = swap(shares)
    got = exchange(pay)
    with jax.named_scope("final"):
        tr = [(lhs[i],) + tuple(s[1:]) for i, s in enumerate((weights, firsts, seconds))]
        shapes = [t.shape for t in tr[0]]
        outs = []
        for dtype in (F32, F32, F32, BF16):
            outs += [sds(s, dtype) for s in shapes]
        outs += [sds((1, 1)), sds((width, batch))]
        local = (*tr[0], *tr[1], *tr[2])
        res = call(
            final_kernel, outs, pos, got, shares, theirs, x, wt, kept_a, sent[0][1], sent[1][1], *local,
            smem=(0,), hbm=tuple(range(5, 9 + len(local))),
            out_specs=tuple(pl.BlockSpec(memory_space=pltpu.VMEM if i == 16 else pltpu.HBM) for i in range(18)),
            scratch=[pltpu.VMEM(v.shape, v.dtype) for v in (wt, kept_a, kept_a) + local]
            + [pltpu.VMEM(v.shape, v.dtype) for i, v in enumerate(outs) if i != 16]
            + [pltpu.SemaphoreType.DMA((k,)) for k in (len(local), 4, 18)],
            flops=2 * batch * LANES * LANES * 3 * HOPS,
        )
    result = list(res[:16])
    for i in range(0, 16, 4):
        result[i] = result[i].transpose(0, 2, 1)
    return (*result, res[16].reshape(()), res[17].T)


def solution(mesh):
    tables = (P(BOTH, None), P(BOTH), P(BOTH))
    params = (P(None, None, "dp"), P("dp", None), P("dp", None), P(None, "dp"))
    return jax.shard_map(
        on_device,
        mesh=mesh,
        in_specs=tables + params * 3,
        out_specs=params * 4 + (P(), P(BOTH, None)),
        check_vma=False,
    )
```

```python
import functools
import math

import jax
import jax.numpy as jnp
from jax import lax
from jax.experimental import pallas as pl
from jax.experimental.pallas import tpu as pltpu
from jax.sharding import PartitionSpec as P

HOPS = 4
STEP = 7
EPS_NORM = 1e-05
LANES = 128
PCOL = 64
ONE = 100
FREE = LANES - ONE
ROWS, WIDE, CHUNK = 32, 256, 256
BOTH = ("dp", "rep")
F32 = jnp.float32
BF16 = jnp.bfloat16


def dot(left, right, left_dim, right_dim):
    return lax.dot_general(
        left,
        right,
        (((left_dim,), (right_dim,)), ((), ())),
        preferred_element_type=F32,
    )


def call(body, outs, *args, smem=(), hbm=(), after=(), grid=None, in_specs=None, out_specs=None, scratch=(), mib=12, flops=0):
    skip = len(args)
    if in_specs is None:
        spaces = {**{i: pltpu.SMEM for i in smem}, **{i: pltpu.HBM for i in hbm}}
        in_specs = [pl.BlockSpec(memory_space=spaces.get(i, pltpu.VMEM)) for i in range(skip)]
    if out_specs is None:
        out_specs = tuple(pl.BlockSpec(memory_space=pltpu.VMEM) for _ in outs)
    in_specs = list(in_specs) + [pl.BlockSpec(memory_space=pl.ANY) for _ in after]
    args = [pltpu.with_memory_space_constraint(a, pltpu.HBM) if i in hbm else a for i, a in enumerate(args)]
    moved = sum(math.prod(a.shape) * jnp.dtype(a.dtype).itemsize for a in (*args, *outs))

    def kernel(*refs):
        body(*refs[:skip], *refs[skip + len(after) :])

    kwargs = {} if grid is None else {"grid": grid}
    return pl.pallas_call(
        kernel,
        out_shape=tuple(outs),
        in_specs=in_specs,
        out_specs=out_specs,
        scratch_shapes=list(scratch),
        compiler_params=pltpu.CompilerParams(vmem_limit_bytes=mib << 20),
        cost_estimate=pl.CostEstimate(flops=1024, bytes_accessed=1024, transcendentals=0),
        **kwargs,
    )(*args, *[pltpu.with_memory_space_constraint(a, pltpu.HBM) for a in after])


def fetch(sources, buffers, sems):
    copies = [pltpu.make_async_copy(s, b, sems.at[i]) for i, (s, b) in enumerate(zip(sources, buffers))]
    for copy in copies:
        copy.start()

    def wait():
        for copy in copies:
            copy.wait()

    return wait


def sds(shape, dtype=F32):
    return jax.ShapeDtypeStruct(shape, dtype)


def vmem(shape, dtype=F32):
    return pltpu.VMEM(shape, dtype)


def hbm_out(shape, dtype=F32):
    return pltpu.HBM(shape, dtype)


def lane_of(shape):
    return lax.broadcasted_iota(jnp.int32, shape, len(shape) - 1)


def to_cols(rows, first):
    parts = []
    for i in range(4):
        row = rows[first + i : first + i + 1, :]
        parts.append(jnp.transpose(jnp.broadcast_to(row, (LANES, LANES))))
    return jnp.concatenate(parts, axis=0)


def lane_sums(part):
    total = jnp.sum(jnp.transpose(part), axis=0, keepdims=True)
    return jnp.concatenate([total[:, i * LANES : (i + 1) * LANES] for i in range(4)], axis=0)


def fold_lanes(value):
    out = value[:, :LANES]
    for i in range(1, value.shape[1] // LANES):
        out = out + value[:, i * LANES : (i + 1) * LANES]
    return out


def prep_kernel(pos_ref, wb_hbm, wc_hbm, sp_hbm, wm_hbm, own_ref, block_ref, wb_ref, wc_ref, sp_ref, wm_ref, mix_ref, sems):
    wait = fetch((wb_hbm, wc_hbm, sp_hbm, wm_hbm), (wb_ref, wc_ref, sp_ref, wm_ref), sems)
    mr, hid = wm_ref.shape
    own_ref[...] = jnp.zeros_like(own_ref)
    wait()
    wc = wc_ref[...].astype(BF16)
    small = jnp.transpose(sp_ref[...]).astype(BF16)
    own_ref[0:HOPS, :, 0 : wb_ref.shape[2]] = wb_ref[...].astype(BF16)
    own_ref[HOPS, :, 0 : wc.shape[1]] = wc
    own_ref[HOPS, :, PCOL : PCOL + small.shape[1]] = small
    mix_ref[...] = own_ref[0:HOPS]
    mix_ref[0, :, ONE : ONE + small.shape[1]] = small
    mix_ref[1, :, ONE:LANES] = wc[:, :FREE]
    mix_ref[2, :, ONE : ONE + wc.shape[1] - FREE] = wc[:, FREE:]
    first = pos_ref[1] == 0
    part = wc.shape[0] // 2
    for k in range(HOPS):
        block_ref[k * part : (k + 1) * part, :] = jnp.where(first, mix_ref[k, :part], mix_ref[k, part:])
    at = HOPS * part
    for i in range(2):
        left = wm_ref[:, i * LANES : (i + 1) * LANES]
        right = wm_ref[:, hid // 2 + i * LANES : hid // 2 + (i + 1) * LANES]
        block_ref[at + i * mr : at + (i + 1) * mr, :] = jnp.where(first, left, right).astype(BF16)


def stack_kernel(a_ref, b_ref, c_ref, d_ref, out_ref):
    for i, ref in enumerate((a_ref, b_ref, c_ref, d_ref)):
        out_ref[i] = ref[...]


def each_block(pos_ref, arrays):
    for which in range(2):
        half = pos_ref[1] if which == 0 else 1 - pos_ref[1]
        for t in range(4):
            for e in range(4):
                yield arrays[which * 4 + t].at[e], pos_ref[0] ^ (4 * e + t), half


def gather_kernel(idx_ref, tab_ref, x_ref, gram_ref, acc, pad):
    i = pl.program_id(0)
    width = tab_ref.shape[1]
    d_in = tab_ref.shape[0] // HOPS
    batch = idx_ref.shape[1]
    rows = lax.broadcasted_iota(jnp.int16, (width, batch), 0)
    hot = jnp.where(rows == (idx_ref[...] - i * width).astype(jnp.int16), BF16(1.0), BF16(0.0))
    part = dot(tab_ref[...].astype(BF16), hot, 1, 0)

    @pl.when(i == 0)
    def _():
        acc[...] = part

    @pl.when(i > 0)
    def _():
        acc[...] += part

    @pl.when(i == pl.num_programs(0) - 1)
    def _():
        row = lax.broadcasted_iota(jnp.int32, pad.shape, 0)
        pad[...] = jnp.where(row == d_in, 1.0, 0.0)
        for k in range(HOPS):
            pad[0:d_in, :] = acc[k * d_in : (k + 1) * d_in, :]
            x = pad[...].astype(BF16)
            x_ref[k] = x
            gram_ref[k] = dot(x, x, 1, 1)


def sum_spread_kernel(in_ref, out_ref):
    out_ref[...] = jnp.broadcast_to(jnp.sum(in_ref[...], axis=0, keepdims=True), out_ref.shape)


def three_terms(wide):
    terms = []
    for _ in range(3):
        terms.append(wide.astype(BF16))
        wide = wide - terms[-1].astype(F32)
    return terms


def exact_dot(low, wide):
    total = None
    for term in three_terms(wide):
        part = dot(low, term, 1, 0)
        total = part if total is None else total + part
    return total


def assemble_kernel(classes, pos_ref, *refs):
    wb_ref, wm_out, wm_ref, sems = refs[8:]
    hid = wb_ref.shape[1]
    cb = hid // 16
    mr = wm_ref.shape[1] // 16
    part = cb // 2
    first = HOPS * part
    for ref, s, half in each_block(pos_ref, refs[:8]):
        rows = pl.ds(pl.multiple_of(s * mr, mr), mr)
        for i in range(2):
            wm_ref[half * 2 + i, rows, :] = ref[first + i * mr : first + (i + 1) * mr, :]
    stored = fetch((wm_ref,), (wm_out,), sems)
    for ref, s, half in each_block(pos_ref, refs[:8]):
        rows = pl.ds(pl.multiple_of(s * cb + half * part, part), part)
        for j in range(HOPS):
            wb_ref[j, rows, :] = ref[j * part : (j + 1) * part, :]
    lane = lane_of((hid, LANES))
    mixed = [wb_ref[j].astype(F32) for j in range(3)]
    tail = jnp.where((lane >= PCOL) & (lane < PCOL + 5 * HOPS), pltpu.roll(mixed[0], LANES + PCOL - ONE, 1), 0.0)
    tail = jnp.where(lane < FREE, pltpu.roll(mixed[1], LANES - ONE, 1), tail)
    tail = jnp.where((lane >= FREE) & (lane < classes), pltpu.roll(mixed[2], LANES + FREE - ONE, 1), tail)
    wb_ref[HOPS] = tail.astype(BF16)
    for j in range(3):
        wb_ref[j] = jnp.where(lane < ONE, mixed[j], 0.0).astype(BF16)
    stored()


def own_stats(count, rep, gram_ref, own_ref, fix_ref):
    lane = lane_of(fix_ref.shape[1:])
    tail = own_ref[HOPS].astype(F32)
    for i in range(2):
        gram = gram_ref[rep * 2 + i]
        w = own_ref[rep * 2 + i]
        wg = exact_dot(w, gram)
        mean = wg[:, ONE : ONE + 1] / count
        second = jnp.sum(wg * w.astype(F32), axis=1, keepdims=True) / count
        inv = lax.rsqrt(second - mean * mean + EPS_NORM)
        gain = jnp.where(rep == 0, tail[:, PCOL + i : PCOL + i + 1], tail[:, PCOL + 2 + i : PCOL + 3 + i])
        block = wg - mean * gram[ONE : ONE + 1, :]
        for j, value in enumerate((mean, inv, gain * inv)):
            block = jnp.where(lane == ONE + j, value, block)
        fix_ref[i] = block


def stats_kernel(count, pos_ref, gram_ref, wb_ref, own_ref, ws_ref, coef_ref, mu_ref, wt_ref, fix_ref):
    own_stats(count, pos_ref[1], gram_ref, own_ref, fix_ref)
    hid = wb_ref.shape[1]
    small = jnp.transpose(wb_ref[HOPS].astype(F32))
    row = lax.broadcasted_iota(jnp.int32, (16, hid), 0)

    def at(i):
        return small[PCOL + i : PCOL + i + 1, :]

    def columns(values):
        block = jnp.zeros((16, hid), F32)
        for i, value in enumerate(values):
            block = jnp.where(row == i, value, block)
        return jnp.transpose(jnp.concatenate([block, jnp.zeros((LANES - 16, hid), F32)], axis=0))

    mu_ref[...] = jnp.zeros_like(mu_ref)
    for k in range(HOPS):
        gram = gram_ref[k]
        mu_ref[k : k + 1, :] = gram[ONE : ONE + 1, :] / count
        wide = jnp.transpose(wb_ref[k].astype(F32))
        w = wide.astype(BF16)
        wt_ref[k] = w
        wg = None
        for term in three_terms(gram):
            part = dot(term, w, 1, 0)
            wg = part if wg is None else wg + part
        mean = wg[ONE : ONE + 1, :] / count
        second = jnp.sum(wg * wide, axis=0, keepdims=True) / count
        inv = lax.rsqrt(second - mean * mean + EPS_NORM)
        gain, shift, slope, join = at(k), at(HOPS + k), at(2 * HOPS + k), at(3 * HOPS + k)
        v = gain * inv
        half = 0.5 * v
        scaled = jnp.where(
            lax.broadcasted_iota(jnp.int32, wide.shape, 0) == ONE, 0.5 * shift - half * mean, half * wide
        )
        scaled = jnp.transpose(scaled)
        high = scaled.astype(BF16)
        ws_ref[k, :, 0:LANES] = high
        ws_ref[k, :, LANES : 2 * LANES] = (scaled - high.astype(F32)).astype(BF16)
        scale = 0.5 * (1.0 - join)
        coef_ref[k] = columns(
            (
                0.5 * (1.0 + slope),
                0.5 * (1.0 - slope),
                1.0 + join,
                1.0 - join,
                join / scale,
                scale,
                scale * v * slope,
                scale * 0.5 * v * (1.0 - slope),
            )
        )


def project_units(ws_ref, x_ref, k, rows):
    x = x_ref[k]
    return dot(ws_ref[k, rows, :], jnp.concatenate([x, x], axis=0), 1, 0)


def column_set(ref, hop, at, lanes):
    block = ref[hop, at, :]
    return [jnp.broadcast_to(block[:, i : i + 1], (ROWS, WIDE)) for i in lanes]


def merge_block(wm_ref, rows):
    return jnp.concatenate([wm_ref[i, rows, :] for i in range(wm_ref.shape[0])], axis=1)


def forward_kernel(
    x_ref, ws_ref, coef_ref, wt_ref, fix_ref, wm_hbm, joined_ref, pre2_ref, pay_ref, wt_out, fix_out, pre, wm_ref, sems
):
    wait = fetch((wm_hbm,), (wm_ref,), sems.at[pl.ds(2, 1)])
    stored = fetch((wt_ref, fix_ref), (wt_out, fix_out), sems)
    hid = ws_ref.shape[1]
    batch = x_ref.shape[2]
    per = hid // CHUNK
    jobs = [(k, c) for k in range(HOPS) for c in range(per)]

    def project(i):
        k, c = jobs[i]
        pre[i % 2] = project_units(ws_ref, x_ref, k, slice(c * CHUNK, (c + 1) * CHUNK))

    def units(i):
        k, c = jobs[i]
        for g in range(CHUNK // ROWS):
            at = slice(c * CHUNK + g * ROWS, c * CHUNK + (g + 1) * ROWS)
            cs = column_set(coef_ref, k, at, range(4))
            for b in range(batch // WIDE):
                lanes = slice(b * WIDE, (b + 1) * WIDE)
                u = pre[i % 2, g * ROWS : (g + 1) * ROWS, lanes]
                u = u * (cs[0] + cs[1] * jnp.tanh(u))
                joined_ref[k, at, lanes] = (u * (cs[2] + cs[3] * jnp.tanh(u))).astype(BF16)

    project(0)
    for i in range(len(jobs)):
        if i + 1 < len(jobs):
            project(i + 1)
        units(i)
        if i % per == per - 1:
            k = i // per
            if k == 0:
                wait()
            part = dot(merge_block(wm_ref, slice(k * hid, (k + 1) * hid)), joined_ref[k], 0, 0)
            if k == 0:
                pre2_ref[...] = part
            else:
                pre2_ref[...] += part
    value = pre2_ref[...]
    sums = jnp.concatenate([lane_sums(fold_lanes(value)), lane_sums(fold_lanes(value * value))], axis=0)
    pay_ref[...] = jnp.broadcast_to(sums[None], pay_ref.shape)
    stored()


def par_columns(wb_ref):
    return wb_ref[HOPS][:, PCOL:].astype(F32)[:, 4 * HOPS : 5 * HOPS]


def columns2(count, rows, par):
    mean = to_cols(rows, 0) / count
    inv = lax.rsqrt(to_cols(rows, 4) / count - mean * mean + EPS_NORM)
    shape = mean.shape
    gain = jnp.broadcast_to(par[:, 0:1], shape)
    shift = jnp.broadcast_to(par[:, 1:2], shape)
    slope = jnp.broadcast_to(par[:, 2:3], shape)
    return mean, inv, gain, shift, slope


def head_kernel(
    count, classes, got_ref, pre2_ref, wb_ref, lab_hbm, dy2_ref, pay_ref, class_ref, stat_ref, act, dact, cols, sums, lab_ref, sems
):
    wait = fetch((lab_hbm,), (lab_ref,), sems)
    hid, batch = dy2_ref.shape
    par = par_columns(wb_ref)
    mean, inv, gain, shift, slope = columns2(count, jnp.sum(got_ref[...], axis=0), par)
    stat_ref[0] = mean
    stat_ref[1] = inv
    cols[0] = 0.5 * gain * inv
    cols[1] = 0.5 * (shift - gain * inv * mean)
    cols[2] = 1.0 + slope
    cols[3] = 1.0 - slope
    reps = WIDE // LANES

    def tiled(c, at):
        return jnp.concatenate([cols[c, at, :]] * reps, axis=1)

    def first(g, carry):
        at = pl.ds(pl.multiple_of(g * ROWS, ROWS), ROWS)
        c = [tiled(i, at) for i in range(4)]
        for b in range(batch // WIDE):
            lanes = slice(b * WIDE, (b + 1) * WIDE)
            u = pre2_ref[at, lanes] * c[0] + c[1]
            act[at, lanes] = (u * (c[2] + c[3] * jnp.tanh(u))).astype(BF16)
        return carry

    lax.fori_loop(0, hid // ROWS, first, 0, unroll=4)
    tail = wb_ref[HOPS]
    wc = jnp.where(lane_of(tail.shape) < PCOL, tail.astype(F32), 0.0).astype(BF16)
    logits = dot(wc, act[...], 0, 0)
    row = lax.broadcasted_iota(jnp.int32, (LANES, batch), 0)
    logits = jnp.where(row < classes, logits + par[0:LANES, 3:4], -jnp.inf)
    top = jnp.max(logits, axis=0, keepdims=True)
    e = jnp.exp(logits - top)
    probs = e / jnp.sum(e, axis=0, keepdims=True)
    wait()
    dlog = (probs - jnp.where(row == lab_ref[...], 1.0, 0.0)).astype(BF16)
    grad_class = dot(act[...], dlog, 1, 1)
    bias = jnp.sum(dlog.astype(F32), axis=1, keepdims=True)
    dact[...] = dot(wc, dlog, 1, 0)

    def second(g, carry):
        at = pl.ds(pl.multiple_of(g * ROWS, ROWS), ROWS)
        c = [tiled(i, at) for i in range(4)]
        m = jnp.concatenate([stat_ref[0, at, :]] * reps, axis=1)
        v = jnp.concatenate([stat_ref[1, at, :]] * reps, axis=1)
        acc = [jnp.zeros((ROWS, WIDE), F32) for _ in range(3)]
        for b in range(batch // WIDE):
            lanes = slice(b * WIDE, (b + 1) * WIDE)
            p = pre2_ref[at, lanes]
            d = dact[at, lanes]
            u = p * c[0] + c[1]
            t = jnp.tanh(u)
            w = u * (1.0 - t)
            dy = d * (0.5 * (c[2] + c[3] * (t + w * (1.0 + t))))
            dy2_ref[at, lanes] = dy
            acc[0] = acc[0] + dy
            acc[1] = acc[1] + dy * ((p - m) * v)
            acc[2] = acc[2] + d * w
        for i in range(3):
            sums[i, at, :] = fold_lanes(acc[i])
        return carry

    lax.fori_loop(0, hid // ROWS, second, 0, unroll=4)
    pay = jnp.concatenate([lane_sums(sums[0]), lane_sums(sums[1])], axis=0)
    pay_ref[...] = jnp.broadcast_to(pay[None], pay_ref.shape)
    lane = lane_of((hid, LANES))
    slope_sum = jnp.sum(sums[2], axis=1, keepdims=True)
    bias = jnp.concatenate([bias, jnp.zeros((hid - LANES, 1), F32)], axis=0)
    block = jnp.where(lane < classes, grad_class, 0.0)
    block = jnp.where(lane == PCOL, slope_sum, block)
    class_ref[...] = jnp.where(lane == PCOL + 1, bias, block)


def turn_kernel(
    count, pos_ref, got_ref, stat_ref, wb_ref, pre2_ref, dy2_ref, joined_ref, class_ref, wm_hbm, dpre_ref, keep_ref, send_ref, sum2_ref, wm_ref, cols, sems
):
    wait = fetch((wm_hbm,), (wm_ref,), sems)
    hid, batch = dy2_ref.shape
    half = send_ref.shape[2]
    rows8 = jnp.sum(got_ref[...], axis=0)
    sum2_ref[...] = rows8
    mean, inv = stat_ref[0], stat_ref[1]
    v = jnp.broadcast_to(par_columns(wb_ref)[:, 0:1], mean.shape) * inv
    cols[0] = v
    cols[1] = v * to_cols(rows8, 0) / count
    cols[2] = v * inv * to_cols(rows8, 4) / count
    reps = WIDE // LANES
    for g in range(hid // ROWS):
        at = slice(g * ROWS, (g + 1) * ROWS)
        c = [jnp.concatenate([cols[i, at, :]] * reps, axis=1) for i in range(3)]
        m = jnp.concatenate([stat_ref[0, at, :]] * reps, axis=1)
        for b in range(batch // WIDE):
            lanes = slice(b * WIDE, (b + 1) * WIDE)
            value = c[0] * dy2_ref[at, lanes] - c[1] - (pre2_ref[at, lanes] - m) * c[2]
            dpre_ref[at, lanes] = value.astype(BF16)
    mine = pl.ds(pl.multiple_of(pos_ref[1] * half, half), half)
    theirs = pl.ds(pl.multiple_of((1 - pos_ref[1]) * half, half), half)
    dp, size, _ = send_ref.shape
    per = dp // HOPS
    mr = hid // per
    cb = hid // dp
    for k in range(HOPS):
        other = dot(joined_ref[k], dpre_ref[theirs, :], 1, 1).astype(BF16)
        own = dot(joined_ref[k], dpre_ref[mine, :], 1, 1)
        for j in range(per):
            send_ref[k * per + j, 0:mr, :] = other[j * mr : (j + 1) * mr]
            keep_ref[k * per + j, 0:mr, :] = own[j * mr : (j + 1) * mr]
    first = pos_ref[1] == 0
    for s in range(dp):
        block = class_ref[s * cb : (s + 1) * cb, :]
        wide = jnp.concatenate([block[: cb // 2], block[cb // 2 :]], axis=1)
        send_ref[s, mr:size, :] = jnp.where(first, 0.0, wide).astype(BF16)
        keep_ref[s, mr:size, :] = jnp.where(first, wide, 0.0)
    wait()


SMALLS = 4


def back_kernel(own, first, count, pos_ref, dpre_ref, x_ref, ws_ref, coef_ref, mu_ref, wm_ref, wt_hbm, *refs):
    if own:
        recv_ref, refs = refs[0], refs[1:]
    b_ref, a_out, pre, dj, dyv, sums, a_ref, wt_ref, out_sems = refs
    hid = wt_ref.shape[2]
    batch = x_ref.shape[2]
    per = hid // CHUNK
    jobs = [(k, c) for k in range(count) for c in range(per)]
    base = 2 * (pos_ref[1] if own else 1 - pos_ref[1]) + first
    dp, _, cb, _ = b_ref.shape
    copies = []
    wait_wt = fetch((wt_hbm.at[pl.ds(base, count)],), (wt_ref,), out_sems.at[pl.ds(count, 1)])

    def project(i):
        k, c = jobs[i]
        rows = slice(c * CHUNK, (c + 1) * CHUNK)
        pre[i % 2] = project_units(ws_ref, x_ref, base + k, rows)
        at = pl.ds(pl.multiple_of((base + k) * hid + c * CHUNK, CHUNK), CHUNK)
        dj[i % 2] = dot(merge_block(wm_ref, at), dpre_ref[...], 1, 0)

    def units(i):
        k, c = jobs[i]
        for g in range(CHUNK // ROWS):
            at = slice(c * CHUNK + g * ROWS, c * CHUNK + (g + 1) * ROWS)
            here = slice(g * ROWS, (g + 1) * ROWS)
            p1, q1, s2, s1, r1 = column_set(coef_ref, base + k, at, (0, 1, 4, 6, 7))
            one = jnp.zeros((ROWS, WIDE), F32)
            two = jnp.zeros((ROWS, WIDE), F32)
            for b in range(batch // WIDE):
                lanes = slice(b * WIDE, (b + 1) * WIDE)
                u = pre[i % 2, here, lanes]
                t = jnp.tanh(u)
                u2 = u * (p1 + q1 * t)
                t2 = jnp.tanh(u2)
                d = dj[i % 2, here, lanes]
                w = u2 * (1.0 - t2)
                two = two + d * w
                d = d * (s2 + (1.0 + t2) * (1.0 + w))
                w = u * (1.0 - t)
                one = one + d * w
                dyv[k, at, lanes] = (d * (s1 + r1 * ((1.0 + t) * (1.0 + w)))).astype(BF16)
            sums[k, 0, at, :] = fold_lanes(one)
            sums[k, 1, at, :] = fold_lanes(two)

    def close(k):
        if k == 0:
            wait_wt()
        w = wt_ref[k]
        a_ref[k] = dot(w, dyv[k], 1, 0)
        copies.append(fetch((a_ref.at[k],), (a_out.at[k],), out_sems.at[pl.ds(k, 1)]))
        block = dot(x_ref[base + k], dyv[k], 1, 1)
        row = lax.broadcasted_iota(jnp.int32, block.shape, 0)
        total = block[ONE : ONE + 1, :]
        center = jnp.transpose(jnp.broadcast_to(mu_ref[pl.ds(base + k, 1), :], (LANES, LANES)))
        block = jnp.where(row < ONE, block - jnp.concatenate([center] * (hid // LANES), axis=1) * total, 0.0)
        smalls = (
            total,
            jnp.sum(block * w.astype(F32), axis=0, keepdims=True),
            jnp.sum(jnp.transpose(sums[k, 0] * coef_ref[base + k, :, 5:6]), axis=0, keepdims=True),
            jnp.sum(jnp.transpose(sums[k, 1]), axis=0, keepdims=True),
        )
        for i, value in enumerate(smalls):
            block = jnp.where(row == ONE + i, value, block)
            if not own:
                block = jnp.where(row == ONE + SMALLS + i, value - value.astype(BF16).astype(F32), block)
        block = jnp.transpose(block)
        if own:
            received = jnp.concatenate([recv_ref[s, k] for s in range(dp)], axis=0).astype(F32)
            block = split_smalls(block + join_smalls(received))
        for s in range(dp):
            b_ref[s, k] = block[s * cb : (s + 1) * cb, :].astype(BF16)

    project(0)
    for i in range(len(jobs)):
        if i + 1 < len(jobs):
            project(i + 1)
        units(i)
        if i % per == per - 1:
            close(i // per)
    for done in copies:
        done()


def split_smalls(block):
    lane = lane_of(block.shape)
    rest = block - block.astype(BF16).astype(F32)
    moved = pltpu.roll(rest, SMALLS, 1)
    return jnp.where((lane >= ONE + SMALLS) & (lane < ONE + 2 * SMALLS), moved, block)


def join_smalls(block):
    lane = lane_of(block.shape)
    moved = pltpu.roll(block, LANES - SMALLS, 1)
    block = jnp.where((lane >= ONE) & (lane < ONE + SMALLS), block + moved, block)
    return jnp.where(lane < ONE + SMALLS, block, 0.0)


def split_low_kernel(pos_ref, keep_ref, got_ref, o0_ref, o1_ref, o2_ref, o3_ref):
    low, high = pos_ref[0] % 4, pos_ref[0] // 4
    for t, ref in enumerate((o0_ref, o1_ref, o2_ref, o3_ref)):
        for e in range(4):
            j = jnp.where(pos_ref[1] == 0, e * 4 + (low ^ t), (high ^ t) * 4 + e)
            ref[e] = (keep_ref[j] + got_ref[j].astype(F32)).astype(ref.dtype)


def split_high_kernel(pos_ref, own_ref, g1_ref, g2_ref, g3_ref, o0_ref, o1_ref, o2_ref, o3_ref):
    mine = jnp.where(pos_ref[1] == 0, pos_ref[0] // 4, pos_ref[0] % 4)
    for t, ref in enumerate((o0_ref, o1_ref, o2_ref, o3_ref)):
        j = mine ^ t
        value = own_ref[j] + g1_ref[j].astype(F32) + g2_ref[j].astype(F32) + g3_ref[j].astype(F32)
        ref[...] = value.astype(ref.dtype)


def owner_kernel(
    count, classes, pos_ref, got_ref, sum2_ref, w1_ref, w2_ref, w3_ref, *refs
):
    late = (len(refs) - 7) // 2
    grad_ref, pay_ref = refs[2 + late : 4 + late]
    w0_ref, fix_ref, sems, late_sems = refs[4 + 2 * late :]
    wait = fetch(refs[:2], (w0_ref, fix_ref), sems)
    brought = fetch(refs[2 : 2 + late], refs[4 + late : 4 + 2 * late], late_sems)
    _, _, cb, _ = got_ref.shape
    total = jnp.sum(got_ref[...].astype(F32), axis=0)
    rep = pos_ref[1]
    lane = lane_of((cb, LANES))
    squares = jnp.zeros((1, 1), F32)
    spread = jnp.zeros((cb, LANES), F32)

    def all_sum(v):
        return jnp.sum(jnp.sum(v, axis=1, keepdims=True), axis=0, keepdims=True)

    others = w1_ref[...].astype(F32) + w2_ref[...].astype(F32) + w3_ref[...].astype(F32)
    wait()
    for i in range(2):
        b = join_smalls(total[i])
        wg = fix_ref[i]
        mean, inv, v = [wg[:, ONE + j : ONE + j + 1] for j in range(3)]
        s = b[:, ONE : ONE + 1]
        g = inv * b[:, ONE + 1 : ONE + 2]
        beta = inv * g / count
        alpha = s / count - beta * mean
        fixed = jnp.where(lane < ONE, b - beta * wg, 0.0)
        fixed = jnp.where(lane == ONE, g / v, fixed)
        fixed = jnp.where(lane == ONE + 1, s / v, fixed)
        fixed = jnp.where(lane == ONE + 2, b[:, ONE + 2 : ONE + 3], fixed)
        fixed = jnp.where(lane == ONE + 3, b[:, ONE + 3 : ONE + 4], fixed)
        grad_ref[i * cb : (i + 1) * cb, :] = fixed
        squares = squares + all_sum(fixed * fixed)
        spread = jnp.where(lane == 2 * i, alpha, spread)
        spread = jnp.where(lane == 2 * i + 1, beta, spread)
    wide = w0_ref[...].astype(F32) + others
    mr = wide.shape[0] - cb // 2
    merge = wide[:mr]
    squares = squares + all_sum(merge * merge)
    at = 2 * cb
    for i in range(2):
        grad_ref[at + i * mr : at + (i + 1) * mr, :] = merge[:, i * LANES : (i + 1) * LANES]
    at = at + 2 * mr
    block = jnp.concatenate([wide[mr:, :LANES], wide[mr:, LANES:]], axis=0)
    shift_own = own_column(sum2_ref, 0, pos_ref[0], cb)
    gain_own = own_column(sum2_ref, 4, pos_ref[0], cb)
    block = jnp.where(lane == PCOL + 2, gain_own, block)
    block = jnp.where(lane == PCOL + 3, shift_own, block)
    grad_ref[at : at + cb, :] = block
    squares = squares + jnp.where(rep == 0, all_sum(block * block), 0.0)
    rows = jnp.transpose(jnp.concatenate([spread, jnp.zeros((LANES - cb, LANES), F32)], axis=0))[0:8]
    packed = jnp.concatenate([rows[i : i + 1, :cb] for i in range(4)], axis=1)
    if 4 * cb < LANES:
        packed = jnp.concatenate([packed, jnp.zeros((1, LANES - 4 * cb), F32)], axis=1)
    pay = jnp.concatenate([packed, jnp.where(lane_of((1, LANES)) == 0, squares, 0.0)], axis=0)
    pay_ref[...] = jnp.broadcast_to(pay[None], pay_ref.shape)
    brought()


def own_column(ref, first, me, cb):
    block = (me * cb) // LANES
    row = ref[pl.ds(first + block, 1), :]
    lane = lane_of((cb, LANES))
    sub = lax.broadcasted_iota(jnp.int32, (cb, LANES), 0)
    hit = lane == sub + (me * cb) % LANES
    return jnp.sum(jnp.where(hit, jnp.broadcast_to(row, (cb, LANES)), 0.0), axis=1, keepdims=True)


def adam_into(weight_ref, moment_ref, square_ref, grad, scale, rate, outs, at=Ellipsis):
    new_ref, new_m_ref, new_s_ref, copy_ref = outs
    weight = weight_ref[at]
    clipped = grad * scale
    moment = 0.9 * moment_ref[at] + 0.1 * clipped
    square = 0.999 * square_ref[at] + 0.001 * clipped * clipped
    fix_one = 1.0 - 0.9**STEP
    fix_two = 1.0 - 0.999**STEP
    update = moment / fix_one / (jnp.sqrt(square / fix_two) + 1e-08) + 0.01 * weight
    new = weight - rate * update
    new_ref[at] = new
    new_m_ref[at] = moment
    new_s_ref[at] = square
    copy_ref[at] = new.astype(BF16)


def final_kernel(pos_ref, got_ref, mine_ref, other_ref, x_ref, wt_ref, own_ref, sent_ref, *refs):
    states, outs_hbm, norm_ref, rows_hbm = refs[:12], refs[12:28], refs[28], refs[29]
    outs, rows_ref, out_sems = refs[30:46], refs[46], refs[47]
    weights, firsts, seconds = states[0:4], states[4:8], states[8:12]
    n = got_ref.shape[0]
    cb = weights[0].shape[1]
    blocks = 4
    per = n // 2 // blocks
    lane = lane_of((blocks, LANES))
    parts = [[jnp.zeros((blocks, LANES), F32) for _ in range(4)] for _ in range(2)]
    for r in range(2):
        for j in range(per):
            rows = [got_ref[(b * per + j) * 2 + r, 0:1, :] for b in range(blocks)]
            rows = jnp.concatenate(rows, axis=0)
            here = (lane >= j * cb) & (lane < (j + 1) * cb)
            for i in range(4):
                shift = (j - i) * cb % LANES
                moved = pltpu.roll(rows, shift, 1) if shift else rows
                parts[r][i] = jnp.where(here, moved, parts[r][i])

    def spread_row(r, i):
        return jnp.concatenate([parts[r][i][b : b + 1] for b in range(blocks)], axis=1)

    squares = jnp.sum(got_ref[...], axis=0)[1:2, :]
    norm = jnp.sqrt(jnp.sum(squares, axis=1, keepdims=True))
    norm_ref[...] = norm
    scale = 1.0 / jnp.maximum(norm, 1.0)

    d_in = weights[0].shape[2]
    mr = weights[1].shape[0]
    classes = weights[2].shape[1]
    first = pos_ref[1] == 0
    mine, other = mine_ref[...], other_ref[...]
    low = jnp.where(first, mine, other)
    high = jnp.where(first, other, mine)
    stores = []
    fixes = []
    for k in range(HOPS):
        r, i = k // 2, k % 2
        alpha, beta = spread_row(r, 2 * i), spread_row(r, 2 * i + 1)
        low_w = wt_ref[k]
        right = jnp.where(lax.broadcasted_iota(jnp.int32, low_w.shape, 0) == ONE, alpha, low_w.astype(F32) * beta)
        high_part = right.astype(BF16)
        fix = dot(low_w, high_part, 1, 1) + dot(low_w, (right - high_part.astype(F32)).astype(BF16), 1, 1)
        high_part = fix.astype(BF16)
        fixes.append(jnp.concatenate([high_part, (fix - high_part.astype(F32)).astype(BF16)], axis=1))
    for k in range(HOPS):
        r, i = k // 2, k % 2
        value = jnp.where(pos_ref[1] == r, own_ref[i], sent_ref[i])
        value = value - dot(fixes[k], jnp.concatenate([x_ref[k], x_ref[k]], axis=0), 1, 0)
        rows_ref[k * d_in : (k + 1) * d_in, :] = value[:d_in]
        if i == 1:
            part = pl.ds(r * 2 * d_in, 2 * d_in)
            stores.append(fetch((rows_ref.at[part, :],), (rows_hbm.at[part, :],), out_sems.at[pl.ds(16 + r, 1)]))

    def group(i):
        return [o for o in outs[i::4]]

    hops = [low[0:cb], low[cb : 2 * cb], high[0:cb], high[cb : 2 * cb]]
    for k in range(HOPS):
        adam_into(weights[0], firsts[0], seconds[0], hops[k][:, :d_in], scale, 0.05, group(0), k)
    at = 2 * cb
    for half, part in enumerate((low, high)):
        for i in range(2):
            lanes = (slice(None), slice((2 * half + i) * LANES, (2 * half + i + 1) * LANES))
            grad = part[at + i * mr : at + (i + 1) * mr]
            adam_into(weights[1], firsts[1], seconds[1], grad, scale, 0.05, group(1), lanes)
    at = at + 2 * mr
    block = low[at : at + cb]
    adam_into(weights[2], firsts[2], seconds[2], block[:, :classes], scale, 0.05, group(2))
    lane = lane_of((cb, LANES))
    small = jnp.zeros((cb, LANES), F32)
    for kind in range(4):
        for k in range(HOPS):
            small = jnp.where(lane == kind * HOPS + k, hops[k][:, ONE + kind : ONE + kind + 1], small)
    for i, source in enumerate((2, 3, 0, 1)):
        small = jnp.where(lane == 4 * HOPS + i, block[:, PCOL + source : PCOL + source + 1], small)
    small = jnp.transpose(jnp.concatenate([small, jnp.zeros((LANES - cb, LANES), F32)], axis=0))
    adam_into(weights[3], firsts[3], seconds[3], small[: weights[3].shape[0], :cb], scale, 0.3, group(3))
    stores.append(fetch(outs, outs_hbm, out_sems))
    for done in stores:
        done()


def flip(value, mask, dp):
    return lax.ppermute(value, "dp", [(i, i ^ mask) for i in range(dp)])


def turn_flip(value, digit, dp, stage):
    pairs = []
    for i in range(dp):
        for core in range(2):
            mask = digit if (core + stage) % 2 else 4 * digit
            pairs.append((i * 2 + core, (i ^ mask) * 2 + core))
    return lax.ppermute(value, BOTH, pairs)


def swap(value):
    return lax.ppermute(value, "rep", [(0, 1), (1, 0)])


def exchange(value):
    return lax.all_to_all(value, BOTH, 0, 0, tiled=True)


def weights_plain(wbt, wc, sp, wm, dp):
    cb, classes = wc.shape
    mr, hid = wm.shape
    own = jnp.zeros((HOPS + 1, cb, LANES), BF16)
    own = own.at[:HOPS, :, : wbt.shape[2]].set(wbt.astype(BF16))
    own = own.at[HOPS, :, :classes].set(wc.astype(BF16))
    own = own.at[HOPS, :, PCOL : PCOL + sp.shape[0]].set(sp.T.astype(BF16))
    wb = lax.all_gather(own, "dp", axis=1, tiled=True)
    whole = lax.all_gather(wm.astype(BF16), "dp", axis=0, tiled=True)
    return own, wb, whole.reshape(HOPS * hid, hid // LANES, LANES).transpose(1, 0, 2)


def on_device(table, batch_index, labels, *state):
    weights, firsts, seconds = state[0:4], state[4:8], state[8:12]
    dp, rep = lax.axis_size("dp"), lax.axis_size("rep")
    n = dp * rep
    staged = dp == 16 and rep == 2
    me, core = lax.axis_index("dp"), lax.axis_index("rep")
    pos = jnp.stack([me, core]).astype(jnp.int32)
    batch = batch_index.shape[0]
    count = float(batch * n)
    nodes, width = table.shape
    cb = weights[0].shape[2]
    mr, hid = weights[1].shape
    classes = weights[2].shape[1]
    half = hid // 2
    lhs = [v.transpose(0, 2, 1) for v in (weights[0], firsts[0], seconds[0])]
    idx = batch_index.reshape(1, batch)
    lab = labels.reshape(1, batch)

    if staged:
        with jax.named_scope("prep"):
            sources = (lhs[0], weights[2], weights[3], weights[1])
            size = HOPS * cb // 2 + 2 * mr
            own, block = call(
                prep_kernel,
                [hbm_out((HOPS + 1, cb, LANES), BF16), sds((size, LANES), BF16)],
                pos, *sources,
                smem=(0,), hbm=(1, 2, 3, 4),
                scratch=[pltpu.VMEM(v.shape, F32) for v in sources]
                + [pltpu.VMEM((HOPS, cb, LANES), BF16), pltpu.SemaphoreType.DMA((4,))],
            )
        far = [flip(block, 4 * k, dp) for k in range(1, 4)]

    with jax.named_scope("gather"):
        step = 2048
        x, gram = call(
            gather_kernel,
            [vmem((HOPS, LANES, batch), BF16), hbm_out((HOPS, LANES, LANES))],
            pltpu.with_memory_space_constraint(idx, pltpu.HBM),
            pltpu.with_memory_space_constraint(table.T, pltpu.HBM),
            grid=(nodes // step,),
            in_specs=[
                pl.BlockSpec((1, batch), lambda i: (0, 0)),
                pl.BlockSpec((width, step), lambda i: (0, i)),
            ],
            out_specs=(
                pl.BlockSpec((HOPS, LANES, batch), lambda i: (0, 0, 0)),
                pl.BlockSpec((HOPS, LANES, LANES), lambda i: (0, 0, 0)),
            ),
            scratch=[pltpu.VMEM((width, batch), F32), pltpu.VMEM((LANES, batch), F32)],
            flops=2 * nodes * width * batch,
            after=(own,) if staged else (),
            mib=24,
        )
    with jax.named_scope("gram_sum"):
        parts = gram.reshape(n, HOPS * LANES // n, LANES)
        if staged:
            (stacked,) = call(stack_kernel, [sds((4,) + block.shape, BF16)], block, *far)
            parts, stacked = lax.optimization_barrier((parts, stacked))
        parts = exchange(parts)
        (parts,) = call(sum_spread_kernel, [hbm_out(parts.shape)], parts)
        gram = exchange(parts).reshape(HOPS, LANES, LANES)
    if staged:
        mine = [stacked] + [flip(stacked, t, dp) for t in range(1, 4)]
        mine = mine[:1] + [lax.optimization_barrier((v, parts))[0] for v in mine[1:]]
        with jax.named_scope("weights"):
            whole = (hid // LANES, HOPS * hid, LANES)
            wb, wm = call(
                functools.partial(assemble_kernel, classes),
                [vmem((HOPS + 1, hid, LANES), BF16), hbm_out(whole, BF16)],
                pos, *mine, *[swap(v) for v in mine],
                smem=(0,),
                out_specs=(pl.BlockSpec(memory_space=pltpu.VMEM), pl.BlockSpec(memory_space=pltpu.HBM)),
                scratch=[pltpu.VMEM(whole, BF16), pltpu.SemaphoreType.DMA((1,))],
            )
    else:
        own, wb, wm = weights_plain(lhs[0], weights[2], weights[3], weights[1], dp)
    with jax.named_scope("stats"):
        ws, coef, mu, wt, fix = call(
            functools.partial(stats_kernel, count),
            [
                vmem((HOPS, hid, 2 * LANES), BF16),
                vmem((HOPS, hid, LANES)),
                vmem((8, LANES)),
                vmem((HOPS, LANES, hid), BF16),
                vmem((2, cb, LANES)),
            ],
            pos, gram, wb, own,
            smem=(0,),
        )
    with jax.named_scope("forward"):
        joined, pre2, pay, wt, fix = call(
            forward_kernel,
            [vmem((HOPS, hid, batch), BF16), vmem((hid, batch)), sds((n, 8, LANES))]
            + [hbm_out(v.shape, v.dtype) for v in (wt, fix)],
            x, ws, coef, wt, fix, wm,
            hbm=(5,),
            out_specs=tuple(pl.BlockSpec(memory_space=m) for m in (pltpu.VMEM,) * 3 + (pltpu.HBM,) * 2),
            scratch=[
                pltpu.VMEM((2, CHUNK, batch), F32),
                pltpu.VMEM(wm.shape, BF16),
                pltpu.SemaphoreType.DMA((3,)),
            ],
        )
    got = exchange(pay)
    with jax.named_scope("head"):
        dy2, pay, block2, stat = call(
            functools.partial(head_kernel, count, classes),
            [vmem((hid, batch)), sds((n, 8, LANES)), vmem((hid, LANES)), vmem((2, hid, LANES))],
            got, pre2, wb, lab,
            hbm=(3,),
            scratch=[
                pltpu.VMEM((hid, batch), BF16),
                pltpu.VMEM((hid, batch), F32),
                pltpu.VMEM((4, hid, LANES), F32),
                pltpu.VMEM((3, hid, LANES), F32),
                pltpu.VMEM(lab.shape, lab.dtype),
                pltpu.SemaphoreType.DMA((1,)),
            ],
            flops=6 * batch * hid * LANES,
        )
    got = exchange(pay)
    with jax.named_scope("turn"):
        rows = mr + cb // 2
        dpre, keep, send, sum2, wm = call(
            functools.partial(turn_kernel, count),
            [
                vmem((hid, batch), BF16),
                sds((dp, rows, half)),
                sds((dp, rows, half), BF16),
                vmem((8, LANES)),
                vmem(wm.shape, BF16),
            ],
            pos, got, stat, wb, pre2, dy2, joined, block2, wm,
            smem=(0,), hbm=(8,),
            scratch=[pltpu.VMEM((3, hid, LANES), F32), pltpu.SemaphoreType.DMA((1,))],
            flops=2 * batch * HOPS * hid * hid,
        )

    def back(own_hops, first, num, *more, after=()):
        outs = [(hbm_out if own_hops else sds)((dp, num, cb, LANES), BF16), hbm_out((num, LANES, batch))]
        with jax.named_scope("back"):
            return call(
                functools.partial(back_kernel, own_hops, first, num),
                outs,
                pos, dpre, x, ws, coef, mu, wm, wt, *more,
                smem=(0,),
                hbm=(7,),
                after=after,
                out_specs=(pl.BlockSpec(memory_space=pltpu.VMEM), pl.BlockSpec(memory_space=pltpu.HBM)),
                scratch=[
                    pltpu.VMEM((2, CHUNK, batch), F32),
                    pltpu.VMEM((2, CHUNK, batch), F32),
                    pltpu.VMEM((num, hid, batch), BF16),
                    pltpu.VMEM((num, 2, hid, LANES), F32),
                    pltpu.VMEM((num, LANES, batch), F32),
                    pltpu.VMEM((num, LANES, hid), BF16),
                    pltpu.SemaphoreType.DMA((num + 1,)),
                ],
                mib=16,
            )

    recv = swap(send)
    with jax.named_scope("merge_sum"):
        sent_b, sent_a = back(False, 0, 2)
        recv_b = swap(sent_b)
        if staged:
            shape = (4, rows, half)
            low = call(
                split_low_kernel,
                [vmem(shape)] + [sds(shape, BF16)] * 3,
                pos, keep, recv,
                smem=(0,),
                after=(sent_a,),
            )
            moved = [turn_flip(low[t], t, dp, 1) for t in range(1, 4)]
            kept_b, kept_a = back(True, 0, 2, recv_b, after=(low[1],))
            kept_b, moved = lax.optimization_barrier((kept_b, moved))
            high = call(
                split_high_kernel,
                [sds(shape[1:])] + [sds(shape[1:], BF16)] * 3,
                pos, low[0], *moved,
                smem=(0,),
            )
            wide = [high[0]] + [turn_flip(high[t], t, dp, 0) for t in range(1, 4)]
        else:
            kept_b, kept_a = back(True, 0, 2, recv_b)
            total = lax.psum_scatter(keep + recv.astype(F32), "dp", scatter_dimension=0)
            wide = [total] + [jnp.zeros_like(total)] * 3
    with jax.named_scope("branch_sum"):
        got_b = lax.all_to_all(kept_b, "dp", 0, 0, tiled=True)
    with jax.named_scope("owner"):
        late = (wide[0], fix)
        tr = [(lhs[i],) + tuple(s[1:]) for i, s in enumerate((weights, firsts, seconds))]
        last = (wt, kept_a, sent_a, *tr[0], *tr[1], *tr[2])
        shares, pay, *last = call(
            functools.partial(owner_kernel, count, classes),
            [sds((3 * cb + 2 * mr, LANES)), hbm_out((n, 2, LANES))] + [vmem(v.shape, v.dtype) for v in last],
            pos, got_b, sum2, *wide[1:], *late, *last,
            smem=(0,),
            hbm=tuple(range(6, 8 + len(last))),
            scratch=[pltpu.VMEM(v.shape, v.dtype) for v in late]
            + [pltpu.SemaphoreType.DMA((2,)), pltpu.SemaphoreType.DMA((len(last),))],
        )
    theirs = swap(shares)
    got = exchange(pay)
    with jax.named_scope("final"):
        shapes = [t.shape for t in tr[0]]
        outs = []
        for dtype in (F32, F32, F32, BF16):
            outs += [sds(s, dtype) for s in shapes]
        outs += [sds((1, 1)), sds((width, batch))]
        res = call(
            final_kernel, outs, pos, got, shares, theirs, x, *last,
            smem=(0,),
            out_specs=tuple(pl.BlockSpec(memory_space=pltpu.VMEM if i == 16 else pltpu.HBM) for i in range(18)),
            scratch=[pltpu.VMEM(v.shape, v.dtype) for i, v in enumerate(outs) if i != 16]
            + [pltpu.SemaphoreType.DMA((18,))],
        )
    result = list(res[:16])
    for i in range(0, 16, 4):
        result[i] = result[i].transpose(0, 2, 1)
    return (*result, res[16].reshape(()), res[17].T)


def solution(mesh):
    tables = (P(BOTH, None), P(BOTH), P(BOTH))
    params = (P(None, None, "dp"), P("dp", None), P("dp", None), P(None, "dp"))
    return jax.shard_map(
        on_device,
        mesh=mesh,
        in_specs=tables + params * 3,
        out_specs=params * 4 + (P(), P(BOTH, None)),
        check_vma=False,
    )
```

```python
import functools
import math

import jax
import jax.numpy as jnp
from jax import lax
from jax.experimental import pallas as pl
from jax.experimental.pallas import tpu as pltpu
from jax.sharding import PartitionSpec as P

HOPS = 4
STEP = 7
EPS_NORM = 1e-05
LANES = 128
PCOL = 64
ONE = 100
FREE = LANES - ONE
ROWS, WIDE, CHUNK = 32, 256, 256
BOTH = ("dp", "rep")
F32 = jnp.float32
BF16 = jnp.bfloat16


def dot(left, right, left_dim, right_dim):
    return lax.dot_general(
        left,
        right,
        (((left_dim,), (right_dim,)), ((), ())),
        preferred_element_type=F32,
    )


def call(body, outs, *args, smem=(), hbm=(), after=(), grid=None, in_specs=None, out_specs=None, scratch=(), mib=12, flops=0):
    skip = len(args)
    if in_specs is None:
        spaces = {**{i: pltpu.SMEM for i in smem}, **{i: pltpu.HBM for i in hbm}}
        in_specs = [pl.BlockSpec(memory_space=spaces.get(i, pltpu.VMEM)) for i in range(skip)]
    if out_specs is None:
        out_specs = tuple(pl.BlockSpec(memory_space=pltpu.VMEM) for _ in outs)
    in_specs = list(in_specs) + [pl.BlockSpec(memory_space=pl.ANY) for _ in after]
    args = [pltpu.with_memory_space_constraint(a, pltpu.HBM) if i in hbm else a for i, a in enumerate(args)]
    moved = sum(math.prod(a.shape) * jnp.dtype(a.dtype).itemsize for a in (*args, *outs))

    def kernel(*refs):
        body(*refs[:skip], *refs[skip + len(after) :])

    kwargs = {} if grid is None else {"grid": grid}
    return pl.pallas_call(
        kernel,
        out_shape=tuple(outs),
        in_specs=in_specs,
        out_specs=out_specs,
        scratch_shapes=list(scratch),
        compiler_params=pltpu.CompilerParams(vmem_limit_bytes=mib << 20),
        cost_estimate=pl.CostEstimate(flops=1024, bytes_accessed=1024, transcendentals=0),
        **kwargs,
    )(*args, *[pltpu.with_memory_space_constraint(a, pltpu.HBM) for a in after])


def fetch(sources, buffers, sems):
    copies = [pltpu.make_async_copy(s, b, sems.at[i]) for i, (s, b) in enumerate(zip(sources, buffers))]
    for copy in copies:
        copy.start()

    def wait():
        for copy in copies:
            copy.wait()

    return wait


def sds(shape, dtype=F32):
    return jax.ShapeDtypeStruct(shape, dtype)


def vmem(shape, dtype=F32):
    return pltpu.VMEM(shape, dtype)


def hbm_out(shape, dtype=F32):
    return pltpu.HBM(shape, dtype)


def lane_of(shape):
    return lax.broadcasted_iota(jnp.int32, shape, len(shape) - 1)


def to_cols(rows, first):
    parts = []
    for i in range(4):
        row = rows[first + i : first + i + 1, :]
        parts.append(jnp.transpose(jnp.broadcast_to(row, (LANES, LANES))))
    return jnp.concatenate(parts, axis=0)


def lane_sums(part):
    total = jnp.sum(jnp.transpose(part), axis=0, keepdims=True)
    return jnp.concatenate([total[:, i * LANES : (i + 1) * LANES] for i in range(4)], axis=0)


def fold_lanes(value):
    out = value[:, :LANES]
    for i in range(1, value.shape[1] // LANES):
        out = out + value[:, i * LANES : (i + 1) * LANES]
    return out


def prep_kernel(pos_ref, wb_hbm, wc_hbm, sp_hbm, wm_hbm, own_ref, block_ref, wb_ref, wc_ref, sp_ref, wm_ref, mix_ref, sems):
    wait = fetch((wb_hbm, wc_hbm, sp_hbm, wm_hbm), (wb_ref, wc_ref, sp_ref, wm_ref), sems)
    mr, hid = wm_ref.shape
    own_ref[...] = jnp.zeros_like(own_ref)
    wait()
    wc = wc_ref[...].astype(BF16)
    small = jnp.transpose(sp_ref[...]).astype(BF16)
    own_ref[0:HOPS, :, 0 : wb_ref.shape[2]] = wb_ref[...].astype(BF16)
    own_ref[HOPS, :, 0 : wc.shape[1]] = wc
    own_ref[HOPS, :, PCOL : PCOL + small.shape[1]] = small
    mix_ref[...] = own_ref[0:HOPS]
    mix_ref[0, :, ONE : ONE + small.shape[1]] = small
    mix_ref[1, :, ONE:LANES] = wc[:, :FREE]
    mix_ref[2, :, ONE : ONE + wc.shape[1] - FREE] = wc[:, FREE:]
    first = pos_ref[1] == 0
    part = wc.shape[0] // 2
    for k in range(HOPS):
        block_ref[k * part : (k + 1) * part, :] = jnp.where(first, mix_ref[k, :part], mix_ref[k, part:])
    at = HOPS * part
    for i in range(2):
        left = wm_ref[:, i * LANES : (i + 1) * LANES]
        right = wm_ref[:, hid // 2 + i * LANES : hid // 2 + (i + 1) * LANES]
        block_ref[at + i * mr : at + (i + 1) * mr, :] = jnp.where(first, left, right).astype(BF16)


def stack_kernel(a_ref, b_ref, c_ref, d_ref, out_ref):
    for i, ref in enumerate((a_ref, b_ref, c_ref, d_ref)):
        out_ref[i] = ref[...]


def each_block(pos_ref, arrays):
    for which in range(2):
        half = pos_ref[1] if which == 0 else 1 - pos_ref[1]
        for t in range(4):
            for e in range(4):
                yield arrays[which * 4 + t].at[e], pos_ref[0] ^ (4 * e + t), half


HALF = LANES // 2
QUADS = HALF // 4


def store_grams(grams, out_ref):
    if out_ref.shape[0] == HOPS:
        for k in range(HOPS):
            out_ref[k] = grams[k]
        return
    lane = lane_of((HALF, LANES))
    blocks = [g[:HALF] for g in grams]
    for k in range(0, HOPS, 2):
        blocks.append(jnp.where(lane < HALF, pltpu.roll(grams[k][HALF:], HALF, 1), grams[k + 1][HALF:]))
    for i, block in enumerate(blocks):
        for j in range(QUADS):
            out_ref[i * QUADS + j] = block[4 * j : 4 * j + 4]


def load_grams(in_ref, gram_ref, rest_ref):
    if in_ref.shape[0] == HOPS:
        gram_ref[...] = in_ref[...]
        return
    for i in range(HOPS + HOPS // 2):
        for j in range(QUADS):
            rows = slice(4 * j, 4 * j + 4)
            if i < HOPS:
                gram_ref[i, rows, :] = in_ref[i * QUADS + j]
            else:
                rest_ref[i - HOPS, rows, :] = in_ref[i * QUADS + j]
    lane = lane_of((HALF, LANES))
    for k in range(HOPS):
        upper = jnp.concatenate([gram_ref[k, :HALF, :], jnp.zeros((HALF, LANES), F32)], axis=0)
        rest = rest_ref[k // 2]
        if k % 2 == 0:
            rest = pltpu.roll(rest, HALF, 1)
        gram_ref[k, HALF:, :] = jnp.where(lane < HALF, jnp.transpose(upper)[HALF:], rest)


def gather_kernel(idx_ref, tab_ref, x_ref, gram_ref, acc, pad):
    i = pl.program_id(0)
    width = tab_ref.shape[1]
    d_in = tab_ref.shape[0] // HOPS
    batch = idx_ref.shape[1]
    rows = lax.broadcasted_iota(jnp.int16, (width, batch), 0)
    hot = jnp.where(rows == (idx_ref[...] - i * width).astype(jnp.int16), BF16(1.0), BF16(0.0))
    part = dot(tab_ref[...].astype(BF16), hot, 1, 0)

    @pl.when(i == 0)
    def _():
        acc[...] = part

    @pl.when(i > 0)
    def _():
        acc[...] += part

    @pl.when(i == pl.num_programs(0) - 1)
    def _():
        row = lax.broadcasted_iota(jnp.int32, pad.shape, 0)
        pad[...] = jnp.where(row == d_in, 1.0, 0.0)
        grams = []
        for k in range(HOPS):
            pad[0:d_in, :] = acc[k * d_in : (k + 1) * d_in, :]
            x = pad[...].astype(BF16)
            x_ref[k] = x
            grams.append(dot(x, x, 1, 1))
        store_grams(grams, gram_ref)


def sum_spread_kernel(in_ref, out_ref):
    out_ref[...] = jnp.broadcast_to(jnp.sum(in_ref[...], axis=0, keepdims=True), out_ref.shape)


def three_terms(wide):
    terms = []
    for _ in range(3):
        terms.append(wide.astype(BF16))
        wide = wide - terms[-1].astype(F32)
    return terms


def exact_dot(low, wide):
    total = None
    for term in three_terms(wide):
        part = dot(low, term, 1, 0)
        total = part if total is None else total + part
    return total


def assemble_kernel(classes, pos_ref, order_ref, *refs):
    wb_ref, wm_out, wm_ref, sems = refs[8:]
    hid = wb_ref.shape[1]
    cb = hid // 16
    mr = wm_ref.shape[1] // 16
    part = cb // 2
    first = HOPS * part
    for ref, s, half in each_block(pos_ref, refs[:8]):
        rows = pl.ds(pl.multiple_of(s * mr, mr), mr)
        for i in range(2):
            wm_ref[half * 2 + i, rows, :] = ref[first + i * mr : first + (i + 1) * mr, :]
    stored = fetch((wm_ref,), (wm_out,), sems)
    for ref, s, half in each_block(pos_ref, refs[:8]):
        rows = pl.ds(pl.multiple_of(s * cb + half * part, part), part)
        for j in range(HOPS):
            wb_ref[j, rows, :] = ref[j * part : (j + 1) * part, :]
    lane = lane_of((hid, LANES))
    mixed = [wb_ref[j].astype(F32) for j in range(3)]
    tail = jnp.where((lane >= PCOL) & (lane < PCOL + 5 * HOPS), pltpu.roll(mixed[0], LANES + PCOL - ONE, 1), 0.0)
    tail = jnp.where(lane < FREE, pltpu.roll(mixed[1], LANES - ONE, 1), tail)
    tail = jnp.where((lane >= FREE) & (lane < classes), pltpu.roll(mixed[2], LANES + FREE - ONE, 1), tail)
    wb_ref[HOPS] = tail.astype(BF16)
    for j in range(3):
        wb_ref[j] = jnp.where(lane < ONE, mixed[j], 0.0).astype(BF16)
    stored()


def own_stats_kernel(count, pos_ref, in_ref, own_hbm, gram_ref, fix_ref, rest_ref, own_ref, sems):
    wait = fetch((own_hbm,), (own_ref,), sems)
    load_grams(in_ref, gram_ref, rest_ref)
    wait()
    rep = pos_ref[1]
    lane = lane_of(fix_ref.shape[1:])
    tail = own_ref[HOPS].astype(F32)
    for i in range(2):
        gram = gram_ref[rep * 2 + i]
        w = own_ref[rep * 2 + i]
        wg = exact_dot(w, gram)
        mean = wg[:, ONE : ONE + 1] / count
        second = jnp.sum(wg * w.astype(F32), axis=1, keepdims=True) / count
        inv = lax.rsqrt(second - mean * mean + EPS_NORM)
        gain = jnp.where(rep == 0, tail[:, PCOL + i : PCOL + i + 1], tail[:, PCOL + 2 + i : PCOL + 3 + i])
        block = wg - mean * gram[ONE : ONE + 1, :]
        for j, value in enumerate((mean, inv, gain * inv)):
            block = jnp.where(lane == ONE + j, value, block)
        fix_ref[i] = block


def stats_kernel(count, gram_ref, wb_ref, ws_ref, coef_ref, mu_ref, wt_ref):
    hid = wb_ref.shape[1]
    small = jnp.transpose(wb_ref[HOPS].astype(F32))
    row = lax.broadcasted_iota(jnp.int32, (16, hid), 0)

    def at(i):
        return small[PCOL + i : PCOL + i + 1, :]

    def columns(values):
        block = jnp.zeros((16, hid), F32)
        for i, value in enumerate(values):
            block = jnp.where(row == i, value, block)
        return jnp.transpose(jnp.concatenate([block, jnp.zeros((LANES - 16, hid), F32)], axis=0))

    mu_ref[...] = jnp.zeros_like(mu_ref)
    for k in range(HOPS):
        gram = gram_ref[k]
        mu_ref[k : k + 1, :] = gram[ONE : ONE + 1, :] / count
        wide = jnp.transpose(wb_ref[k].astype(F32))
        w = wide.astype(BF16)
        wt_ref[k] = w
        wg = None
        for term in three_terms(gram):
            part = dot(term, w, 1, 0)
            wg = part if wg is None else wg + part
        mean = wg[ONE : ONE + 1, :] / count
        second = jnp.sum(wg * wide, axis=0, keepdims=True) / count
        inv = lax.rsqrt(second - mean * mean + EPS_NORM)
        gain, shift, slope, join = at(k), at(HOPS + k), at(2 * HOPS + k), at(3 * HOPS + k)
        v = gain * inv
        half = 0.5 * v
        scaled = jnp.where(
            lax.broadcasted_iota(jnp.int32, wide.shape, 0) == ONE, 0.5 * shift - half * mean, half * wide
        )
        scaled = jnp.transpose(scaled)
        high = scaled.astype(BF16)
        ws_ref[k, :, 0:LANES] = high
        ws_ref[k, :, LANES : 2 * LANES] = (scaled - high.astype(F32)).astype(BF16)
        scale = 0.5 * (1.0 - join)
        coef_ref[k] = columns(
            (
                0.5 * (1.0 + slope),
                0.5 * (1.0 - slope),
                1.0 + join,
                1.0 - join,
                join / scale,
                scale,
                scale * v * slope,
                scale * 0.5 * v * (1.0 - slope),
            )
        )


def project_units(ws_ref, x_ref, k, rows):
    x = x_ref[k]
    return dot(ws_ref[k, rows, :], jnp.concatenate([x, x], axis=0), 1, 0)


def column_set(ref, hop, at, lanes):
    block = ref[hop, at, :]
    return [jnp.broadcast_to(block[:, i : i + 1], (ROWS, WIDE)) for i in lanes]


def merge_block(wm_ref, rows):
    return jnp.concatenate([wm_ref[i, rows, :] for i in range(wm_ref.shape[0])], axis=1)


def forward_kernel(
    x_ref, ws_ref, coef_ref, wt_ref, fix_ref, wm_hbm, joined_ref, pre2_ref, pay_ref, wt_out, fix_out, pre, wm_ref, sems
):
    wait = fetch((wm_hbm,), (wm_ref,), sems.at[pl.ds(2, 1)])
    stored = fetch((wt_ref, fix_ref), (wt_out, fix_out), sems)
    hid = ws_ref.shape[1]
    batch = x_ref.shape[2]
    per = hid // CHUNK
    jobs = [(k, c) for k in range(HOPS) for c in range(per)]

    def project(i):
        k, c = jobs[i]
        pre[i % 2] = project_units(ws_ref, x_ref, k, slice(c * CHUNK, (c + 1) * CHUNK))

    def units(i):
        k, c = jobs[i]
        for g in range(CHUNK // ROWS):
            at = slice(c * CHUNK + g * ROWS, c * CHUNK + (g + 1) * ROWS)
            cs = column_set(coef_ref, k, at, range(4))
            for b in range(batch // WIDE):
                lanes = slice(b * WIDE, (b + 1) * WIDE)
                u = pre[i % 2, g * ROWS : (g + 1) * ROWS, lanes]
                u = u * (cs[0] + cs[1] * jnp.tanh(u))
                joined_ref[k, at, lanes] = (u * (cs[2] + cs[3] * jnp.tanh(u))).astype(BF16)

    project(0)
    for i in range(len(jobs)):
        if i + 1 < len(jobs):
            project(i + 1)
        units(i)
        if i % per == per - 1:
            k = i // per
            if k == 0:
                wait()
            part = dot(merge_block(wm_ref, slice(k * hid, (k + 1) * hid)), joined_ref[k], 0, 0)
            if k == 0:
                pre2_ref[...] = part
            else:
                pre2_ref[...] += part
    value = pre2_ref[...]
    sums = jnp.concatenate([lane_sums(fold_lanes(value)), lane_sums(fold_lanes(value * value))], axis=0)
    pay_ref[...] = jnp.broadcast_to(sums[None], pay_ref.shape)
    stored()


def par_columns(wb_ref):
    return wb_ref[HOPS][:, PCOL:].astype(F32)[:, 4 * HOPS : 5 * HOPS]


def columns2(count, rows, par):
    mean = to_cols(rows, 0) / count
    inv = lax.rsqrt(to_cols(rows, 4) / count - mean * mean + EPS_NORM)
    shape = mean.shape
    gain = jnp.broadcast_to(par[:, 0:1], shape)
    shift = jnp.broadcast_to(par[:, 1:2], shape)
    slope = jnp.broadcast_to(par[:, 2:3], shape)
    return mean, inv, gain, shift, slope


def head_kernel(
    count, classes, got_ref, pre2_ref, wb_ref, lab_hbm, dy2_ref, pay_ref, class_ref, stat_ref, act, dact, cols, sums, lab_ref, sems
):
    wait = fetch((lab_hbm,), (lab_ref,), sems)
    hid, batch = dy2_ref.shape
    par = par_columns(wb_ref)
    mean, inv, gain, shift, slope = columns2(count, jnp.sum(got_ref[...], axis=0), par)
    stat_ref[0] = mean
    stat_ref[1] = inv
    cols[0] = 0.5 * gain * inv
    cols[1] = 0.5 * (shift - gain * inv * mean)
    cols[2] = 1.0 + slope
    cols[3] = 1.0 - slope
    reps = WIDE // LANES

    def tiled(c, at):
        return jnp.concatenate([cols[c, at, :]] * reps, axis=1)

    def first(g, carry):
        at = pl.ds(pl.multiple_of(g * ROWS, ROWS), ROWS)
        c = [tiled(i, at) for i in range(4)]
        for b in range(batch // WIDE):
            lanes = slice(b * WIDE, (b + 1) * WIDE)
            u = pre2_ref[at, lanes] * c[0] + c[1]
            act[at, lanes] = (u * (c[2] + c[3] * jnp.tanh(u))).astype(BF16)
        return carry

    lax.fori_loop(0, hid // ROWS, first, 0, unroll=8)
    tail = wb_ref[HOPS]
    wc = jnp.where(lane_of(tail.shape) < PCOL, tail.astype(F32), 0.0).astype(BF16)
    logits = dot(wc, act[...], 0, 0)
    live = -(-classes // 16) * 16
    row = lax.broadcasted_iota(jnp.int32, (live, batch), 0)
    logits = jnp.where(row < classes, logits[:live] + par[0:live, 3:4], -jnp.inf)
    top = jnp.max(logits, axis=0, keepdims=True)
    e = jnp.exp(logits - top)
    probs = e / jnp.sum(e, axis=0, keepdims=True)
    wait()
    dlog = (probs - jnp.where(row == lab_ref[...], 1.0, 0.0)).astype(BF16)
    dlog = jnp.concatenate([dlog, jnp.zeros((LANES - live, batch), BF16)], axis=0)
    grad_class = dot(act[...], dlog, 1, 1)
    bias = jnp.sum(dlog.astype(F32), axis=1, keepdims=True)
    dact[...] = dot(wc, dlog, 1, 0)

    def second(g, carry):
        at = pl.ds(pl.multiple_of(g * ROWS, ROWS), ROWS)
        c = [tiled(i, at) for i in range(4)]
        m = jnp.concatenate([stat_ref[0, at, :]] * reps, axis=1)
        v = jnp.concatenate([stat_ref[1, at, :]] * reps, axis=1)
        acc = [jnp.zeros((ROWS, WIDE), F32) for _ in range(3)]
        for b in range(batch // WIDE):
            lanes = slice(b * WIDE, (b + 1) * WIDE)
            p = pre2_ref[at, lanes]
            d = dact[at, lanes]
            u = p * c[0] + c[1]
            t = jnp.tanh(u)
            w = u * (1.0 - t)
            dy = d * (0.5 * (c[2] + c[3] * (t + w * (1.0 + t))))
            dy2_ref[at, lanes] = dy
            acc[0] = acc[0] + dy
            acc[1] = acc[1] + dy * ((p - m) * v)
            acc[2] = acc[2] + d * w
        for i in range(3):
            sums[i, at, :] = fold_lanes(acc[i])
        return carry

    lax.fori_loop(0, hid // ROWS, second, 0, unroll=8)
    pay = jnp.concatenate([lane_sums(sums[0]), lane_sums(sums[1])], axis=0)
    pay_ref[...] = jnp.broadcast_to(pay[None], pay_ref.shape)
    lane = lane_of((hid, LANES))
    slope_sum = jnp.sum(sums[2], axis=1, keepdims=True)
    bias = jnp.concatenate([bias, jnp.zeros((hid - LANES, 1), F32)], axis=0)
    block = jnp.where(lane < classes, grad_class, 0.0)
    block = jnp.where(lane == PCOL, slope_sum, block)
    class_ref[...] = jnp.where(lane == PCOL + 1, bias, block)


def turn_kernel(
    count, pos_ref, got_ref, stat_ref, wb_ref, pre2_ref, dy2_ref, joined_ref, class_ref, wm_hbm, dpre_ref, keep_ref, send_ref, sum2_ref, wm_ref, cols, sems
):
    wait = fetch((wm_hbm,), (wm_ref,), sems)
    hid, batch = dy2_ref.shape
    half = send_ref.shape[2]
    rows8 = jnp.sum(got_ref[...], axis=0)
    sum2_ref[...] = rows8
    mean, inv = stat_ref[0], stat_ref[1]
    v = jnp.broadcast_to(par_columns(wb_ref)[:, 0:1], mean.shape) * inv
    cols[0] = v
    cols[1] = v * to_cols(rows8, 0) / count
    cols[2] = v * inv * to_cols(rows8, 4) / count
    reps = WIDE // LANES
    for g in range(hid // ROWS):
        at = slice(g * ROWS, (g + 1) * ROWS)
        c = [jnp.concatenate([cols[i, at, :]] * reps, axis=1) for i in range(3)]
        m = jnp.concatenate([stat_ref[0, at, :]] * reps, axis=1)
        for b in range(batch // WIDE):
            lanes = slice(b * WIDE, (b + 1) * WIDE)
            value = c[0] * dy2_ref[at, lanes] - c[1] - (pre2_ref[at, lanes] - m) * c[2]
            dpre_ref[at, lanes] = value.astype(BF16)
    mine = pl.ds(pl.multiple_of(pos_ref[1] * half, half), half)
    theirs = pl.ds(pl.multiple_of((1 - pos_ref[1]) * half, half), half)
    dp, size, _ = send_ref.shape
    per = dp // HOPS
    mr = hid // per
    cb = hid // dp
    for k in range(HOPS):
        other = dot(joined_ref[k], dpre_ref[theirs, :], 1, 1).astype(BF16)
        own = dot(joined_ref[k], dpre_ref[mine, :], 1, 1)
        for j in range(per):
            send_ref[k * per + j, 0:mr, :] = other[j * mr : (j + 1) * mr]
            keep_ref[k * per + j, 0:mr, :] = own[j * mr : (j + 1) * mr]
    first = pos_ref[1] == 0
    for s in range(dp):
        block = class_ref[s * cb : (s + 1) * cb, :]
        wide = jnp.concatenate([block[: cb // 2], block[cb // 2 :]], axis=1)
        send_ref[s, mr:size, :] = jnp.where(first, 0.0, wide).astype(BF16)
        keep_ref[s, mr:size, :] = jnp.where(first, wide, 0.0)
    wait()


SMALLS = 4


def back_kernel(own, first, count, pos_ref, dpre_ref, x_ref, ws_ref, coef_ref, mu_ref, wm_ref, wt_hbm, *refs):
    if own:
        recv_ref, refs = refs[0], refs[1:]
    b_ref, a_out, pre, dj, dyv, sums, a_ref, wt_ref, out_sems = refs
    hid = wt_ref.shape[2]
    batch = x_ref.shape[2]
    per = hid // CHUNK
    jobs = [(k, c) for k in range(count) for c in range(per)]
    base = 2 * (pos_ref[1] if own else 1 - pos_ref[1]) + first
    dp, _, cb, _ = b_ref.shape
    copies = []
    wait_wt = fetch((wt_hbm.at[pl.ds(base, count)],), (wt_ref,), out_sems.at[pl.ds(count, 1)])

    def project(i):
        k, c = jobs[i]
        rows = slice(c * CHUNK, (c + 1) * CHUNK)
        pre[i % 2] = project_units(ws_ref, x_ref, base + k, rows)
        at = pl.ds(pl.multiple_of((base + k) * hid + c * CHUNK, CHUNK), CHUNK)
        dj[i % 2] = dot(merge_block(wm_ref, at), dpre_ref[...], 1, 0)

    def units(i):
        k, c = jobs[i]
        for g in range(CHUNK // ROWS):
            at = slice(c * CHUNK + g * ROWS, c * CHUNK + (g + 1) * ROWS)
            here = slice(g * ROWS, (g + 1) * ROWS)
            p1, q1, s2, s1, r1 = column_set(coef_ref, base + k, at, (0, 1, 4, 6, 7))
            one = jnp.zeros((ROWS, WIDE), F32)
            two = jnp.zeros((ROWS, WIDE), F32)
            for b in range(batch // WIDE):
                lanes = slice(b * WIDE, (b + 1) * WIDE)
                u = pre[i % 2, here, lanes]
                t = jnp.tanh(u)
                u2 = u * (p1 + q1 * t)
                t2 = jnp.tanh(u2)
                d = dj[i % 2, here, lanes]
                w = u2 * (1.0 - t2)
                two = two + d * w
                d = d * (s2 + (1.0 + t2) * (1.0 + w))
                w = u * (1.0 - t)
                one = one + d * w
                dyv[k, at, lanes] = (d * (s1 + r1 * ((1.0 + t) * (1.0 + w)))).astype(BF16)
            sums[k, 0, at, :] = fold_lanes(one)
            sums[k, 1, at, :] = fold_lanes(two)

    def close(k):
        if k == 0:
            wait_wt()
        w = wt_ref[k]
        a_ref[k] = dot(w, dyv[k], 1, 0)
        copies.append(fetch((a_ref.at[k],), (a_out.at[k],), out_sems.at[pl.ds(k, 1)]))
        block = dot(x_ref[base + k], dyv[k], 1, 1)
        row = lax.broadcasted_iota(jnp.int32, block.shape, 0)
        total = block[ONE : ONE + 1, :]
        center = jnp.transpose(jnp.broadcast_to(mu_ref[pl.ds(base + k, 1), :], (LANES, LANES)))
        block = jnp.where(row < ONE, block - jnp.concatenate([center] * (hid // LANES), axis=1) * total, 0.0)
        smalls = (
            total,
            jnp.sum(block * w.astype(F32), axis=0, keepdims=True),
            jnp.sum(jnp.transpose(sums[k, 0] * coef_ref[base + k, :, 5:6]), axis=0, keepdims=True),
            jnp.sum(jnp.transpose(sums[k, 1]), axis=0, keepdims=True),
        )
        for i, value in enumerate(smalls):
            block = jnp.where(row == ONE + i, value, block)
            if not own:
                block = jnp.where(row == ONE + SMALLS + i, value - value.astype(BF16).astype(F32), block)
        block = jnp.transpose(block)
        if own:
            received = jnp.concatenate([recv_ref[s, k] for s in range(dp)], axis=0).astype(F32)
            block = split_smalls(block + join_smalls(received))
        for s in range(dp):
            b_ref[s, k] = block[s * cb : (s + 1) * cb, :].astype(BF16)

    project(0)
    for i in range(len(jobs)):
        if i + 1 < len(jobs):
            project(i + 1)
        units(i)
        if i % per == per - 1:
            close(i // per)
    for done in copies:
        done()


def split_smalls(block):
    lane = lane_of(block.shape)
    rest = block - block.astype(BF16).astype(F32)
    moved = pltpu.roll(rest, SMALLS, 1)
    return jnp.where((lane >= ONE + SMALLS) & (lane < ONE + 2 * SMALLS), moved, block)


def join_smalls(block):
    lane = lane_of(block.shape)
    moved = pltpu.roll(block, LANES - SMALLS, 1)
    block = jnp.where((lane >= ONE) & (lane < ONE + SMALLS), block + moved, block)
    return jnp.where(lane < ONE + SMALLS, block, 0.0)


def split_low_kernel(pos_ref, keep_ref, got_ref, o0_ref, o1_ref, o2_ref, o3_ref):
    low, high = pos_ref[0] % 4, pos_ref[0] // 4
    for t, ref in enumerate((o0_ref, o1_ref, o2_ref, o3_ref)):
        for e in range(4):
            j = jnp.where(pos_ref[1] == 0, e * 4 + (low ^ t), (high ^ t) * 4 + e)
            ref[e] = (keep_ref[j] + got_ref[j].astype(F32)).astype(ref.dtype)


def split_high_kernel(pos_ref, own_ref, g1_ref, g2_ref, g3_ref, o0_ref, o1_ref, o2_ref, o3_ref):
    mine = jnp.where(pos_ref[1] == 0, pos_ref[0] // 4, pos_ref[0] % 4)
    for t, ref in enumerate((o0_ref, o1_ref, o2_ref, o3_ref)):
        j = mine ^ t
        value = own_ref[j] + g1_ref[j].astype(F32) + g2_ref[j].astype(F32) + g3_ref[j].astype(F32)
        ref[...] = value.astype(ref.dtype)


def owner_kernel(
    count, classes, pos_ref, got_ref, sum2_ref, w0_ref, w1_ref, w2_ref, w3_ref, *refs
):
    late = (len(refs) - 6) // 2
    grad_ref, pay_ref = refs[1 + late : 3 + late]
    fix_ref, sems, late_sems = refs[3 + 2 * late :]
    wait = fetch(refs[:1], (fix_ref,), sems)
    brought = fetch(refs[1 : 1 + late], refs[3 + late : 3 + 2 * late], late_sems)
    _, _, cb, _ = got_ref.shape
    total = jnp.sum(got_ref[...].astype(F32), axis=0)
    rep = pos_ref[1]
    lane = lane_of((cb, LANES))
    squares = jnp.zeros((1, 1), F32)
    spread = jnp.zeros((cb, LANES), F32)

    def all_sum(v):
        return jnp.sum(jnp.sum(v, axis=1, keepdims=True), axis=0, keepdims=True)

    others = w1_ref[...].astype(F32) + w2_ref[...].astype(F32) + w3_ref[...].astype(F32)
    wait()
    for i in range(2):
        b = join_smalls(total[i])
        wg = fix_ref[i]
        mean, inv, v = [wg[:, ONE + j : ONE + j + 1] for j in range(3)]
        s = b[:, ONE : ONE + 1]
        g = inv * b[:, ONE + 1 : ONE + 2]
        beta = inv * g / count
        alpha = s / count - beta * mean
        fixed = jnp.where(lane < ONE, b - beta * wg, 0.0)
        fixed = jnp.where(lane == ONE, g / v, fixed)
        fixed = jnp.where(lane == ONE + 1, s / v, fixed)
        fixed = jnp.where(lane == ONE + 2, b[:, ONE + 2 : ONE + 3], fixed)
        fixed = jnp.where(lane == ONE + 3, b[:, ONE + 3 : ONE + 4], fixed)
        grad_ref[i * cb : (i + 1) * cb, :] = fixed
        squares = squares + all_sum(fixed * fixed)
        spread = jnp.where(lane == 2 * i, alpha, spread)
        spread = jnp.where(lane == 2 * i + 1, beta, spread)
    wide = w0_ref[...].astype(F32) + others
    mr = wide.shape[0] - cb // 2
    merge = wide[:mr]
    squares = squares + all_sum(merge * merge)
    at = 2 * cb
    for i in range(2):
        grad_ref[at + i * mr : at + (i + 1) * mr, :] = merge[:, i * LANES : (i + 1) * LANES]
    at = at + 2 * mr
    block = jnp.concatenate([wide[mr:, :LANES], wide[mr:, LANES:]], axis=0)
    shift_own = own_column(sum2_ref, 0, pos_ref[0], cb)
    gain_own = own_column(sum2_ref, 4, pos_ref[0], cb)
    block = jnp.where(lane == PCOL + 2, gain_own, block)
    block = jnp.where(lane == PCOL + 3, shift_own, block)
    grad_ref[at : at + cb, :] = block
    squares = squares + jnp.where(rep == 0, all_sum(block * block), 0.0)
    rows = jnp.transpose(jnp.concatenate([spread, jnp.zeros((LANES - cb, LANES), F32)], axis=0))[0:8]
    packed = jnp.concatenate([rows[i : i + 1, :cb] for i in range(4)], axis=1)
    if 4 * cb < LANES:
        packed = jnp.concatenate([packed, jnp.zeros((1, LANES - 4 * cb), F32)], axis=1)
    pay = jnp.concatenate([packed, jnp.where(lane_of((1, LANES)) == 0, squares, 0.0)], axis=0)
    pay_ref[...] = jnp.broadcast_to(pay[None], pay_ref.shape)
    brought()


def own_column(ref, first, me, cb):
    block = (me * cb) // LANES
    row = ref[pl.ds(first + block, 1), :]
    lane = lane_of((cb, LANES))
    sub = lax.broadcasted_iota(jnp.int32, (cb, LANES), 0)
    hit = lane == sub + (me * cb) % LANES
    return jnp.sum(jnp.where(hit, jnp.broadcast_to(row, (cb, LANES)), 0.0), axis=1, keepdims=True)


def adam_into(weight_ref, moment_ref, square_ref, grad, scale, rate, outs, at=Ellipsis):
    new_ref, new_m_ref, new_s_ref, copy_ref = outs
    weight = weight_ref[at]
    clipped = grad * scale
    moment = 0.9 * moment_ref[at] + 0.1 * clipped
    square = 0.999 * square_ref[at] + 0.001 * clipped * clipped
    fix_one = 1.0 - 0.9**STEP
    fix_two = 1.0 - 0.999**STEP
    update = moment / fix_one / (jnp.sqrt(square / fix_two) + 1e-08) + 0.01 * weight
    new = weight - rate * update
    new_ref[at] = new
    new_m_ref[at] = moment
    new_s_ref[at] = square
    copy_ref[at] = new.astype(BF16)


def final_kernel(pos_ref, got_ref, mine_ref, other_ref, x_ref, wt_ref, own_ref, sent_ref, *refs):
    states, outs_hbm, norm_ref, rows_hbm = refs[:12], refs[12:28], refs[28], refs[29]
    outs, rows_ref, out_sems = refs[30:46], refs[46], refs[47]
    weights, firsts, seconds = states[0:4], states[4:8], states[8:12]
    n = got_ref.shape[0]
    cb = weights[0].shape[1]
    blocks = 4
    per = n // 2 // blocks
    lane = lane_of((blocks, LANES))
    parts = [[jnp.zeros((blocks, LANES), F32) for _ in range(4)] for _ in range(2)]
    for r in range(2):
        for j in range(per):
            rows = [got_ref[(b * per + j) * 2 + r, 0:1, :] for b in range(blocks)]
            rows = jnp.concatenate(rows, axis=0)
            here = (lane >= j * cb) & (lane < (j + 1) * cb)
            for i in range(4):
                shift = (j - i) * cb % LANES
                moved = pltpu.roll(rows, shift, 1) if shift else rows
                parts[r][i] = jnp.where(here, moved, parts[r][i])

    def spread_row(r, i):
        return jnp.concatenate([parts[r][i][b : b + 1] for b in range(blocks)], axis=1)

    squares = jnp.sum(got_ref[...], axis=0)[1:2, :]
    norm = jnp.sqrt(jnp.sum(squares, axis=1, keepdims=True))
    norm_ref[...] = norm
    scale = 1.0 / jnp.maximum(norm, 1.0)

    d_in = weights[0].shape[2]
    mr = weights[1].shape[0]
    classes = weights[2].shape[1]
    first = pos_ref[1] == 0
    mine, other = mine_ref[...], other_ref[...]
    low = jnp.where(first, mine, other)
    high = jnp.where(first, other, mine)
    stores = []
    fixes = []
    for k in range(HOPS):
        r, i = k // 2, k % 2
        alpha, beta = spread_row(r, 2 * i), spread_row(r, 2 * i + 1)
        low_w = wt_ref[k]
        right = jnp.where(lax.broadcasted_iota(jnp.int32, low_w.shape, 0) == ONE, alpha, low_w.astype(F32) * beta)
        high_part = right.astype(BF16)
        fix = dot(low_w, high_part, 1, 1) + dot(low_w, (right - high_part.astype(F32)).astype(BF16), 1, 1)
        high_part = fix.astype(BF16)
        fixes.append(jnp.concatenate([high_part, (fix - high_part.astype(F32)).astype(BF16)], axis=1))
    for k in range(HOPS):
        r, i = k // 2, k % 2
        value = jnp.where(pos_ref[1] == r, own_ref[i], sent_ref[i])
        value = value - dot(fixes[k], jnp.concatenate([x_ref[k], x_ref[k]], axis=0), 1, 0)
        rows_ref[k * d_in : (k + 1) * d_in, :] = value[:d_in]
        if i == 1:
            part = pl.ds(r * 2 * d_in, 2 * d_in)
            stores.append(fetch((rows_ref.at[part, :],), (rows_hbm.at[part, :],), out_sems.at[pl.ds(16 + r, 1)]))

    def group(i):
        return [o for o in outs[i::4]]

    hops = [low[0:cb], low[cb : 2 * cb], high[0:cb], high[cb : 2 * cb]]
    for k in range(HOPS):
        adam_into(weights[0], firsts[0], seconds[0], hops[k][:, :d_in], scale, 0.05, group(0), k)
    at = 2 * cb
    for half, part in enumerate((low, high)):
        for i in range(2):
            lanes = (slice(None), slice((2 * half + i) * LANES, (2 * half + i + 1) * LANES))
            grad = part[at + i * mr : at + (i + 1) * mr]
            adam_into(weights[1], firsts[1], seconds[1], grad, scale, 0.05, group(1), lanes)
    at = at + 2 * mr
    block = low[at : at + cb]
    adam_into(weights[2], firsts[2], seconds[2], block[:, :classes], scale, 0.05, group(2))
    lane = lane_of((cb, LANES))
    small = jnp.zeros((cb, LANES), F32)
    for kind in range(4):
        for k in range(HOPS):
            small = jnp.where(lane == kind * HOPS + k, hops[k][:, ONE + kind : ONE + kind + 1], small)
    for i, source in enumerate((2, 3, 0, 1)):
        small = jnp.where(lane == 4 * HOPS + i, block[:, PCOL + source : PCOL + source + 1], small)
    small = jnp.transpose(jnp.concatenate([small, jnp.zeros((LANES - cb, LANES), F32)], axis=0))
    adam_into(weights[3], firsts[3], seconds[3], small[: weights[3].shape[0], :cb], scale, 0.3, group(3))
    stores.append(fetch(outs, outs_hbm, out_sems))
    for done in stores:
        done()


def flip(value, mask, dp):
    return lax.ppermute(value, "dp", [(i, i ^ mask) for i in range(dp)])


def turn_flip(value, digit, dp, stage):
    pairs = []
    for i in range(dp):
        for core in range(2):
            mask = digit if (core + stage) % 2 else 4 * digit
            pairs.append((i * 2 + core, (i ^ mask) * 2 + core))
    return lax.ppermute(value, BOTH, pairs)


def swap(value):
    return lax.ppermute(value, "rep", [(0, 1), (1, 0)])


def exchange(value):
    return lax.all_to_all(value, BOTH, 0, 0, tiled=True)


def weights_plain(wbt, wc, sp, wm, dp):
    cb, classes = wc.shape
    mr, hid = wm.shape
    own = jnp.zeros((HOPS + 1, cb, LANES), BF16)
    own = own.at[:HOPS, :, : wbt.shape[2]].set(wbt.astype(BF16))
    own = own.at[HOPS, :, :classes].set(wc.astype(BF16))
    own = own.at[HOPS, :, PCOL : PCOL + sp.shape[0]].set(sp.T.astype(BF16))
    wb = lax.all_gather(own, "dp", axis=1, tiled=True)
    whole = lax.all_gather(wm.astype(BF16), "dp", axis=0, tiled=True)
    return own, wb, whole.reshape(HOPS * hid, hid // LANES, LANES).transpose(1, 0, 2)


def on_device(table, batch_index, labels, *state):
    weights, firsts, seconds = state[0:4], state[4:8], state[8:12]
    dp, rep = lax.axis_size("dp"), lax.axis_size("rep")
    n = dp * rep
    staged = dp == 16 and rep == 2
    me, core = lax.axis_index("dp"), lax.axis_index("rep")
    pos = jnp.stack([me, core]).astype(jnp.int32)
    batch = batch_index.shape[0]
    count = float(batch * n)
    nodes, width = table.shape
    cb = weights[0].shape[2]
    mr, hid = weights[1].shape
    classes = weights[2].shape[1]
    half = hid // 2
    lhs = [v.transpose(0, 2, 1) for v in (weights[0], firsts[0], seconds[0])]
    idx = batch_index.reshape(1, batch)
    lab = labels.reshape(1, batch)

    if staged:
        with jax.named_scope("prep"):
            sources = (lhs[0], weights[2], weights[3], weights[1])
            size = HOPS * cb // 2 + 2 * mr
            own, block = call(
                prep_kernel,
                [hbm_out((HOPS + 1, cb, LANES), BF16), sds((size, LANES), BF16)],
                pos, *sources,
                smem=(0,), hbm=(1, 2, 3, 4),
                scratch=[pltpu.VMEM(v.shape, F32) for v in sources]
                + [pltpu.VMEM((HOPS, cb, LANES), BF16), pltpu.SemaphoreType.DMA((4,))],
            )
        far = [flip(block, 4 * k, dp) for k in range(1, 4)]

    with jax.named_scope("gather"):
        step = 2048
        sums = (6 * QUADS, 4, LANES) if 6 * QUADS % n == 0 else (HOPS, LANES, LANES)
        x, gram = call(
            gather_kernel,
            [vmem((HOPS, LANES, batch), BF16), hbm_out(sums)],
            pltpu.with_memory_space_constraint(idx, pltpu.HBM),
            pltpu.with_memory_space_constraint(table.T, pltpu.HBM),
            grid=(nodes // step,),
            in_specs=[
                pl.BlockSpec((1, batch), lambda i: (0, 0)),
                pl.BlockSpec((width, step), lambda i: (0, i)),
            ],
            out_specs=(
                pl.BlockSpec((HOPS, LANES, batch), lambda i: (0, 0, 0)),
                pl.BlockSpec(sums, lambda i: (0, 0, 0)),
            ),
            scratch=[pltpu.VMEM((width, batch), F32), pltpu.VMEM((LANES, batch), F32)],
            flops=2 * nodes * width * batch,
            after=(own,) if staged else (),
            mib=24,
        )
    with jax.named_scope("gram_sum"):
        parts = gram.reshape(n, -1, *sums[1:]) if sums[1] == 4 else gram.reshape(n, -1, LANES)
        if staged:
            (stacked,) = call(stack_kernel, [sds((4,) + block.shape, BF16)], block, *far)
            parts, stacked = lax.optimization_barrier((parts, stacked))
        parts = exchange(parts)
        (parts,) = call(sum_spread_kernel, [hbm_out(parts.shape)], parts)
        gram = exchange(parts).reshape(sums)
    if not staged:
        own, wb, wm = weights_plain(lhs[0], weights[2], weights[3], weights[1], dp)
    with jax.named_scope("own_stats"):
        gram, fix = call(
            functools.partial(own_stats_kernel, count),
            [vmem((HOPS, LANES, LANES)), vmem((2, cb, LANES))],
            pos, gram, own,
            smem=(0,), hbm=(2,),
            scratch=[
                pltpu.VMEM((HOPS // 2, HALF, LANES), F32),
                pltpu.VMEM(own.shape, BF16),
                pltpu.SemaphoreType.DMA((1,)),
            ],
        )
    if staged:
        mine = [stacked] + [flip(stacked, t, dp) for t in range(1, 4)]
        mine = mine[:1] + [lax.optimization_barrier((v, parts))[0] for v in mine[1:]]
        with jax.named_scope("weights"):
            whole = (hid // LANES, HOPS * hid, LANES)
            wb, wm = call(
                functools.partial(assemble_kernel, classes),
                [vmem((HOPS + 1, hid, LANES), BF16), hbm_out(whole, BF16)],
                pos, fix, *mine, *[swap(v) for v in mine],
                smem=(0,),
                out_specs=(pl.BlockSpec(memory_space=pltpu.VMEM), pl.BlockSpec(memory_space=pltpu.HBM)),
                scratch=[pltpu.VMEM(whole, BF16), pltpu.SemaphoreType.DMA((1,))],
            )
    with jax.named_scope("stats"):
        ws, coef, mu, wt = call(
            functools.partial(stats_kernel, count),
            [
                vmem((HOPS, hid, 2 * LANES), BF16),
                vmem((HOPS, hid, LANES)),
                vmem((8, LANES)),
                vmem((HOPS, LANES, hid), BF16),
            ],
            gram, wb,
        )
    with jax.named_scope("forward"):
        joined, pre2, pay, wt, fix = call(
            forward_kernel,
            [vmem((HOPS, hid, batch), BF16), vmem((hid, batch)), sds((n, 8, LANES))]
            + [hbm_out(v.shape, v.dtype) for v in (wt, fix)],
            x, ws, coef, wt, fix, wm,
            hbm=(5,),
            out_specs=tuple(pl.BlockSpec(memory_space=m) for m in (pltpu.VMEM,) * 3 + (pltpu.HBM,) * 2),
            scratch=[
                pltpu.VMEM((2, CHUNK, batch), F32),
                pltpu.VMEM(wm.shape, BF16),
                pltpu.SemaphoreType.DMA((3,)),
            ],
        )
    got = exchange(pay)
    with jax.named_scope("head"):
        dy2, pay, block2, stat = call(
            functools.partial(head_kernel, count, classes),
            [vmem((hid, batch)), sds((n, 8, LANES)), vmem((hid, LANES)), vmem((2, hid, LANES))],
            got, pre2, wb, lab,
            hbm=(3,),
            scratch=[
                pltpu.VMEM((hid, batch), BF16),
                pltpu.VMEM((hid, batch), F32),
                pltpu.VMEM((4, hid, LANES), F32),
                pltpu.VMEM((3, hid, LANES), F32),
                pltpu.VMEM(lab.shape, lab.dtype),
                pltpu.SemaphoreType.DMA((1,)),
            ],
            flops=6 * batch * hid * LANES,
        )
    got = exchange(pay)
    with jax.named_scope("turn"):
        rows = mr + cb // 2
        dpre, keep, send, sum2, wm = call(
            functools.partial(turn_kernel, count),
            [
                vmem((hid, batch), BF16),
                sds((dp, rows, half)),
                sds((dp, rows, half), BF16),
                vmem((8, LANES)),
                vmem(wm.shape, BF16),
            ],
            pos, got, stat, wb, pre2, dy2, joined, block2, wm,
            smem=(0,), hbm=(8,),
            scratch=[pltpu.VMEM((3, hid, LANES), F32), pltpu.SemaphoreType.DMA((1,))],
            flops=2 * batch * HOPS * hid * hid,
        )

    def back(own_hops, first, num, *more, after=()):
        outs = [(hbm_out if own_hops else sds)((dp, num, cb, LANES), BF16), hbm_out((num, LANES, batch))]
        with jax.named_scope("back"):
            return call(
                functools.partial(back_kernel, own_hops, first, num),
                outs,
                pos, dpre, x, ws, coef, mu, wm, wt, *more,
                smem=(0,),
                hbm=(7,),
                after=after,
                out_specs=(pl.BlockSpec(memory_space=pltpu.VMEM), pl.BlockSpec(memory_space=pltpu.HBM)),
                scratch=[
                    pltpu.VMEM((2, CHUNK, batch), F32),
                    pltpu.VMEM((2, CHUNK, batch), F32),
                    pltpu.VMEM((num, hid, batch), BF16),
                    pltpu.VMEM((num, 2, hid, LANES), F32),
                    pltpu.VMEM((num, LANES, batch), F32),
                    pltpu.VMEM((num, LANES, hid), BF16),
                    pltpu.SemaphoreType.DMA((num + 1,)),
                ],
                mib=16,
            )

    recv = swap(send)
    with jax.named_scope("merge_sum"):
        sent_b, sent_a = back(False, 0, 2)
        recv_b = swap(sent_b)
        if staged:
            shape = (4, rows, half)
            low = call(
                split_low_kernel,
                [vmem(shape)] + [sds(shape, BF16)] * 3,
                pos, keep, recv,
                smem=(0,),
                after=(sent_a,),
            )
            moved = [turn_flip(low[t], t, dp, 1) for t in range(1, 4)]
            kept_b, kept_a = back(True, 0, 2, recv_b, after=(low[1],))
            kept_b, moved = lax.optimization_barrier((kept_b, moved))
            high = call(
                split_high_kernel,
                [sds(shape[1:])] + [sds(shape[1:], BF16)] * 3,
                pos, low[0], *moved,
                smem=(0,),
            )
            wide = [high[0]] + [turn_flip(high[t], t, dp, 0) for t in range(1, 4)]
        else:
            kept_b, kept_a = back(True, 0, 2, recv_b)
            total = lax.psum_scatter(keep + recv.astype(F32), "dp", scatter_dimension=0)
            wide = [total] + [jnp.zeros_like(total)] * 3
    with jax.named_scope("branch_sum"):
        got_b = lax.all_to_all(kept_b, "dp", 0, 0, tiled=True)
    with jax.named_scope("owner"):
        tr = [(lhs[i],) + tuple(s[1:]) for i, s in enumerate((weights, firsts, seconds))]
        last = (wt, kept_a, sent_a, *tr[0], *tr[1], *tr[2])
        shares, pay, *last = call(
            functools.partial(owner_kernel, count, classes),
            [sds((3 * cb + 2 * mr, LANES)), hbm_out((n, 2, LANES))] + [vmem(v.shape, v.dtype) for v in last],
            pos, got_b, sum2, *wide, fix, *last,
            smem=(0,),
            hbm=tuple(range(7, 8 + len(last))),
            scratch=[
                pltpu.VMEM(fix.shape, F32),
                pltpu.SemaphoreType.DMA((1,)),
                pltpu.SemaphoreType.DMA((len(last),)),
            ],
        )
    theirs = swap(shares)
    got = exchange(pay)
    with jax.named_scope("final"):
        shapes = [t.shape for t in tr[0]]
        outs = []
        for dtype in (F32, F32, F32, BF16):
            outs += [sds(s, dtype) for s in shapes]
        outs += [sds((1, 1)), sds((width, batch))]
        res = call(
            final_kernel, outs, pos, got, shares, theirs, x, *last,
            smem=(0,),
            out_specs=tuple(pl.BlockSpec(memory_space=pltpu.VMEM if i == 16 else pltpu.HBM) for i in range(18)),
            scratch=[pltpu.VMEM(v.shape, v.dtype) for i, v in enumerate(outs) if i != 16]
            + [pltpu.SemaphoreType.DMA((18,))],
        )
    result = list(res[:16])
    for i in range(0, 16, 4):
        result[i] = result[i].transpose(0, 2, 1)
    return (*result, res[16].reshape(()), res[17].T)


def solution(mesh):
    tables = (P(BOTH, None), P(BOTH), P(BOTH))
    params = (P(None, None, "dp"), P("dp", None), P("dp", None), P(None, "dp"))
    return jax.shard_map(
        on_device,
        mesh=mesh,
        in_specs=tables + params * 3,
        out_specs=params * 4 + (P(), P(BOTH, None)),
        check_vma=False,
    )
```

```python
import functools
import math

import jax
import jax.numpy as jnp
from jax import lax
from jax.experimental import pallas as pl
from jax.experimental.pallas import tpu as pltpu
from jax.sharding import PartitionSpec as P

HOPS = 4
STEP = 7
EPS_NORM = 1e-05
LANES = 128
PCOL = 64
ONE = 100
FREE = LANES - ONE
ROWS, WIDE, CHUNK = 32, 256, 256
BOTH = ("dp", "rep")
F32 = jnp.float32
BF16 = jnp.bfloat16


def dot(left, right, left_dim, right_dim):
    return lax.dot_general(
        left,
        right,
        (((left_dim,), (right_dim,)), ((), ())),
        preferred_element_type=F32,
    )


def call(body, outs, *args, smem=(), hbm=(), after=(), grid=None, in_specs=None, out_specs=None, scratch=(), mib=12, flops=0):
    skip = len(args)
    if in_specs is None:
        spaces = {**{i: pltpu.SMEM for i in smem}, **{i: pltpu.HBM for i in hbm}}
        in_specs = [pl.BlockSpec(memory_space=spaces.get(i, pltpu.VMEM)) for i in range(skip)]
    if out_specs is None:
        out_specs = tuple(pl.BlockSpec(memory_space=pltpu.VMEM) for _ in outs)
    in_specs = list(in_specs) + [pl.BlockSpec(memory_space=pl.ANY) for _ in after]
    args = [pltpu.with_memory_space_constraint(a, pltpu.HBM) if i in hbm else a for i, a in enumerate(args)]
    moved = sum(math.prod(a.shape) * jnp.dtype(a.dtype).itemsize for a in (*args, *outs))

    def kernel(*refs):
        body(*refs[:skip], *refs[skip + len(after) :])

    kwargs = {} if grid is None else {"grid": grid}
    return pl.pallas_call(
        kernel,
        out_shape=tuple(outs),
        in_specs=in_specs,
        out_specs=out_specs,
        scratch_shapes=list(scratch),
        compiler_params=pltpu.CompilerParams(vmem_limit_bytes=mib << 20),
        cost_estimate=pl.CostEstimate(flops=1024, bytes_accessed=1024, transcendentals=0),
        **kwargs,
    )(*args, *[pltpu.with_memory_space_constraint(a, pltpu.HBM) for a in after])


def fetch(sources, buffers, sems):
    copies = [pltpu.make_async_copy(s, b, sems.at[i]) for i, (s, b) in enumerate(zip(sources, buffers))]
    for copy in copies:
        copy.start()

    def wait():
        for copy in copies:
            copy.wait()

    return wait


def sds(shape, dtype=F32):
    return jax.ShapeDtypeStruct(shape, dtype)


def vmem(shape, dtype=F32):
    return pltpu.VMEM(shape, dtype)


def hbm_out(shape, dtype=F32):
    return pltpu.HBM(shape, dtype)


def lane_of(shape):
    return lax.broadcasted_iota(jnp.int32, shape, len(shape) - 1)


def to_cols(rows, first):
    parts = []
    for i in range(4):
        row = rows[first + i : first + i + 1, :]
        parts.append(jnp.transpose(jnp.broadcast_to(row, (LANES, LANES))))
    return jnp.concatenate(parts, axis=0)


def lane_sums(part):
    total = jnp.sum(jnp.transpose(part), axis=0, keepdims=True)
    return jnp.concatenate([total[:, i * LANES : (i + 1) * LANES] for i in range(4)], axis=0)


def fold_lanes(value):
    out = value[:, :LANES]
    for i in range(1, value.shape[1] // LANES):
        out = out + value[:, i * LANES : (i + 1) * LANES]
    return out


def prep_kernel(pos_ref, wb_hbm, wc_hbm, sp_hbm, wm_hbm, own_ref, block_ref, wb_ref, wc_ref, sp_ref, wm_ref, mix_ref, sems):
    wait = fetch((wb_hbm, wc_hbm, sp_hbm, wm_hbm), (wb_ref, wc_ref, sp_ref, wm_ref), sems)
    mr, hid = wm_ref.shape
    own_ref[...] = jnp.zeros_like(own_ref)
    wait()
    wc = wc_ref[...].astype(BF16)
    small = jnp.transpose(sp_ref[...]).astype(BF16)
    own_ref[0:HOPS, :, 0 : wb_ref.shape[2]] = wb_ref[...].astype(BF16)
    own_ref[HOPS, :, 0 : wc.shape[1]] = wc
    own_ref[HOPS, :, PCOL : PCOL + small.shape[1]] = small
    mix_ref[...] = own_ref[0:HOPS]
    mix_ref[0, :, ONE : ONE + small.shape[1]] = small
    mix_ref[1, :, ONE:LANES] = wc[:, :FREE]
    mix_ref[2, :, ONE : ONE + wc.shape[1] - FREE] = wc[:, FREE:]
    first = pos_ref[1] == 0
    part = wc.shape[0] // 2
    for k in range(HOPS):
        block_ref[k * part : (k + 1) * part, :] = jnp.where(first, mix_ref[k, :part], mix_ref[k, part:])
    at = HOPS * part
    for i in range(2):
        left = wm_ref[:, i * LANES : (i + 1) * LANES]
        right = wm_ref[:, hid // 2 + i * LANES : hid // 2 + (i + 1) * LANES]
        block_ref[at + i * mr : at + (i + 1) * mr, :] = jnp.where(first, left, right).astype(BF16)


def stack_kernel(a_ref, b_ref, c_ref, d_ref, out_ref):
    for i, ref in enumerate((a_ref, b_ref, c_ref, d_ref)):
        out_ref[i] = ref[...]


def each_block(pos_ref, arrays):
    for which in range(2):
        half = pos_ref[1] if which == 0 else 1 - pos_ref[1]
        for t in range(4):
            for e in range(4):
                yield arrays[which * 4 + t].at[e], pos_ref[0] ^ (4 * e + t), half


HALF = LANES // 2
QUADS = HALF // 4


def store_grams(grams, out_ref):
    if out_ref.shape[0] == HOPS:
        for k in range(HOPS):
            out_ref[k] = grams[k]
        return
    lane = lane_of((HALF, LANES))
    blocks = [g[:HALF] for g in grams]
    for k in range(0, HOPS, 2):
        blocks.append(jnp.where(lane < HALF, pltpu.roll(grams[k][HALF:], HALF, 1), grams[k + 1][HALF:]))
    for i, block in enumerate(blocks):
        for j in range(QUADS):
            out_ref[i * QUADS + j] = block[4 * j : 4 * j + 4]


def load_grams(in_ref, gram_ref, rest_ref):
    if in_ref.shape[0] == HOPS:
        gram_ref[...] = in_ref[...]
        return
    for i in range(HOPS + HOPS // 2):
        for j in range(QUADS):
            rows = slice(4 * j, 4 * j + 4)
            if i < HOPS:
                gram_ref[i, rows, :] = in_ref[i * QUADS + j]
            else:
                rest_ref[i - HOPS, rows, :] = in_ref[i * QUADS + j]
    lane = lane_of((HALF, LANES))
    for k in range(HOPS):
        upper = jnp.concatenate([gram_ref[k, :HALF, :], jnp.zeros((HALF, LANES), F32)], axis=0)
        rest = rest_ref[k // 2]
        if k % 2 == 0:
            rest = pltpu.roll(rest, HALF, 1)
        gram_ref[k, HALF:, :] = jnp.where(lane < HALF, jnp.transpose(upper)[HALF:], rest)


def gather_kernel(idx_ref, tab_ref, *refs):
    i = pl.program_id(0)
    if len(refs) > 4:
        own_ref, x_ref, gram_ref, own_out, acc, pad, sem = refs
        copy = pltpu.make_async_copy(own_ref, own_out, sem)

        @pl.when(i == 0)
        def _():
            copy.start()

        @pl.when(i == pl.num_programs(0) - 1)
        def _():
            copy.wait()
    else:
        x_ref, gram_ref, acc, pad = refs
    width = tab_ref.shape[1]
    d_in = tab_ref.shape[0] // HOPS
    batch = idx_ref.shape[1]
    rows = lax.broadcasted_iota(jnp.int16, (width, batch), 0)
    hot = jnp.where(rows == (idx_ref[...] - i * width).astype(jnp.int16), BF16(1.0), BF16(0.0))
    part = dot(tab_ref[...].astype(BF16), hot, 1, 0)

    @pl.when(i == 0)
    def _():
        acc[...] = part

    @pl.when(i > 0)
    def _():
        acc[...] += part

    @pl.when(i == pl.num_programs(0) - 1)
    def _():
        row = lax.broadcasted_iota(jnp.int32, pad.shape, 0)
        pad[...] = jnp.where(row == d_in, 1.0, 0.0)
        grams = []
        for k in range(HOPS):
            pad[0:d_in, :] = acc[k * d_in : (k + 1) * d_in, :]
            x = pad[...].astype(BF16)
            x_ref[k] = x
            grams.append(dot(x, x, 1, 1))
        store_grams(grams, gram_ref)


def sum_spread_kernel(in_ref, out_ref):
    out_ref[...] = jnp.broadcast_to(jnp.sum(in_ref[...], axis=0, keepdims=True), out_ref.shape)


def three_terms(wide):
    terms = []
    for _ in range(3):
        terms.append(wide.astype(BF16))
        wide = wide - terms[-1].astype(F32)
    return terms


def exact_dot(low, wide):
    total = None
    for term in three_terms(wide):
        part = dot(low, term, 1, 0)
        total = part if total is None else total + part
    return total


def assemble_kernel(classes, pos_ref, order_ref, *refs):
    wb_ref, wm_out, wm_ref, sems = refs[8:]
    hid = wb_ref.shape[1]
    cb = hid // 16
    mr = wm_ref.shape[1] // 16
    part = cb // 2
    first = HOPS * part
    for ref, s, half in each_block(pos_ref, refs[:8]):
        rows = pl.ds(pl.multiple_of(s * mr, mr), mr)
        for i in range(2):
            wm_ref[half * 2 + i, rows, :] = ref[first + i * mr : first + (i + 1) * mr, :]
    stored = fetch((wm_ref,), (wm_out,), sems)
    for ref, s, half in each_block(pos_ref, refs[:8]):
        rows = pl.ds(pl.multiple_of(s * cb + half * part, part), part)
        for j in range(HOPS):
            wb_ref[j, rows, :] = ref[j * part : (j + 1) * part, :]
    lane = lane_of((hid, LANES))
    mixed = [wb_ref[j].astype(F32) for j in range(3)]
    tail = jnp.where((lane >= PCOL) & (lane < PCOL + 5 * HOPS), pltpu.roll(mixed[0], LANES + PCOL - ONE, 1), 0.0)
    tail = jnp.where(lane < FREE, pltpu.roll(mixed[1], LANES - ONE, 1), tail)
    tail = jnp.where((lane >= FREE) & (lane < classes), pltpu.roll(mixed[2], LANES + FREE - ONE, 1), tail)
    wb_ref[HOPS] = tail.astype(BF16)
    for j in range(3):
        wb_ref[j] = jnp.where(lane < ONE, mixed[j], 0.0).astype(BF16)
    stored()


def own_stats_kernel(count, pos_ref, in_ref, own_hbm, gram_ref, fix_ref, rest_ref, own_ref, sems):
    wait = fetch((own_hbm,), (own_ref,), sems)
    load_grams(in_ref, gram_ref, rest_ref)
    wait()
    rep = pos_ref[1]
    lane = lane_of(fix_ref.shape[1:])
    tail = own_ref[HOPS].astype(F32)
    for i in range(2):
        gram = gram_ref[rep * 2 + i]
        w = own_ref[rep * 2 + i]
        wg = exact_dot(w, gram)
        mean = wg[:, ONE : ONE + 1] / count
        second = jnp.sum(wg * w.astype(F32), axis=1, keepdims=True) / count
        inv = lax.rsqrt(second - mean * mean + EPS_NORM)
        gain = jnp.where(rep == 0, tail[:, PCOL + i : PCOL + i + 1], tail[:, PCOL + 2 + i : PCOL + 3 + i])
        block = wg - mean * gram[ONE : ONE + 1, :]
        for j, value in enumerate((mean, inv, gain * inv)):
            block = jnp.where(lane == ONE + j, value, block)
        fix_ref[i] = block


def stats_kernel(count, gram_ref, wb_ref, ws_ref, coef_ref, mu_ref, wt_ref):
    hid = wb_ref.shape[1]
    small = jnp.transpose(wb_ref[HOPS].astype(F32))
    row = lax.broadcasted_iota(jnp.int32, (16, hid), 0)

    def at(i):
        return small[PCOL + i : PCOL + i + 1, :]

    def columns(values):
        block = jnp.zeros((16, hid), F32)
        for i, value in enumerate(values):
            block = jnp.where(row == i, value, block)
        return jnp.transpose(jnp.concatenate([block, jnp.zeros((LANES - 16, hid), F32)], axis=0))

    mu_ref[...] = jnp.zeros_like(mu_ref)
    for k in range(HOPS):
        gram = gram_ref[k]
        mu_ref[k : k + 1, :] = gram[ONE : ONE + 1, :] / count
        wide = jnp.transpose(wb_ref[k].astype(F32))
        w = wide.astype(BF16)
        wt_ref[k] = w
        wg = None
        for term in three_terms(gram):
            part = dot(term, w, 1, 0)
            wg = part if wg is None else wg + part
        mean = wg[ONE : ONE + 1, :] / count
        second = jnp.sum(wg * wide, axis=0, keepdims=True) / count
        inv = lax.rsqrt(second - mean * mean + EPS_NORM)
        gain, shift, slope, join = at(k), at(HOPS + k), at(2 * HOPS + k), at(3 * HOPS + k)
        v = gain * inv
        half = 0.5 * v
        scaled = jnp.where(
            lax.broadcasted_iota(jnp.int32, wide.shape, 0) == ONE, 0.5 * shift - half * mean, half * wide
        )
        scaled = jnp.transpose(scaled)
        high = scaled.astype(BF16)
        ws_ref[k, :, 0:LANES] = high
        ws_ref[k, :, LANES : 2 * LANES] = (scaled - high.astype(F32)).astype(BF16)
        scale = 0.5 * (1.0 - join)
        coef_ref[k] = columns(
            (
                0.5 * (1.0 + slope),
                0.5 * (1.0 - slope),
                1.0 + join,
                1.0 - join,
                join / scale,
                scale,
                scale * v * slope,
                scale * 0.5 * v * (1.0 - slope),
            )
        )


def project_units(ws_ref, x_ref, k, rows):
    x = x_ref[k]
    return dot(ws_ref[k, rows, :], jnp.concatenate([x, x], axis=0), 1, 0)


def column_set(ref, hop, at, lanes):
    block = ref[hop, at, :]
    return [jnp.broadcast_to(block[:, i : i + 1], (ROWS, WIDE)) for i in lanes]


def merge_block(wm_ref, rows):
    return jnp.concatenate([wm_ref[i, rows, :] for i in range(wm_ref.shape[0])], axis=1)


def forward_kernel(
    x_ref, ws_ref, coef_ref, wt_ref, fix_ref, wm_hbm, joined_ref, pre2_ref, pay_ref, wt_out, fix_out, pre, wm_ref, sems
):
    wait = fetch((wm_hbm,), (wm_ref,), sems.at[pl.ds(2, 1)])
    stored = fetch((wt_ref, fix_ref), (wt_out, fix_out), sems)
    hid = ws_ref.shape[1]
    batch = x_ref.shape[2]
    per = hid // CHUNK
    jobs = [(k, c) for k in range(HOPS) for c in range(per)]

    def project(i):
        k, c = jobs[i]
        pre[i % 2] = project_units(ws_ref, x_ref, k, slice(c * CHUNK, (c + 1) * CHUNK))

    def units(i):
        k, c = jobs[i]
        for g in range(CHUNK // ROWS):
            at = slice(c * CHUNK + g * ROWS, c * CHUNK + (g + 1) * ROWS)
            cs = column_set(coef_ref, k, at, range(4))
            for b in range(batch // WIDE):
                lanes = slice(b * WIDE, (b + 1) * WIDE)
                u = pre[i % 2, g * ROWS : (g + 1) * ROWS, lanes]
                u = u * (cs[0] + cs[1] * jnp.tanh(u))
                joined_ref[k, at, lanes] = (u * (cs[2] + cs[3] * jnp.tanh(u))).astype(BF16)

    project(0)
    for i in range(len(jobs)):
        if i + 1 < len(jobs):
            project(i + 1)
        units(i)
        if i % per == per - 1:
            k = i // per
            if k == 0:
                wait()
            part = dot(merge_block(wm_ref, slice(k * hid, (k + 1) * hid)), joined_ref[k], 0, 0)
            if k == 0:
                pre2_ref[...] = part
            else:
                pre2_ref[...] += part
    value = pre2_ref[...]
    sums = jnp.concatenate([lane_sums(fold_lanes(value)), lane_sums(fold_lanes(value * value))], axis=0)
    pay_ref[...] = jnp.broadcast_to(sums[None], pay_ref.shape)
    stored()


def par_columns(wb_ref):
    return wb_ref[HOPS][:, PCOL:].astype(F32)[:, 4 * HOPS : 5 * HOPS]


def columns2(count, rows, par):
    mean = to_cols(rows, 0) / count
    inv = lax.rsqrt(to_cols(rows, 4) / count - mean * mean + EPS_NORM)
    shape = mean.shape
    gain = jnp.broadcast_to(par[:, 0:1], shape)
    shift = jnp.broadcast_to(par[:, 1:2], shape)
    slope = jnp.broadcast_to(par[:, 2:3], shape)
    return mean, inv, gain, shift, slope


def head_kernel(
    count, classes, got_ref, pre2_ref, wb_ref, lab_hbm, dy2_ref, pay_ref, class_ref, stat_ref, act, dact, cols, sums, lab_ref, sems
):
    wait = fetch((lab_hbm,), (lab_ref,), sems)
    hid, batch = dy2_ref.shape
    par = par_columns(wb_ref)
    mean, inv, gain, shift, slope = columns2(count, jnp.sum(got_ref[...], axis=0), par)
    stat_ref[0] = mean
    stat_ref[1] = inv
    cols[0] = 0.5 * gain * inv
    cols[1] = 0.5 * (shift - gain * inv * mean)
    cols[2] = 1.0 + slope
    cols[3] = 1.0 - slope
    reps = WIDE // LANES

    def tiled(c, at):
        return jnp.concatenate([cols[c, at, :]] * reps, axis=1)

    def first(g, carry):
        at = pl.ds(pl.multiple_of(g * ROWS, ROWS), ROWS)
        c = [tiled(i, at) for i in range(4)]
        for b in range(batch // WIDE):
            lanes = slice(b * WIDE, (b + 1) * WIDE)
            u = pre2_ref[at, lanes] * c[0] + c[1]
            act[at, lanes] = (u * (c[2] + c[3] * jnp.tanh(u))).astype(BF16)
        return carry

    lax.fori_loop(0, hid // ROWS, first, 0, unroll=8)
    tail = wb_ref[HOPS]
    wc = jnp.where(lane_of(tail.shape) < PCOL, tail.astype(F32), 0.0).astype(BF16)
    logits = dot(wc, act[...], 0, 0)
    live = -(-classes // 16) * 16
    row = lax.broadcasted_iota(jnp.int32, (live, batch), 0)
    logits = jnp.where(row < classes, logits[:live] + par[0:live, 3:4], -jnp.inf)
    top = jnp.max(logits, axis=0, keepdims=True)
    e = jnp.exp(logits - top)
    probs = e / jnp.sum(e, axis=0, keepdims=True)
    wait()
    dlog = (probs - jnp.where(row == lab_ref[...], 1.0, 0.0)).astype(BF16)
    dlog = jnp.concatenate([dlog, jnp.zeros((LANES - live, batch), BF16)], axis=0)
    grad_class = dot(act[...], dlog, 1, 1)
    bias = jnp.sum(dlog.astype(F32), axis=1, keepdims=True)
    dact[...] = dot(wc, dlog, 1, 0)

    def second(g, carry):
        at = pl.ds(pl.multiple_of(g * ROWS, ROWS), ROWS)
        c = [tiled(i, at) for i in range(4)]
        m = jnp.concatenate([stat_ref[0, at, :]] * reps, axis=1)
        v = jnp.concatenate([stat_ref[1, at, :]] * reps, axis=1)
        acc = [jnp.zeros((ROWS, WIDE), F32) for _ in range(3)]
        for b in range(batch // WIDE):
            lanes = slice(b * WIDE, (b + 1) * WIDE)
            p = pre2_ref[at, lanes]
            d = dact[at, lanes]
            u = p * c[0] + c[1]
            t = jnp.tanh(u)
            w = u * (1.0 - t)
            dy = d * (0.5 * (c[2] + c[3] * (t + w * (1.0 + t))))
            dy2_ref[at, lanes] = dy
            acc[0] = acc[0] + dy
            acc[1] = acc[1] + dy * ((p - m) * v)
            acc[2] = acc[2] + d * w
        for i in range(3):
            sums[i, at, :] = fold_lanes(acc[i])
        return carry

    lax.fori_loop(0, hid // ROWS, second, 0, unroll=8)
    pay = jnp.concatenate([lane_sums(sums[0]), lane_sums(sums[1])], axis=0)
    pay_ref[...] = jnp.broadcast_to(pay[None], pay_ref.shape)
    lane = lane_of((hid, LANES))
    slope_sum = jnp.sum(sums[2], axis=1, keepdims=True)
    bias = jnp.concatenate([bias, jnp.zeros((hid - LANES, 1), F32)], axis=0)
    block = jnp.where(lane < classes, grad_class, 0.0)
    block = jnp.where(lane == PCOL, slope_sum, block)
    class_ref[...] = jnp.where(lane == PCOL + 1, bias, block)


def turn_kernel(
    count, pos_ref, got_ref, stat_ref, wb_ref, pre2_ref, dy2_ref, joined_ref, class_ref, wm_hbm, dpre_ref, keep_ref, send_ref, sum2_ref, wm_ref, cols, sems
):
    wait = fetch((wm_hbm,), (wm_ref,), sems)
    hid, batch = dy2_ref.shape
    half = send_ref.shape[2]
    rows8 = jnp.sum(got_ref[...], axis=0)
    sum2_ref[...] = rows8
    mean, inv = stat_ref[0], stat_ref[1]
    v = jnp.broadcast_to(par_columns(wb_ref)[:, 0:1], mean.shape) * inv
    cols[0] = v
    cols[1] = v * to_cols(rows8, 0) / count
    cols[2] = v * inv * to_cols(rows8, 4) / count
    reps = WIDE // LANES
    for g in range(hid // ROWS):
        at = slice(g * ROWS, (g + 1) * ROWS)
        c = [jnp.concatenate([cols[i, at, :]] * reps, axis=1) for i in range(3)]
        m = jnp.concatenate([stat_ref[0, at, :]] * reps, axis=1)
        for b in range(batch // WIDE):
            lanes = slice(b * WIDE, (b + 1) * WIDE)
            value = c[0] * dy2_ref[at, lanes] - c[1] - (pre2_ref[at, lanes] - m) * c[2]
            dpre_ref[at, lanes] = value.astype(BF16)
    mine = pl.ds(pl.multiple_of(pos_ref[1] * half, half), half)
    theirs = pl.ds(pl.multiple_of((1 - pos_ref[1]) * half, half), half)
    dp, size, _ = send_ref.shape
    per = dp // HOPS
    mr = hid // per
    cb = hid // dp
    for k in range(HOPS):
        other = dot(joined_ref[k], dpre_ref[theirs, :], 1, 1).astype(BF16)
        own = dot(joined_ref[k], dpre_ref[mine, :], 1, 1)
        for j in range(per):
            send_ref[k * per + j, 0:mr, :] = other[j * mr : (j + 1) * mr]
            keep_ref[k * per + j, 0:mr, :] = own[j * mr : (j + 1) * mr]
    first = pos_ref[1] == 0
    for s in range(dp):
        block = class_ref[s * cb : (s + 1) * cb, :]
        wide = jnp.concatenate([block[: cb // 2], block[cb // 2 :]], axis=1)
        send_ref[s, mr:size, :] = jnp.where(first, 0.0, wide).astype(BF16)
        keep_ref[s, mr:size, :] = jnp.where(first, wide, 0.0)
    wait()


SMALLS = 4


def back_kernel(own, first, count, pos_ref, dpre_ref, x_ref, ws_ref, coef_ref, mu_ref, wm_ref, wt_hbm, *refs):
    if own:
        recv_ref, refs = refs[0], refs[1:]
    b_ref, a_out, pre, dj, dyv, sums, a_ref, wt_ref, out_sems = refs
    hid = wt_ref.shape[2]
    batch = x_ref.shape[2]
    per = hid // CHUNK
    jobs = [(k, c) for k in range(count) for c in range(per)]
    base = 2 * (pos_ref[1] if own else 1 - pos_ref[1]) + first
    dp, _, cb, _ = b_ref.shape
    copies = []
    wait_wt = fetch((wt_hbm.at[pl.ds(base, count)],), (wt_ref,), out_sems.at[pl.ds(count, 1)])

    def project(i):
        k, c = jobs[i]
        rows = slice(c * CHUNK, (c + 1) * CHUNK)
        pre[i % 2] = project_units(ws_ref, x_ref, base + k, rows)
        at = pl.ds(pl.multiple_of((base + k) * hid + c * CHUNK, CHUNK), CHUNK)
        dj[i % 2] = dot(merge_block(wm_ref, at), dpre_ref[...], 1, 0)

    def units(i):
        k, c = jobs[i]
        for g in range(CHUNK // ROWS):
            at = slice(c * CHUNK + g * ROWS, c * CHUNK + (g + 1) * ROWS)
            here = slice(g * ROWS, (g + 1) * ROWS)
            p1, q1, s2, s1, r1 = column_set(coef_ref, base + k, at, (0, 1, 4, 6, 7))
            one = jnp.zeros((ROWS, WIDE), F32)
            two = jnp.zeros((ROWS, WIDE), F32)
            for b in range(batch // WIDE):
                lanes = slice(b * WIDE, (b + 1) * WIDE)
                u = pre[i % 2, here, lanes]
                t = jnp.tanh(u)
                u2 = u * (p1 + q1 * t)
                t2 = jnp.tanh(u2)
                d = dj[i % 2, here, lanes]
                w = u2 * (1.0 - t2)
                two = two + d * w
                d = d * (s2 + (1.0 + t2) * (1.0 + w))
                w = u * (1.0 - t)
                one = one + d * w
                dyv[k, at, lanes] = (d * (s1 + r1 * ((1.0 + t) * (1.0 + w)))).astype(BF16)
            sums[k, 0, at, :] = fold_lanes(one)
            sums[k, 1, at, :] = fold_lanes(two)

    def close(k):
        if k == 0:
            wait_wt()
        w = wt_ref[k]
        a_ref[k] = dot(w, dyv[k], 1, 0)
        copies.append(fetch((a_ref.at[k],), (a_out.at[k],), out_sems.at[pl.ds(k, 1)]))
        block = dot(x_ref[base + k], dyv[k], 1, 1)
        row = lax.broadcasted_iota(jnp.int32, block.shape, 0)
        total = block[ONE : ONE + 1, :]
        center = jnp.transpose(jnp.broadcast_to(mu_ref[pl.ds(base + k, 1), :], (LANES, LANES)))
        block = jnp.where(row < ONE, block - jnp.concatenate([center] * (hid // LANES), axis=1) * total, 0.0)
        smalls = (
            total,
            jnp.sum(block * w.astype(F32), axis=0, keepdims=True),
            jnp.sum(jnp.transpose(sums[k, 0] * coef_ref[base + k, :, 5:6]), axis=0, keepdims=True),
            jnp.sum(jnp.transpose(sums[k, 1]), axis=0, keepdims=True),
        )
        for i, value in enumerate(smalls):
            block = jnp.where(row == ONE + i, value, block)
            if not own:
                block = jnp.where(row == ONE + SMALLS + i, value - value.astype(BF16).astype(F32), block)
        block = jnp.transpose(block)
        if own:
            received = jnp.concatenate([recv_ref[s, k] for s in range(dp)], axis=0).astype(F32)
            block = split_smalls(block + join_smalls(received))
        for s in range(dp):
            b_ref[s, k] = block[s * cb : (s + 1) * cb, :].astype(BF16)

    project(0)
    for i in range(len(jobs)):
        if i + 1 < len(jobs):
            project(i + 1)
        units(i)
        if i % per == per - 1:
            close(i // per)
    for done in copies:
        done()


def split_smalls(block):
    lane = lane_of(block.shape)
    rest = block - block.astype(BF16).astype(F32)
    moved = pltpu.roll(rest, SMALLS, 1)
    return jnp.where((lane >= ONE + SMALLS) & (lane < ONE + 2 * SMALLS), moved, block)


def join_smalls(block):
    lane = lane_of(block.shape)
    moved = pltpu.roll(block, LANES - SMALLS, 1)
    block = jnp.where((lane >= ONE) & (lane < ONE + SMALLS), block + moved, block)
    return jnp.where(lane < ONE + SMALLS, block, 0.0)


def split_low_kernel(pos_ref, keep_ref, got_ref, o0_ref, o1_ref, o2_ref, o3_ref):
    low, high = pos_ref[0] % 4, pos_ref[0] // 4
    for t, ref in enumerate((o0_ref, o1_ref, o2_ref, o3_ref)):
        for e in range(4):
            j = jnp.where(pos_ref[1] == 0, e * 4 + (low ^ t), (high ^ t) * 4 + e)
            ref[e] = (keep_ref[j] + got_ref[j].astype(F32)).astype(ref.dtype)


def split_high_kernel(pos_ref, own_ref, g1_ref, g2_ref, g3_ref, o0_ref, o1_ref, o2_ref, o3_ref):
    mine = jnp.where(pos_ref[1] == 0, pos_ref[0] // 4, pos_ref[0] % 4)
    for t, ref in enumerate((o0_ref, o1_ref, o2_ref, o3_ref)):
        j = mine ^ t
        value = own_ref[j] + g1_ref[j].astype(F32) + g2_ref[j].astype(F32) + g3_ref[j].astype(F32)
        ref[...] = value.astype(ref.dtype)


def owner_kernel(
    count, classes, pos_ref, got_ref, sum2_ref, w0_ref, w1_ref, w2_ref, w3_ref, *refs
):
    late = (len(refs) - 6) // 2
    grad_ref, pay_ref = refs[1 + late : 3 + late]
    fix_ref, sems, late_sems = refs[3 + 2 * late :]
    wait = fetch(refs[:1], (fix_ref,), sems)
    brought = fetch(refs[1 : 1 + late], refs[3 + late : 3 + 2 * late], late_sems)
    _, _, cb, _ = got_ref.shape
    total = jnp.sum(got_ref[...].astype(F32), axis=0)
    rep = pos_ref[1]
    lane = lane_of((cb, LANES))
    squares = jnp.zeros((1, 1), F32)
    spread = jnp.zeros((cb, LANES), F32)

    def all_sum(v):
        return jnp.sum(jnp.sum(v, axis=1, keepdims=True), axis=0, keepdims=True)

    others = w1_ref[...].astype(F32) + w2_ref[...].astype(F32) + w3_ref[...].astype(F32)
    wide = w0_ref[...].astype(F32) + others
    mr = wide.shape[0] - cb // 2
    merge = wide[:mr]
    squares = squares + all_sum(merge * merge)
    at = 2 * cb
    for i in range(2):
        grad_ref[at + i * mr : at + (i + 1) * mr, :] = merge[:, i * LANES : (i + 1) * LANES]
    at = at + 2 * mr
    block = jnp.concatenate([wide[mr:, :LANES], wide[mr:, LANES:]], axis=0)
    shift_own = own_column(sum2_ref, 0, pos_ref[0], cb)
    gain_own = own_column(sum2_ref, 4, pos_ref[0], cb)
    block = jnp.where(lane == PCOL + 2, gain_own, block)
    block = jnp.where(lane == PCOL + 3, shift_own, block)
    grad_ref[at : at + cb, :] = block
    squares = squares + jnp.where(rep == 0, all_sum(block * block), 0.0)
    wait()
    for i in range(2):
        b = join_smalls(total[i])
        wg = fix_ref[i]
        mean, inv, v = [wg[:, ONE + j : ONE + j + 1] for j in range(3)]
        s = b[:, ONE : ONE + 1]
        g = inv * b[:, ONE + 1 : ONE + 2]
        beta = inv * g / count
        alpha = s / count - beta * mean
        fixed = jnp.where(lane < ONE, b - beta * wg, 0.0)
        fixed = jnp.where(lane == ONE, g / v, fixed)
        fixed = jnp.where(lane == ONE + 1, s / v, fixed)
        fixed = jnp.where(lane == ONE + 2, b[:, ONE + 2 : ONE + 3], fixed)
        fixed = jnp.where(lane == ONE + 3, b[:, ONE + 3 : ONE + 4], fixed)
        grad_ref[i * cb : (i + 1) * cb, :] = fixed
        squares = squares + all_sum(fixed * fixed)
        spread = jnp.where(lane == 2 * i, alpha, spread)
        spread = jnp.where(lane == 2 * i + 1, beta, spread)
    rows = jnp.transpose(jnp.concatenate([spread, jnp.zeros((LANES - cb, LANES), F32)], axis=0))[0:8]
    packed = jnp.concatenate([rows[i : i + 1, :cb] for i in range(4)], axis=1)
    if 4 * cb < LANES:
        packed = jnp.concatenate([packed, jnp.zeros((1, LANES - 4 * cb), F32)], axis=1)
    pay = jnp.concatenate([packed, jnp.where(lane_of((1, LANES)) == 0, squares, 0.0)], axis=0)
    pay_ref[...] = jnp.broadcast_to(pay[None], pay_ref.shape)
    brought()


def own_column(ref, first, me, cb):
    block = (me * cb) // LANES
    row = ref[pl.ds(first + block, 1), :]
    lane = lane_of((cb, LANES))
    sub = lax.broadcasted_iota(jnp.int32, (cb, LANES), 0)
    hit = lane == sub + (me * cb) % LANES
    return jnp.sum(jnp.where(hit, jnp.broadcast_to(row, (cb, LANES)), 0.0), axis=1, keepdims=True)


def adam_into(weight_ref, moment_ref, square_ref, grad, scale, rate, outs, at=Ellipsis):
    new_ref, new_m_ref, new_s_ref, copy_ref = outs
    weight = weight_ref[at]
    clipped = grad * scale
    moment = 0.9 * moment_ref[at] + 0.1 * clipped
    square = 0.999 * square_ref[at] + 0.001 * clipped * clipped
    fix_one = 1.0 - 0.9**STEP
    fix_two = 1.0 - 0.999**STEP
    update = moment / fix_one / (jnp.sqrt(square / fix_two) + 1e-08) + 0.01 * weight
    new = weight - rate * update
    new_ref[at] = new
    new_m_ref[at] = moment
    new_s_ref[at] = square
    copy_ref[at] = new.astype(BF16)


def final_kernel(pos_ref, got_ref, mine_ref, other_ref, x_ref, wt_ref, own_ref, sent_ref, *refs):
    states, outs_hbm, norm_ref, rows_hbm = refs[:12], refs[12:28], refs[28], refs[29]
    outs, rows_ref, out_sems = refs[30:46], refs[46], refs[47]
    weights, firsts, seconds = states[0:4], states[4:8], states[8:12]
    n = got_ref.shape[0]
    cb = weights[0].shape[1]
    blocks = 4
    per = n // 2 // blocks
    lane = lane_of((blocks, LANES))
    parts = [[jnp.zeros((blocks, LANES), F32) for _ in range(4)] for _ in range(2)]
    for r in range(2):
        for j in range(per):
            rows = [got_ref[(b * per + j) * 2 + r, 0:1, :] for b in range(blocks)]
            rows = jnp.concatenate(rows, axis=0)
            here = (lane >= j * cb) & (lane < (j + 1) * cb)
            for i in range(4):
                shift = (j - i) * cb % LANES
                moved = pltpu.roll(rows, shift, 1) if shift else rows
                parts[r][i] = jnp.where(here, moved, parts[r][i])

    def spread_row(r, i):
        return jnp.concatenate([parts[r][i][b : b + 1] for b in range(blocks)], axis=1)

    squares = jnp.sum(got_ref[...], axis=0)[1:2, :]
    norm = jnp.sqrt(jnp.sum(squares, axis=1, keepdims=True))
    norm_ref[...] = norm
    scale = 1.0 / jnp.maximum(norm, 1.0)

    d_in = weights[0].shape[2]
    mr = weights[1].shape[0]
    classes = weights[2].shape[1]
    first = pos_ref[1] == 0
    mine, other = mine_ref[...], other_ref[...]
    low = jnp.where(first, mine, other)
    high = jnp.where(first, other, mine)
    stores = []
    fixes = []
    for k in range(HOPS):
        r, i = k // 2, k % 2
        alpha, beta = spread_row(r, 2 * i), spread_row(r, 2 * i + 1)
        low_w = wt_ref[k]
        right = jnp.where(lax.broadcasted_iota(jnp.int32, low_w.shape, 0) == ONE, alpha, low_w.astype(F32) * beta)
        high_part = right.astype(BF16)
        fix = dot(low_w, high_part, 1, 1) + dot(low_w, (right - high_part.astype(F32)).astype(BF16), 1, 1)
        high_part = fix.astype(BF16)
        fixes.append(jnp.concatenate([high_part, (fix - high_part.astype(F32)).astype(BF16)], axis=1))
    for k in range(HOPS):
        r, i = k // 2, k % 2
        value = jnp.where(pos_ref[1] == r, own_ref[i], sent_ref[i])
        value = value - dot(fixes[k], jnp.concatenate([x_ref[k], x_ref[k]], axis=0), 1, 0)
        rows_ref[k * d_in : (k + 1) * d_in, :] = value[:d_in]
        if i == 1:
            part = pl.ds(r * 2 * d_in, 2 * d_in)
            stores.append(fetch((rows_ref.at[part, :],), (rows_hbm.at[part, :],), out_sems.at[pl.ds(16 + r, 1)]))

    def group(i):
        return [o for o in outs[i::4]]

    hops = [low[0:cb], low[cb : 2 * cb], high[0:cb], high[cb : 2 * cb]]
    for k in range(HOPS):
        adam_into(weights[0], firsts[0], seconds[0], hops[k][:, :d_in], scale, 0.05, group(0), k)
    at = 2 * cb
    for half, part in enumerate((low, high)):
        for i in range(2):
            lanes = (slice(None), slice((2 * half + i) * LANES, (2 * half + i + 1) * LANES))
            grad = part[at + i * mr : at + (i + 1) * mr]
            adam_into(weights[1], firsts[1], seconds[1], grad, scale, 0.05, group(1), lanes)
    at = at + 2 * mr
    block = low[at : at + cb]
    adam_into(weights[2], firsts[2], seconds[2], block[:, :classes], scale, 0.05, group(2))
    lane = lane_of((cb, LANES))
    small = jnp.zeros((cb, LANES), F32)
    for kind in range(4):
        for k in range(HOPS):
            small = jnp.where(lane == kind * HOPS + k, hops[k][:, ONE + kind : ONE + kind + 1], small)
    for i, source in enumerate((2, 3, 0, 1)):
        small = jnp.where(lane == 4 * HOPS + i, block[:, PCOL + source : PCOL + source + 1], small)
    small = jnp.transpose(jnp.concatenate([small, jnp.zeros((LANES - cb, LANES), F32)], axis=0))
    adam_into(weights[3], firsts[3], seconds[3], small[: weights[3].shape[0], :cb], scale, 0.3, group(3))
    stores.append(fetch(outs, outs_hbm, out_sems))
    for done in stores:
        done()


def flip(value, mask, dp):
    return lax.ppermute(value, "dp", [(i, i ^ mask) for i in range(dp)])


def turn_flip(value, digit, dp, stage):
    pairs = []
    for i in range(dp):
        for core in range(2):
            mask = digit if (core + stage) % 2 else 4 * digit
            pairs.append((i * 2 + core, (i ^ mask) * 2 + core))
    return lax.ppermute(value, BOTH, pairs)


def swap(value):
    return lax.ppermute(value, "rep", [(0, 1), (1, 0)])


def exchange(value):
    return lax.all_to_all(value, BOTH, 0, 0, tiled=True)


def weights_plain(wbt, wc, sp, wm, dp):
    cb, classes = wc.shape
    mr, hid = wm.shape
    own = jnp.zeros((HOPS + 1, cb, LANES), BF16)
    own = own.at[:HOPS, :, : wbt.shape[2]].set(wbt.astype(BF16))
    own = own.at[HOPS, :, :classes].set(wc.astype(BF16))
    own = own.at[HOPS, :, PCOL : PCOL + sp.shape[0]].set(sp.T.astype(BF16))
    wb = lax.all_gather(own, "dp", axis=1, tiled=True)
    whole = lax.all_gather(wm.astype(BF16), "dp", axis=0, tiled=True)
    return own, wb, whole.reshape(HOPS * hid, hid // LANES, LANES).transpose(1, 0, 2)


def on_device(table, batch_index, labels, *state):
    weights, firsts, seconds = state[0:4], state[4:8], state[8:12]
    dp, rep = lax.axis_size("dp"), lax.axis_size("rep")
    n = dp * rep
    staged = dp == 16 and rep == 2
    me, core = lax.axis_index("dp"), lax.axis_index("rep")
    pos = jnp.stack([me, core]).astype(jnp.int32)
    batch = batch_index.shape[0]
    count = float(batch * n)
    nodes, width = table.shape
    cb = weights[0].shape[2]
    mr, hid = weights[1].shape
    classes = weights[2].shape[1]
    half = hid // 2
    lhs = [v.transpose(0, 2, 1) for v in (weights[0], firsts[0], seconds[0])]
    idx = batch_index.reshape(1, batch)
    lab = labels.reshape(1, batch)

    if staged:
        with jax.named_scope("prep"):
            sources = (lhs[0], weights[2], weights[3], weights[1])
            size = HOPS * cb // 2 + 2 * mr
            own, block = call(
                prep_kernel,
                [vmem((HOPS + 1, cb, LANES), BF16), sds((size, LANES), BF16)],
                pos, *sources,
                smem=(0,), hbm=(1, 2, 3, 4),
                scratch=[pltpu.VMEM(v.shape, F32) for v in sources]
                + [pltpu.VMEM((HOPS, cb, LANES), BF16), pltpu.SemaphoreType.DMA((4,))],
            )
        far = [flip(block, 4 * k, dp) for k in range(1, 4)]

    with jax.named_scope("gather"):
        step = 2048
        sums = (6 * QUADS, 4, LANES) if 6 * QUADS % n == 0 else (HOPS, LANES, LANES)
        passed = [own] if staged else []
        x, gram, *made = call(
            gather_kernel,
            [vmem((HOPS, LANES, batch), BF16), hbm_out(sums)] + [hbm_out(v.shape, v.dtype) for v in passed],
            pltpu.with_memory_space_constraint(idx, pltpu.HBM),
            pltpu.with_memory_space_constraint(table.T, pltpu.HBM),
            *passed,
            grid=(nodes // step,),
            in_specs=[
                pl.BlockSpec((1, batch), lambda i: (0, 0)),
                pl.BlockSpec((width, step), lambda i: (0, i)),
            ]
            + [pl.BlockSpec(memory_space=pltpu.VMEM) for _ in passed],
            out_specs=(
                pl.BlockSpec((HOPS, LANES, batch), lambda i: (0, 0, 0)),
                pl.BlockSpec(sums, lambda i: (0, 0, 0)),
            )
            + tuple(pl.BlockSpec(memory_space=pltpu.HBM) for _ in passed),
            scratch=[pltpu.VMEM((width, batch), F32), pltpu.VMEM((LANES, batch), F32)]
            + [pltpu.SemaphoreType.DMA for _ in passed],
            mib=24,
        )
        if staged:
            own = made[0]
    with jax.named_scope("gram_sum"):
        parts = gram.reshape(n, -1, *sums[1:]) if sums[1] == 4 else gram.reshape(n, -1, LANES)
        if staged:
            (stacked,) = call(stack_kernel, [sds((4,) + block.shape, BF16)], block, *far)
            parts, stacked = lax.optimization_barrier((parts, stacked))
        parts = exchange(parts)
        (parts,) = call(sum_spread_kernel, [hbm_out(parts.shape)], parts)
        gram = exchange(parts).reshape(sums)
    if not staged:
        own, wb, wm = weights_plain(lhs[0], weights[2], weights[3], weights[1], dp)
    with jax.named_scope("own_stats"):
        gram, fix = call(
            functools.partial(own_stats_kernel, count),
            [vmem((HOPS, LANES, LANES)), vmem((2, cb, LANES))],
            pos, gram, own,
            smem=(0,), hbm=(2,),
            scratch=[
                pltpu.VMEM((HOPS // 2, HALF, LANES), F32),
                pltpu.VMEM(own.shape, BF16),
                pltpu.SemaphoreType.DMA((1,)),
            ],
        )
    if staged:
        mine = [stacked] + [flip(stacked, t, dp) for t in range(1, 4)]
        mine = mine[:1] + [lax.optimization_barrier((v, parts))[0] for v in mine[1:]]
        with jax.named_scope("weights"):
            whole = (hid // LANES, HOPS * hid, LANES)
            wb, wm = call(
                functools.partial(assemble_kernel, classes),
                [vmem((HOPS + 1, hid, LANES), BF16), hbm_out(whole, BF16)],
                pos, fix, *mine, *[swap(v) for v in mine],
                smem=(0,),
                out_specs=(pl.BlockSpec(memory_space=pltpu.VMEM), pl.BlockSpec(memory_space=pltpu.HBM)),
                scratch=[pltpu.VMEM(whole, BF16), pltpu.SemaphoreType.DMA((1,))],
            )
    with jax.named_scope("stats"):
        ws, coef, mu, wt = call(
            functools.partial(stats_kernel, count),
            [
                vmem((HOPS, hid, 2 * LANES), BF16),
                vmem((HOPS, hid, LANES)),
                vmem((8, LANES)),
                vmem((HOPS, LANES, hid), BF16),
            ],
            gram, wb,
        )
    with jax.named_scope("forward"):
        joined, pre2, pay, wt, fix = call(
            forward_kernel,
            [vmem((HOPS, hid, batch), BF16), vmem((hid, batch)), sds((n, 8, LANES))]
            + [hbm_out(v.shape, v.dtype) for v in (wt, fix)],
            x, ws, coef, wt, fix, wm,
            hbm=(5,),
            out_specs=tuple(pl.BlockSpec(memory_space=m) for m in (pltpu.VMEM,) * 3 + (pltpu.HBM,) * 2),
            scratch=[
                pltpu.VMEM((2, CHUNK, batch), F32),
                pltpu.VMEM(wm.shape, BF16),
                pltpu.SemaphoreType.DMA((3,)),
            ],
        )
    got = exchange(pay)
    with jax.named_scope("head"):
        dy2, pay, block2, stat = call(
            functools.partial(head_kernel, count, classes),
            [vmem((hid, batch)), sds((n, 8, LANES)), vmem((hid, LANES)), vmem((2, hid, LANES))],
            got, pre2, wb, lab,
            hbm=(3,),
            scratch=[
                pltpu.VMEM((hid, batch), BF16),
                pltpu.VMEM((hid, batch), F32),
                pltpu.VMEM((4, hid, LANES), F32),
                pltpu.VMEM((3, hid, LANES), F32),
                pltpu.VMEM(lab.shape, lab.dtype),
                pltpu.SemaphoreType.DMA((1,)),
            ],
            flops=6 * batch * hid * LANES,
        )
    got = exchange(pay)
    with jax.named_scope("turn"):
        rows = mr + cb // 2
        dpre, keep, send, sum2, wm = call(
            functools.partial(turn_kernel, count),
            [
                vmem((hid, batch), BF16),
                sds((dp, rows, half)),
                sds((dp, rows, half), BF16),
                vmem((8, LANES)),
                vmem(wm.shape, BF16),
            ],
            pos, got, stat, wb, pre2, dy2, joined, block2, wm,
            smem=(0,), hbm=(8,),
            scratch=[pltpu.VMEM((3, hid, LANES), F32), pltpu.SemaphoreType.DMA((1,))],
            flops=2 * batch * HOPS * hid * hid,
        )

    def back(own_hops, first, num, *more, after=()):
        outs = [(hbm_out if own_hops else sds)((dp, num, cb, LANES), BF16), hbm_out((num, LANES, batch))]
        with jax.named_scope("back"):
            return call(
                functools.partial(back_kernel, own_hops, first, num),
                outs,
                pos, dpre, x, ws, coef, mu, wm, wt, *more,
                smem=(0,),
                hbm=(7,),
                after=after,
                out_specs=(pl.BlockSpec(memory_space=pltpu.VMEM), pl.BlockSpec(memory_space=pltpu.HBM)),
                scratch=[
                    pltpu.VMEM((2, CHUNK, batch), F32),
                    pltpu.VMEM((2, CHUNK, batch), F32),
                    pltpu.VMEM((num, hid, batch), BF16),
                    pltpu.VMEM((num, 2, hid, LANES), F32),
                    pltpu.VMEM((num, LANES, batch), F32),
                    pltpu.VMEM((num, LANES, hid), BF16),
                    pltpu.SemaphoreType.DMA((num + 1,)),
                ],
                mib=16,
            )

    recv = swap(send)
    with jax.named_scope("merge_sum"):
        sent_b, sent_a = back(False, 0, 2)
        recv_b = swap(sent_b)
        if staged:
            shape = (4, rows, half)
            low = call(
                split_low_kernel,
                [vmem(shape)] + [sds(shape, BF16)] * 3,
                pos, keep, recv,
                smem=(0,),
                after=(sent_a,),
            )
            away, recv_b = lax.optimization_barrier((low[1:], recv_b))
            moved = [turn_flip(v, t, dp, 1) for t, v in enumerate(away, 1)]
            kept_b, kept_a = back(True, 0, 2, recv_b, after=(low[1],))
            kept_b, moved = lax.optimization_barrier((kept_b, moved))
            high = call(
                split_high_kernel,
                [sds(shape[1:])] + [sds(shape[1:], BF16)] * 3,
                pos, low[0], *moved,
                smem=(0,),
            )
            wide = [high[0]] + [turn_flip(high[t], t, dp, 0) for t in range(1, 4)]
        else:
            kept_b, kept_a = back(True, 0, 2, recv_b)
            total = lax.psum_scatter(keep + recv.astype(F32), "dp", scatter_dimension=0)
            wide = [total] + [jnp.zeros_like(total)] * 3
    with jax.named_scope("branch_sum"):
        got_b = lax.all_to_all(kept_b, "dp", 0, 0, tiled=True)
    with jax.named_scope("owner"):
        tr = [(lhs[i],) + tuple(s[1:]) for i, s in enumerate((weights, firsts, seconds))]
        last = (wt, kept_a, sent_a, *tr[0], *tr[1], *tr[2])
        shares, pay, *last = call(
            functools.partial(owner_kernel, count, classes),
            [sds((3 * cb + 2 * mr, LANES)), hbm_out((n, 2, LANES))] + [vmem(v.shape, v.dtype) for v in last],
            pos, got_b, sum2, *wide, fix, *last,
            smem=(0,),
            hbm=tuple(range(7, 8 + len(last))),
            scratch=[
                pltpu.VMEM(fix.shape, F32),
                pltpu.SemaphoreType.DMA((1,)),
                pltpu.SemaphoreType.DMA((len(last),)),
            ],
        )
    theirs = swap(shares)
    got = exchange(pay)
    with jax.named_scope("final"):
        shapes = [t.shape for t in tr[0]]
        outs = []
        for dtype in (F32, F32, F32, BF16):
            outs += [sds(s, dtype) for s in shapes]
        outs += [sds((1, 1)), sds((width, batch))]
        res = call(
            final_kernel, outs, pos, got, shares, theirs, x, *last,
            smem=(0,),
            out_specs=tuple(pl.BlockSpec(memory_space=pltpu.VMEM if i == 16 else pltpu.HBM) for i in range(18)),
            scratch=[pltpu.VMEM(v.shape, v.dtype) for i, v in enumerate(outs) if i != 16]
            + [pltpu.SemaphoreType.DMA((18,))],
        )
    result = list(res[:16])
    for i in range(0, 16, 4):
        result[i] = result[i].transpose(0, 2, 1)
    return (*result, res[16].reshape(()), res[17].T)


def solution(mesh):
    tables = (P(BOTH, None), P(BOTH), P(BOTH))
    params = (P(None, None, "dp"), P("dp", None), P("dp", None), P(None, "dp"))
    return jax.shard_map(
        on_device,
        mesh=mesh,
        in_specs=tables + params * 3,
        out_specs=params * 4 + (P(), P(BOTH, None)),
        check_vma=False,
    )
```

```python
import functools
import math

import jax
import jax.numpy as jnp
from jax import lax
from jax.experimental import pallas as pl
from jax.experimental.pallas import tpu as pltpu
from jax.sharding import PartitionSpec as P

HOPS = 4
STEP = 7
EPS_NORM = 1e-05
LANES = 128
PCOL = 64
ONE = 100
FREE = LANES - ONE
ROWS, WIDE, CHUNK, SPAN = 32, 256, 256, 512
BOTH = ("dp", "rep")
F32 = jnp.float32
BF16 = jnp.bfloat16


def dot(left, right, left_dim, right_dim):
    return lax.dot_general(
        left,
        right,
        (((left_dim,), (right_dim,)), ((), ())),
        preferred_element_type=F32,
    )


def call(body, outs, *args, smem=(), hbm=(), after=(), grid=None, in_specs=None, out_specs=None, scratch=(), mib=12, flops=0):
    skip = len(args)
    if in_specs is None:
        spaces = {**{i: pltpu.SMEM for i in smem}, **{i: pltpu.HBM for i in hbm}}
        in_specs = [pl.BlockSpec(memory_space=spaces.get(i, pltpu.VMEM)) for i in range(skip)]
    if out_specs is None:
        out_specs = tuple(pl.BlockSpec(memory_space=pltpu.VMEM) for _ in outs)
    in_specs = list(in_specs) + [pl.BlockSpec(memory_space=pl.ANY) for _ in after]
    args = [pltpu.with_memory_space_constraint(a, pltpu.HBM) if i in hbm else a for i, a in enumerate(args)]
    moved = sum(math.prod(a.shape) * jnp.dtype(a.dtype).itemsize for a in (*args, *outs))

    def kernel(*refs):
        body(*refs[:skip], *refs[skip + len(after) :])

    kwargs = {} if grid is None else {"grid": grid}
    return pl.pallas_call(
        kernel,
        out_shape=tuple(outs),
        in_specs=in_specs,
        out_specs=out_specs,
        scratch_shapes=list(scratch),
        compiler_params=pltpu.CompilerParams(vmem_limit_bytes=mib << 20),
        cost_estimate=pl.CostEstimate(flops=1024, bytes_accessed=1024, transcendentals=0),
        **kwargs,
    )(*args, *[pltpu.with_memory_space_constraint(a, pltpu.HBM) for a in after])


def fetch(sources, buffers, sems):
    copies = [pltpu.make_async_copy(s, b, sems.at[i]) for i, (s, b) in enumerate(zip(sources, buffers))]
    for copy in copies:
        copy.start()

    def wait():
        for copy in copies:
            copy.wait()

    return wait


def sds(shape, dtype=F32):
    return jax.ShapeDtypeStruct(shape, dtype)


def vmem(shape, dtype=F32):
    return pltpu.VMEM(shape, dtype)


def hbm_out(shape, dtype=F32):
    return pltpu.HBM(shape, dtype)


def lane_of(shape):
    return lax.broadcasted_iota(jnp.int32, shape, len(shape) - 1)


def to_cols(rows, first):
    parts = []
    for i in range(4):
        row = rows[first + i : first + i + 1, :]
        parts.append(jnp.transpose(jnp.broadcast_to(row, (LANES, LANES))))
    return jnp.concatenate(parts, axis=0)


def lane_sums(part):
    total = jnp.sum(jnp.transpose(part), axis=0, keepdims=True)
    return jnp.concatenate([total[:, i * LANES : (i + 1) * LANES] for i in range(4)], axis=0)


def fold_lanes(value):
    out = value[:, :LANES]
    for i in range(1, value.shape[1] // LANES):
        out = out + value[:, i * LANES : (i + 1) * LANES]
    return out


def prep_kernel(pos_ref, wb_hbm, wc_hbm, sp_hbm, wm_hbm, own_ref, block_ref, wb_ref, wc_ref, sp_ref, wm_ref, mix_ref, sems):
    wait = fetch((wb_hbm, wc_hbm, sp_hbm, wm_hbm), (wb_ref, wc_ref, sp_ref, wm_ref), sems)
    mr, hid = wm_ref.shape
    own_ref[...] = jnp.zeros_like(own_ref)
    wait()
    wc = wc_ref[...].astype(BF16)
    small = jnp.transpose(sp_ref[...]).astype(BF16)
    own_ref[0:HOPS, :, 0 : wb_ref.shape[2]] = wb_ref[...].astype(BF16)
    own_ref[HOPS, :, 0 : wc.shape[1]] = wc
    own_ref[HOPS, :, PCOL : PCOL + small.shape[1]] = small
    mix_ref[...] = own_ref[0:HOPS]
    mix_ref[0, :, ONE : ONE + small.shape[1]] = small
    mix_ref[1, :, ONE:LANES] = wc[:, :FREE]
    mix_ref[2, :, ONE : ONE + wc.shape[1] - FREE] = wc[:, FREE:]
    first = pos_ref[1] == 0
    part = wc.shape[0] // 2
    for k in range(HOPS):
        block_ref[k * part : (k + 1) * part, :] = jnp.where(first, mix_ref[k, :part], mix_ref[k, part:])
    at = HOPS * part
    for i in range(2):
        left = wm_ref[:, i * LANES : (i + 1) * LANES]
        right = wm_ref[:, hid // 2 + i * LANES : hid // 2 + (i + 1) * LANES]
        block_ref[at + i * mr : at + (i + 1) * mr, :] = jnp.where(first, left, right).astype(BF16)


def stack_kernel(a_ref, b_ref, c_ref, d_ref, out_ref):
    for i, ref in enumerate((a_ref, b_ref, c_ref, d_ref)):
        out_ref[i] = ref[...]


def each_block(pos_ref, arrays):
    for which in range(2):
        half = pos_ref[1] if which == 0 else 1 - pos_ref[1]
        for t in range(4):
            for e in range(4):
                yield arrays[which * 4 + t].at[e], pos_ref[0] ^ (4 * e + t), half


HALF = LANES // 2
QUADS = HALF // 4


def store_grams(grams, out_ref):
    if out_ref.shape[0] == HOPS:
        for k in range(HOPS):
            out_ref[k] = grams[k]
        return
    lane = lane_of((HALF, LANES))
    blocks = [g[:HALF] for g in grams]
    for k in range(0, HOPS, 2):
        blocks.append(jnp.where(lane < HALF, pltpu.roll(grams[k][HALF:], HALF, 1), grams[k + 1][HALF:]))
    for i, block in enumerate(blocks):
        for j in range(QUADS):
            out_ref[i * QUADS + j] = block[4 * j : 4 * j + 4]


def load_grams(in_ref, gram_ref, rest_ref):
    if in_ref.shape[0] == HOPS:
        gram_ref[...] = in_ref[...]
        return
    for i in range(HOPS + HOPS // 2):
        for j in range(QUADS):
            rows = slice(4 * j, 4 * j + 4)
            if i < HOPS:
                gram_ref[i, rows, :] = in_ref[i * QUADS + j]
            else:
                rest_ref[i - HOPS, rows, :] = in_ref[i * QUADS + j]
    lane = lane_of((HALF, LANES))
    for k in range(HOPS):
        upper = jnp.concatenate([gram_ref[k, :HALF, :], jnp.zeros((HALF, LANES), F32)], axis=0)
        rest = rest_ref[k // 2]
        if k % 2 == 0:
            rest = pltpu.roll(rest, HALF, 1)
        gram_ref[k, HALF:, :] = jnp.where(lane < HALF, jnp.transpose(upper)[HALF:], rest)


def gather_kernel(idx_ref, tab_ref, *refs):
    i = pl.program_id(0)
    if len(refs) > 4:
        own_ref, x_ref, gram_ref, own_out, acc, pad, sem = refs
        copy = pltpu.make_async_copy(own_ref, own_out, sem)

        @pl.when(i == 0)
        def _():
            copy.start()

        @pl.when(i == pl.num_programs(0) - 1)
        def _():
            copy.wait()
    else:
        x_ref, gram_ref, acc, pad = refs
    width = tab_ref.shape[1]
    d_in = tab_ref.shape[0] // HOPS
    batch = idx_ref.shape[1]
    rows = lax.broadcasted_iota(jnp.int16, (width, batch), 0)
    hot = jnp.where(rows == (idx_ref[...] - i * width).astype(jnp.int16), BF16(1.0), BF16(0.0))
    part = dot(tab_ref[...].astype(BF16), hot, 1, 0)

    @pl.when(i == 0)
    def _():
        acc[...] = part

    @pl.when(i > 0)
    def _():
        acc[...] += part

    @pl.when(i == pl.num_programs(0) - 1)
    def _():
        row = lax.broadcasted_iota(jnp.int32, pad.shape, 0)
        pad[...] = jnp.where(row == d_in, 1.0, 0.0)
        grams = []
        for k in range(HOPS):
            pad[0:d_in, :] = acc[k * d_in : (k + 1) * d_in, :]
            x = pad[...].astype(BF16)
            x_ref[k] = x
            grams.append(dot(x, x, 1, 1))
        store_grams(grams, gram_ref)


def sum_spread_kernel(in_ref, out_ref):
    out_ref[...] = jnp.broadcast_to(jnp.sum(in_ref[...], axis=0, keepdims=True), out_ref.shape)


def three_terms(wide):
    terms = []
    for _ in range(3):
        terms.append(wide.astype(BF16))
        wide = wide - terms[-1].astype(F32)
    return terms


def exact_dot(low, wide):
    total = None
    for term in three_terms(wide):
        part = dot(low, term, 1, 0)
        total = part if total is None else total + part
    return total


def assemble_kernel(classes, pos_ref, order_ref, *refs):
    wb_ref, wm_out, wm_ref, sems = refs[8:]
    hid = wb_ref.shape[1]
    cb = hid // 16
    mr = wm_ref.shape[1] // 16
    part = cb // 2
    first = HOPS * part
    for ref, s, half in each_block(pos_ref, refs[:8]):
        rows = pl.ds(pl.multiple_of(s * mr, mr), mr)
        for i in range(2):
            wm_ref[half * 2 + i, rows, :] = ref[first + i * mr : first + (i + 1) * mr, :]
    stored = fetch((wm_ref,), (wm_out,), sems)
    for ref, s, half in each_block(pos_ref, refs[:8]):
        rows = pl.ds(pl.multiple_of(s * cb + half * part, part), part)
        for j in range(HOPS):
            wb_ref[j, rows, :] = ref[j * part : (j + 1) * part, :]
    lane = lane_of((hid, LANES))
    mixed = [wb_ref[j].astype(F32) for j in range(3)]
    tail = jnp.where((lane >= PCOL) & (lane < PCOL + 5 * HOPS), pltpu.roll(mixed[0], LANES + PCOL - ONE, 1), 0.0)
    tail = jnp.where(lane < FREE, pltpu.roll(mixed[1], LANES - ONE, 1), tail)
    tail = jnp.where((lane >= FREE) & (lane < classes), pltpu.roll(mixed[2], LANES + FREE - ONE, 1), tail)
    wb_ref[HOPS] = tail.astype(BF16)
    for j in range(3):
        wb_ref[j] = jnp.where(lane < ONE, mixed[j], 0.0).astype(BF16)
    stored()


def own_stats_kernel(count, pos_ref, in_ref, own_hbm, gram_ref, fix_ref, rest_ref, own_ref, sems):
    wait = fetch((own_hbm,), (own_ref,), sems)
    load_grams(in_ref, gram_ref, rest_ref)
    wait()
    rep = pos_ref[1]
    lane = lane_of(fix_ref.shape[1:])
    tail = own_ref[HOPS].astype(F32)
    for i in range(2):
        gram = gram_ref[rep * 2 + i]
        w = own_ref[rep * 2 + i]
        wg = exact_dot(w, gram)
        mean = wg[:, ONE : ONE + 1] / count
        second = jnp.sum(wg * w.astype(F32), axis=1, keepdims=True) / count
        inv = lax.rsqrt(second - mean * mean + EPS_NORM)
        gain = jnp.where(rep == 0, tail[:, PCOL + i : PCOL + i + 1], tail[:, PCOL + 2 + i : PCOL + 3 + i])
        block = wg - mean * gram[ONE : ONE + 1, :]
        for j, value in enumerate((mean, inv, gain * inv)):
            block = jnp.where(lane == ONE + j, value, block)
        fix_ref[i] = block


def stats_kernel(count, gram_ref, wb_ref, ws_ref, coef_ref, mu_ref, wt_ref):
    hid = wb_ref.shape[1]
    small = jnp.transpose(wb_ref[HOPS].astype(F32))
    row = lax.broadcasted_iota(jnp.int32, (16, hid), 0)

    def at(i):
        return small[PCOL + i : PCOL + i + 1, :]

    def columns(values):
        block = jnp.zeros((16, hid), F32)
        for i, value in enumerate(values):
            block = jnp.where(row == i, value, block)
        return jnp.transpose(jnp.concatenate([block, jnp.zeros((LANES - 16, hid), F32)], axis=0))

    mu_ref[...] = jnp.zeros_like(mu_ref)
    for k in range(HOPS):
        gram = gram_ref[k]
        mu_ref[k : k + 1, :] = gram[ONE : ONE + 1, :] / count
        wide = jnp.transpose(wb_ref[k].astype(F32))
        w = wide.astype(BF16)
        wt_ref[k] = w
        wg = None
        for term in three_terms(gram):
            part = dot(term, w, 1, 0)
            wg = part if wg is None else wg + part
        mean = wg[ONE : ONE + 1, :] / count
        second = jnp.sum(wg * wide, axis=0, keepdims=True) / count
        inv = lax.rsqrt(second - mean * mean + EPS_NORM)
        gain, shift, slope, join = at(k), at(HOPS + k), at(2 * HOPS + k), at(3 * HOPS + k)
        v = gain * inv
        half = 0.5 * v
        scaled = jnp.where(
            lax.broadcasted_iota(jnp.int32, wide.shape, 0) == ONE, 0.5 * shift - half * mean, half * wide
        )
        scaled = jnp.transpose(scaled)
        high = scaled.astype(BF16)
        ws_ref[k, :, 0:LANES] = high
        ws_ref[k, :, LANES : 2 * LANES] = (scaled - high.astype(F32)).astype(BF16)
        scale = 0.5 * (1.0 - join)
        coef_ref[k] = columns(
            (
                0.5 * (1.0 + slope),
                0.5 * (1.0 - slope),
                1.0 + join,
                1.0 - join,
                join / scale,
                scale,
                scale * v * slope,
                scale * 0.5 * v * (1.0 - slope),
            )
        )


def project_units(ws_ref, x_ref, k, rows):
    x = x_ref[k]
    return dot(ws_ref[k, rows, :], jnp.concatenate([x, x], axis=0), 1, 0)


def column_set(ref, hop, at, lanes):
    block = ref[hop, at, :]
    return [jnp.broadcast_to(block[:, i : i + 1], (ROWS, WIDE)) for i in lanes]


def merge_block(wm_ref, rows):
    return jnp.concatenate([wm_ref[i, rows, :] for i in range(wm_ref.shape[0])], axis=1)


def forward_kernel(
    x_ref, ws_ref, coef_ref, wt_ref, fix_ref, wm_hbm, joined_ref, pre2_ref, pay_ref, wt_out, fix_out, pre, wm_ref, sems
):
    wait = fetch((wm_hbm,), (wm_ref,), sems.at[pl.ds(2, 1)])
    stored = fetch((wt_ref, fix_ref), (wt_out, fix_out), sems)
    hid = ws_ref.shape[1]
    batch = x_ref.shape[2]
    per = hid // CHUNK
    jobs = [(k, c) for k in range(HOPS) for c in range(per)]

    def project(i):
        k, c = jobs[i]
        pre[i % 2] = project_units(ws_ref, x_ref, k, slice(c * CHUNK, (c + 1) * CHUNK))

    def units(i):
        k, c = jobs[i]
        for g in range(CHUNK // ROWS):
            at = slice(c * CHUNK + g * ROWS, c * CHUNK + (g + 1) * ROWS)
            cs = column_set(coef_ref, k, at, range(4))
            for b in range(batch // WIDE):
                lanes = slice(b * WIDE, (b + 1) * WIDE)
                u = pre[i % 2, g * ROWS : (g + 1) * ROWS, lanes]
                u = u * (cs[0] + cs[1] * jnp.tanh(u))
                joined_ref[k, at, lanes] = (u * (cs[2] + cs[3] * jnp.tanh(u))).astype(BF16)

    project(0)
    for i in range(len(jobs)):
        if i + 1 < len(jobs):
            project(i + 1)
        units(i)
        if i % per == per - 1:
            k = i // per
            if k == 0:
                wait()
            part = dot(merge_block(wm_ref, slice(k * hid, (k + 1) * hid)), joined_ref[k], 0, 0)
            if k == 0:
                pre2_ref[...] = part
            else:
                pre2_ref[...] += part
    value = pre2_ref[...]
    sums = jnp.concatenate([lane_sums(fold_lanes(value)), lane_sums(fold_lanes(value * value))], axis=0)
    pay_ref[...] = jnp.broadcast_to(sums[None], pay_ref.shape)
    stored()


def par_columns(wb_ref):
    return wb_ref[HOPS][:, PCOL:].astype(F32)[:, 4 * HOPS : 5 * HOPS]


def columns2(count, rows, par):
    mean = to_cols(rows, 0) / count
    inv = lax.rsqrt(to_cols(rows, 4) / count - mean * mean + EPS_NORM)
    shape = mean.shape
    gain = jnp.broadcast_to(par[:, 0:1], shape)
    shift = jnp.broadcast_to(par[:, 1:2], shape)
    slope = jnp.broadcast_to(par[:, 2:3], shape)
    return mean, inv, gain, shift, slope


def head_kernel(
    count, classes, got_ref, pre2_ref, wb_ref, lab_hbm, dy2_ref, pay_ref, class_ref, stat_ref, act, dact, cols, sums, lab_ref, sems
):
    wait = fetch((lab_hbm,), (lab_ref,), sems)
    hid, batch = dy2_ref.shape
    par = par_columns(wb_ref)
    mean, inv, gain, shift, slope = columns2(count, jnp.sum(got_ref[...], axis=0), par)
    stat_ref[0] = mean
    stat_ref[1] = inv
    cols[0] = 0.5 * gain * inv
    cols[1] = 0.5 * (shift - gain * inv * mean)
    cols[2] = 1.0 + slope
    cols[3] = 1.0 - slope
    reps = WIDE // LANES

    def tiled(c, at):
        return jnp.concatenate([cols[c, at, :]] * reps, axis=1)

    def first(g, carry):
        at = pl.ds(pl.multiple_of(g * ROWS, ROWS), ROWS)
        c = [tiled(i, at) for i in range(4)]
        for b in range(batch // WIDE):
            lanes = slice(b * WIDE, (b + 1) * WIDE)
            u = pre2_ref[at, lanes] * c[0] + c[1]
            act[at, lanes] = (u * (c[2] + c[3] * jnp.tanh(u))).astype(BF16)
        return carry

    lax.fori_loop(0, hid // ROWS, first, 0, unroll=8)
    tail = wb_ref[HOPS]
    wc = jnp.where(lane_of(tail.shape) < PCOL, tail.astype(F32), 0.0).astype(BF16)
    logits = dot(wc, act[...], 0, 0)
    live = -(-classes // 16) * 16
    row = lax.broadcasted_iota(jnp.int32, (live, batch), 0)
    logits = jnp.where(row < classes, logits[:live] + par[0:live, 3:4], -jnp.inf)
    top = jnp.max(logits, axis=0, keepdims=True)
    e = jnp.exp(logits - top)
    probs = e / jnp.sum(e, axis=0, keepdims=True)
    wait()
    dlog = (probs - jnp.where(row == lab_ref[...], 1.0, 0.0)).astype(BF16)
    dlog = jnp.concatenate([dlog, jnp.zeros((LANES - live, batch), BF16)], axis=0)
    grad_class = dot(act[...], dlog, 1, 1)
    bias = jnp.sum(dlog.astype(F32), axis=1, keepdims=True)
    dact[...] = dot(wc, dlog, 1, 0)

    def second(g, carry):
        at = pl.ds(pl.multiple_of(g * ROWS, ROWS), ROWS)
        c = [tiled(i, at) for i in range(4)]
        m = jnp.concatenate([stat_ref[0, at, :]] * reps, axis=1)
        v = jnp.concatenate([stat_ref[1, at, :]] * reps, axis=1)
        acc = [jnp.zeros((ROWS, WIDE), F32) for _ in range(3)]
        for b in range(batch // WIDE):
            lanes = slice(b * WIDE, (b + 1) * WIDE)
            p = pre2_ref[at, lanes]
            d = dact[at, lanes]
            u = p * c[0] + c[1]
            t = jnp.tanh(u)
            w = u * (1.0 - t)
            dy = d * (0.5 * (c[2] + c[3] * (t + w * (1.0 + t))))
            dy2_ref[at, lanes] = dy
            acc[0] = acc[0] + dy
            acc[1] = acc[1] + dy * ((p - m) * v)
            acc[2] = acc[2] + d * w
        for i in range(3):
            sums[i, at, :] = fold_lanes(acc[i])
        return carry

    lax.fori_loop(0, hid // ROWS, second, 0, unroll=8)
    pay = jnp.concatenate([lane_sums(sums[0]), lane_sums(sums[1])], axis=0)
    pay_ref[...] = jnp.broadcast_to(pay[None], pay_ref.shape)
    lane = lane_of((hid, LANES))
    slope_sum = jnp.sum(sums[2], axis=1, keepdims=True)
    bias = jnp.concatenate([bias, jnp.zeros((hid - LANES, 1), F32)], axis=0)
    block = jnp.where(lane < classes, grad_class, 0.0)
    block = jnp.where(lane == PCOL, slope_sum, block)
    class_ref[...] = jnp.where(lane == PCOL + 1, bias, block)


def turn_kernel(
    count, pos_ref, got_ref, stat_ref, wb_ref, pre2_ref, dy2_ref, joined_ref, class_ref, wm_hbm, dpre_ref, keep_ref, send_ref, sum2_ref, wm_ref, cols, sems
):
    wait = fetch((wm_hbm,), (wm_ref,), sems)
    hid, batch = dy2_ref.shape
    half = send_ref.shape[2]
    rows8 = jnp.sum(got_ref[...], axis=0)
    sum2_ref[...] = rows8
    mean, inv = stat_ref[0], stat_ref[1]
    v = jnp.broadcast_to(par_columns(wb_ref)[:, 0:1], mean.shape) * inv
    cols[0] = v
    cols[1] = v * to_cols(rows8, 0) / count
    cols[2] = v * inv * to_cols(rows8, 4) / count
    reps = WIDE // LANES
    for g in range(hid // ROWS):
        at = slice(g * ROWS, (g + 1) * ROWS)
        c = [jnp.concatenate([cols[i, at, :]] * reps, axis=1) for i in range(3)]
        m = jnp.concatenate([stat_ref[0, at, :]] * reps, axis=1)
        for b in range(batch // WIDE):
            lanes = slice(b * WIDE, (b + 1) * WIDE)
            value = c[0] * dy2_ref[at, lanes] - c[1] - (pre2_ref[at, lanes] - m) * c[2]
            dpre_ref[at, lanes] = value.astype(BF16)
    mine = pl.ds(pl.multiple_of(pos_ref[1] * half, half), half)
    theirs = pl.ds(pl.multiple_of((1 - pos_ref[1]) * half, half), half)
    dp, size, _ = send_ref.shape
    per = dp // HOPS
    mr = hid // per
    cb = hid // dp
    for k in range(HOPS):
        other = dot(joined_ref[k], dpre_ref[theirs, :], 1, 1).astype(BF16)
        own = dot(joined_ref[k], dpre_ref[mine, :], 1, 1)
        for j in range(per):
            send_ref[k * per + j, 0:mr, :] = other[j * mr : (j + 1) * mr]
            keep_ref[k * per + j, 0:mr, :] = own[j * mr : (j + 1) * mr]
    first = pos_ref[1] == 0
    for s in range(dp):
        block = class_ref[s * cb : (s + 1) * cb, :]
        wide = jnp.concatenate([block[: cb // 2], block[cb // 2 :]], axis=1)
        send_ref[s, mr:size, :] = jnp.where(first, 0.0, wide).astype(BF16)
        keep_ref[s, mr:size, :] = jnp.where(first, wide, 0.0)
    wait()


SMALLS = 4


def back_kernel(own, first, count, pos_ref, dpre_ref, x_ref, ws_ref, coef_ref, mu_ref, wm_ref, wt_hbm, *refs):
    if own:
        recv_ref, refs = refs[0], refs[1:]
    b_ref, a_out, pre, dj, dyv, sums, a_ref, wt_ref, out_sems = refs
    hid = wt_ref.shape[2]
    batch = x_ref.shape[2]
    per = hid // SPAN
    jobs = [(k, c) for k in range(count) for c in range(per)]
    base = 2 * (pos_ref[1] if own else 1 - pos_ref[1]) + first
    dp, _, cb, _ = b_ref.shape
    copies = []
    wait_wt = fetch((wt_hbm.at[pl.ds(base, count)],), (wt_ref,), out_sems.at[pl.ds(count, 1)])

    def project(i):
        k, c = jobs[i]
        rows = slice(c * SPAN, (c + 1) * SPAN)
        pre[i % 2] = project_units(ws_ref, x_ref, base + k, rows)
        at = pl.ds(pl.multiple_of((base + k) * hid + c * SPAN, SPAN), SPAN)
        dj[i % 2] = dot(merge_block(wm_ref, at), dpre_ref[...], 1, 0)

    def units(i):
        k, c = jobs[i]
        for g in range(SPAN // ROWS):
            at = slice(c * SPAN + g * ROWS, c * SPAN + (g + 1) * ROWS)
            here = slice(g * ROWS, (g + 1) * ROWS)
            p1, q1, s2, s1, r1 = column_set(coef_ref, base + k, at, (0, 1, 4, 6, 7))
            one = jnp.zeros((ROWS, WIDE), F32)
            two = jnp.zeros((ROWS, WIDE), F32)
            for b in range(batch // WIDE):
                lanes = slice(b * WIDE, (b + 1) * WIDE)
                u = pre[i % 2, here, lanes]
                t = jnp.tanh(u)
                u2 = u * (p1 + q1 * t)
                t2 = jnp.tanh(u2)
                d = dj[i % 2, here, lanes]
                w = u2 * (1.0 - t2)
                two = two + d * w
                d = d * (s2 + (1.0 + t2) * (1.0 + w))
                w = u * (1.0 - t)
                one = one + d * w
                dyv[k, at, lanes] = (d * (s1 + r1 * ((1.0 + t) * (1.0 + w)))).astype(BF16)
            sums[k, 0, at, :] = fold_lanes(one)
            sums[k, 1, at, :] = fold_lanes(two)

    def close(k):
        if k == 0:
            wait_wt()
        w = wt_ref[k]
        a_ref[k] = dot(w, dyv[k], 1, 0)
        copies.append(fetch((a_ref.at[k],), (a_out.at[k],), out_sems.at[pl.ds(k, 1)]))
        block = dot(x_ref[base + k], dyv[k], 1, 1)
        row = lax.broadcasted_iota(jnp.int32, block.shape, 0)
        total = block[ONE : ONE + 1, :]
        center = jnp.transpose(jnp.broadcast_to(mu_ref[pl.ds(base + k, 1), :], (LANES, LANES)))
        block = jnp.where(row < ONE, block - jnp.concatenate([center] * (hid // LANES), axis=1) * total, 0.0)
        smalls = (
            total,
            jnp.sum(block * w.astype(F32), axis=0, keepdims=True),
            jnp.sum(jnp.transpose(sums[k, 0] * coef_ref[base + k, :, 5:6]), axis=0, keepdims=True),
            jnp.sum(jnp.transpose(sums[k, 1]), axis=0, keepdims=True),
        )
        for i, value in enumerate(smalls):
            block = jnp.where(row == ONE + i, value, block)
            if not own:
                block = jnp.where(row == ONE + SMALLS + i, value - value.astype(BF16).astype(F32), block)
        block = jnp.transpose(block)
        if own:
            received = jnp.concatenate([recv_ref[s, k] for s in range(dp)], axis=0).astype(F32)
            block = split_smalls(block + join_smalls(received))
        for s in range(dp):
            b_ref[s, k] = block[s * cb : (s + 1) * cb, :].astype(BF16)

    project(0)
    for i in range(len(jobs)):
        if i + 1 < len(jobs):
            project(i + 1)
        units(i)
        if i % per == per - 1:
            close(i // per)
    for done in copies:
        done()


def split_smalls(block):
    lane = lane_of(block.shape)
    rest = block - block.astype(BF16).astype(F32)
    moved = pltpu.roll(rest, SMALLS, 1)
    return jnp.where((lane >= ONE + SMALLS) & (lane < ONE + 2 * SMALLS), moved, block)


def join_smalls(block):
    lane = lane_of(block.shape)
    moved = pltpu.roll(block, LANES - SMALLS, 1)
    block = jnp.where((lane >= ONE) & (lane < ONE + SMALLS), block + moved, block)
    return jnp.where(lane < ONE + SMALLS, block, 0.0)


def split_low_kernel(pos_ref, keep_ref, got_ref, o0_ref, o1_ref, o2_ref, o3_ref):
    low, high = pos_ref[0] % 4, pos_ref[0] // 4
    for t, ref in enumerate((o0_ref, o1_ref, o2_ref, o3_ref)):
        for e in range(4):
            j = jnp.where(pos_ref[1] == 0, e * 4 + (low ^ t), (high ^ t) * 4 + e)
            ref[e] = (keep_ref[j] + got_ref[j].astype(F32)).astype(ref.dtype)


def split_high_kernel(pos_ref, own_ref, g1_ref, g2_ref, g3_ref, o0_ref, o1_ref, o2_ref, o3_ref):
    mine = jnp.where(pos_ref[1] == 0, pos_ref[0] // 4, pos_ref[0] % 4)
    for t, ref in enumerate((o0_ref, o1_ref, o2_ref, o3_ref)):
        j = mine ^ t
        value = own_ref[j] + g1_ref[j].astype(F32) + g2_ref[j].astype(F32) + g3_ref[j].astype(F32)
        ref[...] = value.astype(ref.dtype)


def owner_kernel(
    count, classes, pos_ref, got_ref, sum2_ref, w0_ref, w1_ref, w2_ref, w3_ref, *refs
):
    late = (len(refs) - 6) // 2
    grad_ref, pay_ref = refs[1 + late : 3 + late]
    fix_ref, sems, late_sems = refs[3 + 2 * late :]
    wait = fetch(refs[:1], (fix_ref,), sems)
    brought = fetch(refs[1 : 1 + late], refs[3 + late : 3 + 2 * late], late_sems)
    _, _, cb, _ = got_ref.shape
    total = jnp.sum(got_ref[...].astype(F32), axis=0)
    rep = pos_ref[1]
    lane = lane_of((cb, LANES))
    squares = jnp.zeros((1, 1), F32)
    spread = jnp.zeros((cb, LANES), F32)

    def all_sum(v):
        return jnp.sum(jnp.sum(v, axis=1, keepdims=True), axis=0, keepdims=True)

    others = w1_ref[...].astype(F32) + w2_ref[...].astype(F32) + w3_ref[...].astype(F32)
    wide = w0_ref[...].astype(F32) + others
    mr = wide.shape[0] - cb // 2
    merge = wide[:mr]
    squares = squares + all_sum(merge * merge)
    at = 2 * cb
    for i in range(2):
        grad_ref[at + i * mr : at + (i + 1) * mr, :] = merge[:, i * LANES : (i + 1) * LANES]
    at = at + 2 * mr
    block = jnp.concatenate([wide[mr:, :LANES], wide[mr:, LANES:]], axis=0)
    shift_own = own_column(sum2_ref, 0, pos_ref[0], cb)
    gain_own = own_column(sum2_ref, 4, pos_ref[0], cb)
    block = jnp.where(lane == PCOL + 2, gain_own, block)
    block = jnp.where(lane == PCOL + 3, shift_own, block)
    grad_ref[at : at + cb, :] = block
    squares = squares + jnp.where(rep == 0, all_sum(block * block), 0.0)
    wait()
    for i in range(2):
        b = join_smalls(total[i])
        wg = fix_ref[i]
        mean, inv, v = [wg[:, ONE + j : ONE + j + 1] for j in range(3)]
        s = b[:, ONE : ONE + 1]
        g = inv * b[:, ONE + 1 : ONE + 2]
        beta = inv * g / count
        alpha = s / count - beta * mean
        fixed = jnp.where(lane < ONE, b - beta * wg, 0.0)
        fixed = jnp.where(lane == ONE, g / v, fixed)
        fixed = jnp.where(lane == ONE + 1, s / v, fixed)
        fixed = jnp.where(lane == ONE + 2, b[:, ONE + 2 : ONE + 3], fixed)
        fixed = jnp.where(lane == ONE + 3, b[:, ONE + 3 : ONE + 4], fixed)
        grad_ref[i * cb : (i + 1) * cb, :] = fixed
        squares = squares + all_sum(fixed * fixed)
        spread = jnp.where(lane == 2 * i, alpha, spread)
        spread = jnp.where(lane == 2 * i + 1, beta, spread)
    rows = jnp.transpose(jnp.concatenate([spread, jnp.zeros((LANES - cb, LANES), F32)], axis=0))[0:8]
    packed = jnp.concatenate([rows[i : i + 1, :cb] for i in range(4)], axis=1)
    if 4 * cb < LANES:
        packed = jnp.concatenate([packed, jnp.zeros((1, LANES - 4 * cb), F32)], axis=1)
    pay = jnp.concatenate([packed, jnp.where(lane_of((1, LANES)) == 0, squares, 0.0)], axis=0)
    pay_ref[...] = jnp.broadcast_to(pay[None], pay_ref.shape)
    brought()


def own_column(ref, first, me, cb):
    block = (me * cb) // LANES
    row = ref[pl.ds(first + block, 1), :]
    lane = lane_of((cb, LANES))
    sub = lax.broadcasted_iota(jnp.int32, (cb, LANES), 0)
    hit = lane == sub + (me * cb) % LANES
    return jnp.sum(jnp.where(hit, jnp.broadcast_to(row, (cb, LANES)), 0.0), axis=1, keepdims=True)


def adam_into(weight_ref, moment_ref, square_ref, grad, scale, rate, outs, at=Ellipsis):
    new_ref, new_m_ref, new_s_ref, copy_ref = outs
    weight = weight_ref[at]
    clipped = grad * scale
    moment = 0.9 * moment_ref[at] + 0.1 * clipped
    square = 0.999 * square_ref[at] + 0.001 * clipped * clipped
    fix_one = 1.0 - 0.9**STEP
    fix_two = 1.0 - 0.999**STEP
    update = moment / fix_one / (jnp.sqrt(square / fix_two) + 1e-08) + 0.01 * weight
    new = weight - rate * update
    new_ref[at] = new
    new_m_ref[at] = moment
    new_s_ref[at] = square
    copy_ref[at] = new.astype(BF16)


def final_kernel(pos_ref, got_ref, mine_ref, other_ref, x_ref, wt_ref, own_ref, sent_ref, *refs):
    states, outs_hbm, norm_ref, rows_hbm = refs[:12], refs[12:28], refs[28], refs[29]
    outs, rows_ref, out_sems = refs[30:46], refs[46], refs[47]
    weights, firsts, seconds = states[0:4], states[4:8], states[8:12]
    n = got_ref.shape[0]
    cb = weights[0].shape[1]
    blocks = 4
    per = n // 2 // blocks
    lane = lane_of((blocks, LANES))
    parts = [[jnp.zeros((blocks, LANES), F32) for _ in range(4)] for _ in range(2)]
    for r in range(2):
        for j in range(per):
            rows = [got_ref[(b * per + j) * 2 + r, 0:1, :] for b in range(blocks)]
            rows = jnp.concatenate(rows, axis=0)
            here = (lane >= j * cb) & (lane < (j + 1) * cb)
            for i in range(4):
                shift = (j - i) * cb % LANES
                moved = pltpu.roll(rows, shift, 1) if shift else rows
                parts[r][i] = jnp.where(here, moved, parts[r][i])

    def spread_row(r, i):
        return jnp.concatenate([parts[r][i][b : b + 1] for b in range(blocks)], axis=1)

    squares = jnp.sum(got_ref[...], axis=0)[1:2, :]
    norm = jnp.sqrt(jnp.sum(squares, axis=1, keepdims=True))
    norm_ref[...] = norm
    scale = 1.0 / jnp.maximum(norm, 1.0)

    d_in = weights[0].shape[2]
    mr = weights[1].shape[0]
    classes = weights[2].shape[1]
    first = pos_ref[1] == 0
    mine, other = mine_ref[...], other_ref[...]
    low = jnp.where(first, mine, other)
    high = jnp.where(first, other, mine)
    stores = []
    fixes = []
    for k in range(HOPS):
        r, i = k // 2, k % 2
        alpha, beta = spread_row(r, 2 * i), spread_row(r, 2 * i + 1)
        low_w = wt_ref[k]
        right = jnp.where(lax.broadcasted_iota(jnp.int32, low_w.shape, 0) == ONE, alpha, low_w.astype(F32) * beta)
        high_part = right.astype(BF16)
        fix = dot(low_w, high_part, 1, 1) + dot(low_w, (right - high_part.astype(F32)).astype(BF16), 1, 1)
        high_part = fix.astype(BF16)
        fixes.append(jnp.concatenate([high_part, (fix - high_part.astype(F32)).astype(BF16)], axis=1))
    for k in range(HOPS):
        r, i = k // 2, k % 2
        value = jnp.where(pos_ref[1] == r, own_ref[i], sent_ref[i])
        value = value - dot(fixes[k], jnp.concatenate([x_ref[k], x_ref[k]], axis=0), 1, 0)
        rows_ref[k * d_in : (k + 1) * d_in, :] = value[:d_in]
        if i == 1:
            part = pl.ds(r * 2 * d_in, 2 * d_in)
            stores.append(fetch((rows_ref.at[part, :],), (rows_hbm.at[part, :],), out_sems.at[pl.ds(16 + r, 1)]))

    def group(i):
        return [o for o in outs[i::4]]

    hops = [low[0:cb], low[cb : 2 * cb], high[0:cb], high[cb : 2 * cb]]
    for k in range(HOPS):
        adam_into(weights[0], firsts[0], seconds[0], hops[k][:, :d_in], scale, 0.05, group(0), k)
    at = 2 * cb
    for half, part in enumerate((low, high)):
        for i in range(2):
            lanes = (slice(None), slice((2 * half + i) * LANES, (2 * half + i + 1) * LANES))
            grad = part[at + i * mr : at + (i + 1) * mr]
            adam_into(weights[1], firsts[1], seconds[1], grad, scale, 0.05, group(1), lanes)
    at = at + 2 * mr
    block = low[at : at + cb]
    adam_into(weights[2], firsts[2], seconds[2], block[:, :classes], scale, 0.05, group(2))
    lane = lane_of((cb, LANES))
    small = jnp.zeros((cb, LANES), F32)
    for kind in range(4):
        for k in range(HOPS):
            small = jnp.where(lane == kind * HOPS + k, hops[k][:, ONE + kind : ONE + kind + 1], small)
    for i, source in enumerate((2, 3, 0, 1)):
        small = jnp.where(lane == 4 * HOPS + i, block[:, PCOL + source : PCOL + source + 1], small)
    small = jnp.transpose(jnp.concatenate([small, jnp.zeros((LANES - cb, LANES), F32)], axis=0))
    adam_into(weights[3], firsts[3], seconds[3], small[: weights[3].shape[0], :cb], scale, 0.3, group(3))
    stores.append(fetch(outs, outs_hbm, out_sems))
    for done in stores:
        done()


def flip(value, mask, dp):
    return lax.ppermute(value, "dp", [(i, i ^ mask) for i in range(dp)])


def turn_flip(value, digit, dp, stage):
    pairs = []
    for i in range(dp):
        for core in range(2):
            mask = digit if (core + stage) % 2 else 4 * digit
            pairs.append((i * 2 + core, (i ^ mask) * 2 + core))
    return lax.ppermute(value, BOTH, pairs)


def swap(value):
    return lax.ppermute(value, "rep", [(0, 1), (1, 0)])


def exchange(value):
    return lax.all_to_all(value, BOTH, 0, 0, tiled=True)


def weights_plain(wbt, wc, sp, wm, dp):
    cb, classes = wc.shape
    mr, hid = wm.shape
    own = jnp.zeros((HOPS + 1, cb, LANES), BF16)
    own = own.at[:HOPS, :, : wbt.shape[2]].set(wbt.astype(BF16))
    own = own.at[HOPS, :, :classes].set(wc.astype(BF16))
    own = own.at[HOPS, :, PCOL : PCOL + sp.shape[0]].set(sp.T.astype(BF16))
    wb = lax.all_gather(own, "dp", axis=1, tiled=True)
    whole = lax.all_gather(wm.astype(BF16), "dp", axis=0, tiled=True)
    return own, wb, whole.reshape(HOPS * hid, hid // LANES, LANES).transpose(1, 0, 2)


def on_device(table, batch_index, labels, *state):
    weights, firsts, seconds = state[0:4], state[4:8], state[8:12]
    dp, rep = lax.axis_size("dp"), lax.axis_size("rep")
    n = dp * rep
    staged = dp == 16 and rep == 2
    me, core = lax.axis_index("dp"), lax.axis_index("rep")
    pos = jnp.stack([me, core]).astype(jnp.int32)
    batch = batch_index.shape[0]
    count = float(batch * n)
    nodes, width = table.shape
    cb = weights[0].shape[2]
    mr, hid = weights[1].shape
    classes = weights[2].shape[1]
    half = hid // 2
    lhs = [v.transpose(0, 2, 1) for v in (weights[0], firsts[0], seconds[0])]
    idx = batch_index.reshape(1, batch)
    lab = labels.reshape(1, batch)

    if staged:
        with jax.named_scope("prep"):
            sources = (lhs[0], weights[2], weights[3], weights[1])
            size = HOPS * cb // 2 + 2 * mr
            own, block = call(
                prep_kernel,
                [vmem((HOPS + 1, cb, LANES), BF16), sds((size, LANES), BF16)],
                pos, *sources,
                smem=(0,), hbm=(1, 2, 3, 4),
                scratch=[pltpu.VMEM(v.shape, F32) for v in sources]
                + [pltpu.VMEM((HOPS, cb, LANES), BF16), pltpu.SemaphoreType.DMA((4,))],
            )
        far = [flip(block, 4 * k, dp) for k in range(1, 4)]

    with jax.named_scope("gather"):
        step = 2048
        sums = (6 * QUADS, 4, LANES) if 6 * QUADS % n == 0 else (HOPS, LANES, LANES)
        passed = [own] if staged else []
        x, gram, *made = call(
            gather_kernel,
            [vmem((HOPS, LANES, batch), BF16), hbm_out(sums)] + [hbm_out(v.shape, v.dtype) for v in passed],
            pltpu.with_memory_space_constraint(idx, pltpu.HBM),
            pltpu.with_memory_space_constraint(table.T, pltpu.HBM),
            *passed,
            grid=(nodes // step,),
            in_specs=[
                pl.BlockSpec((1, batch), lambda i: (0, 0)),
                pl.BlockSpec((width, step), lambda i: (0, i)),
            ]
            + [pl.BlockSpec(memory_space=pltpu.VMEM) for _ in passed],
            out_specs=(
                pl.BlockSpec((HOPS, LANES, batch), lambda i: (0, 0, 0)),
                pl.BlockSpec(sums, lambda i: (0, 0, 0)),
            )
            + tuple(pl.BlockSpec(memory_space=pltpu.HBM) for _ in passed),
            scratch=[pltpu.VMEM((width, batch), F32), pltpu.VMEM((LANES, batch), F32)]
            + [pltpu.SemaphoreType.DMA for _ in passed],
            mib=24,
        )
        if staged:
            own = made[0]
    with jax.named_scope("gram_sum"):
        parts = gram.reshape(n, -1, *sums[1:]) if sums[1] == 4 else gram.reshape(n, -1, LANES)
        if staged:
            (stacked,) = call(stack_kernel, [sds((4,) + block.shape, BF16)], block, *far)
            parts, stacked = lax.optimization_barrier((parts, stacked))
        parts = exchange(parts)
        (parts,) = call(sum_spread_kernel, [hbm_out(parts.shape)], parts)
        gram = exchange(parts).reshape(sums)
    if not staged:
        own, wb, wm = weights_plain(lhs[0], weights[2], weights[3], weights[1], dp)
    with jax.named_scope("own_stats"):
        gram, fix = call(
            functools.partial(own_stats_kernel, count),
            [vmem((HOPS, LANES, LANES)), vmem((2, cb, LANES))],
            pos, gram, own,
            smem=(0,), hbm=(2,),
            scratch=[
                pltpu.VMEM((HOPS // 2, HALF, LANES), F32),
                pltpu.VMEM(own.shape, BF16),
                pltpu.SemaphoreType.DMA((1,)),
            ],
        )
    if staged:
        mine = [stacked] + [flip(stacked, t, dp) for t in range(1, 4)]
        mine = mine[:1] + [lax.optimization_barrier((v, parts))[0] for v in mine[1:]]
        with jax.named_scope("weights"):
            whole = (hid // LANES, HOPS * hid, LANES)
            wb, wm = call(
                functools.partial(assemble_kernel, classes),
                [vmem((HOPS + 1, hid, LANES), BF16), hbm_out(whole, BF16)],
                pos, fix, *mine, *[swap(v) for v in mine],
                smem=(0,),
                out_specs=(pl.BlockSpec(memory_space=pltpu.VMEM), pl.BlockSpec(memory_space=pltpu.HBM)),
                scratch=[pltpu.VMEM(whole, BF16), pltpu.SemaphoreType.DMA((1,))],
            )
    with jax.named_scope("stats"):
        ws, coef, mu, wt = call(
            functools.partial(stats_kernel, count),
            [
                vmem((HOPS, hid, 2 * LANES), BF16),
                vmem((HOPS, hid, LANES)),
                vmem((8, LANES)),
                vmem((HOPS, LANES, hid), BF16),
            ],
            gram, wb,
        )
    with jax.named_scope("forward"):
        joined, pre2, pay, wt, fix = call(
            forward_kernel,
            [vmem((HOPS, hid, batch), BF16), vmem((hid, batch)), sds((n, 8, LANES))]
            + [hbm_out(v.shape, v.dtype) for v in (wt, fix)],
            x, ws, coef, wt, fix, wm,
            hbm=(5,),
            out_specs=tuple(pl.BlockSpec(memory_space=m) for m in (pltpu.VMEM,) * 3 + (pltpu.HBM,) * 2),
            scratch=[
                pltpu.VMEM((2, CHUNK, batch), F32),
                pltpu.VMEM(wm.shape, BF16),
                pltpu.SemaphoreType.DMA((3,)),
            ],
        )
    got = exchange(pay)
    with jax.named_scope("head"):
        dy2, pay, block2, stat = call(
            functools.partial(head_kernel, count, classes),
            [vmem((hid, batch)), sds((n, 8, LANES)), vmem((hid, LANES)), vmem((2, hid, LANES))],
            got, pre2, wb, lab,
            hbm=(3,),
            scratch=[
                pltpu.VMEM((hid, batch), BF16),
                pltpu.VMEM((hid, batch), F32),
                pltpu.VMEM((4, hid, LANES), F32),
                pltpu.VMEM((3, hid, LANES), F32),
                pltpu.VMEM(lab.shape, lab.dtype),
                pltpu.SemaphoreType.DMA((1,)),
            ],
            flops=6 * batch * hid * LANES,
        )
    got = exchange(pay)
    with jax.named_scope("turn"):
        rows = mr + cb // 2
        dpre, keep, send, sum2, wm = call(
            functools.partial(turn_kernel, count),
            [
                vmem((hid, batch), BF16),
                sds((dp, rows, half)),
                sds((dp, rows, half), BF16),
                vmem((8, LANES)),
                vmem(wm.shape, BF16),
            ],
            pos, got, stat, wb, pre2, dy2, joined, block2, wm,
            smem=(0,), hbm=(8,),
            scratch=[pltpu.VMEM((3, hid, LANES), F32), pltpu.SemaphoreType.DMA((1,))],
            flops=2 * batch * HOPS * hid * hid,
        )

    def back(own_hops, first, num, *more, after=()):
        outs = [(hbm_out if own_hops else sds)((dp, num, cb, LANES), BF16), hbm_out((num, LANES, batch))]
        with jax.named_scope("back"):
            return call(
                functools.partial(back_kernel, own_hops, first, num),
                outs,
                pos, dpre, x, ws, coef, mu, wm, wt, *more,
                smem=(0,),
                hbm=(7,),
                after=after,
                out_specs=(pl.BlockSpec(memory_space=pltpu.VMEM), pl.BlockSpec(memory_space=pltpu.HBM)),
                scratch=[
                    pltpu.VMEM((2, SPAN, batch), F32),
                    pltpu.VMEM((2, SPAN, batch), F32),
                    pltpu.VMEM((num, hid, batch), BF16),
                    pltpu.VMEM((num, 2, hid, LANES), F32),
                    pltpu.VMEM((num, LANES, batch), F32),
                    pltpu.VMEM((num, LANES, hid), BF16),
                    pltpu.SemaphoreType.DMA((num + 1,)),
                ],
                mib=24,
            )

    recv = swap(send)
    with jax.named_scope("merge_sum"):
        sent_b, sent_a = back(False, 0, 2)
        recv_b = swap(sent_b)
        if staged:
            shape = (4, rows, half)
            low = call(
                split_low_kernel,
                [vmem(shape)] + [sds(shape, BF16)] * 3,
                pos, keep, recv,
                smem=(0,),
                after=(sent_a,),
            )
            away, recv_b = lax.optimization_barrier((low[1:], recv_b))
            moved = [turn_flip(v, t, dp, 1) for t, v in enumerate(away, 1)]
            kept_b, kept_a = back(True, 0, 2, recv_b)
            kept_b, moved = lax.optimization_barrier((kept_b, moved))
            high = call(
                split_high_kernel,
                [sds(shape[1:])] + [sds(shape[1:], BF16)] * 3,
                pos, low[0], *moved,
                smem=(0,),
            )
            wide = [high[0]] + [turn_flip(high[t], t, dp, 0) for t in range(1, 4)]
        else:
            kept_b, kept_a = back(True, 0, 2, recv_b)
            total = lax.psum_scatter(keep + recv.astype(F32), "dp", scatter_dimension=0)
            wide = [total] + [jnp.zeros_like(total)] * 3
    with jax.named_scope("branch_sum"):
        got_b = lax.all_to_all(kept_b, "dp", 0, 0, tiled=True)
    with jax.named_scope("owner"):
        tr = [(lhs[i],) + tuple(s[1:]) for i, s in enumerate((weights, firsts, seconds))]
        last = (wt, kept_a, sent_a, *tr[0], *tr[1], *tr[2])
        shares, pay, *last = call(
            functools.partial(owner_kernel, count, classes),
            [sds((3 * cb + 2 * mr, LANES)), hbm_out((n, 2, LANES))] + [vmem(v.shape, v.dtype) for v in last],
            pos, got_b, sum2, *wide, fix, *last,
            smem=(0,),
            hbm=tuple(range(7, 8 + len(last))),
            scratch=[
                pltpu.VMEM(fix.shape, F32),
                pltpu.SemaphoreType.DMA((1,)),
                pltpu.SemaphoreType.DMA((len(last),)),
            ],
        )
    theirs = swap(shares)
    got = exchange(pay)
    with jax.named_scope("final"):
        shapes = [t.shape for t in tr[0]]
        outs = []
        for dtype in (F32, F32, F32, BF16):
            outs += [sds(s, dtype) for s in shapes]
        outs += [sds((1, 1)), sds((width, batch))]
        res = call(
            final_kernel, outs, pos, got, shares, theirs, x, *last,
            smem=(0,),
            out_specs=tuple(pl.BlockSpec(memory_space=pltpu.VMEM if i == 16 else pltpu.HBM) for i in range(18)),
            scratch=[pltpu.VMEM(v.shape, v.dtype) for i, v in enumerate(outs) if i != 16]
            + [pltpu.SemaphoreType.DMA((18,))],
        )
    result = list(res[:16])
    for i in range(0, 16, 4):
        result[i] = result[i].transpose(0, 2, 1)
    return (*result, res[16].reshape(()), res[17].T)


def solution(mesh):
    tables = (P(BOTH, None), P(BOTH), P(BOTH))
    params = (P(None, None, "dp"), P("dp", None), P("dp", None), P(None, "dp"))
    return jax.shard_map(
        on_device,
        mesh=mesh,
        in_specs=tables + params * 3,
        out_specs=params * 4 + (P(), P(BOTH, None)),
        check_vma=False,
    )
```

```python
import functools
import math

import jax
import jax.numpy as jnp
from jax import lax
from jax.experimental import pallas as pl
from jax.experimental.pallas import tpu as pltpu
from jax.sharding import PartitionSpec as P

HOPS = 4
STEP = 7
EPS_NORM = 1e-05
LANES = 128
PCOL = 64
ONE = 100
FREE = LANES - ONE
ROWS, WIDE, CHUNK = 32, 256, 256
BOTH = ("dp", "rep")
F32 = jnp.float32
BF16 = jnp.bfloat16


def dot(left, right, left_dim, right_dim):
    return lax.dot_general(
        left,
        right,
        (((left_dim,), (right_dim,)), ((), ())),
        preferred_element_type=F32,
    )


def call(body, outs, *args, smem=(), hbm=(), after=(), grid=None, in_specs=None, out_specs=None, scratch=(), mib=12, flops=0):
    skip = len(args)
    if in_specs is None:
        spaces = {**{i: pltpu.SMEM for i in smem}, **{i: pltpu.HBM for i in hbm}}
        in_specs = [pl.BlockSpec(memory_space=spaces.get(i, pltpu.VMEM)) for i in range(skip)]
    if out_specs is None:
        out_specs = tuple(pl.BlockSpec(memory_space=pltpu.VMEM) for _ in outs)
    in_specs = list(in_specs) + [pl.BlockSpec(memory_space=pl.ANY) for _ in after]
    args = [pltpu.with_memory_space_constraint(a, pltpu.HBM) if i in hbm else a for i, a in enumerate(args)]
    moved = sum(math.prod(a.shape) * jnp.dtype(a.dtype).itemsize for a in (*args, *outs))

    def kernel(*refs):
        body(*refs[:skip], *refs[skip + len(after) :])

    kwargs = {} if grid is None else {"grid": grid}
    return pl.pallas_call(
        kernel,
        out_shape=tuple(outs),
        in_specs=in_specs,
        out_specs=out_specs,
        scratch_shapes=list(scratch),
        compiler_params=pltpu.CompilerParams(vmem_limit_bytes=mib << 20),
        cost_estimate=pl.CostEstimate(flops=1024, bytes_accessed=1024, transcendentals=0),
        **kwargs,
    )(*args, *[pltpu.with_memory_space_constraint(a, pltpu.HBM) for a in after])


def fetch(sources, buffers, sems):
    copies = [pltpu.make_async_copy(s, b, sems.at[i]) for i, (s, b) in enumerate(zip(sources, buffers))]
    for copy in copies:
        copy.start()

    def wait():
        for copy in copies:
            copy.wait()

    return wait


def sds(shape, dtype=F32):
    return jax.ShapeDtypeStruct(shape, dtype)


def vmem(shape, dtype=F32):
    return pltpu.VMEM(shape, dtype)


def hbm_out(shape, dtype=F32):
    return pltpu.HBM(shape, dtype)


def lane_of(shape):
    return lax.broadcasted_iota(jnp.int32, shape, len(shape) - 1)


def to_cols(rows, first):
    parts = []
    for i in range(4):
        row = rows[first + i : first + i + 1, :]
        parts.append(jnp.transpose(jnp.broadcast_to(row, (LANES, LANES))))
    return jnp.concatenate(parts, axis=0)


def lane_sums(part):
    total = jnp.sum(jnp.transpose(part), axis=0, keepdims=True)
    return jnp.concatenate([total[:, i * LANES : (i + 1) * LANES] for i in range(4)], axis=0)


def fold_lanes(value):
    out = value[:, :LANES]
    for i in range(1, value.shape[1] // LANES):
        out = out + value[:, i * LANES : (i + 1) * LANES]
    return out


def prep_kernel(pos_ref, wb_hbm, wc_hbm, sp_hbm, wm_hbm, own_ref, block_ref, wb_ref, wc_ref, sp_ref, wm_ref, mix_ref, sems):
    wait = fetch((wb_hbm, wc_hbm, sp_hbm, wm_hbm), (wb_ref, wc_ref, sp_ref, wm_ref), sems)
    mr, hid = wm_ref.shape
    own_ref[...] = jnp.zeros_like(own_ref)
    wait()
    wc = wc_ref[...].astype(BF16)
    small = jnp.transpose(sp_ref[...]).astype(BF16)
    own_ref[0:HOPS, :, 0 : wb_ref.shape[2]] = wb_ref[...].astype(BF16)
    own_ref[HOPS, :, 0 : wc.shape[1]] = wc
    own_ref[HOPS, :, PCOL : PCOL + small.shape[1]] = small
    mix_ref[...] = own_ref[0:HOPS]
    mix_ref[0, :, ONE : ONE + small.shape[1]] = small
    mix_ref[1, :, ONE:LANES] = wc[:, :FREE]
    mix_ref[2, :, ONE : ONE + wc.shape[1] - FREE] = wc[:, FREE:]
    first = pos_ref[1] == 0
    part = wc.shape[0] // 2
    for k in range(HOPS):
        block_ref[k * part : (k + 1) * part, :] = jnp.where(first, mix_ref[k, :part], mix_ref[k, part:])
    at = HOPS * part
    for i in range(2):
        left = wm_ref[:, i * LANES : (i + 1) * LANES]
        right = wm_ref[:, hid // 2 + i * LANES : hid // 2 + (i + 1) * LANES]
        block_ref[at + i * mr : at + (i + 1) * mr, :] = jnp.where(first, left, right).astype(BF16)


def stack_kernel(a_ref, b_ref, c_ref, d_ref, out_ref):
    for i, ref in enumerate((a_ref, b_ref, c_ref, d_ref)):
        out_ref[i] = ref[...]


def each_block(pos_ref, arrays):
    for which in range(2):
        half = pos_ref[1] if which == 0 else 1 - pos_ref[1]
        for t in range(4):
            for e in range(4):
                yield arrays[which * 4 + t].at[e], pos_ref[0] ^ (4 * e + t), half


HALF = LANES // 2
QUADS = HALF // 4


def store_grams(grams, out_ref):
    if out_ref.shape[0] == HOPS:
        for k in range(HOPS):
            out_ref[k] = grams[k]
        return
    lane = lane_of((HALF, LANES))
    blocks = [g[:HALF] for g in grams]
    for k in range(0, HOPS, 2):
        blocks.append(jnp.where(lane < HALF, pltpu.roll(grams[k][HALF:], HALF, 1), grams[k + 1][HALF:]))
    for i, block in enumerate(blocks):
        for j in range(QUADS):
            out_ref[i * QUADS + j] = block[4 * j : 4 * j + 4]


def load_grams(in_ref, gram_ref, rest_ref):
    if in_ref.shape[0] == HOPS:
        gram_ref[...] = in_ref[...]
        return
    for i in range(HOPS + HOPS // 2):
        for j in range(QUADS):
            rows = slice(4 * j, 4 * j + 4)
            if i < HOPS:
                gram_ref[i, rows, :] = in_ref[i * QUADS + j]
            else:
                rest_ref[i - HOPS, rows, :] = in_ref[i * QUADS + j]
    lane = lane_of((HALF, LANES))
    for k in range(HOPS):
        upper = jnp.concatenate([gram_ref[k, :HALF, :], jnp.zeros((HALF, LANES), F32)], axis=0)
        rest = rest_ref[k // 2]
        if k % 2 == 0:
            rest = pltpu.roll(rest, HALF, 1)
        gram_ref[k, HALF:, :] = jnp.where(lane < HALF, jnp.transpose(upper)[HALF:], rest)


def gather_kernel(idx_ref, tab_ref, *refs):
    i = pl.program_id(0)
    if len(refs) > 4:
        own_ref, x_ref, gram_ref, own_out, acc, pad, sem = refs
        copy = pltpu.make_async_copy(own_ref, own_out, sem)

        @pl.when(i == 0)
        def _():
            copy.start()

        @pl.when(i == pl.num_programs(0) - 1)
        def _():
            copy.wait()
    else:
        x_ref, gram_ref, acc, pad = refs
    width = tab_ref.shape[1]
    d_in = tab_ref.shape[0] // HOPS
    batch = idx_ref.shape[1]
    rows = lax.broadcasted_iota(jnp.int16, (width, batch), 0)
    hot = jnp.where(rows == (idx_ref[...] - i * width).astype(jnp.int16), BF16(1.0), BF16(0.0))
    part = dot(tab_ref[...].astype(BF16), hot, 1, 0)

    @pl.when(i == 0)
    def _():
        acc[...] = part

    @pl.when(i > 0)
    def _():
        acc[...] += part

    @pl.when(i == pl.num_programs(0) - 1)
    def _():
        row = lax.broadcasted_iota(jnp.int32, pad.shape, 0)
        pad[...] = jnp.where(row == d_in, 1.0, 0.0)
        grams = []
        for k in range(HOPS):
            pad[0:d_in, :] = acc[k * d_in : (k + 1) * d_in, :]
            x = pad[...].astype(BF16)
            x_ref[k] = x
            grams.append(dot(x, x, 1, 1))
        store_grams(grams, gram_ref)


def sum_spread_kernel(in_ref, out_ref):
    out_ref[...] = jnp.broadcast_to(jnp.sum(in_ref[...], axis=0, keepdims=True), out_ref.shape)


def three_terms(wide):
    terms = []
    for _ in range(3):
        terms.append(wide.astype(BF16))
        wide = wide - terms[-1].astype(F32)
    return terms


def exact_dot(low, wide):
    total = None
    for term in three_terms(wide):
        part = dot(low, term, 1, 0)
        total = part if total is None else total + part
    return total


def assemble_kernel(classes, pos_ref, order_ref, *refs):
    wb_ref, wm_out, wm_ref, sems = refs[8:]
    hid = wb_ref.shape[1]
    cb = hid // 16
    mr = wm_ref.shape[1] // 16
    part = cb // 2
    first = HOPS * part
    for ref, s, half in each_block(pos_ref, refs[:8]):
        rows = pl.ds(pl.multiple_of(s * mr, mr), mr)
        for i in range(2):
            wm_ref[half * 2 + i, rows, :] = ref[first + i * mr : first + (i + 1) * mr, :]
    stored = fetch((wm_ref,), (wm_out,), sems)
    for ref, s, half in each_block(pos_ref, refs[:8]):
        rows = pl.ds(pl.multiple_of(s * cb + half * part, part), part)
        for j in range(HOPS):
            wb_ref[j, rows, :] = ref[j * part : (j + 1) * part, :]
    lane = lane_of((hid, LANES))
    mixed = [wb_ref[j].astype(F32) for j in range(3)]
    tail = jnp.where((lane >= PCOL) & (lane < PCOL + 5 * HOPS), pltpu.roll(mixed[0], LANES + PCOL - ONE, 1), 0.0)
    tail = jnp.where(lane < FREE, pltpu.roll(mixed[1], LANES - ONE, 1), tail)
    tail = jnp.where((lane >= FREE) & (lane < classes), pltpu.roll(mixed[2], LANES + FREE - ONE, 1), tail)
    wb_ref[HOPS] = tail.astype(BF16)
    for j in range(3):
        wb_ref[j] = jnp.where(lane < ONE, mixed[j], 0.0).astype(BF16)
    stored()


def own_stats_kernel(count, pos_ref, in_ref, own_hbm, gram_ref, fix_ref, rest_ref, own_ref, sems):
    wait = fetch((own_hbm,), (own_ref,), sems)
    load_grams(in_ref, gram_ref, rest_ref)
    wait()
    rep = pos_ref[1]
    lane = lane_of(fix_ref.shape[1:])
    tail = own_ref[HOPS].astype(F32)
    for i in range(2):
        gram = gram_ref[rep * 2 + i]
        w = own_ref[rep * 2 + i]
        wg = exact_dot(w, gram)
        mean = wg[:, ONE : ONE + 1] / count
        second = jnp.sum(wg * w.astype(F32), axis=1, keepdims=True) / count
        inv = lax.rsqrt(second - mean * mean + EPS_NORM)
        gain = jnp.where(rep == 0, tail[:, PCOL + i : PCOL + i + 1], tail[:, PCOL + 2 + i : PCOL + 3 + i])
        block = wg - mean * gram[ONE : ONE + 1, :]
        for j, value in enumerate((mean, inv, gain * inv)):
            block = jnp.where(lane == ONE + j, value, block)
        fix_ref[i] = block


def stats_kernel(count, gram_ref, wb_ref, ws_ref, coef_ref, mu_ref, wt_ref):
    hid = wb_ref.shape[1]
    small = jnp.transpose(wb_ref[HOPS].astype(F32))
    row = lax.broadcasted_iota(jnp.int32, (16, hid), 0)

    def at(i):
        return small[PCOL + i : PCOL + i + 1, :]

    def columns(values):
        block = jnp.zeros((16, hid), F32)
        for i, value in enumerate(values):
            block = jnp.where(row == i, value, block)
        return jnp.transpose(jnp.concatenate([block, jnp.zeros((LANES - 16, hid), F32)], axis=0))

    mu_ref[...] = jnp.zeros_like(mu_ref)
    for k in range(HOPS):
        gram = gram_ref[k]
        mu_ref[k : k + 1, :] = gram[ONE : ONE + 1, :] / count
        wide = jnp.transpose(wb_ref[k].astype(F32))
        w = wide.astype(BF16)
        wt_ref[k] = w
        wg = None
        for term in three_terms(gram):
            part = dot(term, w, 1, 0)
            wg = part if wg is None else wg + part
        mean = wg[ONE : ONE + 1, :] / count
        second = jnp.sum(wg * wide, axis=0, keepdims=True) / count
        inv = lax.rsqrt(second - mean * mean + EPS_NORM)
        gain, shift, slope, join = at(k), at(HOPS + k), at(2 * HOPS + k), at(3 * HOPS + k)
        v = gain * inv
        half = 0.5 * v
        scaled = jnp.where(
            lax.broadcasted_iota(jnp.int32, wide.shape, 0) == ONE, 0.5 * shift - half * mean, half * wide
        )
        scaled = jnp.transpose(scaled)
        high = scaled.astype(BF16)
        ws_ref[k, :, 0:LANES] = high
        ws_ref[k, :, LANES : 2 * LANES] = (scaled - high.astype(F32)).astype(BF16)
        scale = 0.5 * (1.0 - join)
        coef_ref[k] = columns(
            (
                0.5 * (1.0 + slope),
                0.5 * (1.0 - slope),
                1.0 + join,
                1.0 - join,
                join / scale,
                scale,
                scale * v * slope,
                scale * 0.5 * v * (1.0 - slope),
            )
        )


def project_units(ws_ref, x_ref, k, rows):
    x = x_ref[k]
    return dot(ws_ref[k, rows, :], jnp.concatenate([x, x], axis=0), 1, 0)


def column_set(ref, hop, at, lanes):
    block = ref[hop, at, :]
    return [jnp.broadcast_to(block[:, i : i + 1], (ROWS, WIDE)) for i in lanes]


def merge_block(wm_ref, rows):
    return jnp.concatenate([wm_ref[i, rows, :] for i in range(wm_ref.shape[0])], axis=1)


def forward_kernel(
    x_ref, ws_ref, coef_ref, wt_ref, fix_ref, wm_hbm, joined_ref, pre2_ref, pay_ref, wt_out, fix_out, pre, wm_ref, sems
):
    wait = fetch((wm_hbm,), (wm_ref,), sems.at[pl.ds(2, 1)])
    stored = fetch((wt_ref, fix_ref), (wt_out, fix_out), sems)
    hid = ws_ref.shape[1]
    batch = x_ref.shape[2]
    per = hid // CHUNK
    jobs = [(k, c) for k in range(HOPS) for c in range(per)]

    def project(i):
        k, c = jobs[i]
        pre[i % 2] = project_units(ws_ref, x_ref, k, slice(c * CHUNK, (c + 1) * CHUNK))

    def units(i):
        k, c = jobs[i]
        for g in range(CHUNK // ROWS):
            at = slice(c * CHUNK + g * ROWS, c * CHUNK + (g + 1) * ROWS)
            cs = column_set(coef_ref, k, at, range(4))
            for b in range(batch // WIDE):
                lanes = slice(b * WIDE, (b + 1) * WIDE)
                u = pre[i % 2, g * ROWS : (g + 1) * ROWS, lanes]
                u = u * (cs[0] + cs[1] * jnp.tanh(u))
                joined_ref[k, at, lanes] = (u * (cs[2] + cs[3] * jnp.tanh(u))).astype(BF16)

    project(0)
    for i in range(len(jobs)):
        if i + 1 < len(jobs):
            project(i + 1)
        units(i)
        if i % per == per - 1:
            k = i // per
            if k == 0:
                wait()
            part = dot(merge_block(wm_ref, slice(k * hid, (k + 1) * hid)), joined_ref[k], 0, 0)
            if k == 0:
                pre2_ref[...] = part
            else:
                pre2_ref[...] += part
    value = pre2_ref[...]
    sums = jnp.concatenate([lane_sums(fold_lanes(value)), lane_sums(fold_lanes(value * value))], axis=0)
    pay_ref[...] = jnp.broadcast_to(sums[None], pay_ref.shape)
    stored()


def par_columns(wb_ref):
    return wb_ref[HOPS][:, PCOL:].astype(F32)[:, 4 * HOPS : 5 * HOPS]


def columns2(count, rows, par):
    mean = to_cols(rows, 0) / count
    inv = lax.rsqrt(to_cols(rows, 4) / count - mean * mean + EPS_NORM)
    shape = mean.shape
    gain = jnp.broadcast_to(par[:, 0:1], shape)
    shift = jnp.broadcast_to(par[:, 1:2], shape)
    slope = jnp.broadcast_to(par[:, 2:3], shape)
    return mean, inv, gain, shift, slope


def head_kernel(
    count, classes, got_ref, pre2_ref, wb_ref, lab_hbm, dy2_ref, pay_ref, class_ref, stat_ref, act, dact, cols, sums, lab_ref, sems
):
    wait = fetch((lab_hbm,), (lab_ref,), sems)
    hid, batch = dy2_ref.shape
    par = par_columns(wb_ref)
    mean, inv, gain, shift, slope = columns2(count, jnp.sum(got_ref[...], axis=0), par)
    stat_ref[0] = mean
    stat_ref[1] = inv
    cols[0] = 0.5 * gain * inv
    cols[1] = 0.5 * (shift - gain * inv * mean)
    cols[2] = 1.0 + slope
    cols[3] = 1.0 - slope
    reps = WIDE // LANES

    def tiled(c, at):
        return jnp.concatenate([cols[c, at, :]] * reps, axis=1)

    def first(g, carry):
        at = pl.ds(pl.multiple_of(g * ROWS, ROWS), ROWS)
        c = [tiled(i, at) for i in range(4)]
        for b in range(batch // WIDE):
            lanes = slice(b * WIDE, (b + 1) * WIDE)
            u = pre2_ref[at, lanes] * c[0] + c[1]
            act[at, lanes] = (u * (c[2] + c[3] * jnp.tanh(u))).astype(BF16)
        return carry

    lax.fori_loop(0, hid // ROWS, first, 0, unroll=8)
    tail = wb_ref[HOPS]
    wc = jnp.where(lane_of(tail.shape) < PCOL, tail.astype(F32), 0.0).astype(BF16)
    logits = dot(wc, act[...], 0, 0)
    live = -(-classes // 16) * 16
    row = lax.broadcasted_iota(jnp.int32, (live, batch), 0)
    logits = jnp.where(row < classes, logits[:live] + par[0:live, 3:4], -jnp.inf)
    top = jnp.max(logits, axis=0, keepdims=True)
    e = jnp.exp(logits - top)
    probs = e / jnp.sum(e, axis=0, keepdims=True)
    wait()
    dlog = (probs - jnp.where(row == lab_ref[...], 1.0, 0.0)).astype(BF16)
    dlog = jnp.concatenate([dlog, jnp.zeros((LANES - live, batch), BF16)], axis=0)
    grad_class = dot(act[...], dlog, 1, 1)
    bias = jnp.sum(dlog.astype(F32), axis=1, keepdims=True)
    dact[...] = dot(wc, dlog, 1, 0)

    def second(g, carry):
        at = pl.ds(pl.multiple_of(g * ROWS, ROWS), ROWS)
        c = [tiled(i, at) for i in range(4)]
        m = jnp.concatenate([stat_ref[0, at, :]] * reps, axis=1)
        v = jnp.concatenate([stat_ref[1, at, :]] * reps, axis=1)
        acc = [jnp.zeros((ROWS, WIDE), F32) for _ in range(3)]
        for b in range(batch // WIDE):
            lanes = slice(b * WIDE, (b + 1) * WIDE)
            p = pre2_ref[at, lanes]
            d = dact[at, lanes]
            u = p * c[0] + c[1]
            t = jnp.tanh(u)
            w = u * (1.0 - t)
            dy = d * (0.5 * (c[2] + c[3] * (t + w * (1.0 + t))))
            dy2_ref[at, lanes] = dy
            acc[0] = acc[0] + dy
            acc[1] = acc[1] + dy * ((p - m) * v)
            acc[2] = acc[2] + d * w
        for i in range(3):
            sums[i, at, :] = fold_lanes(acc[i])
        return carry

    lax.fori_loop(0, hid // ROWS, second, 0, unroll=8)
    pay = jnp.concatenate([lane_sums(sums[0]), lane_sums(sums[1])], axis=0)
    pay_ref[...] = jnp.broadcast_to(pay[None], pay_ref.shape)
    lane = lane_of((hid, LANES))
    slope_sum = jnp.sum(sums[2], axis=1, keepdims=True)
    bias = jnp.concatenate([bias, jnp.zeros((hid - LANES, 1), F32)], axis=0)
    block = jnp.where(lane < classes, grad_class, 0.0)
    block = jnp.where(lane == PCOL, slope_sum, block)
    class_ref[...] = jnp.where(lane == PCOL + 1, bias, block)


def turn_kernel(
    count, pos_ref, got_ref, stat_ref, wb_ref, pre2_ref, dy2_ref, joined_ref, class_ref, wm_hbm, dpre_ref, keep_ref, send_ref, sum2_ref, wm_ref, cols, sems
):
    wait = fetch((wm_hbm,), (wm_ref,), sems)
    hid, batch = dy2_ref.shape
    half = send_ref.shape[2]
    rows8 = jnp.sum(got_ref[...], axis=0)
    sum2_ref[...] = rows8
    mean, inv = stat_ref[0], stat_ref[1]
    v = jnp.broadcast_to(par_columns(wb_ref)[:, 0:1], mean.shape) * inv
    cols[0] = v
    cols[1] = v * to_cols(rows8, 0) / count
    cols[2] = v * inv * to_cols(rows8, 4) / count
    reps = WIDE // LANES
    for g in range(hid // ROWS):
        at = slice(g * ROWS, (g + 1) * ROWS)
        c = [jnp.concatenate([cols[i, at, :]] * reps, axis=1) for i in range(3)]
        m = jnp.concatenate([stat_ref[0, at, :]] * reps, axis=1)
        for b in range(batch // WIDE):
            lanes = slice(b * WIDE, (b + 1) * WIDE)
            value = c[0] * dy2_ref[at, lanes] - c[1] - (pre2_ref[at, lanes] - m) * c[2]
            dpre_ref[at, lanes] = value.astype(BF16)
    mine = pl.ds(pl.multiple_of(pos_ref[1] * half, half), half)
    theirs = pl.ds(pl.multiple_of((1 - pos_ref[1]) * half, half), half)
    dp, size, _ = send_ref.shape
    per = dp // HOPS
    mr = hid // per
    cb = hid // dp
    for k in range(HOPS):
        other = dot(joined_ref[k], dpre_ref[theirs, :], 1, 1).astype(BF16)
        own = dot(joined_ref[k], dpre_ref[mine, :], 1, 1)
        for j in range(per):
            send_ref[k * per + j, 0:mr, :] = other[j * mr : (j + 1) * mr]
            keep_ref[k * per + j, 0:mr, :] = own[j * mr : (j + 1) * mr]
    first = pos_ref[1] == 0
    for s in range(dp):
        block = class_ref[s * cb : (s + 1) * cb, :]
        wide = jnp.concatenate([block[: cb // 2], block[cb // 2 :]], axis=1)
        send_ref[s, mr:size, :] = jnp.where(first, 0.0, wide).astype(BF16)
        keep_ref[s, mr:size, :] = jnp.where(first, wide, 0.0)
    wait()


SMALLS = 4


def back_kernel(own, first, count, pos_ref, dpre_ref, x_ref, ws_ref, coef_ref, mu_ref, wm_ref, wt_hbm, *refs):
    if own:
        recv_ref, refs = refs[0], refs[1:]
    b_ref, a_out, pre, dj, dyv, sums, a_ref, wt_ref, out_sems = refs
    hid = wt_ref.shape[2]
    batch = x_ref.shape[2]
    per = hid // CHUNK
    jobs = [(k, c) for k in range(count) for c in range(per)]
    base = 2 * (pos_ref[1] if own else 1 - pos_ref[1]) + first
    dp, _, cb, _ = b_ref.shape
    copies = []
    wait_wt = fetch((wt_hbm.at[pl.ds(base, count)],), (wt_ref,), out_sems.at[pl.ds(count, 1)])

    def project(i):
        k, c = jobs[i]
        rows = slice(c * CHUNK, (c + 1) * CHUNK)
        pre[i % 2] = project_units(ws_ref, x_ref, base + k, rows)
        at = pl.ds(pl.multiple_of((base + k) * hid + c * CHUNK, CHUNK), CHUNK)
        dj[i % 2] = dot(merge_block(wm_ref, at), dpre_ref[...], 1, 0)

    def units(i):
        k, c = jobs[i]
        for g in range(CHUNK // ROWS):
            at = slice(c * CHUNK + g * ROWS, c * CHUNK + (g + 1) * ROWS)
            here = slice(g * ROWS, (g + 1) * ROWS)
            p1, q1, s2, s1, r1 = column_set(coef_ref, base + k, at, (0, 1, 4, 6, 7))
            one = jnp.zeros((ROWS, WIDE), F32)
            two = jnp.zeros((ROWS, WIDE), F32)
            for b in range(batch // WIDE):
                lanes = slice(b * WIDE, (b + 1) * WIDE)
                u = pre[i % 2, here, lanes]
                t = jnp.tanh(u)
                u2 = u * (p1 + q1 * t)
                t2 = jnp.tanh(u2)
                d = dj[i % 2, here, lanes]
                w = u2 * (1.0 - t2)
                two = two + d * w
                d = d * (s2 + (1.0 + t2) * (1.0 + w))
                w = u * (1.0 - t)
                one = one + d * w
                dyv[k, at, lanes] = (d * (s1 + r1 * ((1.0 + t) * (1.0 + w)))).astype(BF16)
            sums[k, 0, at, :] = fold_lanes(one)
            sums[k, 1, at, :] = fold_lanes(two)

    def close(k):
        if k == 0:
            wait_wt()
        w = wt_ref[k]
        a_ref[k] = dot(w, dyv[k], 1, 0)
        copies.append(fetch((a_ref.at[k],), (a_out.at[k],), out_sems.at[pl.ds(k, 1)]))
        block = dot(x_ref[base + k], dyv[k], 1, 1)
        row = lax.broadcasted_iota(jnp.int32, block.shape, 0)
        total = block[ONE : ONE + 1, :]
        center = jnp.transpose(jnp.broadcast_to(mu_ref[pl.ds(base + k, 1), :], (LANES, LANES)))
        block = jnp.where(row < ONE, block - jnp.concatenate([center] * (hid // LANES), axis=1) * total, 0.0)
        smalls = (
            total,
            jnp.sum(block * w.astype(F32), axis=0, keepdims=True),
            jnp.sum(jnp.transpose(sums[k, 0] * coef_ref[base + k, :, 5:6]), axis=0, keepdims=True),
            jnp.sum(jnp.transpose(sums[k, 1]), axis=0, keepdims=True),
        )
        for i, value in enumerate(smalls):
            block = jnp.where(row == ONE + i, value, block)
            if not own:
                block = jnp.where(row == ONE + SMALLS + i, value - value.astype(BF16).astype(F32), block)
        block = jnp.transpose(block)
        if own:
            received = jnp.concatenate([recv_ref[s, k] for s in range(dp)], axis=0).astype(F32)
            block = split_smalls(block + join_smalls(received))
        for s in range(dp):
            b_ref[s, k] = block[s * cb : (s + 1) * cb, :].astype(BF16)

    project(0)
    for i in range(len(jobs)):
        if i + 1 < len(jobs):
            project(i + 1)
        units(i)
        if i % per == per - 1:
            close(i // per)
    for done in copies:
        done()


def split_smalls(block):
    lane = lane_of(block.shape)
    rest = block - block.astype(BF16).astype(F32)
    moved = pltpu.roll(rest, SMALLS, 1)
    return jnp.where((lane >= ONE + SMALLS) & (lane < ONE + 2 * SMALLS), moved, block)


def join_smalls(block):
    lane = lane_of(block.shape)
    moved = pltpu.roll(block, LANES - SMALLS, 1)
    block = jnp.where((lane >= ONE) & (lane < ONE + SMALLS), block + moved, block)
    return jnp.where(lane < ONE + SMALLS, block, 0.0)


def split_low_kernel(pos_ref, keep_ref, got_ref, o0_ref, o1_ref, o2_ref, o3_ref):
    low, high = pos_ref[0] % 4, pos_ref[0] // 4
    for t, ref in enumerate((o0_ref, o1_ref, o2_ref, o3_ref)):
        for e in range(4):
            j = jnp.where(pos_ref[1] == 0, e * 4 + (low ^ t), (high ^ t) * 4 + e)
            ref[e] = (keep_ref[j] + got_ref[j].astype(F32)).astype(ref.dtype)


def split_high_kernel(pos_ref, own_ref, g1_ref, g2_ref, g3_ref, o0_ref, o1_ref, o2_ref, o3_ref):
    mine = jnp.where(pos_ref[1] == 0, pos_ref[0] // 4, pos_ref[0] % 4)
    for t, ref in enumerate((o0_ref, o1_ref, o2_ref, o3_ref)):
        j = mine ^ t
        value = own_ref[j] + g1_ref[j].astype(F32) + g2_ref[j].astype(F32) + g3_ref[j].astype(F32)
        ref[...] = value.astype(ref.dtype)


def owner_kernel(
    count, classes, pos_ref, got_ref, sum2_ref, w0_ref, w1_ref, w2_ref, w3_ref, *refs
):
    late = (len(refs) - 6) // 2
    grad_ref, pay_ref = refs[1 + late : 3 + late]
    fix_ref, sems, late_sems = refs[3 + 2 * late :]
    wait = fetch(refs[:1], (fix_ref,), sems)
    brought = fetch(refs[1 : 1 + late], refs[3 + late : 3 + 2 * late], late_sems)
    _, _, cb, _ = got_ref.shape
    total = jnp.sum(got_ref[...].astype(F32), axis=0)
    rep = pos_ref[1]
    lane = lane_of((cb, LANES))
    squares = jnp.zeros((1, 1), F32)
    spread = jnp.zeros((cb, LANES), F32)

    def all_sum(v):
        return jnp.sum(jnp.sum(v, axis=1, keepdims=True), axis=0, keepdims=True)

    others = w1_ref[...].astype(F32) + w2_ref[...].astype(F32) + w3_ref[...].astype(F32)
    wide = w0_ref[...].astype(F32) + others
    mr = wide.shape[0] - cb // 2
    merge = wide[:mr]
    squares = squares + all_sum(merge * merge)
    at = 2 * cb
    for i in range(2):
        grad_ref[at + i * mr : at + (i + 1) * mr, :] = merge[:, i * LANES : (i + 1) * LANES]
    at = at + 2 * mr
    block = jnp.concatenate([wide[mr:, :LANES], wide[mr:, LANES:]], axis=0)
    shift_own = own_column(sum2_ref, 0, pos_ref[0], cb)
    gain_own = own_column(sum2_ref, 4, pos_ref[0], cb)
    block = jnp.where(lane == PCOL + 2, gain_own, block)
    block = jnp.where(lane == PCOL + 3, shift_own, block)
    grad_ref[at : at + cb, :] = block
    squares = squares + jnp.where(rep == 0, all_sum(block * block), 0.0)
    wait()
    for i in range(2):
        b = join_smalls(total[i])
        wg = fix_ref[i]
        mean, inv, v = [wg[:, ONE + j : ONE + j + 1] for j in range(3)]
        s = b[:, ONE : ONE + 1]
        g = inv * b[:, ONE + 1 : ONE + 2]
        beta = inv * g / count
        alpha = s / count - beta * mean
        fixed = jnp.where(lane < ONE, b - beta * wg, 0.0)
        fixed = jnp.where(lane == ONE, g / v, fixed)
        fixed = jnp.where(lane == ONE + 1, s / v, fixed)
        fixed = jnp.where(lane == ONE + 2, b[:, ONE + 2 : ONE + 3], fixed)
        fixed = jnp.where(lane == ONE + 3, b[:, ONE + 3 : ONE + 4], fixed)
        grad_ref[i * cb : (i + 1) * cb, :] = fixed
        squares = squares + all_sum(fixed * fixed)
        spread = jnp.where(lane == 2 * i, alpha, spread)
        spread = jnp.where(lane == 2 * i + 1, beta, spread)
    rows = jnp.transpose(jnp.concatenate([spread, jnp.zeros((LANES - cb, LANES), F32)], axis=0))[0:8]
    packed = jnp.concatenate([rows[i : i + 1, :cb] for i in range(4)], axis=1)
    if 4 * cb < LANES:
        packed = jnp.concatenate([packed, jnp.zeros((1, LANES - 4 * cb), F32)], axis=1)
    pay = jnp.concatenate([packed, jnp.where(lane_of((1, LANES)) == 0, squares, 0.0)], axis=0)
    pay_ref[...] = jnp.broadcast_to(pay[None], pay_ref.shape)
    brought()


def own_column(ref, first, me, cb):
    block = (me * cb) // LANES
    row = ref[pl.ds(first + block, 1), :]
    lane = lane_of((cb, LANES))
    sub = lax.broadcasted_iota(jnp.int32, (cb, LANES), 0)
    hit = lane == sub + (me * cb) % LANES
    return jnp.sum(jnp.where(hit, jnp.broadcast_to(row, (cb, LANES)), 0.0), axis=1, keepdims=True)


def adam_into(weight_ref, moment_ref, square_ref, grad, scale, rate, outs, at=Ellipsis):
    new_ref, new_m_ref, new_s_ref, copy_ref = outs
    weight = weight_ref[at]
    clipped = grad * scale
    moment = 0.9 * moment_ref[at] + 0.1 * clipped
    square = 0.999 * square_ref[at] + 0.001 * clipped * clipped
    fix_one = 1.0 - 0.9**STEP
    fix_two = 1.0 - 0.999**STEP
    update = moment / fix_one / (jnp.sqrt(square / fix_two) + 1e-08) + 0.01 * weight
    new = weight - rate * update
    new_ref[at] = new
    new_m_ref[at] = moment
    new_s_ref[at] = square
    copy_ref[at] = new.astype(BF16)


def final_kernel(pos_ref, got_ref, mine_ref, other_ref, x_ref, wt_ref, own_ref, sent_ref, *refs):
    states, outs_hbm, norm_ref, rows_hbm = refs[:12], refs[12:28], refs[28], refs[29]
    outs, rows_ref, out_sems = refs[30:46], refs[46], refs[47]
    weights, firsts, seconds = states[0:4], states[4:8], states[8:12]
    n = got_ref.shape[0]
    cb = weights[0].shape[1]
    blocks = 4
    per = n // 2 // blocks
    lane = lane_of((blocks, LANES))
    parts = [[jnp.zeros((blocks, LANES), F32) for _ in range(4)] for _ in range(2)]
    for r in range(2):
        for j in range(per):
            rows = [got_ref[(b * per + j) * 2 + r, 0:1, :] for b in range(blocks)]
            rows = jnp.concatenate(rows, axis=0)
            here = (lane >= j * cb) & (lane < (j + 1) * cb)
            for i in range(4):
                shift = (j - i) * cb % LANES
                moved = pltpu.roll(rows, shift, 1) if shift else rows
                parts[r][i] = jnp.where(here, moved, parts[r][i])

    def spread_row(r, i):
        return jnp.concatenate([parts[r][i][b : b + 1] for b in range(blocks)], axis=1)

    squares = jnp.sum(got_ref[...], axis=0)[1:2, :]
    norm = jnp.sqrt(jnp.sum(squares, axis=1, keepdims=True))
    norm_ref[...] = norm
    scale = 1.0 / jnp.maximum(norm, 1.0)

    d_in = weights[0].shape[2]
    mr = weights[1].shape[0]
    classes = weights[2].shape[1]
    first = pos_ref[1] == 0
    mine, other = mine_ref[...], other_ref[...]
    low = jnp.where(first, mine, other)
    high = jnp.where(first, other, mine)
    stores = []
    fixes = []
    for k in range(HOPS):
        r, i = k // 2, k % 2
        alpha, beta = spread_row(r, 2 * i), spread_row(r, 2 * i + 1)
        low_w = wt_ref[k]
        right = jnp.where(lax.broadcasted_iota(jnp.int32, low_w.shape, 0) == ONE, alpha, low_w.astype(F32) * beta)
        high_part = right.astype(BF16)
        fix = dot(low_w, high_part, 1, 1) + dot(low_w, (right - high_part.astype(F32)).astype(BF16), 1, 1)
        high_part = fix.astype(BF16)
        fixes.append(jnp.concatenate([high_part, (fix - high_part.astype(F32)).astype(BF16)], axis=1))
    for k in range(HOPS):
        r, i = k // 2, k % 2
        value = jnp.where(pos_ref[1] == r, own_ref[i], sent_ref[i])
        value = value - dot(fixes[k], jnp.concatenate([x_ref[k], x_ref[k]], axis=0), 1, 0)
        rows_ref[k * d_in : (k + 1) * d_in, :] = value[:d_in]
        if i == 1:
            part = pl.ds(r * 2 * d_in, 2 * d_in)
            stores.append(fetch((rows_ref.at[part, :],), (rows_hbm.at[part, :],), out_sems.at[pl.ds(16 + r, 1)]))

    def group(i):
        return [o for o in outs[i::4]]

    hops = [low[0:cb], low[cb : 2 * cb], high[0:cb], high[cb : 2 * cb]]
    for k in range(HOPS):
        adam_into(weights[0], firsts[0], seconds[0], hops[k][:, :d_in], scale, 0.05, group(0), k)
    at = 2 * cb
    for half, part in enumerate((low, high)):
        for i in range(2):
            lanes = (slice(None), slice((2 * half + i) * LANES, (2 * half + i + 1) * LANES))
            grad = part[at + i * mr : at + (i + 1) * mr]
            adam_into(weights[1], firsts[1], seconds[1], grad, scale, 0.05, group(1), lanes)
    at = at + 2 * mr
    block = low[at : at + cb]
    adam_into(weights[2], firsts[2], seconds[2], block[:, :classes], scale, 0.05, group(2))
    lane = lane_of((cb, LANES))
    small = jnp.zeros((cb, LANES), F32)
    for kind in range(4):
        for k in range(HOPS):
            small = jnp.where(lane == kind * HOPS + k, hops[k][:, ONE + kind : ONE + kind + 1], small)
    for i, source in enumerate((2, 3, 0, 1)):
        small = jnp.where(lane == 4 * HOPS + i, block[:, PCOL + source : PCOL + source + 1], small)
    small = jnp.transpose(jnp.concatenate([small, jnp.zeros((LANES - cb, LANES), F32)], axis=0))
    adam_into(weights[3], firsts[3], seconds[3], small[: weights[3].shape[0], :cb], scale, 0.3, group(3))
    stores.append(fetch(outs, outs_hbm, out_sems))
    for done in stores:
        done()


def flip(value, mask, dp):
    return lax.ppermute(value, "dp", [(i, i ^ mask) for i in range(dp)])


def turn_flip(value, digit, dp, stage):
    pairs = []
    for i in range(dp):
        for core in range(2):
            mask = digit if (core + stage) % 2 else 4 * digit
            pairs.append((i * 2 + core, (i ^ mask) * 2 + core))
    return lax.ppermute(value, BOTH, pairs)


def swap(value):
    return lax.ppermute(value, "rep", [(0, 1), (1, 0)])


def exchange(value):
    return lax.all_to_all(value, BOTH, 0, 0, tiled=True)


def weights_plain(wbt, wc, sp, wm, dp):
    cb, classes = wc.shape
    mr, hid = wm.shape
    own = jnp.zeros((HOPS + 1, cb, LANES), BF16)
    own = own.at[:HOPS, :, : wbt.shape[2]].set(wbt.astype(BF16))
    own = own.at[HOPS, :, :classes].set(wc.astype(BF16))
    own = own.at[HOPS, :, PCOL : PCOL + sp.shape[0]].set(sp.T.astype(BF16))
    wb = lax.all_gather(own, "dp", axis=1, tiled=True)
    whole = lax.all_gather(wm.astype(BF16), "dp", axis=0, tiled=True)
    return own, wb, whole.reshape(HOPS * hid, hid // LANES, LANES).transpose(1, 0, 2)


def on_device(table, batch_index, labels, *state):
    weights, firsts, seconds = state[0:4], state[4:8], state[8:12]
    dp, rep = lax.axis_size("dp"), lax.axis_size("rep")
    n = dp * rep
    staged = dp == 16 and rep == 2
    me, core = lax.axis_index("dp"), lax.axis_index("rep")
    pos = jnp.stack([me, core]).astype(jnp.int32)
    batch = batch_index.shape[0]
    count = float(batch * n)
    nodes, width = table.shape
    cb = weights[0].shape[2]
    mr, hid = weights[1].shape
    classes = weights[2].shape[1]
    half = hid // 2
    lhs = [v.transpose(0, 2, 1) for v in (weights[0], firsts[0], seconds[0])]
    idx = batch_index.reshape(1, batch)
    lab = labels.reshape(1, batch)

    if staged:
        with jax.named_scope("prep"):
            sources = (lhs[0], weights[2], weights[3], weights[1])
            size = HOPS * cb // 2 + 2 * mr
            own, block = call(
                prep_kernel,
                [vmem((HOPS + 1, cb, LANES), BF16), sds((size, LANES), BF16)],
                pos, *sources,
                smem=(0,), hbm=(1, 2, 3, 4),
                scratch=[pltpu.VMEM(v.shape, F32) for v in sources]
                + [pltpu.VMEM((HOPS, cb, LANES), BF16), pltpu.SemaphoreType.DMA((4,))],
            )
        far = [flip(block, 4 * k, dp) for k in range(1, 4)]

    with jax.named_scope("gather"):
        step = 2048
        sums = (6 * QUADS, 4, LANES) if 6 * QUADS % n == 0 else (HOPS, LANES, LANES)
        passed = [own] if staged else []
        x, gram, *made = call(
            gather_kernel,
            [vmem((HOPS, LANES, batch), BF16), hbm_out(sums)] + [hbm_out(v.shape, v.dtype) for v in passed],
            pltpu.with_memory_space_constraint(idx, pltpu.HBM),
            pltpu.with_memory_space_constraint(table.T, pltpu.HBM),
            *passed,
            grid=(nodes // step,),
            in_specs=[
                pl.BlockSpec((1, batch), lambda i: (0, 0)),
                pl.BlockSpec((width, step), lambda i: (0, i)),
            ]
            + [pl.BlockSpec(memory_space=pltpu.VMEM) for _ in passed],
            out_specs=(
                pl.BlockSpec((HOPS, LANES, batch), lambda i: (0, 0, 0)),
                pl.BlockSpec(sums, lambda i: (0, 0, 0)),
            )
            + tuple(pl.BlockSpec(memory_space=pltpu.HBM) for _ in passed),
            scratch=[pltpu.VMEM((width, batch), F32), pltpu.VMEM((LANES, batch), F32)]
            + [pltpu.SemaphoreType.DMA for _ in passed],
            mib=24,
        )
        if staged:
            own = made[0]
    with jax.named_scope("gram_sum"):
        parts = gram.reshape(n, -1, *sums[1:]) if sums[1] == 4 else gram.reshape(n, -1, LANES)
        if staged:
            (stacked,) = call(stack_kernel, [sds((4,) + block.shape, BF16)], block, *far)
            parts, stacked = lax.optimization_barrier((parts, stacked))
        parts = exchange(parts)
        (parts,) = call(sum_spread_kernel, [hbm_out(parts.shape)], parts)
        gram = exchange(parts).reshape(sums)
    if not staged:
        own, wb, wm = weights_plain(lhs[0], weights[2], weights[3], weights[1], dp)
    with jax.named_scope("own_stats"):
        gram, fix = call(
            functools.partial(own_stats_kernel, count),
            [vmem((HOPS, LANES, LANES)), vmem((2, cb, LANES))],
            pos, gram, own,
            smem=(0,), hbm=(2,),
            scratch=[
                pltpu.VMEM((HOPS // 2, HALF, LANES), F32),
                pltpu.VMEM(own.shape, BF16),
                pltpu.SemaphoreType.DMA((1,)),
            ],
        )
    if staged:
        mine = [stacked] + [flip(stacked, t, dp) for t in range(1, 4)]
        mine = mine[:1] + [lax.optimization_barrier((v, parts))[0] for v in mine[1:]]
        with jax.named_scope("weights"):
            whole = (hid // LANES, HOPS * hid, LANES)
            wb, wm = call(
                functools.partial(assemble_kernel, classes),
                [vmem((HOPS + 1, hid, LANES), BF16), hbm_out(whole, BF16)],
                pos, fix, *mine, *[swap(v) for v in mine],
                smem=(0,),
                out_specs=(pl.BlockSpec(memory_space=pltpu.VMEM), pl.BlockSpec(memory_space=pltpu.HBM)),
                scratch=[pltpu.VMEM(whole, BF16), pltpu.SemaphoreType.DMA((1,))],
            )
    with jax.named_scope("stats"):
        ws, coef, mu, wt = call(
            functools.partial(stats_kernel, count),
            [
                vmem((HOPS, hid, 2 * LANES), BF16),
                vmem((HOPS, hid, LANES)),
                vmem((8, LANES)),
                vmem((HOPS, LANES, hid), BF16),
            ],
            gram, wb,
        )
    with jax.named_scope("forward"):
        joined, pre2, pay, wt, fix = call(
            forward_kernel,
            [vmem((HOPS, hid, batch), BF16), vmem((hid, batch)), sds((n, 8, LANES))]
            + [hbm_out(v.shape, v.dtype) for v in (wt, fix)],
            x, ws, coef, wt, fix, wm,
            hbm=(5,),
            out_specs=tuple(pl.BlockSpec(memory_space=m) for m in (pltpu.VMEM,) * 3 + (pltpu.HBM,) * 2),
            scratch=[
                pltpu.VMEM((2, CHUNK, batch), F32),
                pltpu.VMEM(wm.shape, BF16),
                pltpu.SemaphoreType.DMA((3,)),
            ],
        )
    got = exchange(pay)
    with jax.named_scope("head"):
        dy2, pay, block2, stat = call(
            functools.partial(head_kernel, count, classes),
            [vmem((hid, batch)), sds((n, 8, LANES)), vmem((hid, LANES)), vmem((2, hid, LANES))],
            got, pre2, wb, lab,
            hbm=(3,),
            scratch=[
                pltpu.VMEM((hid, batch), BF16),
                pltpu.VMEM((hid, batch), F32),
                pltpu.VMEM((4, hid, LANES), F32),
                pltpu.VMEM((3, hid, LANES), F32),
                pltpu.VMEM(lab.shape, lab.dtype),
                pltpu.SemaphoreType.DMA((1,)),
            ],
            flops=6 * batch * hid * LANES,
        )
    got = exchange(pay)
    with jax.named_scope("turn"):
        rows = mr + cb // 2
        dpre, keep, send, sum2, wm = call(
            functools.partial(turn_kernel, count),
            [
                vmem((hid, batch), BF16),
                sds((dp, rows, half)),
                sds((dp, rows, half), BF16),
                vmem((8, LANES)),
                vmem(wm.shape, BF16),
            ],
            pos, got, stat, wb, pre2, dy2, joined, block2, wm,
            smem=(0,), hbm=(8,),
            scratch=[pltpu.VMEM((3, hid, LANES), F32), pltpu.SemaphoreType.DMA((1,))],
            flops=2 * batch * HOPS * hid * hid,
        )

    def back(own_hops, first, num, *more, after=()):
        outs = [(hbm_out if own_hops else sds)((dp, num, cb, LANES), BF16), hbm_out((num, LANES, batch))]
        with jax.named_scope("back"):
            return call(
                functools.partial(back_kernel, own_hops, first, num),
                outs,
                pos, dpre, x, ws, coef, mu, wm, wt, *more,
                smem=(0,),
                hbm=(7,),
                after=after,
                out_specs=(pl.BlockSpec(memory_space=pltpu.VMEM), pl.BlockSpec(memory_space=pltpu.HBM)),
                scratch=[
                    pltpu.VMEM((2, CHUNK, batch), F32),
                    pltpu.VMEM((2, CHUNK, batch), F32),
                    pltpu.VMEM((num, hid, batch), BF16),
                    pltpu.VMEM((num, 2, hid, LANES), F32),
                    pltpu.VMEM((num, LANES, batch), F32),
                    pltpu.VMEM((num, LANES, hid), BF16),
                    pltpu.SemaphoreType.DMA((num + 1,)),
                ],
                mib=16,
            )

    recv = swap(send)
    with jax.named_scope("merge_sum"):
        sent_b, sent_a = back(False, 0, 2)
        recv_b = swap(sent_b)
        if staged:
            shape = (4, rows, half)
            low = call(
                split_low_kernel,
                [vmem(shape)] + [sds(shape, BF16)] * 3,
                pos, keep, recv,
                smem=(0,),
                after=(sent_a,),
            )
            away, recv_b = lax.optimization_barrier((low[1:], recv_b))
            moved = [turn_flip(away[t - 1], t, dp, 1) for t in (3, 2, 1)]
            kept_b, kept_a = back(True, 0, 2, recv_b)
            kept_b, moved = lax.optimization_barrier((kept_b, moved))
            high = call(
                split_high_kernel,
                [sds(shape[1:])] + [sds(shape[1:], BF16)] * 3,
                pos, low[0], *moved,
                smem=(0,),
            )
            wide = [high[0]] + [turn_flip(high[t], t, dp, 0) for t in range(1, 4)]
        else:
            kept_b, kept_a = back(True, 0, 2, recv_b)
            total = lax.psum_scatter(keep + recv.astype(F32), "dp", scatter_dimension=0)
            wide = [total] + [jnp.zeros_like(total)] * 3
    with jax.named_scope("branch_sum"):
        got_b = lax.all_to_all(kept_b, "dp", 0, 0, tiled=True)
    with jax.named_scope("owner"):
        tr = [(lhs[i],) + tuple(s[1:]) for i, s in enumerate((weights, firsts, seconds))]
        last = (wt, kept_a, sent_a, *tr[0], *tr[1], *tr[2])
        shares, pay, *last = call(
            functools.partial(owner_kernel, count, classes),
            [sds((3 * cb + 2 * mr, LANES)), hbm_out((n, 2, LANES))] + [vmem(v.shape, v.dtype) for v in last],
            pos, got_b, sum2, *wide, fix, *last,
            smem=(0,),
            hbm=tuple(range(7, 8 + len(last))),
            scratch=[
                pltpu.VMEM(fix.shape, F32),
                pltpu.SemaphoreType.DMA((1,)),
                pltpu.SemaphoreType.DMA((len(last),)),
            ],
        )
    theirs = swap(shares)
    got = exchange(pay)
    with jax.named_scope("final"):
        shapes = [t.shape for t in tr[0]]
        outs = []
        for dtype in (F32, F32, F32, BF16):
            outs += [sds(s, dtype) for s in shapes]
        outs += [sds((1, 1)), sds((width, batch))]
        res = call(
            final_kernel, outs, pos, got, shares, theirs, x, *last,
            smem=(0,),
            out_specs=tuple(pl.BlockSpec(memory_space=pltpu.VMEM if i == 16 else pltpu.HBM) for i in range(18)),
            scratch=[pltpu.VMEM(v.shape, v.dtype) for i, v in enumerate(outs) if i != 16]
            + [pltpu.SemaphoreType.DMA((18,))],
        )
    result = list(res[:16])
    for i in range(0, 16, 4):
        result[i] = result[i].transpose(0, 2, 1)
    return (*result, res[16].reshape(()), res[17].T)


def solution(mesh):
    tables = (P(BOTH, None), P(BOTH), P(BOTH))
    params = (P(None, None, "dp"), P("dp", None), P("dp", None), P(None, "dp"))
    return jax.shard_map(
        on_device,
        mesh=mesh,
        in_specs=tables + params * 3,
        out_specs=params * 4 + (P(), P(BOTH, None)),
        check_vma=False,
    )
```
